32 devices in a mesh: dp: 16 (over z, y, x), head: 2 (over core).
Axes of the slice: x: 2, y: 2, z: 4, core: 2. Of those that a mesh axis runs over, the one named last changes fastest.
Arguments:
- tokens: bfloat16 [8192, 2048], P('dp'), may hold values from -6 to 6
- seq_count: int32 [16], P('dp'), may hold values from 1 to 2
- valid_len: int32 [32], P('dp'), may hold values from 128 to 256
- attn_gain: bfloat16 [2048], P('dp'), may hold values from 0.5 to 1.5
- ffn_gain: bfloat16 [2048], P('dp'), may hold values from 0.5 to 1.5
- q_weight: bfloat16 [2048, 2048], P('dp', 'head'), may hold values from -0.25 to 0.25
- k_weight: bfloat16 [2048, 2048], P('dp', 'head'), may hold values from -0.25 to 0.25
- v_weight: bfloat16 [2048, 2048], P('dp', 'head'), may hold values from -0.125 to 0.125
- forget_weight: bfloat16 [2048, 256], P('dp', 'head'), may hold values from -0.125 to 0.125
- out_weight: bfloat16 [2048, 2048], P('dp', 'head'), may hold values from -1.5 to 1.5
- gate_weight: bfloat16 [2048, 5632], P('dp', 'head'), may hold values from -0.125 to 0.125
- up_weight: bfloat16 [2048, 5632], P('dp', 'head'), may hold values from -0.125 to 0.125
- down_weight: bfloat16 [2048, 5632], P('dp', 'head'), may hold values from -0.078125 to 0.078125
- cotangent: float32 [8192, 2048], P('dp'), may hold values from -6 to 6
Outputs:
- block_out: bfloat16 [8192, 2048], P('dp')
- input_grad: float32 [8192, 2048], P('dp')
- attn_gain_grad: float32 [2048], P('dp')
- ffn_gain_grad: float32 [2048], P('dp')
- q_grad: float32 [2048, 2048], P('dp', 'head')
- k_grad: float32 [2048, 2048], P('dp', 'head')
- v_grad: float32 [2048, 2048], P('dp', 'head')
- forget_grad: float32 [2048, 256], P('dp', 'head')
- out_grad: float32 [2048, 2048], P('dp', 'head')
- gate_grad: float32 [2048, 5632], P('dp', 'head')
- up_grad: float32 [2048, 5632], P('dp', 'head')
- down_grad: float32 [2048, 5632], P('dp', 'head')
The draws below stay inside these ranges and needn't reach their ends.
All inputs are finite; a program needn't handle non-finite values.
Results may differ from the reference program's by a relative error of at most 0.0089.
Values may be sent and summed in bfloat16 or wider, within the bound.
A program may use at most 256 MiB of HBM per device.

```python
import jax
import jax.numpy as jnp
from jax import lax

D = 2048
HEADS = 4
SLOTS = 64
FF = 5632
KDIM = 512
SEQ_LEN = 256
SEQ_DEV = 2
TOK_DEV = 512
SEQS = 32
TOKENS = 8192
N_DP = 16


def touch_ends(values, rng, least, largest):
    longest = values.shape.index(max(values.shape))
    spots = []
    for shift in (0, 1):
        where = [jax.random.randint(jax.random.fold_in(rng, axis), (), 0, length) for axis, length in enumerate(values.shape)]
        where[longest] = (where[longest] + shift) % values.shape[longest]
        spots.append(tuple(where))
    return values.at[spots[0]].set(least).at[spots[1]].set(largest)


def block_scale(rng, shape, cuts, smallest, top_value):
    def one(axis_at, shards_of):
        draws = jax.random.uniform(jax.random.fold_in(jax.random.fold_in(rng, 6), axis_at), (shards_of,), jnp.float32, smallest / len(cuts), top_value / len(cuts))
        return jnp.repeat(jnp.exp(draws), shape[axis_at] // shards_of).reshape((-1,) + (1,) * (len(shape) - axis_at - 1))

    level = one(*cuts[0])
    for cut in cuts[1:]:
        level = level * one(*cut)
    return level


def scatter_about(key, dims, deviation, most, shards=(), kind=jnp.bfloat16):
    values = deviation * jax.random.normal(key, dims, jnp.float32)
    if shards:
        values = values * block_scale(key, dims, shards, -0.22, 0.18)
    return jnp.clip(values, -most, most).astype(kind)


def setup_inputs(seed: int = 0) -> dict:
    splits = jax.random.split(jax.random.key(seed), 15)
    tokens = scatter_about(splits[0], (TOKENS, D), 1.0, 6.0, ((0, 16),))
    seq_count = touch_ends(jax.random.randint(splits[1], (N_DP,), 1, SEQ_DEV + 1), jax.random.fold_in(splits[1], 1), 1, SEQ_DEV).astype(jnp.int32)
    valid_len = touch_ends(jax.random.randint(splits[2], (SEQS,), SEQ_LEN // 2, SEQ_LEN + 1), jax.random.fold_in(splits[2], 1), SEQ_LEN // 2, SEQ_LEN).astype(jnp.int32)
    attn_gain = jnp.clip(1.0 + 0.1 * jax.random.normal(splits[3], (D,), jnp.float32), 0.5, 1.5).astype(jnp.bfloat16)
    ffn_gain = jnp.clip(1.0 + 0.1 * jax.random.normal(splits[4], (D,), jnp.float32), 0.5, 1.5).astype(jnp.bfloat16)
    q_weight = scatter_about(splits[5], (D, D), (D // 4) ** -0.5, 0.25, ((0, 16), (1, 2)))
    k_weight = scatter_about(splits[6], (D, D), (D // 4) ** -0.5, 0.25, ((0, 16), (1, 2)))
    v_weight = scatter_about(splits[7], (D, D), D ** -0.5, 0.125, ((0, 16), (1, 2)))
    forget_weight = scatter_about(splits[8], (D, HEADS * SLOTS), D ** -0.5, 0.125, ((0, 16), (1, 2)))
    out_weight = scatter_about(splits[9], (D, D), (max(4, D // 128)) ** -0.5, 1.5, ((0, 16), (1, 2)))
    gate_weight = scatter_about(splits[10], (D, FF), D ** -0.5, 0.125, ((0, 16), (1, 2)))
    up_weight = scatter_about(splits[11], (D, FF), D ** -0.5, 0.125, ((0, 16), (1, 2)))
    down_weight = scatter_about(splits[12], (D, FF), FF ** -0.5, 0.078125, ((0, 16), (1, 2)))
    cotangent = scatter_about(splits[13], (TOKENS, D), 1.0, 6.0, ((0, 16),), jnp.float32)
    return {"tokens": tokens, "seq_count": seq_count, "valid_len": valid_len, "attn_gain": attn_gain, "ffn_gain": ffn_gain, "q_weight": q_weight, "k_weight": k_weight, "v_weight": v_weight, "forget_weight": forget_weight, "out_weight": out_weight, "gate_weight": gate_weight, "up_weight": up_weight, "down_weight": down_weight, "cotangent": cotangent}


@jax.custom_vjp
def low(v):
    return lax.optimization_barrier(v.astype(jnp.bfloat16)).astype(jnp.float32)

@jax.custom_vjp
def low_back(v):
    return v

def low_keep(v):
    return (low(v), None)

def low_pass(kept, grad):
    return (grad,)

def back_keep(v):
    return (v, None)

def back_low(kept, grad):
    return (low(grad),)
low.defvjp(low_keep, low_pass)
low_back.defvjp(back_keep, back_low)

def einsum_high(form, left, right):
    return jnp.einsum(form, left, right, precision=lax.Precision.HIGHEST)

def matmul_high(left, right):
    return jnp.dot(left, right, precision=lax.Precision.HIGHEST)

def rms_norm(values, gain):
    return values * lax.rsqrt(lax.optimization_barrier(jnp.mean(values * values, axis=-1, keepdims=True)) + 1e-06) * gain

def swiglu(gate_vals, up_vals):
    return jax.nn.silu(gate_vals) * up_vals

def block_step(states, block):
    key_state, value_state = states
    query_block, key_block, value_block, forget_block = block
    width = query_block.shape[0]
    totals = jnp.cumsum(forget_block, axis=0)
    writes = -jnp.expm1(forget_block)
    order = jnp.arange(width, dtype=jnp.int32)
    lower = (order[:, None] >= order[None, :])[:, :, None]
    spread = jnp.where(lower, totals[:, None, :] - totals[None, :, :], 0.0)
    decays = jnp.where(lower, jnp.exp(spread), 0.0) * writes[None, :, :]
    products = einsum_high('td,id->ti', query_block, key_block)
    carried = jnp.exp(totals)
    scores = einsum_high('ti,tim->tm', products, decays) + carried * einsum_high('td,md->tm', query_block, key_state)
    weights = jax.nn.softmax(scores, axis=-1)
    mixing = einsum_high('tm,tim->ti', weights, decays)
    result = einsum_high('ti,id->td', mixing, value_block) + einsum_high('tm,md->td', weights * carried, value_state)
    final = totals[-1]
    tails = jnp.exp(final[None, :] - totals) * writes
    key_next = jnp.exp(final)[:, None] * key_state + einsum_high('im,id->md', tails, key_block)
    value_next = jnp.exp(final)[:, None] * value_state + einsum_high('im,id->md', tails, value_block)
    return ((key_next, value_next), result)

def scan_slots(query, keys, values_in, forget):
    width = min(64, SEQ_LEN)
    count = SEQ_LEN // width
    pieces = (query.reshape(count, width, KDIM), keys.reshape(count, width, KDIM), values_in.reshape(count, width, KDIM), forget.reshape(count, width, SLOTS))
    start = (jnp.zeros((SLOTS, KDIM), jnp.float32), jnp.zeros((SLOTS, KDIM), jnp.float32))
    ignored, outputs = lax.scan(jax.checkpoint(block_step), start, pieces)
    return outputs.reshape(SEQ_LEN, KDIM)

def mixer(query_proj, key_proj, value_proj, forget_proj):
    rows = query_proj.shape[0]
    seq_total = rows // SEQ_LEN
    head_total = forget_proj.shape[1] // SLOTS

    def split(values, width):
        shaped = values.reshape(seq_total, SEQ_LEN, head_total, width).transpose(0, 2, 1, 3)
        return shaped.reshape(seq_total * head_total, SEQ_LEN, width)
    query = split(jax.nn.silu(query_proj), KDIM) * KDIM ** (-0.5)
    keys = split(jax.nn.silu(key_proj), KDIM)
    values_in = split(value_proj, KDIM)
    forget = split(jax.nn.log_sigmoid(forget_proj) / 8.0, SLOTS)
    outputs = jax.vmap(scan_slots)(query, keys, values_in, forget)
    outputs = outputs.reshape(seq_total, head_total, SEQ_LEN, KDIM).transpose(0, 2, 1, 3)
    return outputs.reshape(rows, head_total * KDIM)

def forward(inputs, live, params):
    gain_attn, gain_ffn, w_query, w_key, w_value, w_forget, w_out, w_gate, w_up, w_down = params
    attn_in = low(rms_norm(inputs, gain_attn))
    query_proj = low_back(matmul_high(attn_in, w_query))
    key_proj = low_back(matmul_high(attn_in, w_key))
    value_proj = low_back(matmul_high(attn_in, w_value))
    forget_proj = low_back(matmul_high(attn_in, w_forget))
    mixed = low(mixer(query_proj, key_proj, value_proj, forget_proj))
    attn = low_back(matmul_high(mixed, w_out.T))
    resid = inputs + attn
    ffn_in = low(rms_norm(resid, gain_ffn))
    gate_vals = low_back(matmul_high(ffn_in, w_gate))
    up_vals = low_back(matmul_high(ffn_in, w_up))
    hidden = low(swiglu(gate_vals, up_vals))
    ffn = low_back(matmul_high(hidden, w_down.T))
    return live * (resid + ffn)

def reference(tokens, seq_count, valid_len, attn_gain, ffn_gain, q_weight, k_weight, v_weight, forget_weight, out_weight, gate_weight, up_weight, down_weight, cotangent):
    params = tuple((w.astype(jnp.float32) for w in (attn_gain, ffn_gain, q_weight, k_weight, v_weight, forget_weight, out_weight, gate_weight, up_weight, down_weight)))
    places = jnp.arange(TOKENS, dtype=jnp.int32)
    owners = places // TOK_DEV
    slot_ids = places % TOK_DEV // SEQ_LEN
    inside = places % SEQ_LEN
    live = ((slot_ids < seq_count[owners]) & (inside < valid_len[places // SEQ_LEN])).astype(jnp.float32)[:, None]
    seq_total = TOKENS // SEQ_LEN
    per_group = max(1, 4096 // SEQ_LEN)
    while seq_total % per_group != 0:
        per_group = per_group - 1
    group_rows = per_group * SEQ_LEN
    groups = TOKENS // group_rows
    pieces = (tokens.astype(jnp.float32).reshape(groups, group_rows, D), cotangent.astype(jnp.float32).reshape(groups, group_rows, D), live.reshape(groups, group_rows, 1))

    def step(totals, piece):
        inputs, grad_out, live_rows = piece
        outputs, backward = jax.vjp(lambda xin, pin: forward(xin, live_rows, pin), inputs, params)
        grad_in, grad_params = backward(grad_out)
        return (tuple((a + b for a, b in zip(totals, grad_params))), (outputs, grad_in))
    zeros = tuple((jnp.zeros_like(p) for p in params))
    totals, (outputs, grad_in) = lax.scan(step, zeros, pieces)
    return (outputs.reshape(TOKENS, D).astype(jnp.bfloat16), grad_in.reshape(TOKENS, D), totals[0], totals[1], totals[2], totals[3], totals[4], totals[5], totals[6], totals[7], totals[8], totals[9])
```

```python
import functools
import jax
import jax.numpy as jnp
from jax import lax
from jax.experimental import pallas as pl
from jax.experimental.pallas import tpu as pltpu
from jax.sharding import PartitionSpec as P

SLOTS = 64
KDIM = 512
SEQ_LEN = 256
HALF = 128
F32, BF16 = jnp.float32, jnp.bfloat16
WIDE = 3 * KDIM + 128
NT = (((1,), (1,)), ((), ()))
NN = (((1,), (0,)), ((), ()))
TN = (((0,), (0,)), ((), ()))
LEVELS = (8, 16, 32, 64)


def split(value):
    high = value.astype(BF16)
    return high, (value - high.astype(F32)).astype(BF16)


def dot3(left, right, dims):
    one = functools.partial(lax.dot_general, dimension_numbers=dims, preferred_element_type=F32)
    return one(left[0], right[0]) + (one(left[0], right[1]) + one(left[1], right[0]))


def silu_parts(value):
    gate = 1.0 / (1.0 + jnp.exp(-value))
    return gate, value * gate


def level_mask(size):
    row = lax.broadcasted_iota(jnp.int32, (HALF, HALF), 0) // size
    col = lax.broadcasted_iota(jnp.int32, (HALF, HALF), 1) // size
    return (row == col + 1) & (row % 2 == 1)


def band_mask(back):
    row = lax.broadcasted_iota(jnp.int32, (HALF, HALF), 0)
    col = lax.broadcasted_iota(jnp.int32, (HALF, HALF), 1)
    return (row == col + back) & (row // 8 == col // 8)


def down(value, back):
    return value if back == 0 else pltpu.roll(value, back, 0)


def up(value, back):
    return value if back == 0 else pltpu.roll(value, SEQ_LEN - back, 0)


def gates(forget):
    lane = lax.broadcasted_iota(jnp.int32, forget.shape, 1) < SLOTS
    place = lax.broadcasted_iota(jnp.int32, forget.shape, 0)
    forget = jnp.where(lane, forget, 0.0)
    tail = jnp.exp(-jnp.abs(forget))
    log_decay = (jnp.minimum(forget, 0.0) - jnp.log1p(tail)) * 0.125
    log_decay = jnp.where(lane, log_decay, 0.0)
    g = log_decay
    series = 1.0 + g * (1.0 / 7.0)
    for n in (6.0, 5.0, 4.0, 3.0, 2.0):
        series = 1.0 + g * (1.0 / n) * series
    writes = jnp.where(g > -0.3, -g * series, 1.0 - jnp.exp(g))
    writes = jnp.where(lane, writes, 0.0)
    ahead, behind = g, g
    for step in (1, 2, 4):
        ahead = ahead + jnp.where(place % 8 >= step, down(ahead, step), 0.0)
        behind = behind + jnp.where(place % 8 < 8 - step, up(behind, step), 0.0)
    behind = jnp.where(place % 8 < 7, up(behind, 1), 0.0)
    aheads, behinds = {8: ahead}, {8: behind}
    size = 8
    while size < HALF:
        first = ahead.reshape(SEQ_LEN // (2 * size), 2, size, 128)
        last = behind.reshape(SEQ_LEN // (2 * size), 2, size, 128)
        left, right = first[:, 0:1], first[:, 1:2]
        left_sum, right_sum = left[:, :, size - 1 :], right[:, :, size - 1 :]
        ahead = jnp.concatenate([left, right + left_sum], axis=1).reshape(SEQ_LEN, 128)
        behind = jnp.concatenate([last[:, 0:1] + right_sum, last[:, 1:2]], axis=1).reshape(SEQ_LEN, 128)
        size *= 2
        aheads[size], behinds[size] = ahead, behind
    return lane, place, g, writes, aheads, behinds


def near_decays(place, aheads, back):
    ahead = aheads[8]
    gap = jnp.where(place % 8 >= back, ahead - down(ahead, back), 0.0)
    return jnp.where(place % 8 >= back, jnp.exp(gap), 0.0)


def halves(value):
    return value[:HALF], value[HALF:]


def to_slots(blocks, cross, place, writes, aheads, behinds, nears):
    grow = {size: jnp.exp(aheads[size]) for size in LEVELS}
    keep = {size: split(jnp.exp(behinds[size]) * writes) for size in LEVELS}
    outs = []
    for half in range(2):
        here = slice(half * HALF, (half + 1) * HALF)
        block = blocks[half]
        parts = split(block)
        total = None
        for size in LEVELS:
            mask = level_mask(size)
            masked = tuple(jnp.where(mask, part, jnp.zeros_like(part)) for part in parts)
            term = grow[size][here] * dot3(masked, tuple(k[here] for k in keep[size]), NN)
            total = term if total is None else total + term
        for back in range(8):
            near = jnp.sum(jnp.where(band_mask(back), block, 0.0), axis=1, keepdims=True)
            total = total + near * nears[back][here]
        if half == 1:
            far = split((jnp.exp(behinds[HALF]) * writes)[:HALF])
            total = total + jnp.exp(aheads[HALF])[HALF:] * dot3(split(cross), far, NN)
        outs.append(total)
    return jnp.concatenate(outs, axis=0)


def to_tokens(slots, writes, aheads, behinds, nears):
    blocks = []
    for half in range(2):
        here = slice(half * HALF, (half + 1) * HALF)
        total = jnp.zeros((HALF, HALF), F32)
        for size in LEVELS:
            left = split((slots * jnp.exp(aheads[size]))[here])
            right = split((jnp.exp(behinds[size]) * writes)[here])
            total = jnp.where(level_mask(size), dot3(left, right, NT), total)
        for back in range(8):
            near = jnp.sum(slots[here] * nears[back][here], axis=1, keepdims=True)
            total = jnp.where(band_mask(back), near, total)
        blocks.append(total)
    left = split((slots * jnp.exp(aheads[HALF]))[HALF:])
    right = split((jnp.exp(behinds[HALF]) * writes)[:HALF])
    return blocks, dot3(left, right, NT)


def forward_kernel(q_ref, k_ref, v_ref, f_ref, o_ref, p_ref, s_ref, a_ref, b_ref):
    query = split(silu_parts(q_ref[...])[1] * KDIM ** (-0.5))
    keys = split(silu_parts(k_ref[...])[1])
    values = split(v_ref[...])
    lane, place, g, writes, aheads, behinds = gates(f_ref[...])
    nears = [near_decays(place, aheads, back) * down(writes, back) for back in range(8)]
    q0, q1 = tuple(x[:HALF] for x in query), tuple(x[HALF:] for x in query)
    k0, k1 = tuple(x[:HALF] for x in keys), tuple(x[HALF:] for x in keys)
    blocks = (dot3(q0, k0, NT), dot3(q1, k1, NT))
    cross = dot3(q1, k0, NT)
    scores = to_slots(blocks, cross, place, writes, aheads, behinds, nears)
    shown = jnp.where(lane, scores, -1e30)
    weights = jnp.exp(shown - jnp.max(shown, axis=1, keepdims=True))
    weights = jnp.where(lane, weights, 0.0)
    weights = weights / jnp.sum(weights, axis=1, keepdims=True)
    mixes, mix_cross = to_tokens(weights, writes, aheads, behinds, nears)
    v0 = tuple(x[:HALF] for x in values)
    o_ref[:HALF, :] = dot3(split(mixes[0]), v0, NN).astype(o_ref.dtype)
    row = jnp.concatenate([mix_cross, mixes[1]], axis=1)
    o_ref[HALF:, :] = dot3(split(row), values, NN).astype(o_ref.dtype)
    p_ref[...] = weights
    s_ref[...] = scores
    a_ref[:HALF, :] = jnp.concatenate([blocks[0], jnp.zeros_like(cross)], axis=1)
    a_ref[HALF:, :] = jnp.concatenate([cross, blocks[1]], axis=1)
    b_ref[:HALF, :] = jnp.concatenate([mixes[0], jnp.zeros_like(cross)], axis=1)
    b_ref[HALF:, :] = row


def backward_kernel(q_ref, k_ref, v_ref, f_ref, p_ref, s_ref, a_ref, b_ref, d_ref, out_ref):
    lane, place, g, writes, aheads, behinds = gates(f_ref[...])
    spans = [near_decays(place, aheads, back) for back in range(8)]
    nears = [spans[back] * down(writes, back) for back in range(8)]
    weights, scores = p_ref[...], s_ref[...]
    products, mixing = a_ref[...], b_ref[...]
    grad = split(d_ref[...])
    g0, g1 = tuple(x[:HALF] for x in grad), tuple(x[HALF:] for x in grad)
    values = split(v_ref[...])
    v0, v1 = tuple(x[:HALF] for x in values), tuple(x[HALF:] for x in values)
    m_parts = split(mixing)
    dv0 = dot3(tuple(x[:, :HALF] for x in m_parts), grad, TN)
    dv1 = dot3(tuple(x[HALF:, HALF:] for x in m_parts), g1, TN)
    out_ref[:HALF, 2 * KDIM : 3 * KDIM] = dv0.astype(BF16)
    out_ref[HALF:, 2 * KDIM : 3 * KDIM] = dv1.astype(BF16)
    mix_blocks = (dot3(g0, v0, NT), dot3(g1, v1, NT))
    mix_cross = dot3(g1, v0, NT)
    d_weights = to_slots(mix_blocks, mix_cross, place, writes, aheads, behinds, nears)
    inner = jnp.sum(weights * d_weights, axis=1, keepdims=True)
    d_scores = weights * (d_weights - inner)
    d_blocks, d_cross = to_tokens(d_scores, writes, aheads, behinds, nears)
    q_gate, q_act = silu_parts(q_ref[...])
    k_gate, k_act = silu_parts(k_ref[...])
    scale = KDIM ** (-0.5)
    query, keys = split(q_act * scale), split(k_act)
    k0 = tuple(x[:HALF] for x in keys)
    low = split(jnp.concatenate([d_cross, d_blocks[1]], axis=1))
    top = split(d_blocks[0])
    dq = jnp.concatenate([dot3(top, k0, NN), dot3(low, keys, NN)], axis=0)
    first = tuple(jnp.concatenate([t, l[:, :HALF]], axis=0) for t, l in zip(top, low))
    dk0 = dot3(first, query, TN)
    dk1 = dot3(tuple(x[:, HALF:] for x in low), tuple(x[HALF:] for x in query), TN)
    dk = jnp.concatenate([dk0, dk1], axis=0)
    out_ref[:, :KDIM] = (dq * scale * (q_gate + q_act * (1.0 - q_gate))).astype(BF16)
    out_ref[:, KDIM : 2 * KDIM] = (dk * (k_gate + k_act * (1.0 - k_gate))).astype(BF16)
    parts = []
    for half in range(2):
        here = slice(half * HALF, (half + 1) * HALF)
        both = jnp.concatenate([mix_blocks[half], products[here, here]], axis=0)
        both_parts = split(both)
        total = None
        for size in LEVELS:
            mask = level_mask(size)
            mask = jnp.concatenate([mask, mask], axis=0)
            grow = jnp.exp(aheads[size][here])
            right = split(jnp.concatenate([weights[here] * grow, d_scores[here] * grow], axis=0))
            left = tuple(jnp.where(mask, part, jnp.zeros_like(part)) for part in both_parts)
            term = jnp.exp(behinds[size][here]) * dot3(left, right, TN)
            total = term if total is None else total + term
        parts.append(total)
    grow = jnp.exp(aheads[HALF][HALF:])
    left = split(jnp.concatenate([mix_cross, products[HALF:, :HALF]], axis=0))
    right = split(jnp.concatenate([weights[HALF:] * grow, d_scores[HALF:] * grow], axis=0))
    parts[0] = parts[0] + jnp.exp(behinds[HALF][:HALF]) * dot3(left, right, TN)
    reach = jnp.concatenate(parts, axis=0)
    for back in range(8):
        mask = band_mask(back)
        near_mix = jnp.concatenate([jnp.sum(jnp.where(mask, mix_blocks[h], 0.0), axis=1, keepdims=True) for h in range(2)], axis=0)
        near_pro = jnp.concatenate(
            [jnp.sum(jnp.where(mask, products[h * HALF : (h + 1) * HALF, h * HALF : (h + 1) * HALF], 0.0), axis=1, keepdims=True) for h in range(2)],
            axis=0,
        )
        reach = reach + up((near_mix * weights + near_pro * d_scores) * spans[back], back)
    d_sum = weights * d_weights + d_scores * scores - writes * reach
    step = 1
    while step < SEQ_LEN:
        d_sum = d_sum + jnp.where(place < SEQ_LEN - step, up(d_sum, step), 0.0)
        step *= 2
    d_log = d_sum - reach * jnp.exp(g)
    d_forget = d_log * 0.125 / (1.0 + jnp.exp(f_ref[...]))
    out_ref[:, 3 * KDIM :] = jnp.where(lane, d_forget, 0.0).astype(BF16)


def spec(width, column):
    return pl.BlockSpec((SEQ_LEN, width), lambda i: (i, column))


IN_SPECS = [spec(KDIM, 0), spec(KDIM, 1), spec(KDIM, 2), spec(128, 3 * KDIM // 128)]


def mixer_forward(proj):
    rows = proj.shape[0]
    shape = lambda width, kind: jax.ShapeDtypeStruct((rows, width), kind)
    return pl.pallas_call(
        forward_kernel,
        grid=(rows // SEQ_LEN,),
        in_specs=IN_SPECS,
        out_specs=[spec(KDIM, 0), spec(128, 0), spec(128, 0), spec(SEQ_LEN, 0), spec(SEQ_LEN, 0)],
        out_shape=[shape(KDIM, BF16), shape(128, F32), shape(128, F32), shape(SEQ_LEN, F32), shape(SEQ_LEN, F32)],
        compiler_params=pltpu.CompilerParams(vmem_limit_bytes=48 << 20),
        cost_estimate=pl.CostEstimate(flops=rows * 3000000, bytes_accessed=rows * 10000, transcendentals=rows * 3000),
        name="mixer_forward",
    )(proj, proj, proj, proj)


def mixer_backward(proj, saved, grad):
    rows = proj.shape[0]
    weights, scores, products, mixing = saved
    return pl.pallas_call(
        backward_kernel,
        grid=(rows // SEQ_LEN,),
        in_specs=IN_SPECS + [spec(128, 0), spec(128, 0), spec(SEQ_LEN, 0), spec(SEQ_LEN, 0), spec(KDIM, 0)],
        out_specs=spec(WIDE, 0),
        out_shape=jax.ShapeDtypeStruct((rows, WIDE), BF16),
        compiler_params=pltpu.CompilerParams(vmem_limit_bytes=48 << 20),
        cost_estimate=pl.CostEstimate(flops=rows * 9000000, bytes_accessed=rows * 16000, transcendentals=rows * 5000),
        name="mixer_backward",
    )(proj, proj, proj, proj, weights, scores, products, mixing, grad)


PAD = 128 - SLOTS


class Ring:
    def __init__(self, count):
        self.count = count
        self.stages = []
        left, stride = count // 2, count
        while left > 1:
            size = 4 if left % 4 == 0 else 2
            stride //= size
            left //= size
            self.stages.append((stride, size))

    def perm(self, stride, size, shift):
        moves = []
        for source in range(self.count):
            digit = source // stride % size
            moves.append((source, source + ((digit + shift) % size - digit) * stride))
        return moves

    def send(self, value, stage, shift):
        stride, size = stage
        return lax.ppermute(value, "dp", self.perm(stride, size, shift % size))

    def swap(self, value):
        return lax.ppermute(value, "dp", self.perm(1, 2, 1))

    def digit(self, stage):
        return lax.axis_index("dp") // stage[0] % stage[1]

    def gather(self, block):
        blocks = [block]
        for stage in self.stages:
            more = list(blocks)
            for shift in range(1, stage[1]):
                more += [self.send(one, stage, -shift) for one in blocks]
            blocks = more
        return blocks

    def scatter(self, make):
        def level(depth, offset, width):
            if depth == len(self.stages):
                return lambda inner: make(offset + inner)
            return None

        widths = [1]
        for stage in self.stages:
            widths.append(widths[-1] * stage[1])

        def total(depth, index):
            if depth == len(self.stages):
                return make(index)
            stage = self.stages[depth]
            parts = []
            for shift in range(1, stage[1]):
                sent = total(depth + 1, index + shift * widths[depth]).astype(BF16)
                parts.append(self.send(sent, stage, shift))
            mine = total(depth + 1, index)
            for part in parts:
                mine = mine + part.astype(F32)
            return mine

        return total(0, 0)

    def order(self, value, width, back=False):
        parts = [value[:, i * width : (i + 1) * width] for i in range(self.count // 2)]
        stages = self.stages
        if back:
            parts = self.turn_digits(parts, [s[1] for s in stages[::-1]])
        inner = len(parts)
        for stage in stages:
            size = stage[1]
            inner //= size
            digit = self.digit(stage)
            new = []
            for place in range(len(parts)):
                at = place // inner % size
                base = place - at * inner
                picks = []
                for k in range(size):
                    picks.append(parts[base + ((at - k) % size if back else (at + k) % size) * inner])
                one = picks[0]
                for k in range(1, size):
                    one = jnp.where(digit == k, picks[k], one)
                new.append(one)
            parts = new
        if not back:
            parts = self.turn_digits(parts, [s[1] for s in stages])
        return jnp.concatenate(parts, axis=1)

    def turn_digits(self, parts, sizes):
        count = len(parts)
        out = [None] * count
        for index in range(count):
            rest, digits = index, []
            for size in reversed(sizes):
                digits.append(rest % size)
                rest //= size
            new = 0
            for digit, size in zip(digits, reversed(sizes)):
                new = new * size + digit
            out[new] = parts[index]
        return out


def mm(left, right, dims=NN, kind=F32):
    return lax.dot_general(left, right, dims, preferred_element_type=F32).astype(kind)


def rms(values):
    return lax.rsqrt(jnp.mean(values * values, axis=-1, keepdims=True) + 1e-06)


def norm_back(values, gain, grad):
    scale = rms(values)
    scaled = gain * grad
    inner = jnp.mean(scaled * values, axis=-1, keepdims=True)
    return scale * scaled - values * (scale * scale * scale * inner), jnp.sum(grad * values * scale, axis=0)


def body(
    tokens,
    seq_count,
    valid_len,
    attn_gain,
    ffn_gain,
    q_weight,
    k_weight,
    v_weight,
    forget_weight,
    out_weight,
    gate_weight,
    up_weight,
    down_weight,
    cotangent,
    *,
    ring,
):
    shard = q_weight.shape[0]
    width = 2 * shard
    core = lax.axis_index("head")
    even = lax.axis_index("dp") % 2 == 0
    first = core == 0
    rows = tokens.shape[0]

    def other_core(value):
        return lax.ppermute(value, "head", [(0, 1), (1, 0)])

    def pair_rows(mine, theirs, axis=0):
        return jnp.where(
            even, jnp.concatenate([mine, theirs], axis=axis), jnp.concatenate([theirs, mine], axis=axis)
        )

    def gather(parts):
        left = jnp.concatenate([p[0] for p in parts], axis=1)
        right = jnp.concatenate([p[1] for p in parts], axis=1)
        mine, theirs = jnp.where(even, left, right), jnp.where(even, right, left)
        return jnp.concatenate(ring.gather(pair_rows(mine, ring.swap(theirs))), axis=0)

    def cut(weight):
        half = weight.shape[1] // 2
        return (weight[:, :half], weight[:, half:])

    def quad_gather(mine):
        chips = jnp.concatenate([mine, ring.swap(mine)], axis=0)
        return jnp.concatenate([chips, other_core(chips)], axis=0)

    def quad_scatter(make):
        theirs = other_core(make(slice(2 * SEQ_LEN, 4 * SEQ_LEN)))
        far = make(slice(SEQ_LEN, 2 * SEQ_LEN)) + theirs[SEQ_LEN:]
        near = make(slice(0, SEQ_LEN)) + theirs[:SEQ_LEN]
        return near + ring.swap(far.astype(BF16)).astype(F32)

    def whole_rows(mine):
        theirs = other_core(mine)
        return jnp.where(
            first, jnp.concatenate([mine, theirs], axis=0), jnp.concatenate([theirs, mine], axis=0)
        )

    def weight_sum(act, grads):
        def make(index):
            return mm(act[:, index * width : (index + 1) * width], grads, TN)

        done = ring.scatter(make)
        mine = jnp.where(even, done[:shard], done[shard:])
        theirs = ring.swap(jnp.where(even, done[shard:], done[:shard]))
        return (jnp.where(even, mine, theirs), jnp.where(even, theirs, mine))

    gains = jnp.concatenate(
        [attn_gain[:, None], ffn_gain[:, None], jnp.zeros((shard, PAD - 2), BF16)], axis=1
    )
    w_in = gather([cut(q_weight), cut(k_weight), cut(v_weight), cut(forget_weight), (gains, gains)])
    w_out = gather([cut(out_weight)])
    w_gate = gather([cut(gate_weight)])
    w_up = gather([cut(up_weight)])
    w_down = gather([cut(down_weight)])
    gain_attn = w_in[:, WIDE - PAD].astype(F32)[None, :]
    gain_ffn = w_in[:, WIDE - PAD + 1].astype(F32)[None, :]

    def own(value):
        return ring.order(jnp.where(first, value[:SEQ_LEN], value[SEQ_LEN:]), width)

    places = lax.broadcasted_iota(jnp.int32, (SEQ_LEN, 1), 0)
    length = jnp.where(first, valid_len[0], valid_len[1])
    live = ((core < seq_count[0]) & (places < length)).astype(F32)
    own_tokens = own(tokens)
    d_res = live * own(cotangent)
    d_ffn = quad_gather(d_res.astype(BF16))
    inputs = quad_gather(own_tokens).astype(F32)
    attn_in = (inputs * rms(inputs) * gain_attn).astype(BF16)
    proj = mm(attn_in, w_in)
    mixed, *saved = mixer_forward(proj)
    own_inputs = own_tokens.astype(F32)
    resid = own_inputs + quad_scatter(lambda r: mm(mixed[r], w_out, NT))
    ffn_in = quad_gather((resid * rms(resid) * gain_ffn).astype(BF16))
    gate, up_vals = mm(ffn_in, w_gate), mm(ffn_in, w_up)
    sig = jax.nn.sigmoid(gate)
    hidden = (gate * sig * up_vals).astype(BF16)
    down_sum = weight_sum(d_ffn, hidden)
    d_hidden = mm(d_ffn, w_down)
    d_gate = (d_hidden * up_vals * (sig * (1.0 + gate * (1.0 - sig)))).astype(BF16)
    d_up = (d_hidden * (gate * sig)).astype(BF16)
    d_ffn_in = quad_scatter(lambda r: mm(d_gate[r], w_gate, NT) + mm(d_up[r], w_up, NT))
    gate_sum = weight_sum(ffn_in, d_gate)
    up_sum = weight_sum(ffn_in, d_up)
    ffn = quad_scatter(lambda r: mm(hidden[r], w_down, NT))
    block_out = whole_rows(ring.order((live * (resid + ffn)).astype(BF16), width, back=True))
    d_norm, ffn_gain_part = norm_back(resid, gain_ffn, d_ffn_in)
    d_h = d_res + d_norm
    d_attn = quad_gather(d_h.astype(BF16))
    d_mixed = mm(d_attn, w_out)
    d_proj = mixer_backward(proj, saved, d_mixed)
    d_attn_in = quad_scatter(lambda r: mm(d_proj[r], w_in, NT))
    out_sum = weight_sum(d_attn, mixed)
    in_sum = weight_sum(attn_in, d_proj)
    d_input, attn_gain_part = norm_back(own_inputs, gain_attn, d_attn_in)
    input_grad = whole_rows(ring.order(d_h + d_input, width, back=True))

    both = jnp.stack([attn_gain_part, ffn_gain_part], axis=0)
    both = both + other_core(both)
    both = both.reshape(2, ring.count // 2, width)
    for stage in ring.stages[::-1]:
        size = stage[1]
        both = both.reshape(2, size, -1, width)
        parts = [ring.send(both[:, shift], stage, shift) for shift in range(1, size)]
        both = both[:, 0]
        for part in parts:
            both = both + part
    both = both.reshape(2, 2, shard)
    both = jnp.where(even, both[:, 0], both[:, 1]) + ring.swap(jnp.where(even, both[:, 1], both[:, 0]))

    def columns(pieces, start, stop):
        return jnp.concatenate([p[:, start:stop] for p in pieces], axis=1)

    return (
        block_out,
        input_grad,
        both[0],
        both[1],
        columns(in_sum, 0, KDIM),
        columns(in_sum, KDIM, 2 * KDIM),
        columns(in_sum, 2 * KDIM, 3 * KDIM),
        columns(in_sum, 3 * KDIM, 3 * KDIM + SLOTS),
        columns(out_sum, 0, KDIM),
        jnp.concatenate(gate_sum, axis=1),
        jnp.concatenate(up_sum, axis=1),
        jnp.concatenate(down_sum, axis=1),
    )


def solution(mesh):
    ring = Ring(mesh.shape["dp"])
    split_one, split_two = P("dp"), P("dp", "head")
    row = P("dp", None)
    in_specs = (row, split_one, split_one, split_one, split_one) + (split_two,) * 8 + (row,)
    out_specs = (row, row, split_one, split_one) + (split_two,) * 8
    return jax.shard_map(
        functools.partial(body, ring=ring),
        mesh=mesh,
        in_specs=in_specs,
        out_specs=out_specs,
        check_vma=False,
    )
```

```python
import functools
import jax
import jax.numpy as jnp
from jax import lax
from jax.experimental import pallas as pl
from jax.experimental.pallas import tpu as pltpu
from jax.sharding import PartitionSpec as P

SLOTS = 64
KDIM = 512
SEQ_LEN = 256
HALF = 128
F32, BF16 = jnp.float32, jnp.bfloat16
WIDE = 3 * KDIM + 128
NT = (((1,), (1,)), ((), ()))
NN = (((1,), (0,)), ((), ()))
TN = (((0,), (0,)), ((), ()))
LEVELS = (8, 16, 32, 64)


def split(value):
    high = value.astype(BF16)
    return high, (value - high.astype(F32)).astype(BF16)


def dot3(left, right, dims):
    one = functools.partial(lax.dot_general, dimension_numbers=dims, preferred_element_type=F32)
    return one(left[0], right[0]) + (one(left[0], right[1]) + one(left[1], right[0]))


def silu_parts(value):
    gate = 1.0 / (1.0 + jnp.exp(-value))
    return gate, value * gate


def level_mask(size):
    row = lax.broadcasted_iota(jnp.int32, (HALF, HALF), 0) // size
    col = lax.broadcasted_iota(jnp.int32, (HALF, HALF), 1) // size
    return (row == col + 1) & (row % 2 == 1)


def band_mask(back):
    row = lax.broadcasted_iota(jnp.int32, (HALF, HALF), 0)
    col = lax.broadcasted_iota(jnp.int32, (HALF, HALF), 1)
    return (row == col + back) & (row // 8 == col // 8)


def down(value, back):
    return value if back == 0 else pltpu.roll(value, back, 0)


def up(value, back):
    return value if back == 0 else pltpu.roll(value, SEQ_LEN - back, 0)


def gates(forget):
    lane = lax.broadcasted_iota(jnp.int32, forget.shape, 1) < SLOTS
    place = lax.broadcasted_iota(jnp.int32, forget.shape, 0)
    forget = jnp.where(lane, forget, 0.0)
    tail = jnp.exp(-jnp.abs(forget))
    log_decay = (jnp.minimum(forget, 0.0) - jnp.log1p(tail)) * 0.125
    log_decay = jnp.where(lane, log_decay, 0.0)
    g = log_decay
    series = 1.0 + g * (1.0 / 7.0)
    for n in (6.0, 5.0, 4.0, 3.0, 2.0):
        series = 1.0 + g * (1.0 / n) * series
    writes = jnp.where(g > -0.3, -g * series, 1.0 - jnp.exp(g))
    writes = jnp.where(lane, writes, 0.0)
    ahead, behind = g, g
    for step in (1, 2, 4):
        ahead = ahead + jnp.where(place % 8 >= step, down(ahead, step), 0.0)
        behind = behind + jnp.where(place % 8 < 8 - step, up(behind, step), 0.0)
    behind = jnp.where(place % 8 < 7, up(behind, 1), 0.0)
    aheads, behinds = {8: ahead}, {8: behind}
    size = 8
    while size < HALF:
        first = ahead.reshape(SEQ_LEN // (2 * size), 2, size, 128)
        last = behind.reshape(SEQ_LEN // (2 * size), 2, size, 128)
        left, right = first[:, 0:1], first[:, 1:2]
        left_sum, right_sum = left[:, :, size - 1 :], right[:, :, size - 1 :]
        ahead = jnp.concatenate([left, right + left_sum], axis=1).reshape(SEQ_LEN, 128)
        behind = jnp.concatenate([last[:, 0:1] + right_sum, last[:, 1:2]], axis=1).reshape(SEQ_LEN, 128)
        size *= 2
        aheads[size], behinds[size] = ahead, behind
    return lane, place, g, writes, aheads, behinds


def near_decays(place, aheads, back):
    ahead = aheads[8]
    gap = jnp.where(place % 8 >= back, ahead - down(ahead, back), 0.0)
    return jnp.where(place % 8 >= back, jnp.exp(gap), 0.0)


def halves(value):
    return value[:HALF], value[HALF:]


def to_slots(blocks, cross, place, writes, aheads, behinds, nears):
    grow = {size: jnp.exp(aheads[size]) for size in LEVELS}
    keep = {size: split(jnp.exp(behinds[size]) * writes) for size in LEVELS}
    outs = []
    for half in range(2):
        here = slice(half * HALF, (half + 1) * HALF)
        block = blocks[half]
        parts = split(block)
        total = None
        for size in LEVELS:
            mask = level_mask(size)
            masked = tuple(jnp.where(mask, part, jnp.zeros_like(part)) for part in parts)
            term = grow[size][here] * dot3(masked, tuple(k[here] for k in keep[size]), NN)
            total = term if total is None else total + term
        for back in range(8):
            near = jnp.sum(jnp.where(band_mask(back), block, 0.0), axis=1, keepdims=True)
            total = total + near * nears[back][here]
        if half == 1:
            far = split((jnp.exp(behinds[HALF]) * writes)[:HALF])
            total = total + jnp.exp(aheads[HALF])[HALF:] * dot3(split(cross), far, NN)
        outs.append(total)
    return jnp.concatenate(outs, axis=0)


def to_tokens(slots, writes, aheads, behinds, nears):
    blocks = []
    for half in range(2):
        here = slice(half * HALF, (half + 1) * HALF)
        total = jnp.zeros((HALF, HALF), F32)
        for size in LEVELS:
            left = split((slots * jnp.exp(aheads[size]))[here])
            right = split((jnp.exp(behinds[size]) * writes)[here])
            total = jnp.where(level_mask(size), dot3(left, right, NT), total)
        for back in range(8):
            near = jnp.sum(slots[here] * nears[back][here], axis=1, keepdims=True)
            total = jnp.where(band_mask(back), near, total)
        blocks.append(total)
    left = split((slots * jnp.exp(aheads[HALF]))[HALF:])
    right = split((jnp.exp(behinds[HALF]) * writes)[:HALF])
    return blocks, dot3(left, right, NT)


def forward_kernel(q_ref, k_ref, v_ref, f_ref, o_ref, p_ref, s_ref, a_ref, b_ref):
    query = split(silu_parts(q_ref[...])[1] * KDIM ** (-0.5))
    keys = split(silu_parts(k_ref[...])[1])
    values = split(v_ref[...])
    lane, place, g, writes, aheads, behinds = gates(f_ref[...])
    nears = [near_decays(place, aheads, back) * down(writes, back) for back in range(8)]
    q0, q1 = tuple(x[:HALF] for x in query), tuple(x[HALF:] for x in query)
    k0, k1 = tuple(x[:HALF] for x in keys), tuple(x[HALF:] for x in keys)
    blocks = (dot3(q0, k0, NT), dot3(q1, k1, NT))
    cross = dot3(q1, k0, NT)
    scores = to_slots(blocks, cross, place, writes, aheads, behinds, nears)
    shown = jnp.where(lane, scores, -1e30)
    weights = jnp.exp(shown - jnp.max(shown, axis=1, keepdims=True))
    weights = jnp.where(lane, weights, 0.0)
    weights = weights / jnp.sum(weights, axis=1, keepdims=True)
    mixes, mix_cross = to_tokens(weights, writes, aheads, behinds, nears)
    v0 = tuple(x[:HALF] for x in values)
    o_ref[:HALF, :] = dot3(split(mixes[0]), v0, NN).astype(o_ref.dtype)
    row = jnp.concatenate([mix_cross, mixes[1]], axis=1)
    o_ref[HALF:, :] = dot3(split(row), values, NN).astype(o_ref.dtype)
    p_ref[...] = weights
    s_ref[...] = scores
    a_ref[:HALF, :] = jnp.concatenate([blocks[0], jnp.zeros_like(cross)], axis=1)
    a_ref[HALF:, :] = jnp.concatenate([cross, blocks[1]], axis=1)
    b_ref[:HALF, :] = jnp.concatenate([mixes[0], jnp.zeros_like(cross)], axis=1)
    b_ref[HALF:, :] = row


def backward_kernel(q_ref, k_ref, v_ref, f_ref, p_ref, s_ref, a_ref, b_ref, d_ref, out_ref):
    lane, place, g, writes, aheads, behinds = gates(f_ref[...])
    spans = [near_decays(place, aheads, back) for back in range(8)]
    nears = [spans[back] * down(writes, back) for back in range(8)]
    weights, scores = p_ref[...], s_ref[...]
    products, mixing = a_ref[...], b_ref[...]
    grad = split(d_ref[...])
    g0, g1 = tuple(x[:HALF] for x in grad), tuple(x[HALF:] for x in grad)
    values = split(v_ref[...])
    v0, v1 = tuple(x[:HALF] for x in values), tuple(x[HALF:] for x in values)
    m_parts = split(mixing)
    dv0 = dot3(tuple(x[:, :HALF] for x in m_parts), grad, TN)
    dv1 = dot3(tuple(x[HALF:, HALF:] for x in m_parts), g1, TN)
    out_ref[:HALF, 2 * KDIM : 3 * KDIM] = dv0.astype(BF16)
    out_ref[HALF:, 2 * KDIM : 3 * KDIM] = dv1.astype(BF16)
    mix_blocks = (dot3(g0, v0, NT), dot3(g1, v1, NT))
    mix_cross = dot3(g1, v0, NT)
    d_weights = to_slots(mix_blocks, mix_cross, place, writes, aheads, behinds, nears)
    inner = jnp.sum(weights * d_weights, axis=1, keepdims=True)
    d_scores = weights * (d_weights - inner)
    d_blocks, d_cross = to_tokens(d_scores, writes, aheads, behinds, nears)
    q_gate, q_act = silu_parts(q_ref[...])
    k_gate, k_act = silu_parts(k_ref[...])
    scale = KDIM ** (-0.5)
    query, keys = split(q_act * scale), split(k_act)
    k0 = tuple(x[:HALF] for x in keys)
    low = split(jnp.concatenate([d_cross, d_blocks[1]], axis=1))
    top = split(d_blocks[0])
    dq = jnp.concatenate([dot3(top, k0, NN), dot3(low, keys, NN)], axis=0)
    first = tuple(jnp.concatenate([t, l[:, :HALF]], axis=0) for t, l in zip(top, low))
    dk0 = dot3(first, query, TN)
    dk1 = dot3(tuple(x[:, HALF:] for x in low), tuple(x[HALF:] for x in query), TN)
    dk = jnp.concatenate([dk0, dk1], axis=0)
    out_ref[:, :KDIM] = (dq * scale * (q_gate + q_act * (1.0 - q_gate))).astype(BF16)
    out_ref[:, KDIM : 2 * KDIM] = (dk * (k_gate + k_act * (1.0 - k_gate))).astype(BF16)
    parts = []
    for half in range(2):
        here = slice(half * HALF, (half + 1) * HALF)
        both = jnp.concatenate([mix_blocks[half], products[here, here]], axis=0)
        both_parts = split(both)
        total = None
        for size in LEVELS:
            mask = level_mask(size)
            mask = jnp.concatenate([mask, mask], axis=0)
            grow = jnp.exp(aheads[size][here])
            right = split(jnp.concatenate([weights[here] * grow, d_scores[here] * grow], axis=0))
            left = tuple(jnp.where(mask, part, jnp.zeros_like(part)) for part in both_parts)
            term = jnp.exp(behinds[size][here]) * dot3(left, right, TN)
            total = term if total is None else total + term
        parts.append(total)
    grow = jnp.exp(aheads[HALF][HALF:])
    left = split(jnp.concatenate([mix_cross, products[HALF:, :HALF]], axis=0))
    right = split(jnp.concatenate([weights[HALF:] * grow, d_scores[HALF:] * grow], axis=0))
    parts[0] = parts[0] + jnp.exp(behinds[HALF][:HALF]) * dot3(left, right, TN)
    reach = jnp.concatenate(parts, axis=0)
    for back in range(8):
        mask = band_mask(back)
        near_mix = jnp.concatenate([jnp.sum(jnp.where(mask, mix_blocks[h], 0.0), axis=1, keepdims=True) for h in range(2)], axis=0)
        near_pro = jnp.concatenate(
            [jnp.sum(jnp.where(mask, products[h * HALF : (h + 1) * HALF, h * HALF : (h + 1) * HALF], 0.0), axis=1, keepdims=True) for h in range(2)],
            axis=0,
        )
        reach = reach + up((near_mix * weights + near_pro * d_scores) * spans[back], back)
    d_sum = weights * d_weights + d_scores * scores - writes * reach
    step = 1
    while step < SEQ_LEN:
        d_sum = d_sum + jnp.where(place < SEQ_LEN - step, up(d_sum, step), 0.0)
        step *= 2
    d_log = d_sum - reach * jnp.exp(g)
    d_forget = d_log * 0.125 / (1.0 + jnp.exp(f_ref[...]))
    out_ref[:, 3 * KDIM :] = jnp.where(lane, d_forget, 0.0).astype(BF16)


def spec(width, column):
    return pl.BlockSpec((SEQ_LEN, width), lambda i: (i, column))


IN_SPECS = [spec(KDIM, 0), spec(KDIM, 1), spec(KDIM, 2), spec(128, 3 * KDIM // 128)]


def mixer_forward(proj):
    rows = proj.shape[0]
    shape = lambda width, kind: jax.ShapeDtypeStruct((rows, width), kind)
    return pl.pallas_call(
        forward_kernel,
        grid=(rows // SEQ_LEN,),
        in_specs=IN_SPECS,
        out_specs=[spec(KDIM, 0), spec(128, 0), spec(128, 0), spec(SEQ_LEN, 0), spec(SEQ_LEN, 0)],
        out_shape=[shape(KDIM, BF16), shape(128, F32), shape(128, F32), shape(SEQ_LEN, F32), shape(SEQ_LEN, F32)],
        compiler_params=pltpu.CompilerParams(vmem_limit_bytes=48 << 20),
        cost_estimate=pl.CostEstimate(flops=rows * 3000000, bytes_accessed=rows * 10000, transcendentals=rows * 3000),
        name="mixer_forward",
    )(proj, proj, proj, proj)


def mixer_backward(proj, saved, grad):
    rows = proj.shape[0]
    weights, scores, products, mixing = saved
    return pl.pallas_call(
        backward_kernel,
        grid=(rows // SEQ_LEN,),
        in_specs=IN_SPECS + [spec(128, 0), spec(128, 0), spec(SEQ_LEN, 0), spec(SEQ_LEN, 0), spec(KDIM, 0)],
        out_specs=spec(WIDE, 0),
        out_shape=jax.ShapeDtypeStruct((rows, WIDE), BF16),
        compiler_params=pltpu.CompilerParams(vmem_limit_bytes=48 << 20),
        cost_estimate=pl.CostEstimate(flops=rows * 9000000, bytes_accessed=rows * 16000, transcendentals=rows * 5000),
        name="mixer_backward",
    )(proj, proj, proj, proj, weights, scores, products, mixing, grad)


MESH = pl.DeviceIdType.MESH
ANY = pl.BlockSpec(memory_space=pl.ANY)


def places():
    dp, core = lax.axis_index("dp"), lax.axis_index("head")
    x, y, z = dp % 2, dp // 2 % 2, dp // 4
    rest = dp % 4
    return {
        "x": (dp + 1 - 2 * x, core),
        "y": (dp + 2 - 4 * y, core),
        "up": ((z + 1) % 4 * 4 + rest, core),
        "down": ((z + 3) % 4 * 4 + rest, core),
        "core": (dp, 1 - core),
    }, x


def greet(peers):
    ready = pltpu.get_barrier_semaphore()
    for peer in peers:
        pl.semaphore_signal(ready, inc=1, device_id=peer, device_id_type=MESH)
    pl.semaphore_wait(ready, len(peers))


def remote(source, target, sends, recvs, peer):
    return pltpu.make_async_remote_copy(
        src_ref=source, dst_ref=target, send_sem=sends, recv_sem=recvs, device_id=peer, device_id_type=MESH
    )


def gather_kernel(chunks, count, *refs):
    total = len(chunks)
    mine, theirs = refs[:total], refs[total : 2 * total]
    full = refs[2 * total : 2 * total + count]
    local, xs, xr, zs, zr, ys, yr = refs[2 * total + count :]
    peers, x = places()
    half = mine[0].shape[0]
    rows = pl.ds(pl.multiple_of(x * half, half), half)
    greet([peers[name] for name in ("x", "y", "up", "down")])

    def block(c, index):
        array, start, width, _ = chunks[c]
        return full[array].at[index, :, pl.ds(start, width)]

    def keep(c):
        array, start, width, _ = chunks[c]
        return pltpu.make_async_copy(mine[c], full[array].at[0, rows, pl.ds(start, width)], local.at[c])

    def swap(c):
        array, start, width, _ = chunks[c]
        return remote(theirs[c], full[array].at[0, rows, pl.ds(start, width)], xs.at[c], xr.at[c], peers["x"])

    def rise(c, step, upper):
        source = (5 - step) % 4
        return remote(
            block(c, source + 4 * upper), block(c, 4 - step + 4 * upper), zs.at[c, upper, step - 1], zr.at[c, upper, step - 1], peers["up"]
        )

    def cross(c, index):
        return remote(block(c, index), block(c, 4 + index), ys.at[c, index], yr.at[c, index], peers["y"])

    order = range(total)
    for c in order:
        swap(c).start()
        keep(c).start()
    for c in order:
        keep(c).wait()
        swap(c).wait_recv()
        rise(c, 1, 0).start()
        cross(c, 0).start()
    for step in (1, 2, 3):
        if step == 1:
            for c in order:
                if chunks[c][3]:
                    cross(c, 0).wait_recv()
                    rise(c, 1, 1).start()
        for c in order:
            for upper in (0, 1) if chunks[c][3] else (0,):
                rise(c, step, upper).wait_recv()
                if step < 3:
                    rise(c, step + 1, upper).start()
            if not chunks[c][3]:
                cross(c, 4 - step).start()
    for c in order:
        swap(c).wait_send()
        for index in range(1 if chunks[c][3] else 4):
            copy = cross(c, index)
            copy.wait_send()
            if not chunks[c][3]:
                copy.wait_recv()
        for upper in (0, 1) if chunks[c][3] else (0,):
            for step in (1, 2, 3):
                rise(c, step, upper).wait_send()


def gather_call(chunks, widths, mine, theirs, ident):
    total = len(chunks)
    half = mine[0].shape[0]
    sems = pltpu.SemaphoreType.DMA
    full = pl.pallas_call(
        functools.partial(gather_kernel, chunks, len(widths)),
        in_specs=[ANY] * (2 * total),
        out_specs=[ANY] * len(widths),
        out_shape=[jax.ShapeDtypeStruct((8, 2 * half, width), BF16) for width in widths],
        scratch_shapes=[
            sems((total,)),
            sems((total,)),
            sems((total,)),
            sems((total, 2, 3)),
            sems((total, 2, 3)),
            sems((total, 4)),
            sems((total, 4)),
        ],
        compiler_params=pltpu.CompilerParams(collective_id=ident, has_side_effects=True),
        name="gather_weights",
    )(*mine, *theirs)
    return [one.reshape(16 * half, one.shape[2]) for one in full]


def scatter_kernel(chunks, count, *refs):
    total = len(chunks)
    terms = refs[:count]
    outs = refs[count : count + total]
    others = refs[count + total : count + 2 * total]
    scratch = refs[count + 2 * total :]
    own, from_y, from_z, to_z, final = (scratch[i * total : (i + 1) * total] for i in range(5))
    local, ys, yr, zs, zr, xs, xr, last = scratch[5 * total :]
    peers, x = places()
    rows = terms[0].shape[1]
    half = rows // 2
    greet([peers[name] for name in ("x", "y", "up", "down")])

    def block(c, index):
        array, start, width = chunks[c]
        return terms[array].at[index, :, pl.ds(start, width)]

    def cross(c, index):
        return remote(block(c, 4 + index), from_y[c].at[index], ys.at[c, index], yr.at[c, index], peers["y"])

    def load(c, index):
        return pltpu.make_async_copy(block(c, index), own[c].at[index], local.at[c, index])

    def rise(c, step):
        return remote(to_z[c].at[step], from_z[c].at[step], zs.at[c, step], zr.at[c, step], peers["up"])

    mine = pl.ds(pl.multiple_of(x * half, half), half)
    away = pl.ds(pl.multiple_of((1 - x) * half, half), half)

    def swap(c):
        return remote(final[c].at[away], others[c], xs.at[c], xr.at[c], peers["x"])

    def leave(c):
        return pltpu.make_async_copy(final[c].at[mine], outs[c], last.at[c])

    order = range(total)
    for index in (3, 2, 1, 0):
        for c in order:
            cross(c, index).start()
            load(c, index).start()
    for step in range(4):
        index = 3 - step
        for c in order:
            cross(c, index).wait_recv()
            load(c, index).wait()
            if step:
                rise(c, step - 1).wait_recv()
            piece = 32

            def add(i, carry, c=c, step=step, index=index):
                part = pl.ds(pl.multiple_of(i * piece, piece), piece)
                value = own[c][index, part].astype(F32) + from_y[c][index, part].astype(F32)
                if step:
                    value = value + from_z[c][step - 1, part].astype(F32)
                if step < 3:
                    to_z[c][step, part] = value.astype(BF16)
                else:
                    final[c][part] = value
                return carry

            lax.fori_loop(0, rows // piece, add, 0)
            if step < 3:
                rise(c, step).start()
            else:
                swap(c).start()
                leave(c).start()
    for c in order:
        for index in range(4):
            cross(c, index).wait_send()
        for step in range(3):
            rise(c, step).wait_send()
        leave(c).wait()
        swap(c).wait()


def scatter_call(chunks, terms, ident):
    total = len(chunks)
    rows = terms[0].shape[0] // 8
    terms = [term.reshape(8, rows, term.shape[1]) for term in terms]
    sems = pltpu.SemaphoreType.DMA
    scratch = []
    for depth, kind in ((4, BF16), (4, BF16), (3, BF16), (3, BF16)):
        scratch += [pltpu.VMEM((depth, rows, width), kind) for _, _, width in chunks]
    scratch += [pltpu.VMEM((rows, width), F32) for _, _, width in chunks]
    outs = pl.pallas_call(
        functools.partial(scatter_kernel, chunks, len(terms)),
        in_specs=[ANY] * len(terms),
        out_specs=[ANY] * (2 * total),
        out_shape=[jax.ShapeDtypeStruct((rows // 2, width), F32) for _, _, width in chunks] * 2,
        scratch_shapes=scratch
        + [
            sems((total, 4)),
            sems((total, 4)),
            sems((total, 4)),
            sems((total, 3)),
            sems((total, 3)),
            sems((total,)),
            sems((total,)),
            sems((total,)),
        ],
        compiler_params=pltpu.CompilerParams(collective_id=ident, has_side_effects=True, vmem_limit_bytes=56 << 20),
        name="sum_gradients",
    )(*terms)
    return outs[:total], outs[total:]


PAD = 128 - SLOTS


class Ring:
    def __init__(self, count):
        self.count = count
        self.stages = []
        left, stride = count // 2, count
        while left > 1:
            size = 4 if left % 4 == 0 else 2
            stride //= size
            left //= size
            self.stages.append((stride, size))

    def perm(self, stride, size, shift):
        moves = []
        for source in range(self.count):
            digit = source // stride % size
            moves.append((source, source + ((digit + shift) % size - digit) * stride))
        return moves

    def send(self, value, stage, shift):
        stride, size = stage
        return lax.ppermute(value, "dp", self.perm(stride, size, shift % size))

    def swap(self, value):
        return lax.ppermute(value, "dp", self.perm(1, 2, 1))

    def digit(self, stage):
        return lax.axis_index("dp") // stage[0] % stage[1]

    def gather(self, block):
        blocks = [block]
        for stage in self.stages:
            more = list(blocks)
            for shift in range(1, stage[1]):
                more += [self.send(one, stage, -shift) for one in blocks]
            blocks = more
        return blocks

    def scatter(self, make):
        def level(depth, offset, width):
            if depth == len(self.stages):
                return lambda inner: make(offset + inner)
            return None

        widths = [1]
        for stage in self.stages:
            widths.append(widths[-1] * stage[1])

        def total(depth, index):
            if depth == len(self.stages):
                return make(index)
            stage = self.stages[depth]
            parts = []
            for shift in range(1, stage[1]):
                sent = total(depth + 1, index + shift * widths[depth]).astype(BF16)
                parts.append(self.send(sent, stage, shift))
            mine = total(depth + 1, index)
            for part in parts:
                mine = mine + part.astype(F32)
            return mine

        return total(0, 0)

    def order(self, value, width, back=False):
        parts = [value[:, i * width : (i + 1) * width] for i in range(self.count // 2)]
        stages = self.stages
        if back:
            parts = self.turn_digits(parts, [s[1] for s in stages[::-1]])
        inner = len(parts)
        for stage in stages:
            size = stage[1]
            inner //= size
            digit = self.digit(stage)
            new = []
            for place in range(len(parts)):
                at = place // inner % size
                base = place - at * inner
                picks = []
                for k in range(size):
                    picks.append(parts[base + ((at - k) % size if back else (at + k) % size) * inner])
                one = picks[0]
                for k in range(1, size):
                    one = jnp.where(digit == k, picks[k], one)
                new.append(one)
            parts = new
        if not back:
            parts = self.turn_digits(parts, [s[1] for s in stages])
        return jnp.concatenate(parts, axis=1)

    def turn_digits(self, parts, sizes):
        count = len(parts)
        out = [None] * count
        for index in range(count):
            rest, digits = index, []
            for size in reversed(sizes):
                digits.append(rest % size)
                rest //= size
            new = 0
            for digit, size in zip(digits, reversed(sizes)):
                new = new * size + digit
            out[new] = parts[index]
        return out


def mm(left, right, dims=NN, kind=F32):
    return lax.dot_general(left, right, dims, preferred_element_type=F32).astype(kind)


def rms(values):
    return lax.rsqrt(jnp.mean(values * values, axis=-1, keepdims=True) + 1e-06)


def norm_back(values, gain, grad):
    scale = rms(values)
    scaled = gain * grad
    inner = jnp.mean(scaled * values, axis=-1, keepdims=True)
    return scale * scaled - values * (scale * scale * scale * inner), jnp.sum(grad * values * scale, axis=0)


def body(
    tokens,
    seq_count,
    valid_len,
    attn_gain,
    ffn_gain,
    q_weight,
    k_weight,
    v_weight,
    forget_weight,
    out_weight,
    gate_weight,
    up_weight,
    down_weight,
    cotangent,
    *,
    ring,
):
    shard = q_weight.shape[0]
    width = 2 * shard
    core = lax.axis_index("head")
    even = lax.axis_index("dp") % 2 == 0
    first = core == 0
    rows = tokens.shape[0]

    def other_core(value):
        return lax.ppermute(value, "head", [(0, 1), (1, 0)])

    def pair_rows(mine, theirs, axis=0):
        return jnp.where(
            even, jnp.concatenate([mine, theirs], axis=axis), jnp.concatenate([theirs, mine], axis=axis)
        )

    def gather(parts):
        left = jnp.concatenate([p[0] for p in parts], axis=1)
        right = jnp.concatenate([p[1] for p in parts], axis=1)
        mine, theirs = jnp.where(even, left, right), jnp.where(even, right, left)
        return jnp.concatenate(ring.gather(pair_rows(mine, ring.swap(theirs))), axis=0)

    def gather_all(groups, layout, ident):
        if ring.count != 16:
            arrays = {}
            for group, chunk in zip(groups, layout):
                arrays.setdefault(chunk[0], []).append((chunk[1], group))
            return [gather([g for _, g in sorted(arrays[i], key=lambda one: one[0])]) for i in sorted(arrays)]
        mine = [jnp.where(even, left, right) for left, right in groups]
        theirs = [jnp.where(even, right, left) for left, right in groups]
        widths = {}
        for array, start, size, _ in layout:
            widths[array] = max(widths.get(array, 0), start + size)
        return gather_call(layout, [widths[i] for i in sorted(widths)], mine, theirs, ident)

    def scatter_all(pairs, layout, ident):
        if ring.count != 16:
            sums = [weight_sum(act, grads) for act, grads in pairs]
            return [tuple(p[:, start : start + size] for p in sums[array]) for array, start, size in layout]
        terms = [mm(act, grads, TN, BF16) for act, grads in pairs]
        mine, theirs = scatter_call(layout, terms, ident)
        return [(jnp.where(even, m, t), jnp.where(even, t, m)) for m, t in zip(mine, theirs)]

    def cut(weight):
        half = weight.shape[1] // 2
        return (weight[:, :half], weight[:, half:])

    def quad_gather(mine):
        chips = jnp.concatenate([mine, ring.swap(mine)], axis=0)
        return jnp.concatenate([chips, other_core(chips)], axis=0)

    def quad_scatter(make):
        theirs = other_core(make(slice(2 * SEQ_LEN, 4 * SEQ_LEN)))
        far = make(slice(SEQ_LEN, 2 * SEQ_LEN)) + theirs[SEQ_LEN:]
        near = make(slice(0, SEQ_LEN)) + theirs[:SEQ_LEN]
        return near + ring.swap(far.astype(BF16)).astype(F32)

    def whole_rows(mine):
        theirs = other_core(mine)
        return jnp.where(
            first, jnp.concatenate([mine, theirs], axis=0), jnp.concatenate([theirs, mine], axis=0)
        )

    def weight_sum(act, grads):
        def make(index):
            return mm(act[:, index * width : (index + 1) * width], grads, TN)

        done = ring.scatter(make)
        mine = jnp.where(even, done[:shard], done[shard:])
        theirs = ring.swap(jnp.where(even, done[shard:], done[:shard]))
        return (jnp.where(even, mine, theirs), jnp.where(even, theirs, mine))

    gains = jnp.concatenate(
        [attn_gain[:, None], ffn_gain[:, None], jnp.zeros((shard, PAD - 2), BF16)], axis=1
    )
    small = tuple(jnp.concatenate([part, gains], axis=1) for part in cut(forget_weight))
    w_in, w_out = gather_all(
        [small, cut(q_weight), cut(k_weight), cut(v_weight), cut(out_weight)],
        ((0, 3 * KDIM, 128, False), (0, 0, KDIM, False), (0, KDIM, KDIM, False), (0, 2 * KDIM, KDIM, False), (1, 0, KDIM, True)),
        0,
    )
    hid = gate_weight.shape[1] // 2
    low, high = hid // 256 * 128, hid - hid // 256 * 128
    down_left, down_right = cut(down_weight)
    w_gate, w_up, w_down = gather_all(
        [cut(gate_weight), cut(up_weight), (down_left[:, :low], down_right[:, :low]), (down_left[:, low:], down_right[:, low:])],
        ((0, 0, hid, False), (1, 0, hid, False), (2, 0, low, False), (2, low, high, True)),
        1,
    )
    gain_attn = w_in[:, WIDE - PAD].astype(F32)[None, :]
    gain_ffn = w_in[:, WIDE - PAD + 1].astype(F32)[None, :]

    def own(value):
        return ring.order(jnp.where(first, value[:SEQ_LEN], value[SEQ_LEN:]), width)

    places = lax.broadcasted_iota(jnp.int32, (SEQ_LEN, 1), 0)
    length = jnp.where(first, valid_len[0], valid_len[1])
    live = ((core < seq_count[0]) & (places < length)).astype(F32)
    own_tokens = own(tokens)
    d_res = live * own(cotangent)
    d_ffn = quad_gather(d_res.astype(BF16))
    inputs = quad_gather(own_tokens).astype(F32)
    attn_in = (inputs * rms(inputs) * gain_attn).astype(BF16)
    proj = mm(attn_in, w_in)
    mixed, *saved = mixer_forward(proj)
    own_inputs = own_tokens.astype(F32)
    resid = own_inputs + quad_scatter(lambda r: mm(mixed[r], w_out, NT))
    ffn_in = quad_gather((resid * rms(resid) * gain_ffn).astype(BF16))
    gate, up_vals = mm(ffn_in, w_gate), mm(ffn_in, w_up)
    sig = jax.nn.sigmoid(gate)
    hidden = (gate * sig * up_vals).astype(BF16)
    d_hidden = mm(d_ffn, w_down)
    d_gate = (d_hidden * up_vals * (sig * (1.0 + gate * (1.0 - sig)))).astype(BF16)
    d_up = (d_hidden * (gate * sig)).astype(BF16)
    d_ffn_in = quad_scatter(lambda r: mm(d_gate[r], w_gate, NT) + mm(d_up[r], w_up, NT))
    down_sum, gate_sum, up_sum = scatter_all(
        [(d_ffn, hidden), (ffn_in, d_gate), (ffn_in, d_up)], tuple((i, 0, hid) for i in range(3)), 2
    )
    ffn = quad_scatter(lambda r: mm(hidden[r], w_down, NT))
    block_out = whole_rows(ring.order((live * (resid + ffn)).astype(BF16), width, back=True))
    d_norm, ffn_gain_part = norm_back(resid, gain_ffn, d_ffn_in)
    d_h = d_res + d_norm
    d_attn = quad_gather(d_h.astype(BF16))
    d_mixed = mm(d_attn, w_out)
    d_proj = mixer_backward(proj, saved, d_mixed)
    d_attn_in = quad_scatter(lambda r: mm(d_proj[r], w_in, NT))
    out_sum, *in_sum = scatter_all(
        [(d_attn, mixed), (attn_in, d_proj)],
        ((0, 0, KDIM), (1, 0, KDIM), (1, KDIM, KDIM), (1, 2 * KDIM, KDIM), (1, 3 * KDIM, 128)),
        3,
    )
    d_input, attn_gain_part = norm_back(own_inputs, gain_attn, d_attn_in)
    input_grad = whole_rows(ring.order(d_h + d_input, width, back=True))

    both = jnp.stack([attn_gain_part, ffn_gain_part], axis=0)
    both = both + other_core(both)
    both = both.reshape(2, ring.count // 2, width)
    for stage in ring.stages[::-1]:
        size = stage[1]
        both = both.reshape(2, size, -1, width)
        parts = [ring.send(both[:, shift], stage, shift) for shift in range(1, size)]
        both = both[:, 0]
        for part in parts:
            both = both + part
    both = both.reshape(2, 2, shard)
    both = jnp.where(even, both[:, 0], both[:, 1]) + ring.swap(jnp.where(even, both[:, 1], both[:, 0]))

    def columns(pieces, start, stop):
        return jnp.concatenate([p[:, start:stop] for p in pieces], axis=1)

    return (
        block_out,
        input_grad,
        both[0],
        both[1],
        columns(in_sum[0], 0, KDIM),
        columns(in_sum[1], 0, KDIM),
        columns(in_sum[2], 0, KDIM),
        columns(in_sum[3], 0, SLOTS),
        columns(out_sum, 0, KDIM),
        jnp.concatenate(gate_sum, axis=1),
        jnp.concatenate(up_sum, axis=1),
        jnp.concatenate(down_sum, axis=1),
    )


def solution(mesh):
    ring = Ring(mesh.shape["dp"])
    split_one, split_two = P("dp"), P("dp", "head")
    row = P("dp", None)
    in_specs = (row, split_one, split_one, split_one, split_one) + (split_two,) * 8 + (row,)
    out_specs = (row, row, split_one, split_one) + (split_two,) * 8
    return jax.shard_map(
        functools.partial(body, ring=ring),
        mesh=mesh,
        in_specs=in_specs,
        out_specs=out_specs,
        check_vma=False,
    )
```

```python
import functools
import jax
import jax.numpy as jnp
from jax import lax
from jax.experimental import pallas as pl
from jax.experimental.pallas import tpu as pltpu
from jax.sharding import PartitionSpec as P

SLOTS = 64
KDIM = 512
SEQ_LEN = 256
HALF = 128
F32, BF16 = jnp.float32, jnp.bfloat16
WIDE = 3 * KDIM + 128
NT = (((1,), (1,)), ((), ()))
NN = (((1,), (0,)), ((), ()))
TN = (((0,), (0,)), ((), ()))
LEVELS = (8, 16, 32, 64)


def split(value):
    high = value.astype(BF16)
    return high, (value - high.astype(F32)).astype(BF16)


def dot3(left, right, dims):
    one = functools.partial(lax.dot_general, dimension_numbers=dims, preferred_element_type=F32)
    return one(left[0], right[0]) + (one(left[0], right[1]) + one(left[1], right[0]))


def silu_parts(value):
    gate = 1.0 / (1.0 + jnp.exp(-value))
    return gate, value * gate


def level_mask(size):
    row = lax.broadcasted_iota(jnp.int32, (HALF, HALF), 0) // size
    col = lax.broadcasted_iota(jnp.int32, (HALF, HALF), 1) // size
    return (row == col + 1) & (row % 2 == 1)


def band_mask(back):
    row = lax.broadcasted_iota(jnp.int32, (HALF, HALF), 0)
    col = lax.broadcasted_iota(jnp.int32, (HALF, HALF), 1)
    return (row == col + back) & (row // 8 == col // 8)


def down(value, back):
    return value if back == 0 else pltpu.roll(value, back, 0)


def up(value, back):
    return value if back == 0 else pltpu.roll(value, SEQ_LEN - back, 0)


def gates(forget):
    lane = lax.broadcasted_iota(jnp.int32, forget.shape, 1) < SLOTS
    place = lax.broadcasted_iota(jnp.int32, forget.shape, 0)
    forget = jnp.where(lane, forget, 0.0)
    tail = jnp.exp(-jnp.abs(forget))
    log_decay = (jnp.minimum(forget, 0.0) - jnp.log1p(tail)) * 0.125
    log_decay = jnp.where(lane, log_decay, 0.0)
    g = log_decay
    series = 1.0 + g * (1.0 / 7.0)
    for n in (6.0, 5.0, 4.0, 3.0, 2.0):
        series = 1.0 + g * (1.0 / n) * series
    writes = jnp.where(g > -0.3, -g * series, 1.0 - jnp.exp(g))
    writes = jnp.where(lane, writes, 0.0)
    ahead, behind = g, g
    for step in (1, 2, 4):
        ahead = ahead + jnp.where(place % 8 >= step, down(ahead, step), 0.0)
        behind = behind + jnp.where(place % 8 < 8 - step, up(behind, step), 0.0)
    behind = jnp.where(place % 8 < 7, up(behind, 1), 0.0)
    aheads, behinds = {8: ahead}, {8: behind}
    size = 8
    while size < HALF:
        first = ahead.reshape(SEQ_LEN // (2 * size), 2, size, 128)
        last = behind.reshape(SEQ_LEN // (2 * size), 2, size, 128)
        left, right = first[:, 0:1], first[:, 1:2]
        left_sum, right_sum = left[:, :, size - 1 :], right[:, :, size - 1 :]
        ahead = jnp.concatenate([left, right + left_sum], axis=1).reshape(SEQ_LEN, 128)
        behind = jnp.concatenate([last[:, 0:1] + right_sum, last[:, 1:2]], axis=1).reshape(SEQ_LEN, 128)
        size *= 2
        aheads[size], behinds[size] = ahead, behind
    return lane, place, g, writes, aheads, behinds


def near_decays(place, aheads, back):
    ahead = aheads[8]
    gap = jnp.where(place % 8 >= back, ahead - down(ahead, back), 0.0)
    return jnp.where(place % 8 >= back, jnp.exp(gap), 0.0)


def halves(value):
    return value[:HALF], value[HALF:]


def to_slots(blocks, cross, place, writes, aheads, behinds, nears):
    grow = {size: jnp.exp(aheads[size]) for size in LEVELS}
    keep = {size: split(jnp.exp(behinds[size]) * writes) for size in LEVELS}
    outs = []
    for half in range(2):
        here = slice(half * HALF, (half + 1) * HALF)
        block = blocks[half]
        parts = split(block)
        total = None
        for size in LEVELS:
            mask = level_mask(size)
            masked = tuple(jnp.where(mask, part, jnp.zeros_like(part)) for part in parts)
            term = grow[size][here] * dot3(masked, tuple(k[here] for k in keep[size]), NN)
            total = term if total is None else total + term
        for back in range(8):
            near = jnp.sum(jnp.where(band_mask(back), block, 0.0), axis=1, keepdims=True)
            total = total + near * nears[back][here]
        if half == 1:
            far = split((jnp.exp(behinds[HALF]) * writes)[:HALF])
            total = total + jnp.exp(aheads[HALF])[HALF:] * dot3(split(cross), far, NN)
        outs.append(total)
    return jnp.concatenate(outs, axis=0)


def to_tokens(slots, writes, aheads, behinds, nears):
    blocks = []
    for half in range(2):
        here = slice(half * HALF, (half + 1) * HALF)
        total = jnp.zeros((HALF, HALF), F32)
        for size in LEVELS:
            left = split((slots * jnp.exp(aheads[size]))[here])
            right = split((jnp.exp(behinds[size]) * writes)[here])
            total = jnp.where(level_mask(size), dot3(left, right, NT), total)
        for back in range(8):
            near = jnp.sum(slots[here] * nears[back][here], axis=1, keepdims=True)
            total = jnp.where(band_mask(back), near, total)
        blocks.append(total)
    left = split((slots * jnp.exp(aheads[HALF]))[HALF:])
    right = split((jnp.exp(behinds[HALF]) * writes)[:HALF])
    return blocks, dot3(left, right, NT)


def forward_kernel(q_ref, k_ref, v_ref, f_ref, o_ref, p_ref, s_ref, a_ref, b_ref):
    query = split(silu_parts(q_ref[...])[1] * KDIM ** (-0.5))
    keys = split(silu_parts(k_ref[...])[1])
    values = split(v_ref[...])
    lane, place, g, writes, aheads, behinds = gates(f_ref[...])
    nears = [near_decays(place, aheads, back) * down(writes, back) for back in range(8)]
    q0, q1 = tuple(x[:HALF] for x in query), tuple(x[HALF:] for x in query)
    k0, k1 = tuple(x[:HALF] for x in keys), tuple(x[HALF:] for x in keys)
    blocks = (dot3(q0, k0, NT), dot3(q1, k1, NT))
    cross = dot3(q1, k0, NT)
    scores = to_slots(blocks, cross, place, writes, aheads, behinds, nears)
    shown = jnp.where(lane, scores, -1e30)
    weights = jnp.exp(shown - jnp.max(shown, axis=1, keepdims=True))
    weights = jnp.where(lane, weights, 0.0)
    weights = weights / jnp.sum(weights, axis=1, keepdims=True)
    mixes, mix_cross = to_tokens(weights, writes, aheads, behinds, nears)
    v0 = tuple(x[:HALF] for x in values)
    o_ref[:HALF, :] = dot3(split(mixes[0]), v0, NN).astype(o_ref.dtype)
    row = jnp.concatenate([mix_cross, mixes[1]], axis=1)
    o_ref[HALF:, :] = dot3(split(row), values, NN).astype(o_ref.dtype)
    p_ref[...] = weights
    s_ref[...] = scores
    a_ref[:HALF, :] = jnp.concatenate([blocks[0], jnp.zeros_like(cross)], axis=1)
    a_ref[HALF:, :] = jnp.concatenate([cross, blocks[1]], axis=1)
    b_ref[:HALF, :] = jnp.concatenate([mixes[0], jnp.zeros_like(cross)], axis=1)
    b_ref[HALF:, :] = row


def backward_kernel(q_ref, k_ref, v_ref, f_ref, p_ref, s_ref, a_ref, b_ref, d_ref, out_ref):
    lane, place, g, writes, aheads, behinds = gates(f_ref[...])
    spans = [near_decays(place, aheads, back) for back in range(8)]
    nears = [spans[back] * down(writes, back) for back in range(8)]
    weights, scores = p_ref[...], s_ref[...]
    products, mixing = a_ref[...], b_ref[...]
    grad = split(d_ref[...])
    g0, g1 = tuple(x[:HALF] for x in grad), tuple(x[HALF:] for x in grad)
    values = split(v_ref[...])
    v0, v1 = tuple(x[:HALF] for x in values), tuple(x[HALF:] for x in values)
    m_parts = split(mixing)
    dv0 = dot3(tuple(x[:, :HALF] for x in m_parts), grad, TN)
    dv1 = dot3(tuple(x[HALF:, HALF:] for x in m_parts), g1, TN)
    out_ref[:HALF, 2 * KDIM : 3 * KDIM] = dv0.astype(BF16)
    out_ref[HALF:, 2 * KDIM : 3 * KDIM] = dv1.astype(BF16)
    mix_blocks = (dot3(g0, v0, NT), dot3(g1, v1, NT))
    mix_cross = dot3(g1, v0, NT)
    d_weights = to_slots(mix_blocks, mix_cross, place, writes, aheads, behinds, nears)
    inner = jnp.sum(weights * d_weights, axis=1, keepdims=True)
    d_scores = weights * (d_weights - inner)
    d_blocks, d_cross = to_tokens(d_scores, writes, aheads, behinds, nears)
    q_gate, q_act = silu_parts(q_ref[...])
    k_gate, k_act = silu_parts(k_ref[...])
    scale = KDIM ** (-0.5)
    query, keys = split(q_act * scale), split(k_act)
    k0 = tuple(x[:HALF] for x in keys)
    low = split(jnp.concatenate([d_cross, d_blocks[1]], axis=1))
    top = split(d_blocks[0])
    dq = jnp.concatenate([dot3(top, k0, NN), dot3(low, keys, NN)], axis=0)
    first = tuple(jnp.concatenate([t, l[:, :HALF]], axis=0) for t, l in zip(top, low))
    dk0 = dot3(first, query, TN)
    dk1 = dot3(tuple(x[:, HALF:] for x in low), tuple(x[HALF:] for x in query), TN)
    dk = jnp.concatenate([dk0, dk1], axis=0)
    out_ref[:, :KDIM] = (dq * scale * (q_gate + q_act * (1.0 - q_gate))).astype(BF16)
    out_ref[:, KDIM : 2 * KDIM] = (dk * (k_gate + k_act * (1.0 - k_gate))).astype(BF16)
    parts = []
    for half in range(2):
        here = slice(half * HALF, (half + 1) * HALF)
        both = jnp.concatenate([mix_blocks[half], products[here, here]], axis=0)
        both_parts = split(both)
        total = None
        for size in LEVELS:
            mask = level_mask(size)
            mask = jnp.concatenate([mask, mask], axis=0)
            grow = jnp.exp(aheads[size][here])
            right = split(jnp.concatenate([weights[here] * grow, d_scores[here] * grow], axis=0))
            left = tuple(jnp.where(mask, part, jnp.zeros_like(part)) for part in both_parts)
            term = jnp.exp(behinds[size][here]) * dot3(left, right, TN)
            total = term if total is None else total + term
        parts.append(total)
    grow = jnp.exp(aheads[HALF][HALF:])
    left = split(jnp.concatenate([mix_cross, products[HALF:, :HALF]], axis=0))
    right = split(jnp.concatenate([weights[HALF:] * grow, d_scores[HALF:] * grow], axis=0))
    parts[0] = parts[0] + jnp.exp(behinds[HALF][:HALF]) * dot3(left, right, TN)
    reach = jnp.concatenate(parts, axis=0)
    for back in range(8):
        mask = band_mask(back)
        near_mix = jnp.concatenate([jnp.sum(jnp.where(mask, mix_blocks[h], 0.0), axis=1, keepdims=True) for h in range(2)], axis=0)
        near_pro = jnp.concatenate(
            [jnp.sum(jnp.where(mask, products[h * HALF : (h + 1) * HALF, h * HALF : (h + 1) * HALF], 0.0), axis=1, keepdims=True) for h in range(2)],
            axis=0,
        )
        reach = reach + up((near_mix * weights + near_pro * d_scores) * spans[back], back)
    d_sum = weights * d_weights + d_scores * scores - writes * reach
    step = 1
    while step < SEQ_LEN:
        d_sum = d_sum + jnp.where(place < SEQ_LEN - step, up(d_sum, step), 0.0)
        step *= 2
    d_log = d_sum - reach * jnp.exp(g)
    d_forget = d_log * 0.125 / (1.0 + jnp.exp(f_ref[...]))
    out_ref[:, 3 * KDIM :] = jnp.where(lane, d_forget, 0.0).astype(BF16)


def spec(width, column):
    return pl.BlockSpec((SEQ_LEN, width), lambda i: (i, column))


IN_SPECS = [spec(KDIM, 0), spec(KDIM, 1), spec(KDIM, 2), spec(128, 3 * KDIM // 128)]


def mixer_forward(proj):
    rows = proj.shape[0]
    shape = lambda width, kind: jax.ShapeDtypeStruct((rows, width), kind)
    return pl.pallas_call(
        forward_kernel,
        grid=(rows // SEQ_LEN,),
        in_specs=IN_SPECS,
        out_specs=[spec(KDIM, 0), spec(128, 0), spec(128, 0), spec(SEQ_LEN, 0), spec(SEQ_LEN, 0)],
        out_shape=[shape(KDIM, BF16), shape(128, F32), shape(128, F32), shape(SEQ_LEN, F32), shape(SEQ_LEN, F32)],
        compiler_params=pltpu.CompilerParams(vmem_limit_bytes=48 << 20),
        cost_estimate=pl.CostEstimate(flops=rows * 3000000, bytes_accessed=rows * 10000, transcendentals=rows * 3000),
        name="mixer_forward",
    )(proj, proj, proj, proj)


def mixer_backward(proj, saved, grad):
    rows = proj.shape[0]
    weights, scores, products, mixing = saved
    return pl.pallas_call(
        backward_kernel,
        grid=(rows // SEQ_LEN,),
        in_specs=IN_SPECS + [spec(128, 0), spec(128, 0), spec(SEQ_LEN, 0), spec(SEQ_LEN, 0), spec(KDIM, 0)],
        out_specs=spec(WIDE, 0),
        out_shape=jax.ShapeDtypeStruct((rows, WIDE), BF16),
        compiler_params=pltpu.CompilerParams(vmem_limit_bytes=48 << 20),
        cost_estimate=pl.CostEstimate(flops=rows * 9000000, bytes_accessed=rows * 16000, transcendentals=rows * 5000),
        name="mixer_backward",
    )(proj, proj, proj, proj, weights, scores, products, mixing, grad)


MESH = pl.DeviceIdType.MESH
ANY = pl.BlockSpec(memory_space=pl.ANY)
VMEM = pl.BlockSpec(memory_space=pltpu.VMEM)
DMA = pltpu.SemaphoreType.DMA
PIECE = 32


class Place:
    def __init__(self):
        dp = lax.axis_index("dp")
        self.core = lax.axis_index("head")
        self.x, self.y, self.z = dp % 2, dp // 2 % 2, dp // 4
        rest = dp % 4
        self.peers = {
            "x": (dp + 1 - 2 * self.x, self.core),
            "y": (dp + 2 - 4 * self.y, self.core),
            "up": ((self.z + 1) % 4 * 4 + rest, self.core),
            "down": ((self.z + 3) % 4 * 4 + rest, self.core),
            "core": (dp, 1 - self.core),
        }

    def greet(self):
        ready = pltpu.get_barrier_semaphore()
        for peer in self.peers.values():
            pl.semaphore_signal(ready, inc=1, device_id=peer, device_id_type=MESH)
        pl.semaphore_wait(ready, len(self.peers))

    def copy(self, name, source, target, sems):
        return pltpu.make_async_remote_copy(
            src_ref=source,
            dst_ref=target,
            send_sem=sems[0],
            recv_sem=sems[1],
            device_id=self.peers[name],
            device_id_type=MESH,
        )

    def half(self, size, other=False):
        place = 1 - self.x if other else self.x
        return pl.ds(pl.multiple_of(place * size, size), size)

    def columns(self, index, size):
        natural = (self.z + index % 4) % 4 * 2 + (self.y + index // 4) % 2
        return pl.ds(pl.multiple_of(natural * size, size), size)


class Sems:
    def __init__(self, ref):
        self.ref, self.used = ref, 0

    def one(self):
        self.used += 1
        return self.ref.at[self.used - 1]

    def two(self):
        return (self.one(), self.one())


def pieces(rows, work):
    def step(i, carry):
        work(pl.ds(pl.multiple_of(i * PIECE, PIECE), PIECE))
        return carry

    lax.fori_loop(0, rows // PIECE, step, 0)


class Keep:
    def __init__(self, sems, source, target, stage):
        self.load = pltpu.make_async_copy(source, stage, sems.one())
        self.store = pltpu.make_async_copy(stage, target, sems.one())

    def start(self):
        self.load.start()

    def turn(self):
        self.load.wait()
        self.store.start()

    def wait(self):
        self.store.wait()


class Quad:
    def __init__(self, place, sems, source, target):
        near = [pltpu.make_async_copy(source, target.at[0], sems.one())]
        self.swap = place.copy("x", source, target.at[1], sems.two())
        self.core = place.copy("core", source, target.at[2], sems.two())
        self.last = place.copy("core", target.at[1], target.at[3], sems.two())
        self.near = near

    def start(self):
        self.swap.start()
        self.core.start()
        for copy in self.near:
            copy.start()

    def forward(self):
        self.swap.wait_recv()
        self.last.start()

    def finish(self):
        self.swap.wait_send()
        self.core.wait()
        self.last.wait()
        for copy in self.near:
            copy.wait()


class QuadSum:
    def __init__(self, place, sems, terms, scratch):
        self.near, self.theirs, self.far, self.swapped = scratch
        self.core = place.copy("core", terms.at[pl.ds(2, 2)], self.theirs, sems.two())
        self.load = pltpu.make_async_copy(terms.at[pl.ds(0, 2)], self.near, sems.one())
        self.swap = place.copy("x", self.far, self.swapped, sems.two())

    def start(self):
        self.core.start()
        self.load.start()

    def middle(self):
        self.core.wait()
        self.load.wait()

        def add(part):
            self.far[part] = (self.near[1, part] + self.theirs[1, part]).astype(BF16)

        pieces(SEQ_LEN, add)
        self.swap.start()

    def ready(self):
        self.swap.wait()

    def read(self, part):
        return self.near[0, part] + self.theirs[0, part] + self.swapped[part].astype(F32)


def quad_scratch(width):
    return [
        pltpu.VMEM((2, SEQ_LEN, width), F32),
        pltpu.VMEM((2, SEQ_LEN, width), F32),
        pltpu.VMEM((SEQ_LEN, width), BF16),
        pltpu.VMEM((SEQ_LEN, width), BF16),
    ]


class Leave:
    def __init__(self, place, sems, source, target):
        rows = pl.ds(pl.multiple_of(place.core * SEQ_LEN, SEQ_LEN), SEQ_LEN)
        width = source.shape[1] // 8
        self.copies, self.here = [], []
        for index in range(8):
            part = source.at[:, pl.ds(index * width, width)]
            there = target.at[rows, place.columns(index, width)]
            self.copies.append(place.copy("core", part, there, sems.two()))
            self.here.append(pltpu.make_async_copy(part, there, sems.one()))

    def start(self):
        for copy in self.copies + self.here:
            copy.start()

    def finish(self):
        for copy in self.copies + self.here:
            copy.wait()


def gather_first_kernel(
    tokens, q_w, k_w, v_w, small, out_w, gate_w, up_w, down_w, w_in, w_out, ffn, seqs, stage, held, sem
):
    place, sems = Place(), Sems(sem)
    shard = q_w.shape[0]
    rows = place.half(shard)
    hid = gate_w.shape[1] // 2
    chunks = [
        (small, 128, w_in, 3 * KDIM, False, True),
        (q_w, KDIM, w_in, 0, False, True),
        (k_w, KDIM, w_in, KDIM, False, True),
        (v_w, KDIM, w_in, 2 * KDIM, False, True),
        (out_w, KDIM, w_out, 0, True, True),
        (gate_w, hid, ffn, 0, False, False),
        (up_w, hid, ffn, hid, False, False),
        (down_w, hid, ffn, 2 * hid, False, False),
    ]
    place.greet()
    swaps, keeps, rises, crosses = [], [], [], []
    used = 0
    for source, width, target, first, y_first, beyond in chunks:
        cols = pl.ds(first, width)
        where = target.at[0, rows, cols] if beyond else target.at[rows, cols]
        swaps.append(place.copy("x", source.at[:, place.half(width, True)], where, sems.two()))
        keeps.append(Keep(sems, source.at[:, place.half(width)], where, stage.at[:, pl.ds(used, width)]))
        used += width
        if not beyond:
            continue

        def block(index, target=target, cols=cols):
            return target.at[index, :, cols]

        rises.append(
            [
                [place.copy("up", block((4 - step) % 4 + 4 * u), block(3 - step + 4 * u), sems.two()) for step in range(3)]
                for u in range(2 if y_first else 1)
            ]
        )
        crosses.append(
            [place.copy("y", block(i), block(4 + i), sems.two()) for i in range(1 if y_first else 4)]
        )
    for swap, keep in zip(swaps[:5], keeps[:5]):
        swap.start()
        keep.start()
    width = tokens.shape[1] // 8
    mine = pl.ds(pl.multiple_of(place.core * SEQ_LEN, SEQ_LEN), SEQ_LEN)
    near, far, side, last = [], [], [], []
    for index in range(8):
        part = tokens.at[mine, place.columns(index, width)]
        cols = pl.ds(index * width, width)
        far.append(place.copy("x", part, seqs.at[1, :, cols], sems.two()))
        side.append(place.copy("core", part, seqs.at[2, :, cols], sems.two()))
        near.append(Keep(sems, part, seqs.at[0, :, cols], held.at[:, cols]))
    last.append(place.copy("core", seqs.at[1], seqs.at[3], sems.two()))
    for copy in far + side + near:
        copy.start()
    for swap, keep in zip(swaps[5:], keeps[5:]):
        swap.start()
        keep.start()
    for keep in keeps + near:
        keep.turn()
    for c in range(5):
        keeps[c].wait()
        swaps[c].wait_recv()
        rises[c][0][0].start()
        crosses[c][0].start()
    for step in range(3):
        if step == 0:
            for c in range(5):
                if chunks[c][4]:
                    crosses[c][0].wait_recv()
                    rises[c][1][0].start()
        if step == 1:
            for copy in far:
                copy.wait_recv()
            last[0].start()
        for c in range(5):
            for rise in rises[c]:
                rise[step].wait_recv()
                if step < 2:
                    rise[step + 1].start()
            if not chunks[c][4]:
                crosses[c][3 - step].start()
    for c in range(5):
        for cross in crosses[c]:
            cross.wait_send()
        if not chunks[c][4]:
            for cross in crosses[c]:
                cross.wait_recv()
        for rise in rises[c]:
            for copy in rise:
                copy.wait_send()
    for swap in swaps[:5]:
        swap.wait_send()
    for swap, keep in zip(swaps[5:], keeps[5:]):
        swap.wait()
        keep.wait()
    for copy in far:
        copy.wait_send()
    for copy in side + near + last:
        copy.wait()


def gather_ffn_kernel(
    hid, cut, b0, b3, b4, terms, tokens, gain, d_ffn, w_gate, w_up, w_down, resid, ffn_in, d_all, s0, s1, s2, s3, kept, normed, inputs, low, stage, sem
):
    place, sems = Place(), Sems(sem)
    chunks = [
        (0, hid, w_gate, 0, False),
        (hid, hid, w_up, 0, False),
        (2 * hid, cut, w_down, 0, False),
        (2 * hid + cut, hid - cut, w_down, cut, True),
    ]
    keeps, rises, crosses = [], [], []
    for first, width, target, start, y_first in chunks:
        cols, source = pl.ds(start, width), pl.ds(first, width)

        def block(index, target=target, cols=cols):
            return target.at[index, :, cols]

        keeps += [
            Keep(sems, b.at[:, source], block(i), stage.at[at, :, source])
            for at, (b, i) in enumerate(((b0, 0), (b3, 3), (b4, 4)))
        ]
        lower = [
            place.copy("up", b3.at[:, source], block(2), sems.two()),
            place.copy("up", block(2), block(1), sems.two()),
        ]
        high = []
        if y_first:
            high = [
                place.copy("up", b4.at[:, source], block(7), sems.two()),
                place.copy("up", block(7), block(6), sems.two()),
                place.copy("up", block(6), block(5), sems.two()),
            ]
            crosses.append([])
        else:
            crosses.append(
                [
                    place.copy("y", b3.at[:, source], block(7), sems.two()),
                    place.copy("y", block(2), block(6), sems.two()),
                    place.copy("y", block(1), block(5), sems.two()),
                ]
            )
        rises.append((lower, high))
    total = QuadSum(place, sems, terms, (s0, s1, s2, s3))
    cot = Quad(place, sems, low, d_all)
    fetch_low = pltpu.make_async_copy(d_ffn, low, sems.one())
    out = Quad(place, sems, normed, ffn_in)
    fetch = pltpu.make_async_copy(tokens.at[0], inputs, sems.one())
    save = pltpu.make_async_copy(kept, resid, sems.one())
    place.greet()
    total.start()
    fetch.start()
    fetch_low.start()
    for (lower, high), cross in zip(rises, crosses):
        lower[0].start()
        for copy in high[:1] + cross[:1]:
            copy.start()
    for copy in keeps:
        copy.start()
    total.middle()
    for copy in keeps:
        copy.turn()
    fetch.wait()
    for c, ((lower, high), cross) in enumerate(zip(rises, crosses)):
        if c == 2:
            total.ready()

            def norm(part):
                value = total.read(part) + inputs[part].astype(F32)
                kept[part] = value
                normed[part] = (value * rms(value) * gain[...]).astype(BF16)

            pieces(SEQ_LEN, norm)
            out.start()
            save.start()
            fetch_low.wait()
            cot.start()
        lower[0].wait_recv()
        lower[1].start()
        for copy in cross[1:2]:
            copy.start()
        if high:
            high[0].wait_recv()
            high[1].start()
    for c, ((lower, high), cross) in enumerate(zip(rises, crosses)):
        lower[1].wait_recv()
        for copy in cross[2:]:
            copy.start()
        if high:
            high[1].wait_recv()
            high[2].start()
        if c == 1:
            out.forward()
    cot.forward()
    for (lower, high), cross in zip(rises, crosses):
        for copy in cross:
            copy.wait()
        for copy in high[2:]:
            copy.wait_recv()
        for copy in lower + high:
            copy.wait_send()
    for copy in keeps:
        copy.wait()
    out.finish()
    cot.finish()
    save.wait()


class Sum:
    def __init__(self, place, sems, terms, given, result, first, width, scratch):
        self.own, self.other, self.from_z, self.to_z, self.final = scratch
        cols = pl.ds(first, width)
        self.loads, self.crosses = [], []
        for index in range(4):
            self.loads.append(pltpu.make_async_copy(terms.at[index, :, cols], self.own.at[index], sems.one()))
            if given is None:
                self.crosses.append(place.copy("y", terms.at[4 + index, :, cols], self.other.at[index], sems.two()))
            else:
                self.loads.append(pltpu.make_async_copy(given.at[index, :, cols], self.other.at[index], sems.one()))
        self.per = len(self.loads) // 4
        self.rises = [place.copy("up", self.to_z.at[i], self.from_z.at[i], sems.two()) for i in range(3)]
        half = self.final.shape[0] // 2
        there = result.at[:, place.half(width)]
        self.leave = pltpu.make_async_copy(self.final.at[place.half(half)], there, sems.one())
        self.swap = place.copy("x", self.final.at[place.half(half, True)], there, sems.two())

    def start(self, step):
        index = 3 - step
        for copy in self.crosses[index : index + 1] + self.loads[index * self.per : (index + 1) * self.per]:
            copy.start()

    def step(self, step):
        index = 3 - step
        for copy in self.loads[index * self.per : (index + 1) * self.per]:
            copy.wait()
        for copy in self.crosses[index : index + 1]:
            copy.wait_recv()
        if step:
            self.rises[step - 1].wait_recv()

        def add(part):
            value = self.own[index, part].astype(F32) + self.other[index, part].astype(F32)
            if step:
                value = value + self.from_z[step - 1, part].astype(F32)
            if step < 3:
                self.to_z[step, part] = value.astype(BF16)
            else:
                self.final[part] = value

        pieces(self.final.shape[0], add)
        if step < 3:
            self.rises[step].start()
        else:
            self.swap.start()
            self.leave.start()

    def finish(self):
        for copy in self.crosses + self.rises:
            copy.wait_send()
        self.leave.wait()
        self.swap.wait()


def sum_scratch(rows, width):
    return [pltpu.VMEM((depth, rows, width), BF16) for depth in (4, 4, 3, 3)] + [pltpu.VMEM((rows, width), F32)]


def norm_back_piece(value, gain, grad):
    scale = rms(value)
    scaled = gain * grad
    inner = jnp.mean(scaled * value, axis=-1, keepdims=True)
    gains = (grad * value * scale).reshape(PIECE // 8, 8, value.shape[1])
    return scale * scaled - value * (scale * scale * scale * inner), jnp.sum(gains, axis=0)


def sum_ffn_kernel(
    hid, gate, down, given, terms, resid, gain, d_res, out_terms, live, gate_sum, down_sum, d_h, d_attn, gain_sum, block_out, *scratch
):
    *scratch, sem = scratch
    place, sems = Place(), Sems(sem)
    first = Sum(place, sems, down, given, down_sum, 0, hid, scratch[0:5])
    second = Sum(place, sems, gate, None, gate_sum, 0, hid, scratch[5:10])
    back = QuadSum(place, sems, terms, scratch[10:14])
    ahead = QuadSum(place, sems, out_terms, scratch[14:18])
    value, res, low, shown = scratch[18:22]
    quad = Quad(place, sems, low, d_attn)
    leave = Leave(place, sems, shown, block_out)
    fetch = [pltpu.make_async_copy(resid, value, sems.one()), pltpu.make_async_copy(d_res, res, sems.one())]
    save = pltpu.make_async_copy(res, d_h, sems.one())
    place.greet()
    back.start()
    for step in range(4):
        second.start(step)
        first.start(step)
    for copy in fetch:
        copy.start()
    ahead.start()
    first.step(0)
    back.middle()
    ahead.middle()
    second.step(0)
    for copy in fetch:
        copy.wait()
    first.step(1)
    back.ready()
    gain_sum[...] = jnp.zeros_like(gain_sum)

    def norm(part):
        d_norm, gains = norm_back_piece(value[part], gain[...], back.read(part))
        grad = res[part] + d_norm
        res[part] = grad
        low[part] = grad.astype(BF16)
        gain_sum[...] += gains

    pieces(SEQ_LEN, norm)
    quad.start()
    save.start()
    second.step(1)
    first.step(2)
    ahead.ready()

    def show(part):
        shown[part] = (live[part, :1] * (value[part] + ahead.read(part))).astype(BF16)

    pieces(SEQ_LEN, show)
    leave.start()
    second.step(2)
    quad.forward()
    first.step(3)
    second.step(3)
    quad.finish()
    save.wait()
    leave.finish()
    first.finish()
    second.finish()


def sum_last_kernel(
    hid, up, given, out_t, in_t, terms, tokens, gain, d_h, ffn_gains, up_sum, out_sum, q_sum, k_sum, v_sum, f_sum, grad, gain_sum, *scratch
):
    *scratch, sem = scratch
    place, sems = Place(), Sems(sem)
    sums = []
    for terms_in, given_in, result, start, width in (
        (up, given, up_sum, 0, hid),
        (out_t, None, out_sum, 0, KDIM),
        (in_t, None, q_sum, 0, KDIM),
        (in_t, None, k_sum, KDIM, KDIM),
        (in_t, None, v_sum, 2 * KDIM, KDIM),
        (in_t, None, f_sum, 3 * KDIM, 128),
    ):
        sums.append(Sum(place, sems, terms_in, given_in, result, start, width, scratch[: 5]))
        scratch = scratch[5:]
    back = QuadSum(place, sems, terms, scratch[0:4])
    value, res, gains, parts, met, crossed, risen, rising, last, swapped = scratch[4:]
    leave = Leave(place, sems, res, grad)
    fetch = [pltpu.make_async_copy(tokens.at[0], value, sems.one()), pltpu.make_async_copy(d_h, res, sems.one())]
    meet = place.copy("core", parts, met, sems.two())
    cross = place.copy("y", parts.at[pl.ds(4, 4)], crossed, sems.two())
    rise = [place.copy("up", rising.at[i], risen.at[i], sems.two()) for i in range(3)]
    swap = place.copy("x", last.at[1 - place.x], swapped, sems.two())
    place.greet()
    back.start()
    for step in range(4):
        for one in sums:
            one.start(step)
    for copy in fetch:
        copy.start()
    sums[0].step(0)
    back.middle()
    for one in sums[1:]:
        one.step(0)
    for copy in fetch:
        copy.wait()
    gains[...] = jnp.zeros_like(gains)
    back.ready()

    def norm(part):
        d_norm, added = norm_back_piece(value[part].astype(F32), gain[...], back.read(part))
        res[part] = res[part] + d_norm
        gains[...] += added

    pieces(SEQ_LEN, norm)
    leave.start()
    width = res.shape[1] // 8
    parts[...] = jnp.zeros_like(parts)
    for row, source in enumerate((gains[...], ffn_gains[...])):
        summed = jnp.sum(source, axis=0, keepdims=True)
        for index in range(8):
            parts[index, row : row + 1, :] = summed[:, index * width : (index + 1) * width]
    meet.start()
    for one in sums:
        one.step(1)
    meet.wait()
    parts[...] = parts[...] + met[...]
    cross.start()
    for one in sums:
        one.step(2)
    cross.wait()
    rising[0] = parts[3] + crossed[3]
    rise[0].start()
    for one in sums:
        one.step(3)
    for step in (1, 2):
        rise[step - 1].wait_recv()
        rising[step] = parts[3 - step] + crossed[3 - step] + risen[step - 1]
        rise[step].start()
    rise[2].wait_recv()
    total = parts[0] + crossed[0] + risen[2]
    last[0] = total[:, : width // 2]
    last[1] = total[:, width // 2 :]
    swap.start()
    swap.wait()
    gain_sum[...] = last[place.x] + swapped[...]
    for copy in rise:
        copy.wait_send()
    leave.finish()
    for one in sums:
        one.finish()


def call(kernel, name, ident, inputs, specs, outputs, out_specs, scratch, sems):
    return pl.pallas_call(
        kernel,
        in_specs=specs,
        out_specs=out_specs,
        out_shape=[jax.ShapeDtypeStruct(shape, kind) for shape, kind in outputs],
        scratch_shapes=scratch + [DMA((sems,))],
        compiler_params=pltpu.CompilerParams(collective_id=ident, has_side_effects=True, vmem_limit_bytes=60 << 20),
        name=name,
    )(*inputs)


PAD = 128 - SLOTS


class Ring:
    def __init__(self, count):
        self.count = count
        self.stages = []
        left, stride = count // 2, count
        while left > 1:
            size = 4 if left % 4 == 0 else 2
            stride //= size
            left //= size
            self.stages.append((stride, size))

    def perm(self, stride, size, shift):
        moves = []
        for source in range(self.count):
            digit = source // stride % size
            moves.append((source, source + ((digit + shift) % size - digit) * stride))
        return moves

    def send(self, value, stage, shift):
        stride, size = stage
        return lax.ppermute(value, "dp", self.perm(stride, size, shift % size))

    def swap(self, value):
        return lax.ppermute(value, "dp", self.perm(1, 2, 1))

    def digit(self, stage):
        return lax.axis_index("dp") // stage[0] % stage[1]

    def gather(self, block):
        blocks = [block]
        for stage in self.stages:
            more = list(blocks)
            for shift in range(1, stage[1]):
                more += [self.send(one, stage, -shift) for one in blocks]
            blocks = more
        return blocks

    def scatter(self, make):
        def level(depth, offset, width):
            if depth == len(self.stages):
                return lambda inner: make(offset + inner)
            return None

        widths = [1]
        for stage in self.stages:
            widths.append(widths[-1] * stage[1])

        def total(depth, index):
            if depth == len(self.stages):
                return make(index)
            stage = self.stages[depth]
            parts = []
            for shift in range(1, stage[1]):
                sent = total(depth + 1, index + shift * widths[depth]).astype(BF16)
                parts.append(self.send(sent, stage, shift))
            mine = total(depth + 1, index)
            for part in parts:
                mine = mine + part.astype(F32)
            return mine

        return total(0, 0)

    def order(self, value, width, back=False):
        parts = [value[:, i * width : (i + 1) * width] for i in range(self.count // 2)]
        stages = self.stages
        if back:
            parts = self.turn_digits(parts, [s[1] for s in stages[::-1]])
        inner = len(parts)
        for stage in stages:
            size = stage[1]
            inner //= size
            digit = self.digit(stage)
            new = []
            for place in range(len(parts)):
                at = place // inner % size
                base = place - at * inner
                picks = []
                for k in range(size):
                    picks.append(parts[base + ((at - k) % size if back else (at + k) % size) * inner])
                one = picks[0]
                for k in range(1, size):
                    one = jnp.where(digit == k, picks[k], one)
                new.append(one)
            parts = new
        if not back:
            parts = self.turn_digits(parts, [s[1] for s in stages])
        return jnp.concatenate(parts, axis=1)

    def turn_digits(self, parts, sizes):
        count = len(parts)
        out = [None] * count
        for index in range(count):
            rest, digits = index, []
            for size in reversed(sizes):
                digits.append(rest % size)
                rest //= size
            new = 0
            for digit, size in zip(digits, reversed(sizes)):
                new = new * size + digit
            out[new] = parts[index]
        return out


def mm(left, right, dims=NN, kind=F32):
    return lax.dot_general(left, right, dims, preferred_element_type=F32).astype(kind)


def rms(values):
    return lax.rsqrt(jnp.mean(values * values, axis=-1, keepdims=True) + 1e-06)


def norm_back(values, gain, grad):
    scale = rms(values)
    scaled = gain * grad
    inner = jnp.mean(scaled * values, axis=-1, keepdims=True)
    return scale * scaled - values * (scale * scale * scale * inner), jnp.sum(grad * values * scale, axis=0)


def body_by_permutes(
    tokens,
    seq_count,
    valid_len,
    attn_gain,
    ffn_gain,
    q_weight,
    k_weight,
    v_weight,
    forget_weight,
    out_weight,
    gate_weight,
    up_weight,
    down_weight,
    cotangent,
    *,
    ring,
):
    shard = q_weight.shape[0]
    width = 2 * shard
    core = lax.axis_index("head")
    even = lax.axis_index("dp") % 2 == 0
    first = core == 0
    rows = tokens.shape[0]

    def other_core(value):
        return lax.ppermute(value, "head", [(0, 1), (1, 0)])

    def pair_rows(mine, theirs, axis=0):
        return jnp.where(
            even, jnp.concatenate([mine, theirs], axis=axis), jnp.concatenate([theirs, mine], axis=axis)
        )

    def gather(parts):
        left = jnp.concatenate([p[0] for p in parts], axis=1)
        right = jnp.concatenate([p[1] for p in parts], axis=1)
        mine, theirs = jnp.where(even, left, right), jnp.where(even, right, left)
        return jnp.concatenate(ring.gather(pair_rows(mine, ring.swap(theirs))), axis=0)

    def cut(weight):
        half = weight.shape[1] // 2
        return (weight[:, :half], weight[:, half:])

    def quad_gather(mine):
        chips = jnp.concatenate([mine, ring.swap(mine)], axis=0)
        return jnp.concatenate([chips, other_core(chips)], axis=0)

    def quad_scatter(make):
        theirs = other_core(make(slice(2 * SEQ_LEN, 4 * SEQ_LEN)))
        far = make(slice(SEQ_LEN, 2 * SEQ_LEN)) + theirs[SEQ_LEN:]
        near = make(slice(0, SEQ_LEN)) + theirs[:SEQ_LEN]
        return near + ring.swap(far.astype(BF16)).astype(F32)

    def whole_rows(mine):
        theirs = other_core(mine)
        return jnp.where(
            first, jnp.concatenate([mine, theirs], axis=0), jnp.concatenate([theirs, mine], axis=0)
        )

    def weight_sum(act, grads):
        def make(index):
            return mm(act[:, index * width : (index + 1) * width], grads, TN)

        done = ring.scatter(make)
        mine = jnp.where(even, done[:shard], done[shard:])
        theirs = ring.swap(jnp.where(even, done[shard:], done[:shard]))
        return (jnp.where(even, mine, theirs), jnp.where(even, theirs, mine))

    gains = jnp.concatenate(
        [attn_gain[:, None], ffn_gain[:, None], jnp.zeros((shard, PAD - 2), BF16)], axis=1
    )
    w_in = gather([cut(q_weight), cut(k_weight), cut(v_weight), cut(forget_weight), (gains, gains)])
    w_out = gather([cut(out_weight)])
    w_gate = gather([cut(gate_weight)])
    w_up = gather([cut(up_weight)])
    w_down = gather([cut(down_weight)])
    gain_attn = w_in[:, WIDE - PAD].astype(F32)[None, :]
    gain_ffn = w_in[:, WIDE - PAD + 1].astype(F32)[None, :]

    def own(value):
        return ring.order(jnp.where(first, value[:SEQ_LEN], value[SEQ_LEN:]), width)

    places = lax.broadcasted_iota(jnp.int32, (SEQ_LEN, 1), 0)
    length = jnp.where(first, valid_len[0], valid_len[1])
    live = ((core < seq_count[0]) & (places < length)).astype(F32)
    own_tokens = own(tokens)
    d_res = live * own(cotangent)
    d_ffn = quad_gather(d_res.astype(BF16))
    inputs = quad_gather(own_tokens).astype(F32)
    attn_in = (inputs * rms(inputs) * gain_attn).astype(BF16)
    proj = mm(attn_in, w_in)
    mixed, *saved = mixer_forward(proj)
    own_inputs = own_tokens.astype(F32)
    resid = own_inputs + quad_scatter(lambda r: mm(mixed[r], w_out, NT))
    ffn_in = quad_gather((resid * rms(resid) * gain_ffn).astype(BF16))
    gate, up_vals = mm(ffn_in, w_gate), mm(ffn_in, w_up)
    sig = jax.nn.sigmoid(gate)
    hidden = (gate * sig * up_vals).astype(BF16)
    d_hidden = mm(d_ffn, w_down)
    d_gate = (d_hidden * up_vals * (sig * (1.0 + gate * (1.0 - sig)))).astype(BF16)
    d_up = (d_hidden * (gate * sig)).astype(BF16)
    d_ffn_in = quad_scatter(lambda r: mm(d_gate[r], w_gate, NT) + mm(d_up[r], w_up, NT))
    down_sum = weight_sum(d_ffn, hidden)
    gate_sum = weight_sum(ffn_in, d_gate)
    up_sum = weight_sum(ffn_in, d_up)
    ffn = quad_scatter(lambda r: mm(hidden[r], w_down, NT))
    block_out = whole_rows(ring.order((live * (resid + ffn)).astype(BF16), width, back=True))
    d_norm, ffn_gain_part = norm_back(resid, gain_ffn, d_ffn_in)
    d_h = d_res + d_norm
    d_attn = quad_gather(d_h.astype(BF16))
    d_mixed = mm(d_attn, w_out)
    d_proj = mixer_backward(proj, saved, d_mixed)
    d_attn_in = quad_scatter(lambda r: mm(d_proj[r], w_in, NT))
    out_sum = weight_sum(d_attn, mixed)
    in_sum = weight_sum(attn_in, d_proj)
    d_input, attn_gain_part = norm_back(own_inputs, gain_attn, d_attn_in)
    input_grad = whole_rows(ring.order(d_h + d_input, width, back=True))

    both = jnp.stack([attn_gain_part, ffn_gain_part], axis=0)
    both = both + other_core(both)
    both = both.reshape(2, ring.count // 2, width)
    for stage in ring.stages[::-1]:
        size = stage[1]
        both = both.reshape(2, size, -1, width)
        parts = [ring.send(both[:, shift], stage, shift) for shift in range(1, size)]
        both = both[:, 0]
        for part in parts:
            both = both + part
    both = both.reshape(2, 2, shard)
    both = jnp.where(even, both[:, 0], both[:, 1]) + ring.swap(jnp.where(even, both[:, 1], both[:, 0]))

    def columns(pieces, start, stop):
        return jnp.concatenate([p[:, start:stop] for p in pieces], axis=1)

    return (
        block_out,
        input_grad,
        both[0],
        both[1],
        columns(in_sum, 0, KDIM),
        columns(in_sum, KDIM, 2 * KDIM),
        columns(in_sum, 2 * KDIM, 3 * KDIM),
        columns(in_sum, 3 * KDIM, 3 * KDIM + SLOTS),
        columns(out_sum, 0, KDIM),
        jnp.concatenate(gate_sum, axis=1),
        jnp.concatenate(up_sum, axis=1),
        jnp.concatenate(down_sum, axis=1),
    )


def body_by_kernels(
    tokens,
    seq_count,
    valid_len,
    attn_gain,
    ffn_gain,
    q_weight,
    k_weight,
    v_weight,
    forget_weight,
    out_weight,
    gate_weight,
    up_weight,
    down_weight,
    cotangent,
    *,
    ring,
):
    shard, dim = q_weight.shape[0], tokens.shape[1]
    width, hid = 2 * shard, gate_weight.shape[1] // 2
    core = lax.axis_index("head")
    first = core == 0
    up_z, over_y = (lambda value: ring.send(value, ring.stages[0], 1)), (lambda value: ring.send(value, ring.stages[1], 1))
    rows4 = (4, SEQ_LEN, dim)
    blocks = lambda value: value.reshape(-1, width, value.shape[-1])
    flat = lambda value: value.reshape(-1, value.shape[-1])
    half = dim // 2

    gains = jnp.concatenate([attn_gain[:, None], ffn_gain[:, None], jnp.zeros((shard, PAD - 2), BF16)], axis=1)
    small = jnp.concatenate([forget_weight[:, :SLOTS], gains, forget_weight[:, SLOTS:], gains], axis=1)
    w_in, w_out, part0, seqs = call(
        gather_first_kernel,
        "gather_first",
        0,
        (tokens, q_weight, k_weight, v_weight, small, out_weight, gate_weight, up_weight, down_weight),
        [ANY] * 9,
        [((8, width, WIDE), BF16), ((8, width, KDIM), BF16), ((width, 3 * hid), BF16), (rows4, BF16)],
        [ANY] * 4,
        [pltpu.VMEM((shard, 4 * KDIM + 128 + 3 * hid), BF16), pltpu.VMEM((SEQ_LEN, dim), BF16)],
        200,
    )
    part3, part4 = up_z(part0), over_y(part0)
    w_in, w_out = flat(w_in), flat(w_out)
    gain_attn = w_in[:, WIDE - PAD].astype(F32)[None, :]
    gain_ffn = w_in[:, WIDE - PAD + 1].astype(F32)[None, :]
    inputs = flat(seqs).astype(F32)
    attn_in = (inputs * rms(inputs) * gain_attn).astype(BF16)
    proj = mm(attn_in, w_in)
    mixed, *saved = mixer_forward(proj)
    attn_terms = mm(mixed, w_out, NT).reshape(rows4)
    places = lax.broadcasted_iota(jnp.int32, (SEQ_LEN, 1), 0)
    length = jnp.where(first, valid_len[0], valid_len[1])
    live = ((core < seq_count[0]) & (places < length)).astype(F32)
    d_res = live * ring.order(jnp.where(first, cotangent[:SEQ_LEN], cotangent[SEQ_LEN:]), width)
    cut = hid // 256 * 128 + 128
    w_gate, w_up, w_down, resid, ffn_in, d_ffn = call(
        functools.partial(gather_ffn_kernel, hid, cut),
        "gather_ffn",
        1,
        (part0, part3, part4, attn_terms, seqs, gain_ffn, d_res.astype(BF16)),
        [ANY] * 5 + [VMEM, ANY],
        [((8, width, hid), BF16)] * 3 + [((SEQ_LEN, dim), F32), (rows4, BF16), (rows4, BF16)],
        [ANY] * 6,
        quad_scratch(dim)
        + [pltpu.VMEM((SEQ_LEN, dim), F32), pltpu.VMEM((SEQ_LEN, dim), BF16)]
        + [pltpu.VMEM((SEQ_LEN, dim), BF16)] * 2
        + [pltpu.VMEM((3, width, 3 * hid), BF16)],
        160,
    )
    w_gate, w_up, w_down, ffn_in, d_ffn = map(flat, (w_gate, w_up, w_down, ffn_in, d_ffn))
    gate, up_vals = mm(ffn_in, w_gate), mm(ffn_in, w_up)
    sig = jax.nn.sigmoid(gate)
    hidden = (gate * sig * up_vals).astype(BF16)
    down_given = over_y(mm(d_ffn[:, half:], hidden, TN, BF16))
    down_terms = mm(d_ffn[:, :half], hidden, TN, BF16)
    d_hidden = mm(d_ffn, w_down)
    d_gate = (d_hidden * up_vals * (sig * (1.0 + gate * (1.0 - sig)))).astype(BF16)
    d_up = (d_hidden * (gate * sig)).astype(BF16)
    up_given = over_y(mm(ffn_in[:, half:], d_up, TN, BF16))
    up_terms = mm(ffn_in[:, :half], d_up, TN, BF16)
    gate_terms = mm(ffn_in, d_gate, TN, BF16)
    ffn_terms = mm(hidden, w_down, NT).reshape(rows4)
    d_ffn_terms = (mm(d_gate, w_gate, NT) + mm(d_up, w_up, NT)).reshape(rows4)
    gate_sum, down_sum, d_h, d_attn, ffn_gains, block_out = call(
        functools.partial(sum_ffn_kernel, hid),
        "sum_ffn",
        2,
        (
            blocks(gate_terms),
            blocks(down_terms),
            blocks(down_given),
            d_ffn_terms,
            resid,
            gain_ffn,
            d_res,
            ffn_terms,
            jnp.broadcast_to(live, (SEQ_LEN, 128)),
        ),
        [ANY] * 5 + [VMEM, ANY, ANY, VMEM],
        [
            ((shard, 2 * hid), F32),
            ((shard, 2 * hid), F32),
            ((SEQ_LEN, dim), F32),
            (rows4, BF16),
            ((8, dim), F32),
            ((2 * SEQ_LEN, dim), BF16),
        ],
        [ANY] * 4 + [VMEM, ANY],
        sum_scratch(width, hid) * 2
        + quad_scratch(dim) * 2
        + [
            pltpu.VMEM((SEQ_LEN, dim), F32),
            pltpu.VMEM((SEQ_LEN, dim), F32),
            pltpu.VMEM((SEQ_LEN, dim), BF16),
            pltpu.VMEM((SEQ_LEN, dim), BF16),
        ],
        160,
    )
    d_attn = flat(d_attn)
    d_proj = mixer_backward(proj, saved, mm(d_attn, w_out))
    d_attn_terms = mm(d_proj, w_in, NT).reshape(rows4)
    tail = width // 2
    up_sum, out_sum, q_sum, k_sum, v_sum, f_sum, input_grad, gain_sums = call(
        functools.partial(sum_last_kernel, hid),
        "sum_last",
        3,
        (
            blocks(up_terms),
            blocks(up_given),
            blocks(mm(d_attn, mixed, TN, BF16)),
            blocks(mm(attn_in, d_proj, TN, BF16)),
            d_attn_terms,
            seqs,
            gain_attn,
            d_h,
            ffn_gains,
        ),
        [ANY] * 6 + [VMEM, ANY, VMEM],
        [((shard, 2 * hid), F32)]
        + [((shard, 2 * KDIM), F32)] * 4
        + [((shard, 256), F32), ((2 * SEQ_LEN, dim), F32), ((8, tail), F32)],
        [ANY] * 7 + [VMEM],
        sum_scratch(width, hid)
        + sum_scratch(width, KDIM) * 4
        + sum_scratch(width, 128)
        + quad_scratch(dim)
        + [
            pltpu.VMEM((SEQ_LEN, dim), BF16),
            pltpu.VMEM((SEQ_LEN, dim), F32),
            pltpu.VMEM((8, dim), F32),
            pltpu.VMEM((8, 8, width), F32),
            pltpu.VMEM((8, 8, width), F32),
            pltpu.VMEM((4, 8, width), F32),
            pltpu.VMEM((3, 8, width), F32),
            pltpu.VMEM((3, 8, width), F32),
            pltpu.VMEM((2, 8, tail), F32),
            pltpu.VMEM((8, tail), F32),
        ],
        240,
    )
    f_grad = jnp.concatenate([f_sum[:, :SLOTS], f_sum[:, 128 : 128 + SLOTS]], axis=1)
    return (
        block_out,
        input_grad,
        gain_sums[0],
        gain_sums[1],
        q_sum,
        k_sum,
        v_sum,
        f_grad,
        out_sum,
        gate_sum,
        up_sum,
        down_sum,
    )


def solution(mesh):
    ring = Ring(mesh.shape["dp"])
    body = body_by_kernels if ring.count == 16 else body_by_permutes
    split_one, split_two = P("dp"), P("dp", "head")
    row = P("dp", None)
    in_specs = (row, split_one, split_one, split_one, split_one) + (split_two,) * 8 + (row,)
    out_specs = (row, row, split_one, split_one) + (split_two,) * 8
    return jax.shard_map(
        functools.partial(body, ring=ring),
        mesh=mesh,
        in_specs=in_specs,
        out_specs=out_specs,
        check_vma=False,
    )
```

```python
import functools
import jax
import jax.numpy as jnp
from jax import lax
from jax.experimental import pallas as pl
from jax.experimental.pallas import tpu as pltpu
from jax.sharding import PartitionSpec as P

SLOTS = 64
KDIM = 512
SEQ_LEN = 256
HALF = 128
F32, BF16 = jnp.float32, jnp.bfloat16
WIDE = 3 * KDIM + 128
NT = (((1,), (1,)), ((), ()))
NN = (((1,), (0,)), ((), ()))
TN = (((0,), (0,)), ((), ()))
LEVELS = (8, 16, 32, 64)


def split(value):
    high = value.astype(BF16)
    return high, (value - high.astype(F32)).astype(BF16)


def dot3(left, right, dims):
    one = functools.partial(lax.dot_general, dimension_numbers=dims, preferred_element_type=F32)
    return one(left[0], right[0]) + (one(left[0], right[1]) + one(left[1], right[0]))


def silu_parts(value):
    gate = 1.0 / (1.0 + jnp.exp(-value))
    return gate, value * gate


def level_mask(size):
    row = lax.broadcasted_iota(jnp.int32, (HALF, HALF), 0) // size
    col = lax.broadcasted_iota(jnp.int32, (HALF, HALF), 1) // size
    return (row == col + 1) & (row % 2 == 1)


def band_mask(back):
    row = lax.broadcasted_iota(jnp.int32, (HALF, HALF), 0)
    col = lax.broadcasted_iota(jnp.int32, (HALF, HALF), 1)
    return (row == col + back) & (row // 8 == col // 8)


def down(value, back):
    return value if back == 0 else pltpu.roll(value, back, 0)


def up(value, back):
    return value if back == 0 else pltpu.roll(value, SEQ_LEN - back, 0)


def gates(forget):
    lane = lax.broadcasted_iota(jnp.int32, forget.shape, 1) < SLOTS
    place = lax.broadcasted_iota(jnp.int32, forget.shape, 0)
    forget = jnp.where(lane, forget, 0.0)
    tail = jnp.exp(-jnp.abs(forget))
    log_decay = (jnp.minimum(forget, 0.0) - jnp.log1p(tail)) * 0.125
    log_decay = jnp.where(lane, log_decay, 0.0)
    g = log_decay
    series = 1.0 + g * (1.0 / 7.0)
    for n in (6.0, 5.0, 4.0, 3.0, 2.0):
        series = 1.0 + g * (1.0 / n) * series
    writes = jnp.where(g > -0.3, -g * series, 1.0 - jnp.exp(g))
    writes = jnp.where(lane, writes, 0.0)
    ahead, behind = g, g
    for step in (1, 2, 4):
        ahead = ahead + jnp.where(place % 8 >= step, down(ahead, step), 0.0)
        behind = behind + jnp.where(place % 8 < 8 - step, up(behind, step), 0.0)
    behind = jnp.where(place % 8 < 7, up(behind, 1), 0.0)
    aheads, behinds = {8: ahead}, {8: behind}
    size = 8
    while size < HALF:
        first = ahead.reshape(SEQ_LEN // (2 * size), 2, size, 128)
        last = behind.reshape(SEQ_LEN // (2 * size), 2, size, 128)
        left, right = first[:, 0:1], first[:, 1:2]
        left_sum, right_sum = left[:, :, size - 1 :], right[:, :, size - 1 :]
        ahead = jnp.concatenate([left, right + left_sum], axis=1).reshape(SEQ_LEN, 128)
        behind = jnp.concatenate([last[:, 0:1] + right_sum, last[:, 1:2]], axis=1).reshape(SEQ_LEN, 128)
        size *= 2
        aheads[size], behinds[size] = ahead, behind
    return lane, place, g, writes, aheads, behinds


def near_decays(place, aheads, back):
    ahead = aheads[8]
    gap = jnp.where(place % 8 >= back, ahead - down(ahead, back), 0.0)
    return jnp.where(place % 8 >= back, jnp.exp(gap), 0.0)


def halves(value):
    return value[:HALF], value[HALF:]


def to_slots(blocks, cross, place, writes, aheads, behinds, nears):
    grow = {size: jnp.exp(aheads[size]) for size in LEVELS}
    keep = {size: split(jnp.exp(behinds[size]) * writes) for size in LEVELS}
    outs = []
    for half in range(2):
        here = slice(half * HALF, (half + 1) * HALF)
        block = blocks[half]
        parts = split(block)
        total = None
        for size in LEVELS:
            mask = level_mask(size)
            masked = tuple(jnp.where(mask, part, jnp.zeros_like(part)) for part in parts)
            term = grow[size][here] * dot3(masked, tuple(k[here] for k in keep[size]), NN)
            total = term if total is None else total + term
        for back in range(8):
            near = jnp.sum(jnp.where(band_mask(back), block, 0.0), axis=1, keepdims=True)
            total = total + near * nears[back][here]
        if half == 1:
            far = split((jnp.exp(behinds[HALF]) * writes)[:HALF])
            total = total + jnp.exp(aheads[HALF])[HALF:] * dot3(split(cross), far, NN)
        outs.append(total)
    return jnp.concatenate(outs, axis=0)


def to_tokens(slots, writes, aheads, behinds, nears):
    blocks = []
    for half in range(2):
        here = slice(half * HALF, (half + 1) * HALF)
        total = jnp.zeros((HALF, HALF), F32)
        for size in LEVELS:
            left = split((slots * jnp.exp(aheads[size]))[here])
            right = split((jnp.exp(behinds[size]) * writes)[here])
            total = jnp.where(level_mask(size), dot3(left, right, NT), total)
        for back in range(8):
            near = jnp.sum(slots[here] * nears[back][here], axis=1, keepdims=True)
            total = jnp.where(band_mask(back), near, total)
        blocks.append(total)
    left = split((slots * jnp.exp(aheads[HALF]))[HALF:])
    right = split((jnp.exp(behinds[HALF]) * writes)[:HALF])
    return blocks, dot3(left, right, NT)


def forward_kernel(q_ref, k_ref, v_ref, f_ref, o_ref, p_ref, s_ref, a_ref, b_ref):
    query = split(silu_parts(q_ref[...])[1] * KDIM ** (-0.5))
    keys = split(silu_parts(k_ref[...])[1])
    values = split(v_ref[...])
    lane, place, g, writes, aheads, behinds = gates(f_ref[...])
    nears = [near_decays(place, aheads, back) * down(writes, back) for back in range(8)]
    q0, q1 = tuple(x[:HALF] for x in query), tuple(x[HALF:] for x in query)
    k0, k1 = tuple(x[:HALF] for x in keys), tuple(x[HALF:] for x in keys)
    blocks = (dot3(q0, k0, NT), dot3(q1, k1, NT))
    cross = dot3(q1, k0, NT)
    scores = to_slots(blocks, cross, place, writes, aheads, behinds, nears)
    shown = jnp.where(lane, scores, -1e30)
    weights = jnp.exp(shown - jnp.max(shown, axis=1, keepdims=True))
    weights = jnp.where(lane, weights, 0.0)
    weights = weights / jnp.sum(weights, axis=1, keepdims=True)
    mixes, mix_cross = to_tokens(weights, writes, aheads, behinds, nears)
    v0 = tuple(x[:HALF] for x in values)
    o_ref[:HALF, :] = dot3(split(mixes[0]), v0, NN).astype(o_ref.dtype)
    row = jnp.concatenate([mix_cross, mixes[1]], axis=1)
    o_ref[HALF:, :] = dot3(split(row), values, NN).astype(o_ref.dtype)
    p_ref[...] = weights
    s_ref[...] = scores
    a_ref[:HALF, :] = jnp.concatenate([blocks[0], jnp.zeros_like(cross)], axis=1)
    a_ref[HALF:, :] = jnp.concatenate([cross, blocks[1]], axis=1)
    b_ref[:HALF, :] = jnp.concatenate([mixes[0], jnp.zeros_like(cross)], axis=1)
    b_ref[HALF:, :] = row


def backward_kernel(q_ref, k_ref, v_ref, f_ref, p_ref, s_ref, a_ref, b_ref, d_ref, out_ref):
    lane, place, g, writes, aheads, behinds = gates(f_ref[...])
    spans = [near_decays(place, aheads, back) for back in range(8)]
    nears = [spans[back] * down(writes, back) for back in range(8)]
    weights, scores = p_ref[...], s_ref[...]
    products, mixing = a_ref[...], b_ref[...]
    grad = split(d_ref[...])
    g0, g1 = tuple(x[:HALF] for x in grad), tuple(x[HALF:] for x in grad)
    values = split(v_ref[...])
    v0, v1 = tuple(x[:HALF] for x in values), tuple(x[HALF:] for x in values)
    m_parts = split(mixing)
    dv0 = dot3(tuple(x[:, :HALF] for x in m_parts), grad, TN)
    dv1 = dot3(tuple(x[HALF:, HALF:] for x in m_parts), g1, TN)
    out_ref[:HALF, 2 * KDIM : 3 * KDIM] = dv0.astype(BF16)
    out_ref[HALF:, 2 * KDIM : 3 * KDIM] = dv1.astype(BF16)
    mix_blocks = (dot3(g0, v0, NT), dot3(g1, v1, NT))
    mix_cross = dot3(g1, v0, NT)
    d_weights = to_slots(mix_blocks, mix_cross, place, writes, aheads, behinds, nears)
    inner = jnp.sum(weights * d_weights, axis=1, keepdims=True)
    d_scores = weights * (d_weights - inner)
    d_blocks, d_cross = to_tokens(d_scores, writes, aheads, behinds, nears)
    q_gate, q_act = silu_parts(q_ref[...])
    k_gate, k_act = silu_parts(k_ref[...])
    scale = KDIM ** (-0.5)
    query, keys = split(q_act * scale), split(k_act)
    k0 = tuple(x[:HALF] for x in keys)
    low = split(jnp.concatenate([d_cross, d_blocks[1]], axis=1))
    top = split(d_blocks[0])
    dq = jnp.concatenate([dot3(top, k0, NN), dot3(low, keys, NN)], axis=0)
    first = tuple(jnp.concatenate([t, l[:, :HALF]], axis=0) for t, l in zip(top, low))
    dk0 = dot3(first, query, TN)
    dk1 = dot3(tuple(x[:, HALF:] for x in low), tuple(x[HALF:] for x in query), TN)
    dk = jnp.concatenate([dk0, dk1], axis=0)
    out_ref[:, :KDIM] = (dq * scale * (q_gate + q_act * (1.0 - q_gate))).astype(BF16)
    out_ref[:, KDIM : 2 * KDIM] = (dk * (k_gate + k_act * (1.0 - k_gate))).astype(BF16)
    parts = []
    for half in range(2):
        here = slice(half * HALF, (half + 1) * HALF)
        both = jnp.concatenate([mix_blocks[half], products[here, here]], axis=0)
        both_parts = split(both)
        total = None
        for size in LEVELS:
            mask = level_mask(size)
            mask = jnp.concatenate([mask, mask], axis=0)
            grow = jnp.exp(aheads[size][here])
            right = split(jnp.concatenate([weights[here] * grow, d_scores[here] * grow], axis=0))
            left = tuple(jnp.where(mask, part, jnp.zeros_like(part)) for part in both_parts)
            term = jnp.exp(behinds[size][here]) * dot3(left, right, TN)
            total = term if total is None else total + term
        parts.append(total)
    grow = jnp.exp(aheads[HALF][HALF:])
    left = split(jnp.concatenate([mix_cross, products[HALF:, :HALF]], axis=0))
    right = split(jnp.concatenate([weights[HALF:] * grow, d_scores[HALF:] * grow], axis=0))
    parts[0] = parts[0] + jnp.exp(behinds[HALF][:HALF]) * dot3(left, right, TN)
    reach = jnp.concatenate(parts, axis=0)
    for back in range(8):
        mask = band_mask(back)
        near_mix = jnp.concatenate([jnp.sum(jnp.where(mask, mix_blocks[h], 0.0), axis=1, keepdims=True) for h in range(2)], axis=0)
        near_pro = jnp.concatenate(
            [jnp.sum(jnp.where(mask, products[h * HALF : (h + 1) * HALF, h * HALF : (h + 1) * HALF], 0.0), axis=1, keepdims=True) for h in range(2)],
            axis=0,
        )
        reach = reach + up((near_mix * weights + near_pro * d_scores) * spans[back], back)
    d_sum = weights * d_weights + d_scores * scores - writes * reach
    step = 1
    while step < SEQ_LEN:
        d_sum = d_sum + jnp.where(place < SEQ_LEN - step, up(d_sum, step), 0.0)
        step *= 2
    d_log = d_sum - reach * jnp.exp(g)
    d_forget = d_log * 0.125 / (1.0 + jnp.exp(f_ref[...]))
    out_ref[:, 3 * KDIM :] = jnp.where(lane, d_forget, 0.0).astype(BF16)


def spec(width, column):
    return pl.BlockSpec((SEQ_LEN, width), lambda i: (i, column))


IN_SPECS = [spec(KDIM, 0), spec(KDIM, 1), spec(KDIM, 2), spec(128, 3 * KDIM // 128)]


def mixer_forward(proj):
    rows = proj.shape[0]
    shape = lambda width, kind: jax.ShapeDtypeStruct((rows, width), kind)
    return pl.pallas_call(
        forward_kernel,
        grid=(rows // SEQ_LEN,),
        in_specs=IN_SPECS,
        out_specs=[spec(KDIM, 0), spec(128, 0), spec(128, 0), spec(SEQ_LEN, 0), spec(SEQ_LEN, 0)],
        out_shape=[shape(KDIM, BF16), shape(128, F32), shape(128, F32), shape(SEQ_LEN, F32), shape(SEQ_LEN, F32)],
        compiler_params=pltpu.CompilerParams(vmem_limit_bytes=48 << 20),
        cost_estimate=pl.CostEstimate(flops=rows * 3000000, bytes_accessed=rows * 10000, transcendentals=rows * 3000),
        name="mixer_forward",
    )(proj, proj, proj, proj)


def mixer_backward(proj, saved, grad):
    rows = proj.shape[0]
    weights, scores, products, mixing = saved
    return pl.pallas_call(
        backward_kernel,
        grid=(rows // SEQ_LEN,),
        in_specs=IN_SPECS + [spec(128, 0), spec(128, 0), spec(SEQ_LEN, 0), spec(SEQ_LEN, 0), spec(KDIM, 0)],
        out_specs=spec(WIDE, 0),
        out_shape=jax.ShapeDtypeStruct((rows, WIDE), BF16),
        compiler_params=pltpu.CompilerParams(vmem_limit_bytes=48 << 20),
        cost_estimate=pl.CostEstimate(flops=rows * 9000000, bytes_accessed=rows * 16000, transcendentals=rows * 5000),
        name="mixer_backward",
    )(proj, proj, proj, proj, weights, scores, products, mixing, grad)


MESH = pl.DeviceIdType.MESH
ANY = pl.BlockSpec(memory_space=pl.ANY)
VMEM = pl.BlockSpec(memory_space=pltpu.VMEM)
DMA = pltpu.SemaphoreType.DMA
PIECE = 32


class Place:
    def __init__(self):
        dp = lax.axis_index("dp")
        self.core = lax.axis_index("head")
        self.x, self.y, self.z = dp % 2, dp // 2 % 2, dp // 4
        rest = dp % 4
        self.peers = {
            "x": (dp + 1 - 2 * self.x, self.core),
            "y": (dp + 2 - 4 * self.y, self.core),
            "up": ((self.z + 1) % 4 * 4 + rest, self.core),
            "down": ((self.z + 3) % 4 * 4 + rest, self.core),
            "core": (dp, 1 - self.core),
        }

    def greet(self):
        ready = pltpu.get_barrier_semaphore()
        for peer in self.peers.values():
            pl.semaphore_signal(ready, inc=1, device_id=peer, device_id_type=MESH)
        pl.semaphore_wait(ready, len(self.peers))

    def copy(self, name, source, target, sems):
        return pltpu.make_async_remote_copy(
            src_ref=source,
            dst_ref=target,
            send_sem=sems[0],
            recv_sem=sems[1],
            device_id=self.peers[name],
            device_id_type=MESH,
        )

    def half(self, size, other=False):
        place = 1 - self.x if other else self.x
        return pl.ds(pl.multiple_of(place * size, size), size)

    def columns(self, index, size):
        natural = (self.z + index % 4) % 4 * 2 + (self.y + index // 4) % 2
        return pl.ds(pl.multiple_of(natural * size, size), size)


class Sems:
    def __init__(self, ref):
        self.ref, self.used = ref, 0

    def one(self):
        self.used += 1
        return self.ref.at[self.used - 1]

    def two(self):
        return (self.one(), self.one())


def pieces(rows, work):
    def step(i, carry):
        work(pl.ds(pl.multiple_of(i * PIECE, PIECE), PIECE))
        return carry

    lax.fori_loop(0, rows // PIECE, step, 0)


class Keep:
    def __init__(self, sems, source, target, stage):
        self.load = pltpu.make_async_copy(source, stage, sems.one())
        self.store = pltpu.make_async_copy(stage, target, sems.one())

    def start(self):
        self.load.start()

    def turn(self):
        self.load.wait()
        self.store.start()

    def wait(self):
        self.store.wait()


class Quad:
    def __init__(self, place, sems, source, target):
        near = [pltpu.make_async_copy(source, target.at[0], sems.one())]
        self.swap = place.copy("x", source, target.at[1], sems.two())
        self.core = place.copy("core", source, target.at[2], sems.two())
        self.last = place.copy("core", target.at[1], target.at[3], sems.two())
        self.near = near

    def start(self):
        self.swap.start()
        self.core.start()
        for copy in self.near:
            copy.start()

    def forward(self):
        self.swap.wait_recv()
        self.last.start()

    def finish(self):
        self.swap.wait_send()
        self.core.wait()
        self.last.wait()
        for copy in self.near:
            copy.wait()


class QuadSum:
    def __init__(self, place, sems, terms, scratch):
        self.near, self.theirs, self.far, self.swapped = scratch
        self.core = place.copy("core", terms.at[pl.ds(2, 2)], self.theirs, sems.two())
        self.load = pltpu.make_async_copy(terms.at[pl.ds(0, 2)], self.near, sems.one())
        self.swap = place.copy("x", self.far, self.swapped, sems.two())

    def start(self):
        self.core.start()
        self.load.start()

    def middle(self):
        self.core.wait()
        self.load.wait()

        def add(part):
            self.far[part] = (self.near[1, part] + self.theirs[1, part]).astype(BF16)

        pieces(SEQ_LEN, add)
        self.swap.start()

    def ready(self):
        self.swap.wait()

    def read(self, part):
        return self.near[0, part] + self.theirs[0, part] + self.swapped[part].astype(F32)


def quad_scratch(width):
    return [
        pltpu.VMEM((2, SEQ_LEN, width), F32),
        pltpu.VMEM((2, SEQ_LEN, width), F32),
        pltpu.VMEM((SEQ_LEN, width), BF16),
        pltpu.VMEM((SEQ_LEN, width), BF16),
    ]


class Leave:
    def __init__(self, place, sems, source, target):
        rows = pl.ds(pl.multiple_of(place.core * SEQ_LEN, SEQ_LEN), SEQ_LEN)
        width = source.shape[1] // 8
        self.copies, self.here = [], []
        for index in range(8):
            part = source.at[:, pl.ds(index * width, width)]
            there = target.at[rows, place.columns(index, width)]
            self.copies.append(place.copy("core", part, there, sems.two()))
            self.here.append(pltpu.make_async_copy(part, there, sems.one()))

    def start(self):
        for copy in self.copies + self.here:
            copy.start()

    def finish(self):
        for copy in self.copies + self.here:
            copy.wait()


def gather_first_kernel(
    tokens, cot, live, q_w, k_w, v_w, small, out_w, gate_w, up_w, down_w, w_in, w_out, ffn, own, attn_in, d_res, d_ffn, gains,
    stage, seqs, normed, scales, turned, grads, low, sem
):
    place, sems = Place(), Sems(sem)
    shard = q_w.shape[0]
    rows = place.half(shard)
    hid = gate_w.shape[1] // 2
    chunks = [
        (small, 0, 128, w_in, 3 * KDIM, True),
        (q_w, 0, KDIM, w_in, 0, False),
        (k_w, 0, KDIM, w_in, KDIM, False),
        (v_w, 0, KDIM, w_in, 2 * KDIM, False),
        (out_w, 0, KDIM // 2, w_out, 0, True),
        (out_w, KDIM // 2, KDIM // 2, w_out, KDIM // 2, False),
        (gate_w, 0, hid, ffn, 0, False),
        (up_w, 0, hid, ffn, hid, False),
        (down_w, 0, hid, ffn, 2 * hid, False),
    ]
    full = len(chunks) - 3
    swaps, keeps, rises, crosses = [], [], [], []
    used = 0
    for c, (source, offset, width, target, first, y_first) in enumerate(chunks):
        cols = pl.ds(first, width)
        where = target.at[0, rows, cols] if c < full else target.at[rows, cols]
        span = source.shape[1] // 2
        here, there = (pl.ds(pl.multiple_of(at * span + offset, 128), width) for at in (place.x, 1 - place.x))
        swaps.append(place.copy("x", source.at[:, there], where, sems.two()))
        keeps.append(Keep(sems, source.at[:, here], where, stage.at[:, pl.ds(used, width)]))
        used += width
        if c >= full:
            continue

        def block(index, target=target, cols=cols):
            return target.at[index, :, cols]

        rises.append(
            [
                [place.copy("up", block((4 - step) % 4 + 4 * u), block(3 - step + 4 * u), sems.two()) for step in range(3)]
                for u in range(2 if y_first else 1)
            ]
        )
        crosses.append(
            [place.copy("y", block(i), block(4 + i), sems.two()) for i in range(1 if y_first else 4)]
        )
    width = tokens.shape[1] // 8
    mine = pl.ds(pl.multiple_of(place.core * SEQ_LEN, SEQ_LEN), SEQ_LEN)
    far, side, fetch, fetch_cot = [], [], [], []
    for index in range(8):
        part = tokens.at[mine, place.columns(index, width)]
        cols = pl.ds(index * width, width)
        far.append(place.copy("x", part, seqs.at[1, :, cols], sems.two()))
        side.append(place.copy("core", part, seqs.at[2, :, cols], sems.two()))
        fetch.append(pltpu.make_async_copy(part, seqs.at[0, :, cols], sems.one()))
        fetch_cot.append(
            pltpu.make_async_copy(cot.at[mine, place.columns(index, width)], grads.at[:, cols], sems.one())
        )
    last = place.copy("core", seqs.at[1], seqs.at[3], sems.two())
    quad = Quad(place, sems, low, d_ffn)
    save_own = pltpu.make_async_copy(seqs.at[0], own, sems.one())
    save_res = pltpu.make_async_copy(grads, d_res, sems.one())
    save_in = [pltpu.make_async_copy(normed.at[i], attn_in.at[i], sems.one()) for i in range(4)]
    load_gains = [pltpu.make_async_copy(w_in.at[i, :, pl.ds(3 * KDIM, 128)], turned.at[i], sems.one()) for i in range(8)]
    place.greet()
    for swap, keep in zip(swaps[:full], keeps[:full]):
        swap.start()
        keep.start()
    for copy in far + side + fetch + fetch_cot:
        copy.start()
    for swap, keep in zip(swaps[full:], keeps[full:]):
        swap.start()
        keep.start()
    for keep in keeps:
        keep.turn()
    for c in range(full):
        keeps[c].wait()
        swaps[c].wait_recv()
        rises[c][0][0].start()
        crosses[c][0].start()
    for copy in fetch + fetch_cot:
        copy.wait()
    save_own.start()

    def mask(part):
        value = grads[part] * live[part, :1]
        grads[part] = value
        low[part] = value.astype(BF16)

    pieces(SEQ_LEN, mask)
    save_res.start()
    quad.start()
    for c in range(full):
        if chunks[c][5]:
            crosses[c][0].wait_recv()
            rises[c][1][0].start()

    def measure(slot):
        def one(part):
            scales[slot, part] = jnp.broadcast_to(rms(seqs[slot, part].astype(F32)), (PIECE, 128))

        pieces(SEQ_LEN, one)

    def norm(slot):
        def one(part):
            value = seqs[slot, part].astype(F32) * scales[slot, part, :1] * gains[0:1, :]
            normed[slot, part] = value.astype(BF16)

        pieces(SEQ_LEN, one)
        save_in[slot].start()

    for step in range(3):
        for c in range(full):
            for rise in rises[c]:
                rise[step].wait_recv()
                if step < 2:
                    rise[step + 1].start()
            if not chunks[c][5]:
                crosses[c][3 - step].start()
            if step == 0 and c == 1:
                measure(0)
            if step == 0 and c == full - 1:
                for copy in far:
                    copy.wait_recv()
                last.start()
            if step == 1:
                if c == 0:
                    for copy in side:
                        copy.wait_recv()
                    last.wait_recv()
                if 1 <= c <= 3:
                    measure(c)
            if step == 2:
                if c == 0:
                    for copy in load_gains:
                        copy.start()
                    for index, copy in enumerate(load_gains):
                        copy.wait()
                        flipped = turned[index].astype(F32).T
                        gains[0:8, index * width : (index + 1) * width] = flipped[SLOTS : SLOTS + 8]
                if 1 <= c <= 4:
                    norm(c - 1)
    quad.forward()
    for c in range(full):
        for cross in crosses[c]:
            cross.wait_send()
            if not chunks[c][5]:
                cross.wait_recv()
        for rise in rises[c]:
            for copy in rise:
                copy.wait_send()
    for swap in swaps[:full]:
        swap.wait_send()
    for swap, keep in zip(swaps[full:], keeps[full:]):
        swap.wait()
        keep.wait()
    for copy in far + side + [last]:
        copy.wait_send()
    for copy in save_in + [save_own, save_res]:
        copy.wait()
    quad.finish()


def gather_ffn_kernel(
    hid, cut, b0, b3, b4, terms, tokens, gains, w_gate, w_up, w_down, resid, ffn_in, s0, s1, s2, s3, kept, normed, inputs, stage, sem
):
    place, sems = Place(), Sems(sem)
    chunks = [
        (0, hid, w_gate, 0, False),
        (hid, hid, w_up, 0, False),
        (2 * hid, cut, w_down, 0, False),
        (2 * hid + cut, hid - cut, w_down, cut, True),
    ]
    keeps, rises, crosses = [], [], []
    for first, width, target, start, y_first in chunks:
        cols, source = pl.ds(start, width), pl.ds(first, width)

        def block(index, target=target, cols=cols):
            return target.at[index, :, cols]

        keeps += [
            Keep(sems, b.at[:, source], block(i), stage.at[at, :, source])
            for at, (b, i) in enumerate(((b0, 0), (b3, 3), (b4, 4)))
        ]
        lower = [
            place.copy("up", b3.at[:, source], block(2), sems.two()),
            place.copy("up", block(2), block(1), sems.two()),
        ]
        high = []
        if y_first:
            high = [
                place.copy("up", b4.at[:, source], block(7), sems.two()),
                place.copy("up", block(7), block(6), sems.two()),
                place.copy("up", block(6), block(5), sems.two()),
            ]
            crosses.append([])
        else:
            crosses.append(
                [
                    place.copy("y", b3.at[:, source], block(7), sems.two()),
                    place.copy("y", block(2), block(6), sems.two()),
                    place.copy("y", block(1), block(5), sems.two()),
                ]
            )
        rises.append((lower, high))
    total = QuadSum(place, sems, terms, (s0, s1, s2, s3))
    out = Quad(place, sems, normed, ffn_in)
    fetch = pltpu.make_async_copy(tokens, inputs, sems.one())
    save = pltpu.make_async_copy(kept, resid, sems.one())
    place.greet()
    total.start()
    fetch.start()
    for (lower, high), cross in zip(rises, crosses):
        lower[0].start()
        for copy in high[:1] + cross[:1]:
            copy.start()
    for copy in keeps:
        copy.start()
    total.middle()
    for copy in keeps:
        copy.turn()
    fetch.wait()
    for c, ((lower, high), cross) in enumerate(zip(rises, crosses)):
        if c == 2:
            total.ready()

            def norm(part):
                value = total.read(part) + inputs[part].astype(F32)
                kept[part] = value
                normed[part] = (value * rms(value) * gains[1:2, :]).astype(BF16)

            pieces(SEQ_LEN, norm)
            out.start()
            save.start()
        lower[0].wait_recv()
        lower[1].start()
        for copy in cross[1:2]:
            copy.start()
        if high:
            high[0].wait_recv()
            high[1].start()
    for c, ((lower, high), cross) in enumerate(zip(rises, crosses)):
        lower[1].wait_recv()
        for copy in cross[2:]:
            copy.start()
        if high:
            high[1].wait_recv()
            high[2].start()
        if c == 1:
            out.forward()
    for (lower, high), cross in zip(rises, crosses):
        for copy in cross:
            copy.wait()
        for copy in high[2:]:
            copy.wait_recv()
        for copy in lower + high:
            copy.wait_send()
    for copy in keeps:
        copy.wait()
    out.finish()
    save.wait()


class Sum:
    def __init__(self, place, sems, terms, given, result, first, width, scratch, span=None, start=0):
        self.own, self.other, self.from_z, self.to_z, self.final = scratch
        cols = pl.ds(first, width)
        self.loads, self.crosses = [], []
        for index in range(4):
            self.loads.append(pltpu.make_async_copy(terms.at[index, :, cols], self.own.at[index], sems.one()))
            if given is None:
                self.crosses.append(place.copy("y", terms.at[4 + index, :, cols], self.other.at[index], sems.two()))
            else:
                self.loads.append(pltpu.make_async_copy(given.at[index, :, cols], self.other.at[index], sems.one()))
        self.per = len(self.loads) // 4
        self.rises = [place.copy("up", self.to_z.at[i], self.from_z.at[i], sems.two()) for i in range(3)]
        half = self.final.shape[0] // 2
        there = result.at[:, pl.ds(pl.multiple_of(place.x * (span or width) + start, 128), width)]
        self.leave = pltpu.make_async_copy(self.final.at[place.half(half)], there, sems.one())
        self.swap = place.copy("x", self.final.at[place.half(half, True)], there, sems.two())

    def start(self, step):
        index = 3 - step
        for copy in self.crosses[index : index + 1] + self.loads[index * self.per : (index + 1) * self.per]:
            copy.start()

    def step(self, step):
        index = 3 - step
        for copy in self.loads[index * self.per : (index + 1) * self.per]:
            copy.wait()
        for copy in self.crosses[index : index + 1]:
            copy.wait_recv()
        if step:
            self.rises[step - 1].wait_recv()

        def add(part):
            value = self.own[index, part].astype(F32) + self.other[index, part].astype(F32)
            if step:
                value = value + self.from_z[step - 1, part].astype(F32)
            if step < 3:
                self.to_z[step, part] = value.astype(BF16)
            else:
                self.final[part] = value

        pieces(self.final.shape[0], add)
        if step < 3:
            self.rises[step].start()
        else:
            self.swap.start()
            self.leave.start()

    def finish(self):
        for copy in self.crosses + self.rises:
            copy.wait_send()
        self.leave.wait()
        self.swap.wait()


def sum_scratch(rows, width):
    return [pltpu.VMEM((depth, rows, width), BF16) for depth in (4, 4, 3, 3)] + [pltpu.VMEM((rows, width), F32)]


def norm_back_piece(value, gain, grad):
    scale = rms(value)
    scaled = gain * grad
    inner = jnp.mean(scaled * value, axis=-1, keepdims=True)
    gains = (grad * value * scale).reshape(PIECE // 8, 8, value.shape[1])
    return scale * scaled - value * (scale * scale * scale * inner), jnp.sum(gains, axis=0)


def sum_ffn_kernel(hid, part_hid, gate, down, given, down_rest, terms, resid, gains, d_res, gate_sum, down_sum, d_h, d_attn, gain_sum, *scratch):
    *scratch, sem = scratch
    place, sems = Place(), Sems(sem)
    sums = [
        Sum(place, sems, down, given, down_sum, 0, part_hid, scratch[0:5], hid),
        Sum(place, sems, down_rest, None, down_sum, 0, hid - part_hid, scratch[5:10], hid, part_hid),
        Sum(place, sems, gate, None, gate_sum, 0, part_hid, scratch[10:15], hid),
        Sum(place, sems, gate, None, gate_sum, part_hid, hid - part_hid, scratch[15:20], hid, part_hid),
    ]
    back = QuadSum(place, sems, terms, scratch[20:24])
    value, res, low = scratch[24:27]
    quad = Quad(place, sems, low, d_attn)
    fetch = [pltpu.make_async_copy(resid, value, sems.one()), pltpu.make_async_copy(d_res, res, sems.one())]
    save = pltpu.make_async_copy(res, d_h, sems.one())
    place.greet()
    back.start()
    for step in range(4):
        for one in sums:
            one.start(step)
    for copy in fetch:
        copy.start()
    sums[0].step(0)
    back.middle()
    for one in sums[1:]:
        one.step(0)
    for copy in fetch:
        copy.wait()
    sums[0].step(1)
    back.ready()
    gain_sum[...] = jnp.zeros_like(gain_sum)

    def norm(part):
        d_norm, added = norm_back_piece(value[part], gains[1:2, :], back.read(part))
        grad = res[part] + d_norm
        res[part] = grad
        low[part] = grad.astype(BF16)
        gain_sum[...] += added

    pieces(SEQ_LEN, norm)
    quad.start()
    save.start()
    for one in sums[1:]:
        one.step(1)
    for one in sums:
        one.step(2)
    quad.forward()
    for one in sums:
        one.step(3)
    quad.finish()
    save.wait()
    for one in sums:
        one.finish()


def sum_last_kernel(
    hid, part_hid, up, given, up_rest, out_t, in_t, terms, tokens, gain_rows, d_h, ffn_gains, out_terms, resid, live,
    up_sum, out_sum, q_sum, k_sum, v_sum, f_sum, grad, block_out, gain_sum, *scratch
):
    *scratch, sem = scratch
    place, sems = Place(), Sems(sem)
    sums = []
    for terms_in, given_in, result, first, width, span, start in (
        (up, given, up_sum, 0, part_hid, hid, 0),
        (up_rest, None, up_sum, 0, hid - part_hid, hid, part_hid),
        (out_t, None, out_sum, 0, KDIM, None, 0),
        (in_t, None, q_sum, 0, KDIM, None, 0),
        (in_t, None, k_sum, KDIM, KDIM, None, 0),
        (in_t, None, v_sum, 2 * KDIM, KDIM, None, 0),
        (in_t, None, f_sum, 3 * KDIM, 128, None, 0),
    ):
        sums.append(Sum(place, sems, terms_in, given_in, result, first, width, scratch[:5], span, start))
        scratch = scratch[5:]
    back = QuadSum(place, sems, terms, scratch[0:4])
    ahead = QuadSum(place, sems, out_terms, scratch[4:8])
    value, res, kept, shown, gains, parts, met, crossed, risen, rising, last, swapped = scratch[8:]
    leave = Leave(place, sems, res, grad)
    leave_out = Leave(place, sems, shown, block_out)
    fetch = [pltpu.make_async_copy(tokens, value, sems.one()), pltpu.make_async_copy(d_h, res, sems.one())]
    fetch.append(pltpu.make_async_copy(resid, kept, sems.one()))
    meet = place.copy("core", parts, met, sems.two())
    cross = place.copy("y", parts.at[pl.ds(4, 4)], crossed, sems.two())
    rise = [place.copy("up", rising.at[i], risen.at[i], sems.two()) for i in range(3)]
    swap = place.copy("x", last.at[1 - place.x], swapped, sems.two())
    place.greet()
    back.start()
    for step in range(3):
        for one in sums:
            one.start(step)
    for copy in fetch:
        copy.start()
    ahead.start()
    sums[0].step(0)
    back.middle()
    for one in sums[1:]:
        one.step(0)
    for copy in fetch:
        copy.wait()
    gains[...] = jnp.zeros_like(gains)
    back.ready()

    def norm(part):
        d_norm, added = norm_back_piece(value[part].astype(F32), gain_rows[0:1, :], back.read(part))
        res[part] = res[part] + d_norm
        gains[...] += added

    pieces(SEQ_LEN, norm)
    leave.start()
    width = res.shape[1] // 8
    parts[...] = jnp.zeros_like(parts)
    for row, source in enumerate((gains[...], ffn_gains[...])):
        summed = jnp.sum(source, axis=0, keepdims=True)
        for index in range(8):
            parts[index, row : row + 1, :] = summed[:, index * width : (index + 1) * width]
    meet.start()
    sums[0].step(1)
    meet.wait()
    parts[...] = parts[...] + met[...]
    cross.start()
    for one in sums:
        one.start(3)
    for one in sums[1:]:
        one.step(1)
    ahead.middle()
    for one in sums:
        one.step(2)
    cross.wait()
    rising[0] = parts[3] + crossed[3]
    rise[0].start()
    ahead.ready()

    def show(part):
        shown[part] = (live[part, :1] * (kept[part] + ahead.read(part))).astype(BF16)

    pieces(SEQ_LEN, show)
    leave_out.start()
    for one in sums:
        one.step(3)
    for step in (1, 2):
        rise[step - 1].wait_recv()
        rising[step] = parts[3 - step] + crossed[3 - step] + risen[step - 1]
        rise[step].start()
    rise[2].wait_recv()
    total = parts[0] + crossed[0] + risen[2]
    last[0] = total[:, : width // 2]
    last[1] = total[:, width // 2 :]
    swap.start()
    swap.wait()
    gain_sum[...] = last[place.x] + swapped[...]
    for copy in rise:
        copy.wait_send()
    leave.finish()
    leave_out.finish()
    for one in sums:
        one.finish()


def call(kernel, name, ident, inputs, specs, outputs, out_specs, scratch, sems):
    return pl.pallas_call(
        kernel,
        in_specs=specs,
        out_specs=out_specs,
        out_shape=[jax.ShapeDtypeStruct(shape, kind) for shape, kind in outputs],
        scratch_shapes=scratch + [DMA((sems,))],
        compiler_params=pltpu.CompilerParams(collective_id=ident, has_side_effects=True, vmem_limit_bytes=60 << 20),
        name=name,
    )(*inputs)


PAD = 128 - SLOTS
DOWN_EARLY = 768
UP_EARLY = 896


class Ring:
    def __init__(self, count):
        self.count = count
        self.stages = []
        left, stride = count // 2, count
        while left > 1:
            size = 4 if left % 4 == 0 else 2
            stride //= size
            left //= size
            self.stages.append((stride, size))

    def perm(self, stride, size, shift):
        moves = []
        for source in range(self.count):
            digit = source // stride % size
            moves.append((source, source + ((digit + shift) % size - digit) * stride))
        return moves

    def send(self, value, stage, shift):
        stride, size = stage
        return lax.ppermute(value, "dp", self.perm(stride, size, shift % size))

    def swap(self, value):
        return lax.ppermute(value, "dp", self.perm(1, 2, 1))

    def digit(self, stage):
        return lax.axis_index("dp") // stage[0] % stage[1]

    def gather(self, block):
        blocks = [block]
        for stage in self.stages:
            more = list(blocks)
            for shift in range(1, stage[1]):
                more += [self.send(one, stage, -shift) for one in blocks]
            blocks = more
        return blocks

    def scatter(self, make):
        def level(depth, offset, width):
            if depth == len(self.stages):
                return lambda inner: make(offset + inner)
            return None

        widths = [1]
        for stage in self.stages:
            widths.append(widths[-1] * stage[1])

        def total(depth, index):
            if depth == len(self.stages):
                return make(index)
            stage = self.stages[depth]
            parts = []
            for shift in range(1, stage[1]):
                sent = total(depth + 1, index + shift * widths[depth]).astype(BF16)
                parts.append(self.send(sent, stage, shift))
            mine = total(depth + 1, index)
            for part in parts:
                mine = mine + part.astype(F32)
            return mine

        return total(0, 0)

    def order(self, value, width, back=False):
        parts = [value[:, i * width : (i + 1) * width] for i in range(self.count // 2)]
        stages = self.stages
        if back:
            parts = self.turn_digits(parts, [s[1] for s in stages[::-1]])
        inner = len(parts)
        for stage in stages:
            size = stage[1]
            inner //= size
            digit = self.digit(stage)
            new = []
            for place in range(len(parts)):
                at = place // inner % size
                base = place - at * inner
                picks = []
                for k in range(size):
                    picks.append(parts[base + ((at - k) % size if back else (at + k) % size) * inner])
                one = picks[0]
                for k in range(1, size):
                    one = jnp.where(digit == k, picks[k], one)
                new.append(one)
            parts = new
        if not back:
            parts = self.turn_digits(parts, [s[1] for s in stages])
        return jnp.concatenate(parts, axis=1)

    def turn_digits(self, parts, sizes):
        count = len(parts)
        out = [None] * count
        for index in range(count):
            rest, digits = index, []
            for size in reversed(sizes):
                digits.append(rest % size)
                rest //= size
            new = 0
            for digit, size in zip(digits, reversed(sizes)):
                new = new * size + digit
            out[new] = parts[index]
        return out


def mm(left, right, dims=NN, kind=F32):
    return lax.dot_general(left, right, dims, preferred_element_type=F32).astype(kind)


def rms(values):
    return lax.rsqrt(jnp.mean(values * values, axis=-1, keepdims=True) + 1e-06)


def norm_back(values, gain, grad):
    scale = rms(values)
    scaled = gain * grad
    inner = jnp.mean(scaled * values, axis=-1, keepdims=True)
    return scale * scaled - values * (scale * scale * scale * inner), jnp.sum(grad * values * scale, axis=0)


def body_by_permutes(
    tokens,
    seq_count,
    valid_len,
    attn_gain,
    ffn_gain,
    q_weight,
    k_weight,
    v_weight,
    forget_weight,
    out_weight,
    gate_weight,
    up_weight,
    down_weight,
    cotangent,
    *,
    ring,
):
    shard = q_weight.shape[0]
    width = 2 * shard
    core = lax.axis_index("head")
    even = lax.axis_index("dp") % 2 == 0
    first = core == 0
    rows = tokens.shape[0]

    def other_core(value):
        return lax.ppermute(value, "head", [(0, 1), (1, 0)])

    def pair_rows(mine, theirs, axis=0):
        return jnp.where(
            even, jnp.concatenate([mine, theirs], axis=axis), jnp.concatenate([theirs, mine], axis=axis)
        )

    def gather(parts):
        left = jnp.concatenate([p[0] for p in parts], axis=1)
        right = jnp.concatenate([p[1] for p in parts], axis=1)
        mine, theirs = jnp.where(even, left, right), jnp.where(even, right, left)
        return jnp.concatenate(ring.gather(pair_rows(mine, ring.swap(theirs))), axis=0)

    def cut(weight):
        half = weight.shape[1] // 2
        return (weight[:, :half], weight[:, half:])

    def quad_gather(mine):
        chips = jnp.concatenate([mine, ring.swap(mine)], axis=0)
        return jnp.concatenate([chips, other_core(chips)], axis=0)

    def quad_scatter(make):
        theirs = other_core(make(slice(2 * SEQ_LEN, 4 * SEQ_LEN)))
        far = make(slice(SEQ_LEN, 2 * SEQ_LEN)) + theirs[SEQ_LEN:]
        near = make(slice(0, SEQ_LEN)) + theirs[:SEQ_LEN]
        return near + ring.swap(far.astype(BF16)).astype(F32)

    def whole_rows(mine):
        theirs = other_core(mine)
        return jnp.where(
            first, jnp.concatenate([mine, theirs], axis=0), jnp.concatenate([theirs, mine], axis=0)
        )

    def weight_sum(act, grads):
        def make(index):
            return mm(act[:, index * width : (index + 1) * width], grads, TN)

        done = ring.scatter(make)
        mine = jnp.where(even, done[:shard], done[shard:])
        theirs = ring.swap(jnp.where(even, done[shard:], done[:shard]))
        return (jnp.where(even, mine, theirs), jnp.where(even, theirs, mine))

    gains = jnp.concatenate(
        [attn_gain[:, None], ffn_gain[:, None], jnp.zeros((shard, PAD - 2), BF16)], axis=1
    )
    w_in = gather([cut(q_weight), cut(k_weight), cut(v_weight), cut(forget_weight), (gains, gains)])
    w_out = gather([cut(out_weight)])
    w_gate = gather([cut(gate_weight)])
    w_up = gather([cut(up_weight)])
    w_down = gather([cut(down_weight)])
    gain_attn = w_in[:, WIDE - PAD].astype(F32)[None, :]
    gain_ffn = w_in[:, WIDE - PAD + 1].astype(F32)[None, :]

    def own(value):
        return ring.order(jnp.where(first, value[:SEQ_LEN], value[SEQ_LEN:]), width)

    places = lax.broadcasted_iota(jnp.int32, (SEQ_LEN, 1), 0)
    length = jnp.where(first, valid_len[0], valid_len[1])
    live = ((core < seq_count[0]) & (places < length)).astype(F32)
    own_tokens = own(tokens)
    d_res = live * own(cotangent)
    d_ffn = quad_gather(d_res.astype(BF16))
    inputs = quad_gather(own_tokens).astype(F32)
    attn_in = (inputs * rms(inputs) * gain_attn).astype(BF16)
    proj = mm(attn_in, w_in)
    mixed, *saved = mixer_forward(proj)
    own_inputs = own_tokens.astype(F32)
    resid = own_inputs + quad_scatter(lambda r: mm(mixed[r], w_out, NT))
    ffn_in = quad_gather((resid * rms(resid) * gain_ffn).astype(BF16))
    gate, up_vals = mm(ffn_in, w_gate), mm(ffn_in, w_up)
    sig = jax.nn.sigmoid(gate)
    hidden = (gate * sig * up_vals).astype(BF16)
    d_hidden = mm(d_ffn, w_down)
    d_gate = (d_hidden * up_vals * (sig * (1.0 + gate * (1.0 - sig)))).astype(BF16)
    d_up = (d_hidden * (gate * sig)).astype(BF16)
    d_ffn_in = quad_scatter(lambda r: mm(d_gate[r], w_gate, NT) + mm(d_up[r], w_up, NT))
    down_sum = weight_sum(d_ffn, hidden)
    gate_sum = weight_sum(ffn_in, d_gate)
    up_sum = weight_sum(ffn_in, d_up)
    ffn = quad_scatter(lambda r: mm(hidden[r], w_down, NT))
    block_out = whole_rows(ring.order((live * (resid + ffn)).astype(BF16), width, back=True))
    d_norm, ffn_gain_part = norm_back(resid, gain_ffn, d_ffn_in)
    d_h = d_res + d_norm
    d_attn = quad_gather(d_h.astype(BF16))
    d_mixed = mm(d_attn, w_out)
    d_proj = mixer_backward(proj, saved, d_mixed)
    d_attn_in = quad_scatter(lambda r: mm(d_proj[r], w_in, NT))
    out_sum = weight_sum(d_attn, mixed)
    in_sum = weight_sum(attn_in, d_proj)
    d_input, attn_gain_part = norm_back(own_inputs, gain_attn, d_attn_in)
    input_grad = whole_rows(ring.order(d_h + d_input, width, back=True))

    both = jnp.stack([attn_gain_part, ffn_gain_part], axis=0)
    both = both + other_core(both)
    both = both.reshape(2, ring.count // 2, width)
    for stage in ring.stages[::-1]:
        size = stage[1]
        both = both.reshape(2, size, -1, width)
        parts = [ring.send(both[:, shift], stage, shift) for shift in range(1, size)]
        both = both[:, 0]
        for part in parts:
            both = both + part
    both = both.reshape(2, 2, shard)
    both = jnp.where(even, both[:, 0], both[:, 1]) + ring.swap(jnp.where(even, both[:, 1], both[:, 0]))

    def columns(pieces, start, stop):
        return jnp.concatenate([p[:, start:stop] for p in pieces], axis=1)

    return (
        block_out,
        input_grad,
        both[0],
        both[1],
        columns(in_sum, 0, KDIM),
        columns(in_sum, KDIM, 2 * KDIM),
        columns(in_sum, 2 * KDIM, 3 * KDIM),
        columns(in_sum, 3 * KDIM, 3 * KDIM + SLOTS),
        columns(out_sum, 0, KDIM),
        jnp.concatenate(gate_sum, axis=1),
        jnp.concatenate(up_sum, axis=1),
        jnp.concatenate(down_sum, axis=1),
    )


def body_by_kernels(
    tokens,
    seq_count,
    valid_len,
    attn_gain,
    ffn_gain,
    q_weight,
    k_weight,
    v_weight,
    forget_weight,
    out_weight,
    gate_weight,
    up_weight,
    down_weight,
    cotangent,
    *,
    ring,
):
    shard, dim = q_weight.shape[0], tokens.shape[1]
    width, hid = 2 * shard, gate_weight.shape[1] // 2
    core = lax.axis_index("head")
    first = core == 0
    up_z, over_y = (lambda value: ring.send(value, ring.stages[0], 1)), (lambda value: ring.send(value, ring.stages[1], 1))
    rows4 = (4, SEQ_LEN, dim)
    blocks = lambda value: value.reshape(-1, width, value.shape[-1])
    flat = lambda value: value.reshape(-1, value.shape[-1])
    half = dim // 2

    gains = jnp.concatenate([attn_gain[:, None], ffn_gain[:, None], jnp.zeros((shard, PAD - 2), BF16)], axis=1)
    small = jnp.concatenate([forget_weight[:, :SLOTS], gains, forget_weight[:, SLOTS:], gains], axis=1)
    places = lax.broadcasted_iota(jnp.int32, (SEQ_LEN, 128), 0)
    length = jnp.where(first, valid_len[0], valid_len[1])
    live = ((core < seq_count[0]) & (places < length)).astype(F32)
    row = (SEQ_LEN, dim)
    vmem = lambda shape, kind=F32: pltpu.VMEM(shape, kind)
    w_in, w_out, part0, own, attn_in, d_res, d_ffn, gain_rows = call(
        gather_first_kernel,
        "gather_first",
        0,
        (tokens, cotangent, live, q_weight, k_weight, v_weight, small, out_weight, gate_weight, up_weight, down_weight),
        [ANY, ANY, VMEM] + [ANY] * 8,
        [
            ((8, width, WIDE), BF16),
            ((8, width, KDIM), BF16),
            ((width, 3 * hid), BF16),
            (row, BF16),
            (rows4, BF16),
            (row, F32),
            (rows4, BF16),
            ((8, dim), F32),
        ],
        [ANY] * 7 + [VMEM],
        [
            vmem((shard, 4 * KDIM + 128 + 3 * hid), BF16),
            vmem(rows4, BF16),
            vmem(rows4, BF16),
            vmem((4, SEQ_LEN, 128)),
            vmem((8, width, 128), BF16),
            vmem(row),
            vmem(row, BF16),
        ],
        240,
    )
    part3, part4 = up_z(part0), over_y(part0)
    w_in, w_out, attn_in, d_ffn = map(flat, (w_in, w_out, attn_in, d_ffn))
    proj = mm(attn_in, w_in)
    mixed, *saved = mixer_forward(proj)
    attn_terms = mm(mixed, w_out, NT).reshape(rows4)
    cut = hid // 256 * 128 + 128
    w_gate, w_up, w_down, resid, ffn_in = call(
        functools.partial(gather_ffn_kernel, hid, cut),
        "gather_ffn",
        1,
        (part0, part3, part4, attn_terms, own, gain_rows),
        [ANY] * 5 + [VMEM],
        [((8, width, hid), BF16)] * 3 + [(row, F32), (rows4, BF16)],
        [ANY] * 5,
        quad_scratch(dim) + [vmem(row), vmem(row, BF16), vmem(row, BF16), vmem((3, width, 3 * hid), BF16)],
        160,
    )
    w_gate, w_up, w_down, ffn_in = map(flat, (w_gate, w_up, w_down, ffn_in))
    gate, up_vals = mm(ffn_in, w_gate), mm(ffn_in, w_up)
    sig = jax.nn.sigmoid(gate)
    hidden = (gate * sig * up_vals).astype(BF16)
    down_given = over_y(mm(d_ffn[:, half:], hidden[:, :DOWN_EARLY], TN, BF16))
    down_terms = mm(d_ffn[:, :half], hidden[:, :DOWN_EARLY], TN, BF16)
    down_rest = mm(d_ffn, hidden[:, DOWN_EARLY:], TN, BF16)
    d_hidden = mm(d_ffn, w_down)
    d_gate = (d_hidden * up_vals * (sig * (1.0 + gate * (1.0 - sig)))).astype(BF16)
    d_up = (d_hidden * (gate * sig)).astype(BF16)
    gate_terms = mm(ffn_in, d_gate, TN, BF16)
    d_ffn_terms = (mm(d_gate, w_gate, NT) + mm(d_up, w_up, NT)).reshape(rows4)
    gate_sum, down_sum, d_h, d_attn, ffn_gains = call(
        functools.partial(sum_ffn_kernel, hid, DOWN_EARLY),
        "sum_ffn",
        2,
        (
            blocks(gate_terms),
            blocks(down_terms),
            blocks(down_given),
            blocks(down_rest),
            d_ffn_terms,
            resid,
            gain_rows,
            d_res,
        ),
        [ANY] * 6 + [VMEM, ANY],
        [((shard, 2 * hid), F32), ((shard, 2 * hid), F32), (row, F32), (rows4, BF16), ((8, dim), F32)],
        [ANY] * 4 + [VMEM],
        sum_scratch(width, DOWN_EARLY)
        + sum_scratch(width, hid - DOWN_EARLY)
        + sum_scratch(width, DOWN_EARLY)
        + sum_scratch(width, hid - DOWN_EARLY)
        + quad_scratch(dim)
        + [vmem(row), vmem(row), vmem(row, BF16)],
        200,
    )
    d_attn, d_up, hidden, ffn_in = lax.optimization_barrier((flat(d_attn), d_up, hidden, ffn_in))
    up_given = over_y(mm(ffn_in[:, half:], d_up[:, :UP_EARLY], TN, BF16))
    d_proj = mixer_backward(proj, saved, mm(d_attn, w_out))
    d_attn_terms = mm(d_proj, w_in, NT).reshape(rows4)
    up_terms = mm(ffn_in[:, :half], d_up[:, :UP_EARLY], TN, BF16)
    up_rest = mm(ffn_in, d_up[:, UP_EARLY:], TN, BF16)
    ffn_terms = mm(hidden, w_down, NT).reshape(rows4)
    tail = width // 2
    up_sum, out_sum, q_sum, k_sum, v_sum, f_sum, input_grad, block_out, gain_sums = call(
        functools.partial(sum_last_kernel, hid, UP_EARLY),
        "sum_last",
        3,
        (
            blocks(up_terms),
            blocks(up_given),
            blocks(up_rest),
            blocks(mm(d_attn, mixed, TN, BF16)),
            blocks(mm(attn_in, d_proj, TN, BF16)),
            d_attn_terms,
            own,
            gain_rows,
            d_h,
            ffn_gains,
            ffn_terms,
            resid,
            live,
        ),
        [ANY] * 7 + [VMEM, ANY, VMEM, ANY, ANY, VMEM],
        [((shard, 2 * hid), F32)]
        + [((shard, 2 * KDIM), F32)] * 4
        + [((shard, 256), F32), ((2 * SEQ_LEN, dim), F32), ((2 * SEQ_LEN, dim), BF16), ((8, tail), F32)],
        [ANY] * 8 + [VMEM],
        sum_scratch(width, UP_EARLY)
        + sum_scratch(width, hid - UP_EARLY)
        + sum_scratch(width, KDIM) * 4
        + sum_scratch(width, 128)
        + quad_scratch(dim) * 2
        + [vmem(row, BF16), vmem(row), vmem(row), vmem(row, BF16), vmem((8, dim))]
        + [vmem((depth, 8, width)) for depth in (8, 8, 4, 3, 3)]
        + [vmem((2, 8, tail)), vmem((8, tail))],
        280,
    )
    f_grad = jnp.concatenate([f_sum[:, :SLOTS], f_sum[:, 128 : 128 + SLOTS]], axis=1)
    return (
        block_out,
        input_grad,
        gain_sums[0],
        gain_sums[1],
        q_sum,
        k_sum,
        v_sum,
        f_grad,
        out_sum,
        gate_sum,
        up_sum,
        down_sum,
    )


def solution(mesh):
    ring = Ring(mesh.shape["dp"])
    body = body_by_kernels if ring.count == 16 else body_by_permutes
    split_one, split_two = P("dp"), P("dp", "head")
    row = P("dp", None)
    in_specs = (row, split_one, split_one, split_one, split_one) + (split_two,) * 8 + (row,)
    out_specs = (row, row, split_one, split_one) + (split_two,) * 8
    return jax.shard_map(
        functools.partial(body, ring=ring),
        mesh=mesh,
        in_specs=in_specs,
        out_specs=out_specs,
        check_vma=False,
    )
```

```python
import functools
import jax
import jax.numpy as jnp
from jax import lax
from jax.experimental import pallas as pl
from jax.experimental.pallas import tpu as pltpu
from jax.sharding import PartitionSpec as P

SLOTS = 64
KDIM = 512
SEQ_LEN = 256
HALF = 128
F32, BF16 = jnp.float32, jnp.bfloat16
WIDE = 3 * KDIM + 128
NT = (((1,), (1,)), ((), ()))
NN = (((1,), (0,)), ((), ()))
TN = (((0,), (0,)), ((), ()))
LEVELS = (8, 16, 32, 64)


def split(value):
    high = value.astype(BF16)
    return high, (value - high.astype(F32)).astype(BF16)


def dot3(left, right, dims):
    one = functools.partial(lax.dot_general, dimension_numbers=dims, preferred_element_type=F32)
    return one(left[0], right[0]) + (one(left[0], right[1]) + one(left[1], right[0]))


def silu_parts(value):
    gate = 1.0 / (1.0 + jnp.exp(-value))
    return gate, value * gate


def level_mask(size):
    row = lax.broadcasted_iota(jnp.int32, (HALF, HALF), 0) // size
    col = lax.broadcasted_iota(jnp.int32, (HALF, HALF), 1) // size
    return (row == col + 1) & (row % 2 == 1)


def band_mask(back):
    row = lax.broadcasted_iota(jnp.int32, (HALF, HALF), 0)
    col = lax.broadcasted_iota(jnp.int32, (HALF, HALF), 1)
    return (row == col + back) & (row // 8 == col // 8)


def down(value, back):
    return value if back == 0 else pltpu.roll(value, back, 0)


def up(value, back):
    return value if back == 0 else pltpu.roll(value, SEQ_LEN - back, 0)


def gates(forget):
    lane = lax.broadcasted_iota(jnp.int32, forget.shape, 1) < SLOTS
    place = lax.broadcasted_iota(jnp.int32, forget.shape, 0)
    forget = jnp.where(lane, forget, 0.0)
    tail = jnp.exp(-jnp.abs(forget))
    log_decay = (jnp.minimum(forget, 0.0) - jnp.log1p(tail)) * 0.125
    log_decay = jnp.where(lane, log_decay, 0.0)
    g = log_decay
    series = 1.0 + g * (1.0 / 7.0)
    for n in (6.0, 5.0, 4.0, 3.0, 2.0):
        series = 1.0 + g * (1.0 / n) * series
    writes = jnp.where(g > -0.3, -g * series, 1.0 - jnp.exp(g))
    writes = jnp.where(lane, writes, 0.0)
    ahead, behind = g, g
    for step in (1, 2, 4):
        ahead = ahead + jnp.where(place % 8 >= step, down(ahead, step), 0.0)
        behind = behind + jnp.where(place % 8 < 8 - step, up(behind, step), 0.0)
    behind = jnp.where(place % 8 < 7, up(behind, 1), 0.0)
    aheads, behinds = {8: ahead}, {8: behind}
    size = 8
    while size < HALF:
        first = ahead.reshape(SEQ_LEN // (2 * size), 2, size, 128)
        last = behind.reshape(SEQ_LEN // (2 * size), 2, size, 128)
        left, right = first[:, 0:1], first[:, 1:2]
        left_sum, right_sum = left[:, :, size - 1 :], right[:, :, size - 1 :]
        ahead = jnp.concatenate([left, right + left_sum], axis=1).reshape(SEQ_LEN, 128)
        behind = jnp.concatenate([last[:, 0:1] + right_sum, last[:, 1:2]], axis=1).reshape(SEQ_LEN, 128)
        size *= 2
        aheads[size], behinds[size] = ahead, behind
    return lane, place, g, writes, aheads, behinds


def near_decays(place, aheads, back):
    ahead = aheads[8]
    gap = jnp.where(place % 8 >= back, ahead - down(ahead, back), 0.0)
    return jnp.where(place % 8 >= back, jnp.exp(gap), 0.0)


def halves(value):
    return value[:HALF], value[HALF:]


def to_slots(blocks, cross, place, writes, aheads, behinds, nears):
    grow = {size: jnp.exp(aheads[size]) for size in LEVELS}
    keep = {size: split(jnp.exp(behinds[size]) * writes) for size in LEVELS}
    outs = []
    for half in range(2):
        here = slice(half * HALF, (half + 1) * HALF)
        block = blocks[half]
        parts = split(block)
        total = None
        for size in LEVELS:
            mask = level_mask(size)
            masked = tuple(jnp.where(mask, part, jnp.zeros_like(part)) for part in parts)
            term = grow[size][here] * dot3(masked, tuple(k[here] for k in keep[size]), NN)
            total = term if total is None else total + term
        for back in range(8):
            near = jnp.sum(jnp.where(band_mask(back), block, 0.0), axis=1, keepdims=True)
            total = total + near * nears[back][here]
        if half == 1:
            far = split((jnp.exp(behinds[HALF]) * writes)[:HALF])
            total = total + jnp.exp(aheads[HALF])[HALF:] * dot3(split(cross), far, NN)
        outs.append(total)
    return jnp.concatenate(outs, axis=0)


def to_tokens(slots, writes, aheads, behinds, nears):
    blocks = []
    for half in range(2):
        here = slice(half * HALF, (half + 1) * HALF)
        total = jnp.zeros((HALF, HALF), F32)
        for size in LEVELS:
            left = split((slots * jnp.exp(aheads[size]))[here])
            right = split((jnp.exp(behinds[size]) * writes)[here])
            total = jnp.where(level_mask(size), dot3(left, right, NT), total)
        for back in range(8):
            near = jnp.sum(slots[here] * nears[back][here], axis=1, keepdims=True)
            total = jnp.where(band_mask(back), near, total)
        blocks.append(total)
    left = split((slots * jnp.exp(aheads[HALF]))[HALF:])
    right = split((jnp.exp(behinds[HALF]) * writes)[:HALF])
    return blocks, dot3(left, right, NT)


def forward_kernel(q_ref, k_ref, v_ref, f_ref, o_ref, p_ref, s_ref, a_ref, b_ref):
    query = split(silu_parts(q_ref[...])[1] * KDIM ** (-0.5))
    keys = split(silu_parts(k_ref[...])[1])
    values = split(v_ref[...])
    lane, place, g, writes, aheads, behinds = gates(f_ref[...])
    nears = [near_decays(place, aheads, back) * down(writes, back) for back in range(8)]
    q0, q1 = tuple(x[:HALF] for x in query), tuple(x[HALF:] for x in query)
    k0, k1 = tuple(x[:HALF] for x in keys), tuple(x[HALF:] for x in keys)
    blocks = (dot3(q0, k0, NT), dot3(q1, k1, NT))
    cross = dot3(q1, k0, NT)
    scores = to_slots(blocks, cross, place, writes, aheads, behinds, nears)
    shown = jnp.where(lane, scores, -1e30)
    weights = jnp.exp(shown - jnp.max(shown, axis=1, keepdims=True))
    weights = jnp.where(lane, weights, 0.0)
    weights = weights / jnp.sum(weights, axis=1, keepdims=True)
    mixes, mix_cross = to_tokens(weights, writes, aheads, behinds, nears)
    v0 = tuple(x[:HALF] for x in values)
    o_ref[:HALF, :] = dot3(split(mixes[0]), v0, NN).astype(o_ref.dtype)
    row = jnp.concatenate([mix_cross, mixes[1]], axis=1)
    o_ref[HALF:, :] = dot3(split(row), values, NN).astype(o_ref.dtype)
    p_ref[...] = weights
    s_ref[...] = scores
    a_ref[:HALF, :] = jnp.concatenate([blocks[0], jnp.zeros_like(cross)], axis=1)
    a_ref[HALF:, :] = jnp.concatenate([cross, blocks[1]], axis=1)
    b_ref[:HALF, :] = jnp.concatenate([mixes[0], jnp.zeros_like(cross)], axis=1)
    b_ref[HALF:, :] = row


def backward_kernel(q_ref, k_ref, v_ref, f_ref, p_ref, s_ref, a_ref, b_ref, d_ref, out_ref):
    lane, place, g, writes, aheads, behinds = gates(f_ref[...])
    spans = [near_decays(place, aheads, back) for back in range(8)]
    nears = [spans[back] * down(writes, back) for back in range(8)]
    weights, scores = p_ref[...], s_ref[...]
    products, mixing = a_ref[...], b_ref[...]
    grad = split(d_ref[...])
    g0, g1 = tuple(x[:HALF] for x in grad), tuple(x[HALF:] for x in grad)
    values = split(v_ref[...])
    v0, v1 = tuple(x[:HALF] for x in values), tuple(x[HALF:] for x in values)
    m_parts = split(mixing)
    dv0 = dot3(tuple(x[:, :HALF] for x in m_parts), grad, TN)
    dv1 = dot3(tuple(x[HALF:, HALF:] for x in m_parts), g1, TN)
    out_ref[:HALF, 2 * KDIM : 3 * KDIM] = dv0.astype(BF16)
    out_ref[HALF:, 2 * KDIM : 3 * KDIM] = dv1.astype(BF16)
    mix_blocks = (dot3(g0, v0, NT), dot3(g1, v1, NT))
    mix_cross = dot3(g1, v0, NT)
    d_weights = to_slots(mix_blocks, mix_cross, place, writes, aheads, behinds, nears)
    inner = jnp.sum(weights * d_weights, axis=1, keepdims=True)
    d_scores = weights * (d_weights - inner)
    d_blocks, d_cross = to_tokens(d_scores, writes, aheads, behinds, nears)
    q_gate, q_act = silu_parts(q_ref[...])
    k_gate, k_act = silu_parts(k_ref[...])
    scale = KDIM ** (-0.5)
    query, keys = split(q_act * scale), split(k_act)
    k0 = tuple(x[:HALF] for x in keys)
    low = split(jnp.concatenate([d_cross, d_blocks[1]], axis=1))
    top = split(d_blocks[0])
    dq = jnp.concatenate([dot3(top, k0, NN), dot3(low, keys, NN)], axis=0)
    first = tuple(jnp.concatenate([t, l[:, :HALF]], axis=0) for t, l in zip(top, low))
    dk0 = dot3(first, query, TN)
    dk1 = dot3(tuple(x[:, HALF:] for x in low), tuple(x[HALF:] for x in query), TN)
    dk = jnp.concatenate([dk0, dk1], axis=0)
    out_ref[:, :KDIM] = (dq * scale * (q_gate + q_act * (1.0 - q_gate))).astype(BF16)
    out_ref[:, KDIM : 2 * KDIM] = (dk * (k_gate + k_act * (1.0 - k_gate))).astype(BF16)
    parts = []
    for half in range(2):
        here = slice(half * HALF, (half + 1) * HALF)
        both = jnp.concatenate([mix_blocks[half], products[here, here]], axis=0)
        both_parts = split(both)
        total = None
        for size in LEVELS:
            mask = level_mask(size)
            mask = jnp.concatenate([mask, mask], axis=0)
            grow = jnp.exp(aheads[size][here])
            right = split(jnp.concatenate([weights[here] * grow, d_scores[here] * grow], axis=0))
            left = tuple(jnp.where(mask, part, jnp.zeros_like(part)) for part in both_parts)
            term = jnp.exp(behinds[size][here]) * dot3(left, right, TN)
            total = term if total is None else total + term
        parts.append(total)
    grow = jnp.exp(aheads[HALF][HALF:])
    left = split(jnp.concatenate([mix_cross, products[HALF:, :HALF]], axis=0))
    right = split(jnp.concatenate([weights[HALF:] * grow, d_scores[HALF:] * grow], axis=0))
    parts[0] = parts[0] + jnp.exp(behinds[HALF][:HALF]) * dot3(left, right, TN)
    reach = jnp.concatenate(parts, axis=0)
    for back in range(8):
        mask = band_mask(back)
        near_mix = jnp.concatenate([jnp.sum(jnp.where(mask, mix_blocks[h], 0.0), axis=1, keepdims=True) for h in range(2)], axis=0)
        near_pro = jnp.concatenate(
            [jnp.sum(jnp.where(mask, products[h * HALF : (h + 1) * HALF, h * HALF : (h + 1) * HALF], 0.0), axis=1, keepdims=True) for h in range(2)],
            axis=0,
        )
        reach = reach + up((near_mix * weights + near_pro * d_scores) * spans[back], back)
    d_sum = weights * d_weights + d_scores * scores - writes * reach
    step = 1
    while step < SEQ_LEN:
        d_sum = d_sum + jnp.where(place < SEQ_LEN - step, up(d_sum, step), 0.0)
        step *= 2
    d_log = d_sum - reach * jnp.exp(g)
    d_forget = d_log * 0.125 / (1.0 + jnp.exp(f_ref[...]))
    out_ref[:, 3 * KDIM :] = jnp.where(lane, d_forget, 0.0).astype(BF16)


def spec(width, column):
    return pl.BlockSpec((SEQ_LEN, width), lambda i: (i, column))


IN_SPECS = [spec(KDIM, 0), spec(KDIM, 1), spec(KDIM, 2), spec(128, 3 * KDIM // 128)]


def mixer_forward(proj):
    rows = proj.shape[0]
    shape = lambda width, kind: jax.ShapeDtypeStruct((rows, width), kind)
    return pl.pallas_call(
        forward_kernel,
        grid=(rows // SEQ_LEN,),
        in_specs=IN_SPECS,
        out_specs=[spec(KDIM, 0), spec(128, 0), spec(128, 0), spec(SEQ_LEN, 0), spec(SEQ_LEN, 0)],
        out_shape=[shape(KDIM, BF16), shape(128, F32), shape(128, F32), shape(SEQ_LEN, F32), shape(SEQ_LEN, F32)],
        compiler_params=pltpu.CompilerParams(vmem_limit_bytes=48 << 20),
        cost_estimate=pl.CostEstimate(flops=rows * 3000000, bytes_accessed=rows * 10000, transcendentals=rows * 3000),
        name="mixer_forward",
    )(proj, proj, proj, proj)


def mixer_backward(proj, saved, grad):
    rows = proj.shape[0]
    weights, scores, products, mixing = saved
    return pl.pallas_call(
        backward_kernel,
        grid=(rows // SEQ_LEN,),
        in_specs=IN_SPECS + [spec(128, 0), spec(128, 0), spec(SEQ_LEN, 0), spec(SEQ_LEN, 0), spec(KDIM, 0)],
        out_specs=spec(WIDE, 0),
        out_shape=jax.ShapeDtypeStruct((rows, WIDE), BF16),
        compiler_params=pltpu.CompilerParams(vmem_limit_bytes=48 << 20),
        cost_estimate=pl.CostEstimate(flops=rows * 9000000, bytes_accessed=rows * 16000, transcendentals=rows * 5000),
        name="mixer_backward",
    )(proj, proj, proj, proj, weights, scores, products, mixing, grad)


MESH = pl.DeviceIdType.MESH
ANY = pl.BlockSpec(memory_space=pl.ANY)
VMEM = pl.BlockSpec(memory_space=pltpu.VMEM)
DMA = pltpu.SemaphoreType.DMA
PIECE = 32


class Place:
    def __init__(self):
        dp = lax.axis_index("dp")
        self.core = lax.axis_index("head")
        self.x, self.y, self.z = dp % 2, dp // 2 % 2, dp // 4
        rest = dp % 4
        self.peers = {
            "x": (dp + 1 - 2 * self.x, self.core),
            "y": (dp + 2 - 4 * self.y, self.core),
            "up": ((self.z + 1) % 4 * 4 + rest, self.core),
            "down": ((self.z + 3) % 4 * 4 + rest, self.core),
            "core": (dp, 1 - self.core),
        }

    def greet(self):
        ready = pltpu.get_barrier_semaphore()
        for peer in self.peers.values():
            pl.semaphore_signal(ready, inc=1, device_id=peer, device_id_type=MESH)
        pl.semaphore_wait(ready, len(self.peers))

    def copy(self, name, source, target, sems):
        return pltpu.make_async_remote_copy(
            src_ref=source,
            dst_ref=target,
            send_sem=sems[0],
            recv_sem=sems[1],
            device_id=self.peers[name],
            device_id_type=MESH,
        )

    def half(self, size, other=False):
        place = 1 - self.x if other else self.x
        return pl.ds(pl.multiple_of(place * size, size), size)

    def columns(self, index, size):
        natural = (self.z + index % 4) % 4 * 2 + (self.y + index // 4) % 2
        return pl.ds(pl.multiple_of(natural * size, size), size)


class Sems:
    def __init__(self, ref):
        self.ref, self.used = ref, 0

    def one(self):
        self.used += 1
        return self.ref.at[self.used - 1]

    def two(self):
        return (self.one(), self.one())

    def some(self, count):
        first = self.used
        self.used += count
        return lambda index: self.ref.at[first + index]


def pieces(rows, work):
    def step(i, carry):
        work(pl.ds(pl.multiple_of(i * PIECE, PIECE), PIECE))
        return carry

    lax.fori_loop(0, rows // PIECE, step, 0)


class Keep:
    def __init__(self, sems, source, target, stage):
        self.load = pltpu.make_async_copy(source, stage, sems.one())
        self.store = pltpu.make_async_copy(stage, target, sems.one())

    def start(self):
        self.load.start()

    def turn(self):
        self.load.wait()
        self.store.start()

    def wait(self):
        self.store.wait()


class Quad:
    def __init__(self, place, sems, source, target):
        near = [pltpu.make_async_copy(source, target.at[0], sems.one())]
        self.swap = place.copy("x", source, target.at[1], sems.two())
        self.core = place.copy("core", source, target.at[2], sems.two())
        self.last = place.copy("core", target.at[1], target.at[3], sems.two())
        self.near = near

    def start(self):
        self.swap.start()
        self.core.start()
        for copy in self.near:
            copy.start()

    def forward(self):
        self.swap.wait_recv()
        self.last.start()

    def finish(self):
        self.swap.wait_send()
        self.core.wait()
        self.last.wait()
        for copy in self.near:
            copy.wait()


class QuadSum:
    def __init__(self, place, sems, terms, scratch):
        self.near, self.theirs, self.far, self.swapped = scratch
        self.core = place.copy("core", terms.at[pl.ds(2, 2)], self.theirs, sems.two())
        self.load = pltpu.make_async_copy(terms.at[pl.ds(0, 2)], self.near, sems.one())
        self.swap = place.copy("x", self.far, self.swapped, sems.two())

    def start(self):
        self.core.start()
        self.load.start()

    def middle(self):
        self.core.wait()
        self.load.wait()

        def add(part):
            self.far[part] = (self.near[1, part] + self.theirs[1, part]).astype(BF16)

        pieces(SEQ_LEN, add)
        self.swap.start()

    def ready(self):
        self.swap.wait()

    def read(self, part):
        return self.near[0, part] + self.theirs[0, part] + self.swapped[part].astype(F32)


def quad_scratch(width):
    return [
        pltpu.VMEM((2, SEQ_LEN, width), F32),
        pltpu.VMEM((2, SEQ_LEN, width), F32),
        pltpu.VMEM((SEQ_LEN, width), BF16),
        pltpu.VMEM((SEQ_LEN, width), BF16),
    ]


class Leave:
    def __init__(self, place, sems, source, target):
        rows = pl.ds(pl.multiple_of(place.core * SEQ_LEN, SEQ_LEN), SEQ_LEN)
        width = source.shape[1] // 8
        self.copies, self.here = [], []
        for index in range(8):
            part = source.at[:, pl.ds(index * width, width)]
            there = target.at[rows, place.columns(index, width)]
            self.copies.append(place.copy("core", part, there, sems.two()))
            self.here.append(pltpu.make_async_copy(part, there, sems.one()))

    def start(self):
        for copy in self.copies + self.here:
            copy.start()

    def finish(self):
        for copy in self.copies + self.here:
            copy.wait()


def gather_first_kernel(
    tokens, cot, live, q_w, k_w, v_w, small, out_w, gate_w, up_w, down_w, w_in, w_out, ffn, own, attn_in, d_res, d_ffn, gains,
    stage, seqs, normed, scales, turned, grads, low, sem
):
    place, sems = Place(), Sems(sem)
    shard = q_w.shape[0]
    rows = place.half(shard)
    hid = gate_w.shape[1] // 2
    chunks = [
        (small, 0, 128, w_in, 3 * KDIM, True),
        (q_w, 0, KDIM, w_in, 0, False),
        (k_w, 0, KDIM, w_in, KDIM, False),
        (v_w, 0, KDIM, w_in, 2 * KDIM, False),
        (out_w, 0, KDIM // 2, w_out, 0, True),
        (out_w, KDIM // 2, KDIM // 2, w_out, KDIM // 2, False),
        (gate_w, 0, hid, ffn, 0, False),
        (up_w, 0, hid, ffn, hid, False),
        (down_w, 0, hid, ffn, 2 * hid, False),
    ]
    full = len(chunks) - 3
    swaps, keeps, rises, crosses = [], [], [], []
    used = 0
    for c, (source, offset, width, target, first, y_first) in enumerate(chunks):
        cols = pl.ds(first, width)
        where = target.at[0, rows, cols] if c < full else target.at[rows, cols]
        span = source.shape[1] // 2
        here, there = (pl.ds(pl.multiple_of(at * span + offset, 128), width) for at in (place.x, 1 - place.x))
        swaps.append(place.copy("x", source.at[:, there], where, sems.two()))
        keeps.append(Keep(sems, source.at[:, here], where, stage.at[:, pl.ds(used, width)]))
        used += width
        if c >= full:
            continue

        def block(index, target=target, cols=cols):
            return target.at[index, :, cols]

        rises.append(
            [
                [place.copy("up", block((4 - step) % 4 + 4 * u), block(3 - step + 4 * u), sems.two()) for step in range(3)]
                for u in range(2 if y_first else 1)
            ]
        )
        crosses.append(
            [place.copy("y", block(i), block(4 + i), sems.two()) for i in range(1 if y_first else 4)]
        )
    width = tokens.shape[1] // 8
    mine = pl.ds(pl.multiple_of(place.core * SEQ_LEN, SEQ_LEN), SEQ_LEN)
    far, side, fetch, fetch_cot = [], [], [], []
    for index in range(8):
        part = tokens.at[mine, place.columns(index, width)]
        cols = pl.ds(index * width, width)
        far.append(place.copy("x", part, seqs.at[1, :, cols], sems.two()))
        side.append(place.copy("core", part, seqs.at[2, :, cols], sems.two()))
        fetch.append(pltpu.make_async_copy(part, seqs.at[0, :, cols], sems.one()))
        fetch_cot.append(
            pltpu.make_async_copy(cot.at[mine, place.columns(index, width)], grads.at[:, cols], sems.one())
        )
    last = place.copy("core", seqs.at[1], seqs.at[3], sems.two())
    quad = Quad(place, sems, low, d_ffn)
    save_own = pltpu.make_async_copy(seqs.at[0], own, sems.one())
    save_res = pltpu.make_async_copy(grads, d_res, sems.one())
    save_in = [pltpu.make_async_copy(normed.at[i], attn_in.at[i], sems.one()) for i in range(4)]
    load_gains = [pltpu.make_async_copy(w_in.at[i, :, pl.ds(3 * KDIM, 128)], turned.at[i], sems.one()) for i in range(8)]
    place.greet()
    for swap, keep in zip(swaps[:full], keeps[:full]):
        swap.start()
        keep.start()
    for copy in far + side + fetch + fetch_cot:
        copy.start()
    for swap, keep in zip(swaps[full:], keeps[full:]):
        swap.start()
        keep.start()
    for keep in keeps:
        keep.turn()
    for c in range(full):
        keeps[c].wait()
        swaps[c].wait_recv()
        rises[c][0][0].start()
        crosses[c][0].start()
    for copy in fetch + fetch_cot:
        copy.wait()
    save_own.start()

    def mask(part):
        value = grads[part] * live[part, :1]
        grads[part] = value
        low[part] = value.astype(BF16)

    pieces(SEQ_LEN, mask)
    save_res.start()
    quad.start()
    for c in range(full):
        if chunks[c][5]:
            crosses[c][0].wait_recv()
            rises[c][1][0].start()

    def measure(slot):
        def one(part):
            scales[slot, part] = jnp.broadcast_to(rms(seqs[slot, part].astype(F32)), (PIECE, 128))

        pieces(SEQ_LEN, one)

    def norm(slot):
        def one(part):
            value = seqs[slot, part].astype(F32) * scales[slot, part, :1] * gains[0:1, :]
            normed[slot, part] = value.astype(BF16)

        pieces(SEQ_LEN, one)
        save_in[slot].start()

    for step in range(3):
        for c in range(full):
            for rise in rises[c]:
                rise[step].wait_recv()
                if step < 2:
                    rise[step + 1].start()
            if not chunks[c][5]:
                crosses[c][3 - step].start()
            if step == 0 and c == 1:
                measure(0)
            if step == 0 and c == full - 1:
                for copy in far:
                    copy.wait_recv()
                last.start()
            if step == 1:
                if c == 0:
                    for copy in side:
                        copy.wait_recv()
                    last.wait_recv()
                if 1 <= c <= 3:
                    measure(c)
            if step == 2:
                if c == 0:
                    for copy in load_gains:
                        copy.start()
                    for index, copy in enumerate(load_gains):
                        copy.wait()
                        flipped = turned[index].astype(F32).T
                        gains[0:8, index * width : (index + 1) * width] = flipped[SLOTS : SLOTS + 8]
                if 1 <= c <= 4:
                    norm(c - 1)
    quad.forward()
    for c in range(full):
        for cross in crosses[c]:
            cross.wait_send()
            if not chunks[c][5]:
                cross.wait_recv()
        for rise in rises[c]:
            for copy in rise:
                copy.wait_send()
    for swap in swaps[:full]:
        swap.wait_send()
    for swap, keep in zip(swaps[full:], keeps[full:]):
        swap.wait()
        keep.wait()
    for copy in far + side + [last]:
        copy.wait_send()
    for copy in save_in + [save_own, save_res]:
        copy.wait()
    quad.finish()


def gather_ffn_kernel(
    hid, cut, b0, b3, b4, terms, tokens, gains, w_wide, w_down, resid, ffn_in, s0, s1, s2, s3, kept, normed, inputs, stage, sem
):
    place, sems = Place(), Sems(sem)
    chunks = [
        (0, hid, w_wide, 0, False),
        (hid, hid, w_wide, hid, False),
        (2 * hid, cut, w_down, 0, False),
        (2 * hid + cut, hid - cut, w_down, cut, True),
    ]
    keeps, rises, crosses = [], [], []
    for first, width, target, start, y_first in chunks:
        cols, source = pl.ds(start, width), pl.ds(first, width)

        def block(index, target=target, cols=cols):
            return target.at[index, :, cols]

        keeps += [
            Keep(sems, b.at[:, source], block(i), stage.at[at, :, source])
            for at, (b, i) in enumerate(((b0, 0), (b3, 3), (b4, 4)))
        ]
        lower = [
            place.copy("up", b3.at[:, source], block(2), sems.two()),
            place.copy("up", block(2), block(1), sems.two()),
        ]
        high = []
        if y_first:
            high = [
                place.copy("up", b4.at[:, source], block(7), sems.two()),
                place.copy("up", block(7), block(6), sems.two()),
                place.copy("up", block(6), block(5), sems.two()),
            ]
            crosses.append([])
        else:
            crosses.append(
                [
                    place.copy("y", b3.at[:, source], block(7), sems.two()),
                    place.copy("y", block(2), block(6), sems.two()),
                    place.copy("y", block(1), block(5), sems.two()),
                ]
            )
        rises.append((lower, high))
    total = QuadSum(place, sems, terms, (s0, s1, s2, s3))
    out = Quad(place, sems, normed, ffn_in)
    fetch = pltpu.make_async_copy(tokens, inputs, sems.one())
    save = pltpu.make_async_copy(kept, resid, sems.one())
    place.greet()
    total.start()
    fetch.start()
    for (lower, high), cross in zip(rises, crosses):
        lower[0].start()
        for copy in high[:1] + cross[:1]:
            copy.start()
    for copy in keeps:
        copy.start()
    total.middle()
    for copy in keeps:
        copy.turn()
    fetch.wait()
    for c, ((lower, high), cross) in enumerate(zip(rises, crosses)):
        if c == 2:
            total.ready()

            def norm(part):
                value = total.read(part) + inputs[part].astype(F32)
                kept[part] = value
                normed[part] = (value * rms(value) * gains[1:2, :]).astype(BF16)

            pieces(SEQ_LEN, norm)
            out.start()
            save.start()
        lower[0].wait_recv()
        lower[1].start()
        for copy in cross[1:2]:
            copy.start()
        if high:
            high[0].wait_recv()
            high[1].start()
    for c, ((lower, high), cross) in enumerate(zip(rises, crosses)):
        lower[1].wait_recv()
        for copy in cross[2:]:
            copy.start()
        if high:
            high[1].wait_recv()
            high[2].start()
        if c == 1:
            out.forward()
    for (lower, high), cross in zip(rises, crosses):
        for copy in cross:
            copy.wait()
        for copy in high[2:]:
            copy.wait_recv()
        for copy in lower + high:
            copy.wait_send()
    for copy in keeps:
        copy.wait()
    out.finish()
    save.wait()


class Sum:
    def __init__(self, place, sems, terms, given, result, first, width, scratch, span=None, start=0):
        self.own, self.other, self.from_z, self.to_z, self.final = scratch
        cols = pl.ds(first, width)
        self.loads, self.crosses = [], []
        for index in range(4):
            self.loads.append(pltpu.make_async_copy(terms.at[index, :, cols], self.own.at[index], sems.one()))
            if given is None:
                self.crosses.append(place.copy("y", terms.at[4 + index, :, cols], self.other.at[index], sems.two()))
            else:
                self.loads.append(pltpu.make_async_copy(given.at[index], self.other.at[index], sems.one()))
        self.per = len(self.loads) // 4
        self.rises = [place.copy("up", self.to_z.at[i], self.from_z.at[i], sems.two()) for i in range(3)]
        half = self.final.shape[0] // 2
        there = result.at[:, pl.ds(pl.multiple_of(place.x * (span or width) + start, 128), width)]
        self.leave = pltpu.make_async_copy(self.final.at[place.half(half)], there, sems.one())
        self.swap = place.copy("x", self.final.at[place.half(half, True)], there, sems.two())

    def start(self, step):
        index = 3 - step
        for copy in self.crosses[index : index + 1] + self.loads[index * self.per : (index + 1) * self.per]:
            copy.start()

    def step(self, step):
        index = 3 - step
        for copy in self.loads[index * self.per : (index + 1) * self.per]:
            copy.wait()
        for copy in self.crosses[index : index + 1]:
            copy.wait_recv()
        if step:
            self.rises[step - 1].wait_recv()

        def add(part):
            value = self.own[index, part].astype(F32) + self.other[index, part].astype(F32)
            if step:
                value = value + self.from_z[step - 1, part].astype(F32)
            if step < 3:
                self.to_z[step, part] = value.astype(BF16)
            else:
                self.final[part] = value

        pieces(self.final.shape[0], add)
        if step < 3:
            self.rises[step].start()
        else:
            self.swap.start()
            self.leave.start()

    def finish(self):
        for copy in self.crosses + self.rises:
            copy.wait_send()
        self.leave.wait()
        self.swap.wait()


class SumGiven:
    def __init__(self, place, sems, terms, given, result, first, width, scratch, span, start):
        self.own, self.others, self.to_y, self.from_y, self.final = scratch
        cols = pl.ds(first, width)
        self.loads = [
            pltpu.make_async_copy(terms.at[d * (terms.shape[0] // 2), :, cols], self.own.at[d], sems.one())
            for d in range(2)
        ]
        self.loads += [pltpu.make_async_copy(one, self.others.at[i], sems.one()) for i, one in enumerate(given)]
        self.cross = place.copy("y", self.to_y, self.from_y, sems.two())
        half = self.final.shape[0] // 2
        there = result.at[:, pl.ds(pl.multiple_of(place.x * span + start, 128), width)]
        self.leave = pltpu.make_async_copy(self.final.at[place.half(half)], there, sems.one())
        self.swap = place.copy("x", self.final.at[place.half(half, True)], there, sems.two())

    def start(self):
        for copy in self.loads:
            copy.start()

    def first(self):
        for copy in self.loads:
            copy.wait()

        def add(part):
            for d in (1, 0):
                value = self.own[d, part].astype(F32)
                for i in range(3):
                    value = value + self.others[i, d, part].astype(F32)
                if d:
                    self.to_y[part] = value.astype(BF16)
                else:
                    self.final[part] = value

        pieces(self.final.shape[0], add)
        self.cross.start()

    def second(self):
        self.cross.wait_recv()

        def add(part):
            self.final[part] = self.final[part] + self.from_y[part].astype(F32)

        pieces(self.final.shape[0], add)
        self.swap.start()
        self.leave.start()

    def finish(self):
        self.cross.wait_send()
        self.leave.wait()
        self.swap.wait()


def given_scratch(rows, width):
    return [
        pltpu.VMEM((2, rows, width), BF16),
        pltpu.VMEM((3, 2, rows, width), BF16),
        pltpu.VMEM((rows, width), BF16),
        pltpu.VMEM((rows, width), BF16),
        pltpu.VMEM((rows, width), F32),
    ]


def sum_scratch(rows, width):
    return [pltpu.VMEM((depth, rows, width), BF16) for depth in (4, 4, 3, 3)] + [pltpu.VMEM((rows, width), F32)]


class UpTerms:
    def __init__(self, sems, acts, grads, bufs, over, own, parts):
        self.acts, self.grads, self.bufs = acts, grads, bufs
        self.over, self.own, self.parts = over, own, parts
        self.early = over.shape[2]
        self.left, self.right = sems.some(2), sems.some(2)

    def copies(self, slot, left, right):
        early, rest = self.early, self.bufs.shape[2] - self.early
        return (
            pltpu.make_async_copy(self.bufs.at[slot, :, pl.ds(0, early)], left, self.left(slot)),
            pltpu.make_async_copy(self.bufs.at[slot, :, pl.ds(early, rest)], right, self.right(slot)),
        )

    def wait(self, slot):
        for copy in self.copies(slot, self.own.at[0], self.parts[0].at[0]):
            copy.wait()

    def run(self, start, stop):
        width = self.bufs.shape[1]

        def step(i, carry):
            slot, side, away = i % 2, i // 4, i % 4

            @pl.when(i >= 2)
            def _():
                self.wait(slot)

            cols = pl.ds(pl.multiple_of(i * width, width), width)
            self.bufs[slot] = mm(self.acts[:, cols], self.grads[...], TN, BF16)

            @pl.when(side == 0)
            def _():
                self.copies(slot, self.own.at[away], self.parts[0].at[0])[0].start()

            @pl.when(side == 1)
            def _():
                self.copies(slot, self.over.at[away], self.parts[0].at[0])[0].start()

            for place in range(4):

                @pl.when(away == place)
                def _(place=place):
                    self.copies(slot, self.own.at[0], self.parts[place].at[side])[1].start()

            return carry

        lax.fori_loop(start, stop, step, 0)

    def finish(self):
        self.wait(0)
        self.wait(1)


class OutTerms:
    def __init__(self, sems, hidden, weight, stage, bufs, target):
        self.hidden, self.weight, self.stage, self.bufs, self.target = hidden, weight, stage, bufs, target
        self.loads, self.stores = sems.some(2), sems.some(2)

    def load(self, i):
        return pltpu.make_async_copy(self.weight.at[i], self.stage.at[i % 2], self.loads(i % 2))

    def store(self, i):
        width = self.bufs.shape[2]
        cols = pl.ds(pl.multiple_of(i * width, width), width)
        return pltpu.make_async_copy(self.bufs.at[i % 2], self.target.at[:, cols], self.stores(i % 2))

    def run(self, start, stop):
        def step(i, carry):
            self.load(i).wait()

            @pl.when(i < 7)
            def _():
                self.load(i + 1).start()

            @pl.when(i >= 2)
            def _():
                self.store(i).wait()

            self.bufs[i % 2] = mm(self.hidden[...], self.stage[i % 2], NT)
            self.store(i).start()
            return carry

        lax.fori_loop(start, stop, step, 0)

    def finish(self):
        self.store(6).wait()
        self.store(7).wait()


def norm_back_piece(value, gain, grad):
    scale = rms(value)
    scaled = gain * grad
    inner = jnp.mean(scaled * value, axis=-1, keepdims=True)
    gains = (grad * value * scale).reshape(PIECE // 8, 8, value.shape[1])
    return scale * scaled - value * (scale * scale * scale * inner), jnp.sum(gains, axis=0)


def sum_ffn_kernel(
    hid, early, gate_t, down, given, given1, given2, given3, terms, resid, gains, d_res, ffn_in, d_wide, hidden, w_down,
    gate_sum, down_sum, d_h, d_attn, gain_sum, up_over, up_own, up0, up1, up2, up3, out_terms, *scratch
):
    *scratch, sem = scratch
    place, sems = Place(), Sems(sem)
    rest = hid - early
    down_y = Sum(place, sems, down, given, down_sum, 0, early, scratch[0:5], hid)
    down_z = SumGiven(place, sems, down, (given1, given2, given3), down_sum, early, rest, scratch[5:10], hid, early)
    gate = [
        Sum(place, sems, gate_t, None, gate_sum, 0, early, scratch[10:15], hid),
        Sum(place, sems, gate_t, None, gate_sum, early, rest, scratch[15:20], hid, early),
    ]
    back = QuadSum(place, sems, terms, scratch[20:24])
    value, res, low, acts, ups, up_bufs, hid_v, stage, out_bufs = scratch[24:33]
    quad = Quad(place, sems, low, d_attn)
    up = UpTerms(sems, acts, ups, up_bufs, up_over, up_own, (up0, up1, up2, up3))
    out = OutTerms(sems, hid_v, w_down, stage, out_bufs, out_terms)
    ready = [
        pltpu.make_async_copy(ffn_in, acts, sems.one()),
        pltpu.make_async_copy(d_wide.at[:, pl.ds(hid, hid)], ups, sems.one()),
        pltpu.make_async_copy(hidden, hid_v, sems.one()),
    ]
    fetch = [pltpu.make_async_copy(resid, value, sems.one()), pltpu.make_async_copy(d_res, res, sems.one())]
    save = pltpu.make_async_copy(res, d_h, sems.one())
    place.greet()
    back.start()
    for one in (down_y, *gate):
        one.start(0)
    down_z.start()
    for copy in fetch:
        copy.start()
    for one in (down_y, *gate):
        one.start(1)
    down_y.step(0)
    down_z.first()
    for step in (2, 3):
        for one in (down_y, *gate):
            one.start(step)
    for copy in ready:
        copy.start()
    out.load(0).start()
    back.middle()
    for one in gate:
        one.step(0)
    for copy in fetch + ready:
        copy.wait()
    down_y.step(1)
    up.run(0, 4)
    back.ready()
    gain_sum[...] = jnp.zeros_like(gain_sum)

    def norm(part):
        d_norm, added = norm_back_piece(value[part], gains[1:2, :], back.read(part))
        grad = res[part] + d_norm
        res[part] = grad
        low[part] = grad.astype(BF16)
        gain_sum[...] += added

    pieces(SEQ_LEN, norm)
    quad.start()
    save.start()
    for one in gate:
        one.step(1)
    down_y.step(2)
    up.run(4, 8)
    for one in gate:
        one.step(2)
    down_y.step(3)
    out.run(0, 8)
    down_z.second()
    quad.forward()
    for one in gate:
        one.step(3)
    quad.finish()
    save.wait()
    up.finish()
    out.finish()
    for one in (down_y, down_z, *gate):
        one.finish()


def sum_last_kernel(
    hid, early, up, given, up_rest, given1, given2, given3, out_t, in_t, terms, tokens, gain_rows, d_h, ffn_gains, out_terms, resid, live,
    up_sum, out_sum, q_sum, k_sum, v_sum, f_sum, grad, block_out, gain_sum, *scratch
):
    *scratch, sem = scratch
    place, sems = Place(), Sems(sem)
    sums = []
    for terms_in, given_in, result, first, width, span, start in (
        (up, given, up_sum, 0, early, hid, 0),
        (out_t, None, out_sum, 0, KDIM, None, 0),
        (in_t, None, q_sum, 0, KDIM, None, 0),
        (in_t, None, k_sum, KDIM, KDIM, None, 0),
        (in_t, None, v_sum, 2 * KDIM, KDIM, None, 0),
        (in_t, None, f_sum, 3 * KDIM, 128, None, 0),
    ):
        sums.append(Sum(place, sems, terms_in, given_in, result, first, width, scratch[:5], span, start))
        scratch = scratch[5:]
    up_z = SumGiven(place, sems, up_rest, (given1, given2, given3), up_sum, 0, hid - early, scratch[:5], hid, early)
    scratch = scratch[5:]
    back = QuadSum(place, sems, terms, scratch[0:4])
    ahead = QuadSum(place, sems, out_terms, scratch[4:8])
    value, res, kept, shown, gains, parts, met, crossed, risen, rising, last, swapped = scratch[8:]
    leave = Leave(place, sems, res, grad)
    leave_out = Leave(place, sems, shown, block_out)
    fetch = [pltpu.make_async_copy(tokens, value, sems.one()), pltpu.make_async_copy(d_h, res, sems.one())]
    fetch.append(pltpu.make_async_copy(resid, kept, sems.one()))
    meet = place.copy("core", parts, met, sems.two())
    cross = place.copy("y", parts.at[pl.ds(4, 4)], crossed, sems.two())
    rise = [place.copy("up", rising.at[i], risen.at[i], sems.two()) for i in range(3)]
    swap = place.copy("x", last.at[1 - place.x], swapped, sems.two())
    place.greet()
    back.start()
    for one in sums:
        one.start(0)
    up_z.start()
    for copy in fetch:
        copy.start()
    for one in sums:
        one.start(1)
    ahead.start()
    sums[0].step(0)
    up_z.first()
    for one in sums:
        one.start(2)
    back.middle()
    for one in sums[1:]:
        one.step(0)
    for copy in fetch:
        copy.wait()
    gains[...] = jnp.zeros_like(gains)
    back.ready()

    def norm(part):
        d_norm, added = norm_back_piece(value[part].astype(F32), gain_rows[0:1, :], back.read(part))
        res[part] = res[part] + d_norm
        gains[...] += added

    pieces(SEQ_LEN, norm)
    leave.start()
    width = res.shape[1] // 8
    parts[...] = jnp.zeros_like(parts)
    for row, source in enumerate((gains[...], ffn_gains[...])):
        summed = jnp.sum(source, axis=0, keepdims=True)
        for index in range(8):
            parts[index, row : row + 1, :] = summed[:, index * width : (index + 1) * width]
    meet.start()
    sums[0].step(1)
    meet.wait()
    parts[...] = parts[...] + met[...]
    cross.start()
    for one in sums:
        one.start(3)
    for one in sums[1:]:
        one.step(1)
    ahead.middle()
    up_z.second()
    for one in sums:
        one.step(2)
    cross.wait()
    rising[0] = parts[3] + crossed[3]
    rise[0].start()
    ahead.ready()

    def show(part):
        shown[part] = (live[part, :1] * (kept[part] + ahead.read(part))).astype(BF16)

    pieces(SEQ_LEN, show)
    leave_out.start()
    for one in sums:
        one.step(3)
    for step in (1, 2):
        rise[step - 1].wait_recv()
        rising[step] = parts[3 - step] + crossed[3 - step] + risen[step - 1]
        rise[step].start()
    rise[2].wait_recv()
    total = parts[0] + crossed[0] + risen[2]
    last[0] = total[:, : width // 2]
    last[1] = total[:, width // 2 :]
    swap.start()
    swap.wait()
    gain_sum[...] = last[place.x] + swapped[...]
    for copy in rise:
        copy.wait_send()
    leave.finish()
    leave_out.finish()
    up_z.finish()
    for one in sums:
        one.finish()


def call(kernel, name, ident, inputs, specs, outputs, out_specs, scratch, sems):
    return pl.pallas_call(
        kernel,
        in_specs=specs,
        out_specs=out_specs,
        out_shape=[jax.ShapeDtypeStruct(shape, kind) for shape, kind in outputs],
        scratch_shapes=scratch + [DMA((sems,))],
        compiler_params=pltpu.CompilerParams(collective_id=ident, has_side_effects=True, vmem_limit_bytes=60 << 20),
        name=name,
    )(*inputs)


PAD = 128 - SLOTS
EARLY = 896


class Ring:
    def __init__(self, count):
        self.count = count
        self.stages = []
        left, stride = count // 2, count
        while left > 1:
            size = 4 if left % 4 == 0 else 2
            stride //= size
            left //= size
            self.stages.append((stride, size))

    def perm(self, stride, size, shift):
        moves = []
        for source in range(self.count):
            digit = source // stride % size
            moves.append((source, source + ((digit + shift) % size - digit) * stride))
        return moves

    def send(self, value, stage, shift):
        stride, size = stage
        return lax.ppermute(value, "dp", self.perm(stride, size, shift % size))

    def swap(self, value):
        return lax.ppermute(value, "dp", self.perm(1, 2, 1))

    def digit(self, stage):
        return lax.axis_index("dp") // stage[0] % stage[1]

    def gather(self, block):
        blocks = [block]
        for stage in self.stages:
            more = list(blocks)
            for shift in range(1, stage[1]):
                more += [self.send(one, stage, -shift) for one in blocks]
            blocks = more
        return blocks

    def scatter(self, make):
        def level(depth, offset, width):
            if depth == len(self.stages):
                return lambda inner: make(offset + inner)
            return None

        widths = [1]
        for stage in self.stages:
            widths.append(widths[-1] * stage[1])

        def total(depth, index):
            if depth == len(self.stages):
                return make(index)
            stage = self.stages[depth]
            parts = []
            for shift in range(1, stage[1]):
                sent = total(depth + 1, index + shift * widths[depth]).astype(BF16)
                parts.append(self.send(sent, stage, shift))
            mine = total(depth + 1, index)
            for part in parts:
                mine = mine + part.astype(F32)
            return mine

        return total(0, 0)

    def order(self, value, width, back=False):
        parts = [value[:, i * width : (i + 1) * width] for i in range(self.count // 2)]
        stages = self.stages
        if back:
            parts = self.turn_digits(parts, [s[1] for s in stages[::-1]])
        inner = len(parts)
        for stage in stages:
            size = stage[1]
            inner //= size
            digit = self.digit(stage)
            new = []
            for place in range(len(parts)):
                at = place // inner % size
                base = place - at * inner
                picks = []
                for k in range(size):
                    picks.append(parts[base + ((at - k) % size if back else (at + k) % size) * inner])
                one = picks[0]
                for k in range(1, size):
                    one = jnp.where(digit == k, picks[k], one)
                new.append(one)
            parts = new
        if not back:
            parts = self.turn_digits(parts, [s[1] for s in stages])
        return jnp.concatenate(parts, axis=1)

    def turn_digits(self, parts, sizes):
        count = len(parts)
        out = [None] * count
        for index in range(count):
            rest, digits = index, []
            for size in reversed(sizes):
                digits.append(rest % size)
                rest //= size
            new = 0
            for digit, size in zip(digits, reversed(sizes)):
                new = new * size + digit
            out[new] = parts[index]
        return out


def mm(left, right, dims=NN, kind=F32):
    return lax.dot_general(left, right, dims, preferred_element_type=F32).astype(kind)


def rms(values):
    return lax.rsqrt(jnp.mean(values * values, axis=-1, keepdims=True) + 1e-06)


def norm_back(values, gain, grad):
    scale = rms(values)
    scaled = gain * grad
    inner = jnp.mean(scaled * values, axis=-1, keepdims=True)
    return scale * scaled - values * (scale * scale * scale * inner), jnp.sum(grad * values * scale, axis=0)


def body_by_permutes(
    tokens,
    seq_count,
    valid_len,
    attn_gain,
    ffn_gain,
    q_weight,
    k_weight,
    v_weight,
    forget_weight,
    out_weight,
    gate_weight,
    up_weight,
    down_weight,
    cotangent,
    *,
    ring,
):
    shard = q_weight.shape[0]
    width = 2 * shard
    core = lax.axis_index("head")
    even = lax.axis_index("dp") % 2 == 0
    first = core == 0
    rows = tokens.shape[0]

    def other_core(value):
        return lax.ppermute(value, "head", [(0, 1), (1, 0)])

    def pair_rows(mine, theirs, axis=0):
        return jnp.where(
            even, jnp.concatenate([mine, theirs], axis=axis), jnp.concatenate([theirs, mine], axis=axis)
        )

    def gather(parts):
        left = jnp.concatenate([p[0] for p in parts], axis=1)
        right = jnp.concatenate([p[1] for p in parts], axis=1)
        mine, theirs = jnp.where(even, left, right), jnp.where(even, right, left)
        return jnp.concatenate(ring.gather(pair_rows(mine, ring.swap(theirs))), axis=0)

    def cut(weight):
        half = weight.shape[1] // 2
        return (weight[:, :half], weight[:, half:])

    def quad_gather(mine):
        chips = jnp.concatenate([mine, ring.swap(mine)], axis=0)
        return jnp.concatenate([chips, other_core(chips)], axis=0)

    def quad_scatter(make):
        theirs = other_core(make(slice(2 * SEQ_LEN, 4 * SEQ_LEN)))
        far = make(slice(SEQ_LEN, 2 * SEQ_LEN)) + theirs[SEQ_LEN:]
        near = make(slice(0, SEQ_LEN)) + theirs[:SEQ_LEN]
        return near + ring.swap(far.astype(BF16)).astype(F32)

    def whole_rows(mine):
        theirs = other_core(mine)
        return jnp.where(
            first, jnp.concatenate([mine, theirs], axis=0), jnp.concatenate([theirs, mine], axis=0)
        )

    def weight_sum(act, grads):
        def make(index):
            return mm(act[:, index * width : (index + 1) * width], grads, TN)

        done = ring.scatter(make)
        mine = jnp.where(even, done[:shard], done[shard:])
        theirs = ring.swap(jnp.where(even, done[shard:], done[:shard]))
        return (jnp.where(even, mine, theirs), jnp.where(even, theirs, mine))

    gains = jnp.concatenate(
        [attn_gain[:, None], ffn_gain[:, None], jnp.zeros((shard, PAD - 2), BF16)], axis=1
    )
    w_in = gather([cut(q_weight), cut(k_weight), cut(v_weight), cut(forget_weight), (gains, gains)])
    w_out = gather([cut(out_weight)])
    w_gate = gather([cut(gate_weight)])
    w_up = gather([cut(up_weight)])
    w_down = gather([cut(down_weight)])
    gain_attn = w_in[:, WIDE - PAD].astype(F32)[None, :]
    gain_ffn = w_in[:, WIDE - PAD + 1].astype(F32)[None, :]

    def own(value):
        return ring.order(jnp.where(first, value[:SEQ_LEN], value[SEQ_LEN:]), width)

    places = lax.broadcasted_iota(jnp.int32, (SEQ_LEN, 1), 0)
    length = jnp.where(first, valid_len[0], valid_len[1])
    live = ((core < seq_count[0]) & (places < length)).astype(F32)
    own_tokens = own(tokens)
    d_res = live * own(cotangent)
    d_ffn = quad_gather(d_res.astype(BF16))
    inputs = quad_gather(own_tokens).astype(F32)
    attn_in = (inputs * rms(inputs) * gain_attn).astype(BF16)
    proj = mm(attn_in, w_in)
    mixed, *saved = mixer_forward(proj)
    own_inputs = own_tokens.astype(F32)
    resid = own_inputs + quad_scatter(lambda r: mm(mixed[r], w_out, NT))
    ffn_in = quad_gather((resid * rms(resid) * gain_ffn).astype(BF16))
    gate, up_vals = mm(ffn_in, w_gate), mm(ffn_in, w_up)
    sig = jax.nn.sigmoid(gate)
    hidden = (gate * sig * up_vals).astype(BF16)
    d_hidden = mm(d_ffn, w_down)
    d_gate = (d_hidden * up_vals * (sig * (1.0 + gate * (1.0 - sig)))).astype(BF16)
    d_up = (d_hidden * (gate * sig)).astype(BF16)
    d_ffn_in = quad_scatter(lambda r: mm(d_gate[r], w_gate, NT) + mm(d_up[r], w_up, NT))
    down_sum = weight_sum(d_ffn, hidden)
    gate_sum = weight_sum(ffn_in, d_gate)
    up_sum = weight_sum(ffn_in, d_up)
    ffn = quad_scatter(lambda r: mm(hidden[r], w_down, NT))
    block_out = whole_rows(ring.order((live * (resid + ffn)).astype(BF16), width, back=True))
    d_norm, ffn_gain_part = norm_back(resid, gain_ffn, d_ffn_in)
    d_h = d_res + d_norm
    d_attn = quad_gather(d_h.astype(BF16))
    d_mixed = mm(d_attn, w_out)
    d_proj = mixer_backward(proj, saved, d_mixed)
    d_attn_in = quad_scatter(lambda r: mm(d_proj[r], w_in, NT))
    out_sum = weight_sum(d_attn, mixed)
    in_sum = weight_sum(attn_in, d_proj)
    d_input, attn_gain_part = norm_back(own_inputs, gain_attn, d_attn_in)
    input_grad = whole_rows(ring.order(d_h + d_input, width, back=True))

    both = jnp.stack([attn_gain_part, ffn_gain_part], axis=0)
    both = both + other_core(both)
    both = both.reshape(2, ring.count // 2, width)
    for stage in ring.stages[::-1]:
        size = stage[1]
        both = both.reshape(2, size, -1, width)
        parts = [ring.send(both[:, shift], stage, shift) for shift in range(1, size)]
        both = both[:, 0]
        for part in parts:
            both = both + part
    both = both.reshape(2, 2, shard)
    both = jnp.where(even, both[:, 0], both[:, 1]) + ring.swap(jnp.where(even, both[:, 1], both[:, 0]))

    def columns(pieces, start, stop):
        return jnp.concatenate([p[:, start:stop] for p in pieces], axis=1)

    return (
        block_out,
        input_grad,
        both[0],
        both[1],
        columns(in_sum, 0, KDIM),
        columns(in_sum, KDIM, 2 * KDIM),
        columns(in_sum, 2 * KDIM, 3 * KDIM),
        columns(in_sum, 3 * KDIM, 3 * KDIM + SLOTS),
        columns(out_sum, 0, KDIM),
        jnp.concatenate(gate_sum, axis=1),
        jnp.concatenate(up_sum, axis=1),
        jnp.concatenate(down_sum, axis=1),
    )


def body_by_kernels(
    tokens,
    seq_count,
    valid_len,
    attn_gain,
    ffn_gain,
    q_weight,
    k_weight,
    v_weight,
    forget_weight,
    out_weight,
    gate_weight,
    up_weight,
    down_weight,
    cotangent,
    *,
    ring,
):
    shard, dim = q_weight.shape[0], tokens.shape[1]
    width, hid = 2 * shard, gate_weight.shape[1] // 2
    core = lax.axis_index("head")
    first = core == 0
    up_z, over_y = (lambda value: ring.send(value, ring.stages[0], 1)), (lambda value: ring.send(value, ring.stages[1], 1))
    rows4 = (4, SEQ_LEN, dim)
    blocks = lambda value: value.reshape(-1, width, value.shape[-1])
    flat = lambda value: value.reshape(-1, value.shape[-1])
    half = dim // 2

    gains = jnp.concatenate([attn_gain[:, None], ffn_gain[:, None], jnp.zeros((shard, PAD - 2), BF16)], axis=1)
    small = jnp.concatenate([forget_weight[:, :SLOTS], gains, forget_weight[:, SLOTS:], gains], axis=1)
    places = lax.broadcasted_iota(jnp.int32, (SEQ_LEN, 128), 0)
    length = jnp.where(first, valid_len[0], valid_len[1])
    live = ((core < seq_count[0]) & (places < length)).astype(F32)
    row = (SEQ_LEN, dim)
    vmem = lambda shape, kind=F32: pltpu.VMEM(shape, kind)
    w_in, w_out, part0, own, attn_in, d_res, d_ffn, gain_rows = call(
        gather_first_kernel,
        "gather_first",
        0,
        (tokens, cotangent, live, q_weight, k_weight, v_weight, small, out_weight, gate_weight, up_weight, down_weight),
        [ANY, ANY, VMEM] + [ANY] * 8,
        [
            ((8, width, WIDE), BF16),
            ((8, width, KDIM), BF16),
            ((width, 3 * hid), BF16),
            (row, BF16),
            (rows4, BF16),
            (row, F32),
            (rows4, BF16),
            ((8, dim), F32),
        ],
        [ANY] * 7 + [VMEM],
        [
            vmem((shard, 4 * KDIM + 128 + 3 * hid), BF16),
            vmem(rows4, BF16),
            vmem(rows4, BF16),
            vmem((4, SEQ_LEN, 128)),
            vmem((8, width, 128), BF16),
            vmem(row),
            vmem(row, BF16),
        ],
        240,
    )
    part3, part4 = up_z(part0), over_y(part0)
    w_in, w_out, attn_in, d_ffn = map(flat, (w_in, w_out, attn_in, d_ffn))
    proj = mm(attn_in, w_in)
    mixed, *saved = mixer_forward(proj)
    attn_terms = mm(mixed, w_out, NT).reshape(rows4)
    cut = hid // 256 * 128 + 128
    w_wide, w_down, resid, ffn_in = call(
        functools.partial(gather_ffn_kernel, hid, cut),
        "gather_ffn",
        1,
        (part0, part3, part4, attn_terms, own, gain_rows),
        [ANY] * 5 + [VMEM],
        [((8, width, 2 * hid), BF16), ((8, width, hid), BF16), (row, F32), (rows4, BF16)],
        [ANY] * 4,
        quad_scratch(dim) + [vmem(row), vmem(row, BF16), vmem(row, BF16), vmem((3, width, 3 * hid), BF16)],
        160,
    )
    w_wide, w_down, ffn_in = map(flat, (w_wide, w_down, ffn_in))

    def early_terms(terms, start):
        over = over_y(terms[half:, start : start + EARLY])
        rest = blocks(terms)[:, :, start + EARLY : start + hid]
        given = [ring.send(jnp.stack([rest[d], rest[4 + d]]), ring.stages[0], d) for d in (1, 2, 3)]
        return [blocks(over), *given]

    wide = mm(ffn_in, w_wide)
    gate, up_vals = wide[:, :hid], wide[:, hid:]
    sig = jax.nn.sigmoid(gate)
    hidden = (gate * sig * up_vals).astype(BF16)
    down_terms = mm(d_ffn, hidden, TN, BF16)
    down_given = early_terms(down_terms, 0)
    d_hidden = mm(d_ffn, w_down)
    d_gate = (d_hidden * up_vals * (sig * (1.0 + gate * (1.0 - sig)))).astype(BF16)
    d_up = (d_hidden * (gate * sig)).astype(BF16)
    d_wide = jnp.concatenate([d_gate, d_up], axis=1)
    gate_terms = mm(ffn_in, d_wide[:, :hid], TN, BF16)
    d_ffn_terms = mm(d_wide, w_wide, NT).reshape(rows4)
    rest = hid - EARLY
    gate_sum, down_sum, d_h, d_attn, ffn_gains, up_over, up_own, *up_parts, ffn_terms = call(
        functools.partial(sum_ffn_kernel, hid, EARLY),
        "sum_ffn",
        2,
        (
            blocks(gate_terms),
            blocks(down_terms),
            *down_given,
            d_ffn_terms,
            resid,
            gain_rows,
            d_res,
            ffn_in,
            d_wide,
            hidden,
            blocks(w_down),
        ),
        [ANY] * 8 + [VMEM] + [ANY] * 5,
        [((shard, 2 * hid), F32), ((shard, 2 * hid), F32), (row, F32), (rows4, BF16), ((8, dim), F32)]
        + [((4, width, EARLY), BF16)] * 2
        + [((2, width, rest), BF16)] * 4
        + [((4 * SEQ_LEN, dim), F32)],
        [ANY] * 4 + [VMEM] + [ANY] * 7,
        sum_scratch(width, EARLY)
        + given_scratch(width, rest)
        + sum_scratch(width, EARLY)
        + sum_scratch(width, rest)
        + quad_scratch(dim)
        + [vmem(row), vmem(row), vmem(row, BF16)]
        + [vmem((4 * SEQ_LEN, dim), BF16), vmem((4 * SEQ_LEN, hid), BF16), vmem((2, width, hid), BF16)]
        + [vmem((4 * SEQ_LEN, hid), BF16), vmem((2, width, hid), BF16), vmem((2, 4 * SEQ_LEN, width))],
        220,
    )
    d_attn = flat(d_attn)
    up_given = [over_y(up_over)] + [ring.send(up_parts[d], ring.stages[0], d) for d in (1, 2, 3)]
    d_proj = mixer_backward(proj, saved, mm(d_attn, w_out))
    d_attn_terms = mm(d_proj, w_in, NT).reshape(rows4)
    ffn_terms = ffn_terms.reshape(rows4)
    tail = width // 2
    up_sum, out_sum, q_sum, k_sum, v_sum, f_sum, input_grad, block_out, gain_sums = call(
        functools.partial(sum_last_kernel, hid, EARLY),
        "sum_last",
        3,
        (
            up_own,
            up_given[0],
            up_parts[0],
            *up_given[1:],
            blocks(mm(d_attn, mixed, TN, BF16)),
            blocks(mm(attn_in, d_proj, TN, BF16)),
            d_attn_terms,
            own,
            gain_rows,
            d_h,
            ffn_gains,
            ffn_terms,
            resid,
            live,
        ),
        [ANY] * 10 + [VMEM, ANY, VMEM, ANY, ANY, VMEM],
        [((shard, 2 * hid), F32)]
        + [((shard, 2 * KDIM), F32)] * 4
        + [((shard, 256), F32), ((2 * SEQ_LEN, dim), F32), ((2 * SEQ_LEN, dim), BF16), ((8, tail), F32)],
        [ANY] * 8 + [VMEM],
        sum_scratch(width, EARLY)
        + sum_scratch(width, KDIM) * 4
        + sum_scratch(width, 128)
        + given_scratch(width, rest)
        + quad_scratch(dim) * 2
        + [vmem(row, BF16), vmem(row), vmem(row), vmem(row, BF16), vmem((8, dim))]
        + [vmem((depth, 8, width)) for depth in (8, 8, 4, 3, 3)]
        + [vmem((2, 8, tail)), vmem((8, tail))],
        280,
    )
    f_grad = jnp.concatenate([f_sum[:, :SLOTS], f_sum[:, 128 : 128 + SLOTS]], axis=1)
    return (
        block_out,
        input_grad,
        gain_sums[0],
        gain_sums[1],
        q_sum,
        k_sum,
        v_sum,
        f_grad,
        out_sum,
        gate_sum,
        up_sum,
        down_sum,
    )


def solution(mesh):
    ring = Ring(mesh.shape["dp"])
    body = body_by_kernels if ring.count == 16 else body_by_permutes
    split_one, split_two = P("dp"), P("dp", "head")
    row = P("dp", None)
    in_specs = (row, split_one, split_one, split_one, split_one) + (split_two,) * 8 + (row,)
    out_specs = (row, row, split_one, split_one) + (split_two,) * 8
    return jax.shard_map(
        functools.partial(body, ring=ring),
        mesh=mesh,
        in_specs=in_specs,
        out_specs=out_specs,
        check_vma=False,
    )
```

```python
import functools
import jax
import jax.numpy as jnp
from jax import lax
from jax.experimental import pallas as pl
from jax.experimental.pallas import tpu as pltpu
from jax.sharding import PartitionSpec as P

SLOTS = 64
KDIM = 512
SEQ_LEN = 256
HALF = 128
F32, BF16 = jnp.float32, jnp.bfloat16
WIDE = 3 * KDIM + 128
NT = (((1,), (1,)), ((), ()))
NN = (((1,), (0,)), ((), ()))
TN = (((0,), (0,)), ((), ()))
LEVELS = (8, 16, 32, 64)


def split(value):
    high = value.astype(BF16)
    return high, (value - high.astype(F32)).astype(BF16)


def dot3(left, right, dims):
    one = functools.partial(lax.dot_general, dimension_numbers=dims, preferred_element_type=F32)
    return one(left[0], right[0]) + (one(left[0], right[1]) + one(left[1], right[0]))


def silu_parts(value):
    gate = 1.0 / (1.0 + jnp.exp(-value))
    return gate, value * gate


def level_mask(size):
    row = lax.broadcasted_iota(jnp.int32, (HALF, HALF), 0) // size
    col = lax.broadcasted_iota(jnp.int32, (HALF, HALF), 1) // size
    return (row == col + 1) & (row % 2 == 1)


def band_mask(back):
    row = lax.broadcasted_iota(jnp.int32, (HALF, HALF), 0)
    col = lax.broadcasted_iota(jnp.int32, (HALF, HALF), 1)
    return (row == col + back) & (row // 8 == col // 8)


def down(value, back):
    return value if back == 0 else pltpu.roll(value, back, 0)


def up(value, back):
    return value if back == 0 else pltpu.roll(value, SEQ_LEN - back, 0)


def gates(forget):
    lane = lax.broadcasted_iota(jnp.int32, forget.shape, 1) < SLOTS
    place = lax.broadcasted_iota(jnp.int32, forget.shape, 0)
    forget = jnp.where(lane, forget, 0.0)
    tail = jnp.exp(-jnp.abs(forget))
    log_decay = (jnp.minimum(forget, 0.0) - jnp.log1p(tail)) * 0.125
    log_decay = jnp.where(lane, log_decay, 0.0)
    g = log_decay
    series = 1.0 + g * (1.0 / 7.0)
    for n in (6.0, 5.0, 4.0, 3.0, 2.0):
        series = 1.0 + g * (1.0 / n) * series
    writes = jnp.where(g > -0.3, -g * series, 1.0 - jnp.exp(g))
    writes = jnp.where(lane, writes, 0.0)
    ahead, behind = g, g
    for step in (1, 2, 4):
        ahead = ahead + jnp.where(place % 8 >= step, down(ahead, step), 0.0)
        behind = behind + jnp.where(place % 8 < 8 - step, up(behind, step), 0.0)
    behind = jnp.where(place % 8 < 7, up(behind, 1), 0.0)
    aheads, behinds = {8: ahead}, {8: behind}
    size = 8
    while size < HALF:
        first = ahead.reshape(SEQ_LEN // (2 * size), 2, size, 128)
        last = behind.reshape(SEQ_LEN // (2 * size), 2, size, 128)
        left, right = first[:, 0:1], first[:, 1:2]
        left_sum, right_sum = left[:, :, size - 1 :], right[:, :, size - 1 :]
        ahead = jnp.concatenate([left, right + left_sum], axis=1).reshape(SEQ_LEN, 128)
        behind = jnp.concatenate([last[:, 0:1] + right_sum, last[:, 1:2]], axis=1).reshape(SEQ_LEN, 128)
        size *= 2
        aheads[size], behinds[size] = ahead, behind
    return lane, place, g, writes, aheads, behinds


def near_decays(place, aheads, back):
    ahead = aheads[8]
    gap = jnp.where(place % 8 >= back, ahead - down(ahead, back), 0.0)
    return jnp.where(place % 8 >= back, jnp.exp(gap), 0.0)


def halves(value):
    return value[:HALF], value[HALF:]


def to_slots(blocks, cross, place, writes, aheads, behinds, nears):
    grow = {size: jnp.exp(aheads[size]) for size in LEVELS}
    keep = {size: split(jnp.exp(behinds[size]) * writes) for size in LEVELS}
    outs = []
    for half in range(2):
        here = slice(half * HALF, (half + 1) * HALF)
        block = blocks[half]
        parts = split(block)
        total = None
        for size in LEVELS:
            mask = level_mask(size)
            masked = tuple(jnp.where(mask, part, jnp.zeros_like(part)) for part in parts)
            term = grow[size][here] * dot3(masked, tuple(k[here] for k in keep[size]), NN)
            total = term if total is None else total + term
        for back in range(8):
            near = jnp.sum(jnp.where(band_mask(back), block, 0.0), axis=1, keepdims=True)
            total = total + near * nears[back][here]
        if half == 1:
            far = split((jnp.exp(behinds[HALF]) * writes)[:HALF])
            total = total + jnp.exp(aheads[HALF])[HALF:] * dot3(split(cross), far, NN)
        outs.append(total)
    return jnp.concatenate(outs, axis=0)


def to_tokens(slots, writes, aheads, behinds, nears):
    blocks = []
    for half in range(2):
        here = slice(half * HALF, (half + 1) * HALF)
        total = jnp.zeros((HALF, HALF), F32)
        for size in LEVELS:
            left = split((slots * jnp.exp(aheads[size]))[here])
            right = split((jnp.exp(behinds[size]) * writes)[here])
            total = jnp.where(level_mask(size), dot3(left, right, NT), total)
        for back in range(8):
            near = jnp.sum(slots[here] * nears[back][here], axis=1, keepdims=True)
            total = jnp.where(band_mask(back), near, total)
        blocks.append(total)
    left = split((slots * jnp.exp(aheads[HALF]))[HALF:])
    right = split((jnp.exp(behinds[HALF]) * writes)[:HALF])
    return blocks, dot3(left, right, NT)


def forward_kernel(q_ref, k_ref, v_ref, f_ref, o_ref, p_ref, s_ref, a_ref, b_ref):
    query = split(silu_parts(q_ref[...])[1] * KDIM ** (-0.5))
    keys = split(silu_parts(k_ref[...])[1])
    values = split(v_ref[...])
    lane, place, g, writes, aheads, behinds = gates(f_ref[...])
    nears = [near_decays(place, aheads, back) * down(writes, back) for back in range(8)]
    q0, q1 = tuple(x[:HALF] for x in query), tuple(x[HALF:] for x in query)
    k0, k1 = tuple(x[:HALF] for x in keys), tuple(x[HALF:] for x in keys)
    blocks = (dot3(q0, k0, NT), dot3(q1, k1, NT))
    cross = dot3(q1, k0, NT)
    scores = to_slots(blocks, cross, place, writes, aheads, behinds, nears)
    shown = jnp.where(lane, scores, -1e30)
    weights = jnp.exp(shown - jnp.max(shown, axis=1, keepdims=True))
    weights = jnp.where(lane, weights, 0.0)
    weights = weights / jnp.sum(weights, axis=1, keepdims=True)
    mixes, mix_cross = to_tokens(weights, writes, aheads, behinds, nears)
    v0 = tuple(x[:HALF] for x in values)
    o_ref[:HALF, :] = dot3(split(mixes[0]), v0, NN).astype(o_ref.dtype)
    row = jnp.concatenate([mix_cross, mixes[1]], axis=1)
    o_ref[HALF:, :] = dot3(split(row), values, NN).astype(o_ref.dtype)
    p_ref[...] = weights
    s_ref[...] = scores
    a_ref[:HALF, :] = jnp.concatenate([blocks[0], jnp.zeros_like(cross)], axis=1)
    a_ref[HALF:, :] = jnp.concatenate([cross, blocks[1]], axis=1)
    b_ref[:HALF, :] = jnp.concatenate([mixes[0], jnp.zeros_like(cross)], axis=1)
    b_ref[HALF:, :] = row


def backward_kernel(q_ref, k_ref, v_ref, f_ref, p_ref, s_ref, a_ref, b_ref, d_ref, out_ref):
    lane, place, g, writes, aheads, behinds = gates(f_ref[...])
    spans = [near_decays(place, aheads, back) for back in range(8)]
    nears = [spans[back] * down(writes, back) for back in range(8)]
    weights, scores = p_ref[...], s_ref[...]
    products, mixing = a_ref[...], b_ref[...]
    grad = split(d_ref[...])
    g0, g1 = tuple(x[:HALF] for x in grad), tuple(x[HALF:] for x in grad)
    values = split(v_ref[...])
    v0, v1 = tuple(x[:HALF] for x in values), tuple(x[HALF:] for x in values)
    m_parts = split(mixing)
    dv0 = dot3(tuple(x[:, :HALF] for x in m_parts), grad, TN)
    dv1 = dot3(tuple(x[HALF:, HALF:] for x in m_parts), g1, TN)
    out_ref[:HALF, 2 * KDIM : 3 * KDIM] = dv0.astype(BF16)
    out_ref[HALF:, 2 * KDIM : 3 * KDIM] = dv1.astype(BF16)
    mix_blocks = (dot3(g0, v0, NT), dot3(g1, v1, NT))
    mix_cross = dot3(g1, v0, NT)
    d_weights = to_slots(mix_blocks, mix_cross, place, writes, aheads, behinds, nears)
    inner = jnp.sum(weights * d_weights, axis=1, keepdims=True)
    d_scores = weights * (d_weights - inner)
    d_blocks, d_cross = to_tokens(d_scores, writes, aheads, behinds, nears)
    q_gate, q_act = silu_parts(q_ref[...])
    k_gate, k_act = silu_parts(k_ref[...])
    scale = KDIM ** (-0.5)
    query, keys = split(q_act * scale), split(k_act)
    k0 = tuple(x[:HALF] for x in keys)
    low = split(jnp.concatenate([d_cross, d_blocks[1]], axis=1))
    top = split(d_blocks[0])
    dq = jnp.concatenate([dot3(top, k0, NN), dot3(low, keys, NN)], axis=0)
    first = tuple(jnp.concatenate([t, l[:, :HALF]], axis=0) for t, l in zip(top, low))
    dk0 = dot3(first, query, TN)
    dk1 = dot3(tuple(x[:, HALF:] for x in low), tuple(x[HALF:] for x in query), TN)
    dk = jnp.concatenate([dk0, dk1], axis=0)
    out_ref[:, :KDIM] = (dq * scale * (q_gate + q_act * (1.0 - q_gate))).astype(BF16)
    out_ref[:, KDIM : 2 * KDIM] = (dk * (k_gate + k_act * (1.0 - k_gate))).astype(BF16)
    parts = []
    for half in range(2):
        here = slice(half * HALF, (half + 1) * HALF)
        both = jnp.concatenate([mix_blocks[half], products[here, here]], axis=0)
        both_parts = split(both)
        total = None
        for size in LEVELS:
            mask = level_mask(size)
            mask = jnp.concatenate([mask, mask], axis=0)
            grow = jnp.exp(aheads[size][here])
            right = split(jnp.concatenate([weights[here] * grow, d_scores[here] * grow], axis=0))
            left = tuple(jnp.where(mask, part, jnp.zeros_like(part)) for part in both_parts)
            term = jnp.exp(behinds[size][here]) * dot3(left, right, TN)
            total = term if total is None else total + term
        parts.append(total)
    grow = jnp.exp(aheads[HALF][HALF:])
    left = split(jnp.concatenate([mix_cross, products[HALF:, :HALF]], axis=0))
    right = split(jnp.concatenate([weights[HALF:] * grow, d_scores[HALF:] * grow], axis=0))
    parts[0] = parts[0] + jnp.exp(behinds[HALF][:HALF]) * dot3(left, right, TN)
    reach = jnp.concatenate(parts, axis=0)
    for back in range(8):
        mask = band_mask(back)
        near_mix = jnp.concatenate([jnp.sum(jnp.where(mask, mix_blocks[h], 0.0), axis=1, keepdims=True) for h in range(2)], axis=0)
        near_pro = jnp.concatenate(
            [jnp.sum(jnp.where(mask, products[h * HALF : (h + 1) * HALF, h * HALF : (h + 1) * HALF], 0.0), axis=1, keepdims=True) for h in range(2)],
            axis=0,
        )
        reach = reach + up((near_mix * weights + near_pro * d_scores) * spans[back], back)
    d_sum = weights * d_weights + d_scores * scores - writes * reach
    step = 1
    while step < SEQ_LEN:
        d_sum = d_sum + jnp.where(place < SEQ_LEN - step, up(d_sum, step), 0.0)
        step *= 2
    d_log = d_sum - reach * jnp.exp(g)
    d_forget = d_log * 0.125 / (1.0 + jnp.exp(f_ref[...]))
    out_ref[:, 3 * KDIM :] = jnp.where(lane, d_forget, 0.0).astype(BF16)


def spec(width, column):
    return pl.BlockSpec((SEQ_LEN, width), lambda i: (i, column))


IN_SPECS = [spec(KDIM, 0), spec(KDIM, 1), spec(KDIM, 2), spec(128, 3 * KDIM // 128)]


def mixer_forward(proj):
    rows = proj.shape[0]
    shape = lambda width, kind: jax.ShapeDtypeStruct((rows, width), kind)
    return pl.pallas_call(
        forward_kernel,
        grid=(rows // SEQ_LEN,),
        in_specs=IN_SPECS,
        out_specs=[spec(KDIM, 0), spec(128, 0), spec(128, 0), spec(SEQ_LEN, 0), spec(SEQ_LEN, 0)],
        out_shape=[shape(KDIM, BF16), shape(128, F32), shape(128, F32), shape(SEQ_LEN, F32), shape(SEQ_LEN, F32)],
        compiler_params=pltpu.CompilerParams(vmem_limit_bytes=48 << 20),
        cost_estimate=pl.CostEstimate(flops=rows * 3000000, bytes_accessed=rows * 10000, transcendentals=rows * 3000),
        name="mixer_forward",
    )(proj, proj, proj, proj)


def mixer_backward(proj, saved, grad):
    rows = proj.shape[0]
    weights, scores, products, mixing = saved
    return pl.pallas_call(
        backward_kernel,
        grid=(rows // SEQ_LEN,),
        in_specs=IN_SPECS + [spec(128, 0), spec(128, 0), spec(SEQ_LEN, 0), spec(SEQ_LEN, 0), spec(KDIM, 0)],
        out_specs=spec(WIDE, 0),
        out_shape=jax.ShapeDtypeStruct((rows, WIDE), BF16),
        compiler_params=pltpu.CompilerParams(vmem_limit_bytes=48 << 20),
        cost_estimate=pl.CostEstimate(flops=rows * 9000000, bytes_accessed=rows * 16000, transcendentals=rows * 5000),
        name="mixer_backward",
    )(proj, proj, proj, proj, weights, scores, products, mixing, grad)


MESH = pl.DeviceIdType.MESH
ANY = pl.BlockSpec(memory_space=pl.ANY)
VMEM = pl.BlockSpec(memory_space=pltpu.VMEM)
DMA = pltpu.SemaphoreType.DMA
PIECE = 32


class Place:
    def __init__(self):
        dp = lax.axis_index("dp")
        self.core = lax.axis_index("head")
        self.x, self.y, self.z = dp % 2, dp // 2 % 2, dp // 4
        rest = dp % 4
        self.peers = {
            "x": (dp + 1 - 2 * self.x, self.core),
            "y": (dp + 2 - 4 * self.y, self.core),
            "up": ((self.z + 1) % 4 * 4 + rest, self.core),
            "down": ((self.z + 3) % 4 * 4 + rest, self.core),
            "core": (dp, 1 - self.core),
        }

    def greet(self):
        ready = pltpu.get_barrier_semaphore()
        for peer in self.peers.values():
            pl.semaphore_signal(ready, inc=1, device_id=peer, device_id_type=MESH)
        pl.semaphore_wait(ready, len(self.peers))

    def copy(self, name, source, target, sems):
        return pltpu.make_async_remote_copy(
            src_ref=source,
            dst_ref=target,
            send_sem=sems[0],
            recv_sem=sems[1],
            device_id=self.peers[name],
            device_id_type=MESH,
        )

    def half(self, size, other=False):
        place = 1 - self.x if other else self.x
        return pl.ds(pl.multiple_of(place * size, size), size)

    def columns(self, index, size):
        natural = (self.z + index % 4) % 4 * 2 + (self.y + index // 4) % 2
        return pl.ds(pl.multiple_of(natural * size, size), size)


class Sems:
    def __init__(self, ref):
        self.ref, self.used = ref, 0

    def one(self):
        self.used += 1
        return self.ref.at[self.used - 1]

    def two(self):
        return (self.one(), self.one())

    def some(self, count):
        first = self.used
        self.used += count
        return lambda index: self.ref.at[first + index]


def pieces(rows, work):
    def step(i, carry):
        work(pl.ds(pl.multiple_of(i * PIECE, PIECE), PIECE))
        return carry

    lax.fori_loop(0, rows // PIECE, step, 0)


class Keep:
    def __init__(self, sems, source, target, stage):
        self.load = pltpu.make_async_copy(source, stage, sems.one())
        self.store = pltpu.make_async_copy(stage, target, sems.one())

    def start(self):
        self.load.start()

    def turn(self):
        self.load.wait()
        self.store.start()

    def wait(self):
        self.store.wait()


class Quad:
    def __init__(self, place, sems, source, slots):
        self.near = [] if slots[0] is None else [pltpu.make_async_copy(source, slots[0], sems.one())]
        self.swap = place.copy("x", source, slots[1], sems.two())
        self.core = place.copy("core", source, slots[2], sems.two())
        self.last = place.copy("core", slots[1], slots[3], sems.two())

    def start(self):
        self.swap.start()
        self.core.start()
        for copy in self.near:
            copy.start()

    def forward(self):
        self.swap.wait_recv()
        self.last.start()

    def finish(self):
        self.swap.wait_send()
        self.core.wait()
        self.last.wait()
        for copy in self.near:
            copy.wait()


class QuadSum:
    def __init__(self, place, sems, terms, scratch):
        self.near, self.theirs, self.far, self.swapped = scratch
        self.core = place.copy("core", terms.at[pl.ds(2, 2)], self.theirs, sems.two())
        self.load = pltpu.make_async_copy(terms.at[pl.ds(0, 2)], self.near, sems.one())
        self.swap = place.copy("x", self.far, self.swapped, sems.two())

    def start(self):
        self.core.start()
        self.load.start()

    def middle(self):
        self.core.wait()
        self.load.wait()

        def add(part):
            self.far[part] = (self.near[1, part] + self.theirs[1, part]).astype(BF16)

        pieces(SEQ_LEN, add)
        self.swap.start()

    def ready(self):
        self.swap.wait()

    def read(self, part):
        return self.near[0, part] + self.theirs[0, part] + self.swapped[part].astype(F32)


def quad_scratch(width):
    return [
        pltpu.VMEM((2, SEQ_LEN, width), F32),
        pltpu.VMEM((2, SEQ_LEN, width), F32),
        pltpu.VMEM((SEQ_LEN, width), BF16),
        pltpu.VMEM((SEQ_LEN, width), BF16),
    ]


class Leave:
    def __init__(self, place, sems, source, target):
        rows = pl.ds(pl.multiple_of(place.core * SEQ_LEN, SEQ_LEN), SEQ_LEN)
        width = source.shape[1] // 8
        self.copies, self.here = [], []
        for index in range(8):
            part = source.at[:, pl.ds(index * width, width)]
            there = target.at[rows, place.columns(index, width)]
            self.copies.append(place.copy("core", part, there, sems.two()))
            self.here.append(pltpu.make_async_copy(part, there, sems.one()))

    def start(self):
        for copy in self.copies + self.here:
            copy.start()

    def finish(self):
        for copy in self.copies + self.here:
            copy.wait()


def gather_first_kernel(
    tokens, cot, live, q_w, k_w, v_w, small, out_w, gate_w, up_w, down_w, w_in, w_out, ffn, own, attn_in, d_res, d_ffn, gains,
    stage, seqs, normed, scales, turned, grads, low, sem
):
    place, sems = Place(), Sems(sem)
    shard = q_w.shape[0]
    rows = place.half(shard)
    hid = gate_w.shape[1] // 2
    chunks = [
        (small, 0, 128, w_in, 3 * KDIM, True),
        (q_w, 0, KDIM, w_in, 0, False),
        (k_w, 0, KDIM, w_in, KDIM, False),
        (v_w, 0, KDIM, w_in, 2 * KDIM, False),
        (out_w, 0, KDIM // 2, w_out, 0, True),
        (out_w, KDIM // 2, KDIM // 2, w_out, KDIM // 2, False),
        (gate_w, 0, hid, ffn, 0, False),
        (up_w, 0, hid, ffn, hid, False),
        (down_w, 0, hid, ffn, 2 * hid, False),
    ]
    full = len(chunks) - 3
    swaps, keeps, rises, crosses = [], [], [], []
    used = 0
    for c, (source, offset, width, target, first, y_first) in enumerate(chunks):
        cols = pl.ds(first, width)
        where = target.at[0, rows, cols] if c < full else target.at[rows, cols]
        span = source.shape[1] // 2
        here, there = (pl.ds(pl.multiple_of(at * span + offset, 128), width) for at in (place.x, 1 - place.x))
        swaps.append(place.copy("x", source.at[:, there], where, sems.two()))
        keeps.append(Keep(sems, source.at[:, here], where, stage.at[:, pl.ds(used, width)]))
        used += width
        if c >= full:
            continue

        def block(index, target=target, cols=cols):
            return target.at[index, :, cols]

        rises.append(
            [
                [place.copy("up", block((4 - step) % 4 + 4 * u), block(3 - step + 4 * u), sems.two()) for step in range(3)]
                for u in range(2 if y_first else 1)
            ]
        )
        crosses.append(
            [place.copy("y", block(i), block(4 + i), sems.two()) for i in range(1 if y_first else 4)]
        )
    width = tokens.shape[1] // 8
    mine = pl.ds(pl.multiple_of(place.core * SEQ_LEN, SEQ_LEN), SEQ_LEN)
    far, side, fetch, fetch_cot = [], [], [], []
    for index in range(8):
        part = tokens.at[mine, place.columns(index, width)]
        cols = pl.ds(index * width, width)
        far.append(place.copy("x", part, seqs.at[1, :, cols], sems.two()))
        side.append(place.copy("core", part, seqs.at[2, :, cols], sems.two()))
        fetch.append(pltpu.make_async_copy(part, seqs.at[0, :, cols], sems.one()))
        fetch_cot.append(
            pltpu.make_async_copy(cot.at[mine, place.columns(index, width)], grads.at[:, cols], sems.one())
        )
    last = place.copy("core", seqs.at[1], seqs.at[3], sems.two())
    quad = Quad(place, sems, low, [d_ffn.at[i] for i in range(4)])
    save_own = pltpu.make_async_copy(seqs.at[0], own, sems.one())
    save_res = pltpu.make_async_copy(grads, d_res, sems.one())
    save_in = [pltpu.make_async_copy(normed.at[i], attn_in.at[i], sems.one()) for i in range(4)]
    load_gains = [pltpu.make_async_copy(w_in.at[i, :, pl.ds(3 * KDIM, 128)], turned.at[i], sems.one()) for i in range(8)]
    place.greet()
    for swap, keep in zip(swaps[:full], keeps[:full]):
        swap.start()
        keep.start()
    for copy in far + side + fetch + fetch_cot:
        copy.start()
    for swap, keep in zip(swaps[full:], keeps[full:]):
        swap.start()
        keep.start()
    for keep in keeps:
        keep.turn()
    for c in range(full):
        keeps[c].wait()
        swaps[c].wait_recv()
        rises[c][0][0].start()
        crosses[c][0].start()
    for copy in fetch + fetch_cot:
        copy.wait()
    save_own.start()

    def mask(part):
        value = grads[part] * live[part, :1]
        grads[part] = value
        low[part] = value.astype(BF16)

    pieces(SEQ_LEN, mask)
    save_res.start()
    quad.start()
    for c in range(full):
        if chunks[c][5]:
            crosses[c][0].wait_recv()
            rises[c][1][0].start()

    def measure(slot):
        def one(part):
            scales[slot, part] = jnp.broadcast_to(rms(seqs[slot, part].astype(F32)), (PIECE, 128))

        pieces(SEQ_LEN, one)

    def norm(slot):
        def one(part):
            value = seqs[slot, part].astype(F32) * scales[slot, part, :1] * gains[0:1, :]
            normed[slot, part] = value.astype(BF16)

        pieces(SEQ_LEN, one)
        save_in[slot].start()

    for step in range(3):
        for c in range(full):
            for rise in rises[c]:
                rise[step].wait_recv()
                if step < 2:
                    rise[step + 1].start()
            if not chunks[c][5]:
                crosses[c][3 - step].start()
            if step == 0 and c == 1:
                measure(0)
            if step == 0 and c == full - 1:
                for copy in far:
                    copy.wait_recv()
                last.start()
            if step == 1:
                if c == 0:
                    for copy in side:
                        copy.wait_recv()
                    last.wait_recv()
                if 1 <= c <= 3:
                    measure(c)
            if step == 2:
                if c == 0:
                    for copy in load_gains:
                        copy.start()
                    for index, copy in enumerate(load_gains):
                        copy.wait()
                        flipped = turned[index].astype(F32).T
                        gains[0:8, index * width : (index + 1) * width] = flipped[SLOTS : SLOTS + 8]
                if 1 <= c <= 4:
                    norm(c - 1)
    quad.forward()
    for c in range(full):
        for cross in crosses[c]:
            cross.wait_send()
            if not chunks[c][5]:
                cross.wait_recv()
        for rise in rises[c]:
            for copy in rise:
                copy.wait_send()
    for swap in swaps[:full]:
        swap.wait_send()
    for swap, keep in zip(swaps[full:], keeps[full:]):
        swap.wait()
        keep.wait()
    for copy in far + side + [last]:
        copy.wait_send()
    for copy in save_in + [save_own, save_res]:
        copy.wait()
    quad.finish()


class WideMatmul:
    def __init__(self, sems, acts, weight, stage, bufs, lows, wide, hidden):
        self.acts, self.weight, self.stage, self.bufs, self.lows = acts, weight, stage, bufs, lows
        self.wide, self.hidden = wide, hidden
        self.hid = hidden.shape[1]
        self.count = self.hid // 128
        self.loads = [sems.some(2) for _ in range(2)]
        self.stores = [sems.some(2) for _ in range(3)]

    def columns(self, i, side):
        return pl.ds(pl.multiple_of(side * self.hid + i * 128, 128), 128)

    def fetch(self, i):
        return [
            pltpu.make_async_copy(
                self.weight.at[:, self.columns(i, side)],
                self.stage.at[i % 2, :, pl.ds(side * 128, 128)],
                self.loads[side](i % 2),
            )
            for side in range(2)
        ]

    def leave(self, i):
        copies = [
            pltpu.make_async_copy(
                self.bufs.at[i % 2, :, pl.ds(side * 128, 128)],
                self.wide.at[:, self.columns(i, side)],
                self.stores[side](i % 2),
            )
            for side in range(2)
        ]
        return copies + [
            pltpu.make_async_copy(self.lows.at[i % 2], self.hidden.at[:, self.columns(i, 0)], self.stores[2](i % 2))
        ]

    def begin(self):
        for copy in self.fetch(0):
            copy.start()

    def run(self, start, stop):
        def step(i, carry):
            for copy in self.fetch(i):
                copy.wait()

            @pl.when(i + 1 < self.count)
            def _():
                for copy in self.fetch(i + 1):
                    copy.start()

            @pl.when(i >= 2)
            def _():
                for copy in self.leave(i):
                    copy.wait()

            both = mm(self.acts[...], self.stage[i % 2])
            gate = both[:, :128]
            self.bufs[i % 2] = both
            self.lows[i % 2] = (gate / (1.0 + jnp.exp(-gate)) * both[:, 128:]).astype(BF16)
            for copy in self.leave(i):
                copy.start()
            return carry

        lax.fori_loop(start, stop, step, 0)

    def finish(self):
        for i in (self.count - 2, self.count - 1):
            for copy in self.leave(i):
                copy.wait()


def gather_ffn_kernel(
    hid, cut, b0, b3, b4, terms, tokens, gains, w_wide, w_down, resid, ffn_in, wide, hidden,
    s0, s1, s2, s3, kept, acts, inputs, stage, tiles, bufs, lows, sem
):
    place, sems = Place(), Sems(sem)
    rows = b0.shape[0]
    keeps = []

    def block(target, index, start, width):
        return target.at[pl.ds(index * rows, rows), pl.ds(start, width)]

    def chunk(first, width, target, start, y_first):
        source = pl.ds(first, width)
        at = lambda index: block(target, index, start, width)
        for i, (b, index) in enumerate(((b0, 0), (b3, 3), (b4, 4))):
            keeps.append(Keep(sems, b.at[:, source], at(index), stage.at[i, :, source]))
        low = [
            place.copy("up", b3.at[:, source], at(2), sems.two()),
            place.copy("up", at(2), at(1), sems.two()),
        ]
        if y_first:
            return (
                low,
                [
                    place.copy("up", b4.at[:, source], at(7), sems.two()),
                    place.copy("up", at(7), at(6), sems.two()),
                    place.copy("up", at(6), at(5), sems.two()),
                ],
                [],
            )
        return (
            low,
            [],
            [
                place.copy("y", b3.at[:, source], at(7), sems.two()),
                place.copy("y", at(2), at(6), sems.two()),
                place.copy("y", at(1), at(5), sems.two()),
            ],
        )

    gate = chunk(0, hid, w_wide, 0, False)
    up = chunk(hid, hid, w_wide, hid, False)
    down = chunk(2 * hid, cut, w_down, 0, False)
    rest = chunk(2 * hid + cut, hid - cut, w_down, cut, True)
    total = QuadSum(place, sems, terms, (s0, s1, s2, s3))
    slots = [acts.at[pl.ds(i * SEQ_LEN, SEQ_LEN)] for i in range(4)]
    out = Quad(place, sems, slots[0], [None] + slots[1:])
    fetch = pltpu.make_async_copy(tokens, inputs, sems.one())
    save = pltpu.make_async_copy(kept, resid, sems.one())
    save_in = pltpu.make_async_copy(acts, ffn_in, sems.one())
    matmul = WideMatmul(sems, acts, w_wide, tiles, bufs, lows, wide, hidden)
    place.greet()
    total.start()
    fetch.start()
    for low, _, cross in (gate, up):
        low[0].start()
        cross[0].start()
    for copy in keeps:
        copy.start()
    total.middle()
    for copy in keeps:
        copy.turn()
    fetch.wait()
    for low, _, cross in (gate, up):
        low[0].wait_recv()
        low[1].start()
        cross[1].start()
    rest[1][0].start()
    down[0][0].start()
    rest[0][0].start()
    total.ready()

    def norm(part):
        value = total.read(part) + inputs[part].astype(F32)
        kept[part] = value
        acts[part] = (value * rms(value) * gains[1:2, :]).astype(BF16)

    pieces(SEQ_LEN, norm)
    out.start()
    save.start()
    for low, _, cross in (gate, up):
        low[1].wait_recv()
        cross[2].start()
    down[2][0].start()
    rest[1][0].wait_recv()
    rest[1][1].start()
    out.forward()
    down[0][0].wait_recv()
    down[0][1].start()
    down[2][1].start()
    rest[0][0].wait_recv()
    rest[0][1].start()
    out.finish()
    save_in.start()
    for copy in keeps[:6]:
        copy.wait()
    for copy in gate[2] + up[2]:
        copy.wait_recv()
    matmul.begin()
    rest[1][1].wait_recv()
    rest[1][2].start()
    matmul.run(0, 4)
    down[0][1].wait_recv()
    down[2][2].start()
    matmul.run(4, matmul.count)
    for copy in down[2]:
        copy.wait_recv()
    rest[0][1].wait_recv()
    rest[1][2].wait_recv()
    for low, high, cross in (gate, up, down, rest):
        for copy in low + high + cross:
            copy.wait_send()
    for copy in keeps[6:]:
        copy.wait()
    matmul.finish()
    save.wait()
    save_in.wait()


class Sum:
    def __init__(self, place, sems, terms, given, result, first, width, scratch, span=None, start=0):
        self.own, self.other, self.from_z, self.to_z, self.final = scratch
        cols = pl.ds(first, width)
        self.loads, self.crosses = [], []
        for index in range(4):
            self.loads.append(pltpu.make_async_copy(terms.at[index, :, cols], self.own.at[index], sems.one()))
            if given is None:
                self.crosses.append(place.copy("y", terms.at[4 + index, :, cols], self.other.at[index], sems.two()))
            else:
                self.loads.append(pltpu.make_async_copy(given.at[index], self.other.at[index], sems.one()))
        self.per = len(self.loads) // 4
        self.rises = [place.copy("up", self.to_z.at[i], self.from_z.at[i], sems.two()) for i in range(3)]
        half = self.final.shape[0] // 2
        there = result.at[:, pl.ds(pl.multiple_of(place.x * (span or width) + start, 128), width)]
        self.leave = pltpu.make_async_copy(self.final.at[place.half(half)], there, sems.one())
        self.swap = place.copy("x", self.final.at[place.half(half, True)], there, sems.two())

    def start(self, step):
        index = 3 - step
        for copy in self.crosses[index : index + 1] + self.loads[index * self.per : (index + 1) * self.per]:
            copy.start()

    def step(self, step):
        index = 3 - step
        for copy in self.loads[index * self.per : (index + 1) * self.per]:
            copy.wait()
        for copy in self.crosses[index : index + 1]:
            copy.wait_recv()
        if step:
            self.rises[step - 1].wait_recv()

        def add(part):
            value = self.own[index, part].astype(F32) + self.other[index, part].astype(F32)
            if step:
                value = value + self.from_z[step - 1, part].astype(F32)
            if step < 3:
                self.to_z[step, part] = value.astype(BF16)
            else:
                self.final[part] = value

        pieces(self.final.shape[0], add)
        if step < 3:
            self.rises[step].start()
        else:
            self.swap.start()
            self.leave.start()

    def finish(self):
        for copy in self.crosses + self.rises:
            copy.wait_send()
        self.leave.wait()
        self.swap.wait()


class SumGiven:
    def __init__(self, place, sems, terms, given, result, first, width, scratch, span, start):
        self.own, self.others, self.to_y, self.from_y, self.final = scratch
        cols = pl.ds(first, width)
        self.loads = [
            pltpu.make_async_copy(terms.at[d * (terms.shape[0] // 2), :, cols], self.own.at[d], sems.one())
            for d in range(2)
        ]
        self.loads += [pltpu.make_async_copy(one, self.others.at[i], sems.one()) for i, one in enumerate(given)]
        self.cross = place.copy("y", self.to_y, self.from_y, sems.two())
        half = self.final.shape[0] // 2
        there = result.at[:, pl.ds(pl.multiple_of(place.x * span + start, 128), width)]
        self.leave = pltpu.make_async_copy(self.final.at[place.half(half)], there, sems.one())
        self.swap = place.copy("x", self.final.at[place.half(half, True)], there, sems.two())

    def start(self):
        for copy in self.loads:
            copy.start()

    def first(self):
        for copy in self.loads:
            copy.wait()

        def add(part):
            for d in (1, 0):
                value = self.own[d, part].astype(F32)
                for i in range(3):
                    value = value + self.others[i, d, part].astype(F32)
                if d:
                    self.to_y[part] = value.astype(BF16)
                else:
                    self.final[part] = value

        pieces(self.final.shape[0], add)
        self.cross.start()

    def second(self):
        self.cross.wait_recv()

        def add(part):
            self.final[part] = self.final[part] + self.from_y[part].astype(F32)

        pieces(self.final.shape[0], add)
        self.swap.start()
        self.leave.start()

    def finish(self):
        self.cross.wait_send()
        self.leave.wait()
        self.swap.wait()


def given_scratch(rows, width):
    return [
        pltpu.VMEM((2, rows, width), BF16),
        pltpu.VMEM((3, 2, rows, width), BF16),
        pltpu.VMEM((rows, width), BF16),
        pltpu.VMEM((rows, width), BF16),
        pltpu.VMEM((rows, width), F32),
    ]


def sum_scratch(rows, width):
    return [pltpu.VMEM((depth, rows, width), BF16) for depth in (4, 4, 3, 3)] + [pltpu.VMEM((rows, width), F32)]


class UpTerms:
    def __init__(self, sems, acts, grads, bufs, over, own, parts):
        self.acts, self.grads, self.bufs = acts, grads, bufs
        self.over, self.own, self.parts = over, own, parts
        self.early = over.shape[2]
        self.left, self.right = sems.some(2), sems.some(2)

    def copies(self, slot, left, right):
        early, rest = self.early, self.bufs.shape[2] - self.early
        return (
            pltpu.make_async_copy(self.bufs.at[slot, :, pl.ds(0, early)], left, self.left(slot)),
            pltpu.make_async_copy(self.bufs.at[slot, :, pl.ds(early, rest)], right, self.right(slot)),
        )

    def wait(self, slot):
        for copy in self.copies(slot, self.own.at[0], self.parts[0].at[0]):
            copy.wait()

    def run(self, start, stop):
        width = self.bufs.shape[1]

        def step(i, carry):
            slot, side, away = i % 2, i // 4, i % 4

            @pl.when(i >= 2)
            def _():
                self.wait(slot)

            cols = pl.ds(pl.multiple_of(i * width, width), width)
            self.bufs[slot] = mm(self.acts[:, cols], self.grads[...], TN, BF16)

            @pl.when(side == 0)
            def _():
                self.copies(slot, self.own.at[away], self.parts[0].at[0])[0].start()

            @pl.when(side == 1)
            def _():
                self.copies(slot, self.over.at[away], self.parts[0].at[0])[0].start()

            for place in range(4):

                @pl.when(away == place)
                def _(place=place):
                    self.copies(slot, self.own.at[0], self.parts[place].at[side])[1].start()

            return carry

        lax.fori_loop(start, stop, step, 0)

    def finish(self):
        self.wait(0)
        self.wait(1)


class OutTerms:
    def __init__(self, sems, hidden, weight, stage, bufs, target):
        self.hidden, self.weight, self.stage, self.bufs, self.target = hidden, weight, stage, bufs, target
        self.loads, self.stores = sems.some(2), sems.some(2)

    def load(self, i):
        return pltpu.make_async_copy(self.weight.at[i], self.stage.at[i % 2], self.loads(i % 2))

    def store(self, i):
        width = self.bufs.shape[2]
        cols = pl.ds(pl.multiple_of(i * width, width), width)
        return pltpu.make_async_copy(self.bufs.at[i % 2], self.target.at[:, cols], self.stores(i % 2))

    def run(self, start, stop):
        def step(i, carry):
            self.load(i).wait()

            @pl.when(i < 7)
            def _():
                self.load(i + 1).start()

            @pl.when(i >= 2)
            def _():
                self.store(i).wait()

            self.bufs[i % 2] = mm(self.hidden[...], self.stage[i % 2], NT)
            self.store(i).start()
            return carry

        lax.fori_loop(start, stop, step, 0)

    def finish(self):
        self.store(6).wait()
        self.store(7).wait()


def norm_back_piece(value, gain, grad):
    scale = rms(value)
    scaled = gain * grad
    inner = jnp.mean(scaled * value, axis=-1, keepdims=True)
    gains = (grad * value * scale).reshape(PIECE // 8, 8, value.shape[1])
    return scale * scaled - value * (scale * scale * scale * inner), jnp.sum(gains, axis=0)


def sum_ffn_kernel(
    hid, early, gate_t, down, given, given1, given2, given3, terms, resid, gains, d_res, ffn_in, d_wide, hidden, w_down,
    gate_sum, down_sum, d_h, d_attn, gain_sum, up_over, up_own, up0, up1, up2, up3, out_terms, *scratch
):
    *scratch, sem = scratch
    place, sems = Place(), Sems(sem)
    rest = hid - early
    down_y = Sum(place, sems, down, given, down_sum, 0, early, scratch[0:5], hid)
    down_z = SumGiven(place, sems, down, (given1, given2, given3), down_sum, early, rest, scratch[5:10], hid, early)
    gate = [
        Sum(place, sems, gate_t, None, gate_sum, 0, early, scratch[10:15], hid),
        Sum(place, sems, gate_t, None, gate_sum, early, rest, scratch[15:20], hid, early),
    ]
    back = QuadSum(place, sems, terms, scratch[20:24])
    value, res, low, acts, ups, up_bufs, hid_v, stage, out_bufs = scratch[24:33]
    quad = Quad(place, sems, low, [d_attn.at[i] for i in range(4)])
    up = UpTerms(sems, acts, ups, up_bufs, up_over, up_own, (up0, up1, up2, up3))
    out = OutTerms(sems, hid_v, w_down, stage, out_bufs, out_terms)
    ready = [
        pltpu.make_async_copy(ffn_in, acts, sems.one()),
        pltpu.make_async_copy(d_wide.at[:, pl.ds(hid, hid)], ups, sems.one()),
        pltpu.make_async_copy(hidden, hid_v, sems.one()),
    ]
    fetch = [pltpu.make_async_copy(resid, value, sems.one()), pltpu.make_async_copy(d_res, res, sems.one())]
    save = pltpu.make_async_copy(res, d_h, sems.one())
    place.greet()
    back.start()
    for one in (down_y, *gate):
        one.start(0)
    down_z.start()
    for copy in fetch:
        copy.start()
    for one in (down_y, *gate):
        one.start(1)
    down_y.step(0)
    down_z.first()
    for step in (2, 3):
        for one in (down_y, *gate):
            one.start(step)
    for copy in ready:
        copy.start()
    out.load(0).start()
    back.middle()
    for one in gate:
        one.step(0)
    for copy in fetch + ready:
        copy.wait()
    down_y.step(1)
    up.run(0, 4)
    back.ready()
    gain_sum[...] = jnp.zeros_like(gain_sum)

    def norm(part):
        d_norm, added = norm_back_piece(value[part], gains[1:2, :], back.read(part))
        grad = res[part] + d_norm
        res[part] = grad
        low[part] = grad.astype(BF16)
        gain_sum[...] += added

    pieces(SEQ_LEN, norm)
    quad.start()
    save.start()
    for one in gate:
        one.step(1)
    down_y.step(2)
    up.run(4, 8)
    for one in gate:
        one.step(2)
    down_y.step(3)
    out.run(0, 8)
    down_z.second()
    quad.forward()
    for one in gate:
        one.step(3)
    quad.finish()
    save.wait()
    up.finish()
    out.finish()
    for one in (down_y, down_z, *gate):
        one.finish()


def sum_last_kernel(
    hid, early, up, given, up_rest, given1, given2, given3, out_t, in_t, terms, tokens, gain_rows, d_h, ffn_gains, out_terms, resid, live,
    up_sum, out_sum, q_sum, k_sum, v_sum, f_sum, grad, block_out, gain_sum, *scratch
):
    *scratch, sem = scratch
    place, sems = Place(), Sems(sem)
    sums = []
    for terms_in, given_in, result, first, width, span, start in (
        (up, given, up_sum, 0, early, hid, 0),
        (out_t, None, out_sum, 0, KDIM, None, 0),
        (in_t, None, q_sum, 0, KDIM, None, 0),
        (in_t, None, k_sum, KDIM, KDIM, None, 0),
        (in_t, None, v_sum, 2 * KDIM, KDIM, None, 0),
        (in_t, None, f_sum, 3 * KDIM, 128, None, 0),
    ):
        sums.append(Sum(place, sems, terms_in, given_in, result, first, width, scratch[:5], span, start))
        scratch = scratch[5:]
    up_z = SumGiven(place, sems, up_rest, (given1, given2, given3), up_sum, 0, hid - early, scratch[:5], hid, early)
    scratch = scratch[5:]
    back = QuadSum(place, sems, terms, scratch[0:4])
    ahead = QuadSum(place, sems, out_terms, scratch[4:8])
    value, res, kept, shown, gains, parts, met, crossed, risen, rising, last, swapped = scratch[8:]
    leave = Leave(place, sems, res, grad)
    leave_out = Leave(place, sems, shown, block_out)
    fetch = [pltpu.make_async_copy(tokens, value, sems.one()), pltpu.make_async_copy(d_h, res, sems.one())]
    fetch.append(pltpu.make_async_copy(resid, kept, sems.one()))
    meet = place.copy("core", parts, met, sems.two())
    cross = place.copy("y", parts.at[pl.ds(4, 4)], crossed, sems.two())
    rise = [place.copy("up", rising.at[i], risen.at[i], sems.two()) for i in range(3)]
    swap = place.copy("x", last.at[1 - place.x], swapped, sems.two())
    place.greet()
    back.start()
    for one in sums:
        one.start(0)
    up_z.start()
    for copy in fetch:
        copy.start()
    for one in sums:
        one.start(1)
    ahead.start()
    sums[0].step(0)
    up_z.first()
    for one in sums:
        one.start(2)
    back.middle()
    for one in sums[1:]:
        one.step(0)
    for copy in fetch:
        copy.wait()
    gains[...] = jnp.zeros_like(gains)
    back.ready()

    def norm(part):
        d_norm, added = norm_back_piece(value[part].astype(F32), gain_rows[0:1, :], back.read(part))
        res[part] = res[part] + d_norm
        gains[...] += added

    pieces(SEQ_LEN, norm)
    leave.start()
    width = res.shape[1] // 8
    parts[...] = jnp.zeros_like(parts)
    for row, source in enumerate((gains[...], ffn_gains[...])):
        summed = jnp.sum(source, axis=0, keepdims=True)
        for index in range(8):
            parts[index, row : row + 1, :] = summed[:, index * width : (index + 1) * width]
    meet.start()
    sums[0].step(1)
    meet.wait()
    parts[...] = parts[...] + met[...]
    cross.start()
    for one in sums:
        one.start(3)
    for one in sums[1:]:
        one.step(1)
    ahead.middle()
    up_z.second()
    for one in sums:
        one.step(2)
    cross.wait()
    rising[0] = parts[3] + crossed[3]
    rise[0].start()
    ahead.ready()

    def show(part):
        shown[part] = (live[part, :1] * (kept[part] + ahead.read(part))).astype(BF16)

    pieces(SEQ_LEN, show)
    leave_out.start()
    for one in sums:
        one.step(3)
    for step in (1, 2):
        rise[step - 1].wait_recv()
        rising[step] = parts[3 - step] + crossed[3 - step] + risen[step - 1]
        rise[step].start()
    rise[2].wait_recv()
    total = parts[0] + crossed[0] + risen[2]
    last[0] = total[:, : width // 2]
    last[1] = total[:, width // 2 :]
    swap.start()
    swap.wait()
    gain_sum[...] = last[place.x] + swapped[...]
    for copy in rise:
        copy.wait_send()
    leave.finish()
    leave_out.finish()
    up_z.finish()
    for one in sums:
        one.finish()


def call(kernel, name, ident, inputs, specs, outputs, out_specs, scratch, sems):
    return pl.pallas_call(
        kernel,
        in_specs=specs,
        out_specs=out_specs,
        out_shape=[jax.ShapeDtypeStruct(shape, kind) for shape, kind in outputs],
        scratch_shapes=scratch + [DMA((sems,))],
        compiler_params=pltpu.CompilerParams(collective_id=ident, has_side_effects=True, vmem_limit_bytes=60 << 20),
        name=name,
    )(*inputs)


PAD = 128 - SLOTS
EARLY = 896


class Ring:
    def __init__(self, count):
        self.count = count
        self.stages = []
        left, stride = count // 2, count
        while left > 1:
            size = 4 if left % 4 == 0 else 2
            stride //= size
            left //= size
            self.stages.append((stride, size))

    def perm(self, stride, size, shift):
        moves = []
        for source in range(self.count):
            digit = source // stride % size
            moves.append((source, source + ((digit + shift) % size - digit) * stride))
        return moves

    def send(self, value, stage, shift):
        stride, size = stage
        return lax.ppermute(value, "dp", self.perm(stride, size, shift % size))

    def swap(self, value):
        return lax.ppermute(value, "dp", self.perm(1, 2, 1))

    def digit(self, stage):
        return lax.axis_index("dp") // stage[0] % stage[1]

    def gather(self, block):
        blocks = [block]
        for stage in self.stages:
            more = list(blocks)
            for shift in range(1, stage[1]):
                more += [self.send(one, stage, -shift) for one in blocks]
            blocks = more
        return blocks

    def scatter(self, make):
        def level(depth, offset, width):
            if depth == len(self.stages):
                return lambda inner: make(offset + inner)
            return None

        widths = [1]
        for stage in self.stages:
            widths.append(widths[-1] * stage[1])

        def total(depth, index):
            if depth == len(self.stages):
                return make(index)
            stage = self.stages[depth]
            parts = []
            for shift in range(1, stage[1]):
                sent = total(depth + 1, index + shift * widths[depth]).astype(BF16)
                parts.append(self.send(sent, stage, shift))
            mine = total(depth + 1, index)
            for part in parts:
                mine = mine + part.astype(F32)
            return mine

        return total(0, 0)

    def order(self, value, width, back=False):
        parts = [value[:, i * width : (i + 1) * width] for i in range(self.count // 2)]
        stages = self.stages
        if back:
            parts = self.turn_digits(parts, [s[1] for s in stages[::-1]])
        inner = len(parts)
        for stage in stages:
            size = stage[1]
            inner //= size
            digit = self.digit(stage)
            new = []
            for place in range(len(parts)):
                at = place // inner % size
                base = place - at * inner
                picks = []
                for k in range(size):
                    picks.append(parts[base + ((at - k) % size if back else (at + k) % size) * inner])
                one = picks[0]
                for k in range(1, size):
                    one = jnp.where(digit == k, picks[k], one)
                new.append(one)
            parts = new
        if not back:
            parts = self.turn_digits(parts, [s[1] for s in stages])
        return jnp.concatenate(parts, axis=1)

    def turn_digits(self, parts, sizes):
        count = len(parts)
        out = [None] * count
        for index in range(count):
            rest, digits = index, []
            for size in reversed(sizes):
                digits.append(rest % size)
                rest //= size
            new = 0
            for digit, size in zip(digits, reversed(sizes)):
                new = new * size + digit
            out[new] = parts[index]
        return out


def mm(left, right, dims=NN, kind=F32):
    return lax.dot_general(left, right, dims, preferred_element_type=F32).astype(kind)


def rms(values):
    return lax.rsqrt(jnp.mean(values * values, axis=-1, keepdims=True) + 1e-06)


def norm_back(values, gain, grad):
    scale = rms(values)
    scaled = gain * grad
    inner = jnp.mean(scaled * values, axis=-1, keepdims=True)
    return scale * scaled - values * (scale * scale * scale * inner), jnp.sum(grad * values * scale, axis=0)


def body_by_permutes(
    tokens,
    seq_count,
    valid_len,
    attn_gain,
    ffn_gain,
    q_weight,
    k_weight,
    v_weight,
    forget_weight,
    out_weight,
    gate_weight,
    up_weight,
    down_weight,
    cotangent,
    *,
    ring,
):
    shard = q_weight.shape[0]
    width = 2 * shard
    core = lax.axis_index("head")
    even = lax.axis_index("dp") % 2 == 0
    first = core == 0
    rows = tokens.shape[0]

    def other_core(value):
        return lax.ppermute(value, "head", [(0, 1), (1, 0)])

    def pair_rows(mine, theirs, axis=0):
        return jnp.where(
            even, jnp.concatenate([mine, theirs], axis=axis), jnp.concatenate([theirs, mine], axis=axis)
        )

    def gather(parts):
        left = jnp.concatenate([p[0] for p in parts], axis=1)
        right = jnp.concatenate([p[1] for p in parts], axis=1)
        mine, theirs = jnp.where(even, left, right), jnp.where(even, right, left)
        return jnp.concatenate(ring.gather(pair_rows(mine, ring.swap(theirs))), axis=0)

    def cut(weight):
        half = weight.shape[1] // 2
        return (weight[:, :half], weight[:, half:])

    def quad_gather(mine):
        chips = jnp.concatenate([mine, ring.swap(mine)], axis=0)
        return jnp.concatenate([chips, other_core(chips)], axis=0)

    def quad_scatter(make):
        theirs = other_core(make(slice(2 * SEQ_LEN, 4 * SEQ_LEN)))
        far = make(slice(SEQ_LEN, 2 * SEQ_LEN)) + theirs[SEQ_LEN:]
        near = make(slice(0, SEQ_LEN)) + theirs[:SEQ_LEN]
        return near + ring.swap(far.astype(BF16)).astype(F32)

    def whole_rows(mine):
        theirs = other_core(mine)
        return jnp.where(
            first, jnp.concatenate([mine, theirs], axis=0), jnp.concatenate([theirs, mine], axis=0)
        )

    def weight_sum(act, grads):
        def make(index):
            return mm(act[:, index * width : (index + 1) * width], grads, TN)

        done = ring.scatter(make)
        mine = jnp.where(even, done[:shard], done[shard:])
        theirs = ring.swap(jnp.where(even, done[shard:], done[:shard]))
        return (jnp.where(even, mine, theirs), jnp.where(even, theirs, mine))

    gains = jnp.concatenate(
        [attn_gain[:, None], ffn_gain[:, None], jnp.zeros((shard, PAD - 2), BF16)], axis=1
    )
    w_in = gather([cut(q_weight), cut(k_weight), cut(v_weight), cut(forget_weight), (gains, gains)])
    w_out = gather([cut(out_weight)])
    w_gate = gather([cut(gate_weight)])
    w_up = gather([cut(up_weight)])
    w_down = gather([cut(down_weight)])
    gain_attn = w_in[:, WIDE - PAD].astype(F32)[None, :]
    gain_ffn = w_in[:, WIDE - PAD + 1].astype(F32)[None, :]

    def own(value):
        return ring.order(jnp.where(first, value[:SEQ_LEN], value[SEQ_LEN:]), width)

    places = lax.broadcasted_iota(jnp.int32, (SEQ_LEN, 1), 0)
    length = jnp.where(first, valid_len[0], valid_len[1])
    live = ((core < seq_count[0]) & (places < length)).astype(F32)
    own_tokens = own(tokens)
    d_res = live * own(cotangent)
    d_ffn = quad_gather(d_res.astype(BF16))
    inputs = quad_gather(own_tokens).astype(F32)
    attn_in = (inputs * rms(inputs) * gain_attn).astype(BF16)
    proj = mm(attn_in, w_in)
    mixed, *saved = mixer_forward(proj)
    own_inputs = own_tokens.astype(F32)
    resid = own_inputs + quad_scatter(lambda r: mm(mixed[r], w_out, NT))
    ffn_in = quad_gather((resid * rms(resid) * gain_ffn).astype(BF16))
    gate, up_vals = mm(ffn_in, w_gate), mm(ffn_in, w_up)
    sig = jax.nn.sigmoid(gate)
    hidden = (gate * sig * up_vals).astype(BF16)
    d_hidden = mm(d_ffn, w_down)
    d_gate = (d_hidden * up_vals * (sig * (1.0 + gate * (1.0 - sig)))).astype(BF16)
    d_up = (d_hidden * (gate * sig)).astype(BF16)
    d_ffn_in = quad_scatter(lambda r: mm(d_gate[r], w_gate, NT) + mm(d_up[r], w_up, NT))
    down_sum = weight_sum(d_ffn, hidden)
    gate_sum = weight_sum(ffn_in, d_gate)
    up_sum = weight_sum(ffn_in, d_up)
    ffn = quad_scatter(lambda r: mm(hidden[r], w_down, NT))
    block_out = whole_rows(ring.order((live * (resid + ffn)).astype(BF16), width, back=True))
    d_norm, ffn_gain_part = norm_back(resid, gain_ffn, d_ffn_in)
    d_h = d_res + d_norm
    d_attn = quad_gather(d_h.astype(BF16))
    d_mixed = mm(d_attn, w_out)
    d_proj = mixer_backward(proj, saved, d_mixed)
    d_attn_in = quad_scatter(lambda r: mm(d_proj[r], w_in, NT))
    out_sum = weight_sum(d_attn, mixed)
    in_sum = weight_sum(attn_in, d_proj)
    d_input, attn_gain_part = norm_back(own_inputs, gain_attn, d_attn_in)
    input_grad = whole_rows(ring.order(d_h + d_input, width, back=True))

    both = jnp.stack([attn_gain_part, ffn_gain_part], axis=0)
    both = both + other_core(both)
    both = both.reshape(2, ring.count // 2, width)
    for stage in ring.stages[::-1]:
        size = stage[1]
        both = both.reshape(2, size, -1, width)
        parts = [ring.send(both[:, shift], stage, shift) for shift in range(1, size)]
        both = both[:, 0]
        for part in parts:
            both = both + part
    both = both.reshape(2, 2, shard)
    both = jnp.where(even, both[:, 0], both[:, 1]) + ring.swap(jnp.where(even, both[:, 1], both[:, 0]))

    def columns(pieces, start, stop):
        return jnp.concatenate([p[:, start:stop] for p in pieces], axis=1)

    return (
        block_out,
        input_grad,
        both[0],
        both[1],
        columns(in_sum, 0, KDIM),
        columns(in_sum, KDIM, 2 * KDIM),
        columns(in_sum, 2 * KDIM, 3 * KDIM),
        columns(in_sum, 3 * KDIM, 3 * KDIM + SLOTS),
        columns(out_sum, 0, KDIM),
        jnp.concatenate(gate_sum, axis=1),
        jnp.concatenate(up_sum, axis=1),
        jnp.concatenate(down_sum, axis=1),
    )


def body_by_kernels(
    tokens,
    seq_count,
    valid_len,
    attn_gain,
    ffn_gain,
    q_weight,
    k_weight,
    v_weight,
    forget_weight,
    out_weight,
    gate_weight,
    up_weight,
    down_weight,
    cotangent,
    *,
    ring,
):
    shard, dim = q_weight.shape[0], tokens.shape[1]
    width, hid = 2 * shard, gate_weight.shape[1] // 2
    core = lax.axis_index("head")
    first = core == 0
    up_z, over_y = (lambda value: ring.send(value, ring.stages[0], 1)), (lambda value: ring.send(value, ring.stages[1], 1))
    rows4 = (4, SEQ_LEN, dim)
    blocks = lambda value: value.reshape(-1, width, value.shape[-1])
    flat = lambda value: value.reshape(-1, value.shape[-1])
    half = dim // 2

    gains = jnp.concatenate([attn_gain[:, None], ffn_gain[:, None], jnp.zeros((shard, PAD - 2), BF16)], axis=1)
    small = jnp.concatenate([forget_weight[:, :SLOTS], gains, forget_weight[:, SLOTS:], gains], axis=1)
    places = lax.broadcasted_iota(jnp.int32, (SEQ_LEN, 128), 0)
    length = jnp.where(first, valid_len[0], valid_len[1])
    live = ((core < seq_count[0]) & (places < length)).astype(F32)
    row = (SEQ_LEN, dim)
    vmem = lambda shape, kind=F32: pltpu.VMEM(shape, kind)
    w_in, w_out, part0, own, attn_in, d_res, d_ffn, gain_rows = call(
        gather_first_kernel,
        "gather_first",
        0,
        (tokens, cotangent, live, q_weight, k_weight, v_weight, small, out_weight, gate_weight, up_weight, down_weight),
        [ANY, ANY, VMEM] + [ANY] * 8,
        [
            ((8, width, WIDE), BF16),
            ((8, width, KDIM), BF16),
            ((width, 3 * hid), BF16),
            (row, BF16),
            (rows4, BF16),
            (row, F32),
            (rows4, BF16),
            ((8, dim), F32),
        ],
        [ANY] * 7 + [VMEM],
        [
            vmem((shard, 4 * KDIM + 128 + 3 * hid), BF16),
            vmem(rows4, BF16),
            vmem(rows4, BF16),
            vmem((4, SEQ_LEN, 128)),
            vmem((8, width, 128), BF16),
            vmem(row),
            vmem(row, BF16),
        ],
        240,
    )
    part3, part4 = up_z(part0), over_y(part0)
    w_in, w_out, attn_in, d_ffn = map(flat, (w_in, w_out, attn_in, d_ffn))
    proj = mm(attn_in, w_in)
    mixed, *saved = mixer_forward(proj)
    attn_terms = mm(mixed, w_out, NT).reshape(rows4)
    cut = hid // 256 * 128 + 128
    tokens4 = 4 * SEQ_LEN
    w_wide, w_down, resid, ffn_in, wide, hidden = call(
        functools.partial(gather_ffn_kernel, hid, cut),
        "gather_ffn",
        1,
        (part0, part3, part4, attn_terms, own, gain_rows),
        [ANY] * 5 + [VMEM],
        [
            ((dim, 2 * hid), BF16),
            ((dim, hid), BF16),
            (row, F32),
            ((tokens4, dim), BF16),
            ((tokens4, 2 * hid), F32),
            ((tokens4, hid), BF16),
        ],
        [ANY] * 6,
        quad_scratch(dim)
        + [vmem(row), vmem((tokens4, dim), BF16), vmem(row, BF16), vmem((3, width, 3 * hid), BF16)]
        + [vmem((2, dim, 256), BF16), vmem((2, tokens4, 256)), vmem((2, tokens4, 128), BF16)],
        160,
    )

    def early_terms(terms, start):
        over = over_y(terms[half:, start : start + EARLY])
        rest = blocks(terms)[:, :, start + EARLY : start + hid]
        given = [ring.send(jnp.stack([rest[d], rest[4 + d]]), ring.stages[0], d) for d in (1, 2, 3)]
        return [blocks(over), *given]

    gate, up_vals = wide[:, :hid], wide[:, hid:]
    sig = jax.nn.sigmoid(gate)
    down_terms = mm(d_ffn, hidden, TN, BF16)
    down_given = early_terms(down_terms, 0)
    d_hidden = mm(d_ffn, w_down)
    d_gate = (d_hidden * up_vals * (sig * (1.0 + gate * (1.0 - sig)))).astype(BF16)
    d_up = (d_hidden * (gate * sig)).astype(BF16)
    d_wide = jnp.concatenate([d_gate, d_up], axis=1)
    gate_terms = mm(ffn_in, d_wide[:, :hid], TN, BF16)
    d_ffn_terms = mm(d_wide, w_wide, NT).reshape(rows4)
    rest = hid - EARLY
    gate_sum, down_sum, d_h, d_attn, ffn_gains, up_over, up_own, *up_parts, ffn_terms = call(
        functools.partial(sum_ffn_kernel, hid, EARLY),
        "sum_ffn",
        2,
        (
            blocks(gate_terms),
            blocks(down_terms),
            *down_given,
            d_ffn_terms,
            resid,
            gain_rows,
            d_res,
            ffn_in,
            d_wide,
            hidden,
            blocks(w_down),
        ),
        [ANY] * 8 + [VMEM] + [ANY] * 5,
        [((shard, 2 * hid), F32), ((shard, 2 * hid), F32), (row, F32), (rows4, BF16), ((8, dim), F32)]
        + [((4, width, EARLY), BF16)] * 2
        + [((2, width, rest), BF16)] * 4
        + [((4 * SEQ_LEN, dim), F32)],
        [ANY] * 4 + [VMEM] + [ANY] * 7,
        sum_scratch(width, EARLY)
        + given_scratch(width, rest)
        + sum_scratch(width, EARLY)
        + sum_scratch(width, rest)
        + quad_scratch(dim)
        + [vmem(row), vmem(row), vmem(row, BF16)]
        + [vmem((4 * SEQ_LEN, dim), BF16), vmem((4 * SEQ_LEN, hid), BF16), vmem((2, width, hid), BF16)]
        + [vmem((4 * SEQ_LEN, hid), BF16), vmem((2, width, hid), BF16), vmem((2, 4 * SEQ_LEN, width))],
        220,
    )
    d_attn = flat(d_attn)
    up_given = [over_y(up_over)] + [ring.send(up_parts[d], ring.stages[0], d) for d in (1, 2, 3)]
    d_proj = mixer_backward(proj, saved, mm(d_attn, w_out))
    d_attn_terms = mm(d_proj, w_in, NT).reshape(rows4)
    ffn_terms = ffn_terms.reshape(rows4)
    tail = width // 2
    up_sum, out_sum, q_sum, k_sum, v_sum, f_sum, input_grad, block_out, gain_sums = call(
        functools.partial(sum_last_kernel, hid, EARLY),
        "sum_last",
        3,
        (
            up_own,
            up_given[0],
            up_parts[0],
            *up_given[1:],
            blocks(mm(d_attn, mixed, TN, BF16)),
            blocks(mm(attn_in, d_proj, TN, BF16)),
            d_attn_terms,
            own,
            gain_rows,
            d_h,
            ffn_gains,
            ffn_terms,
            resid,
            live,
        ),
        [ANY] * 10 + [VMEM, ANY, VMEM, ANY, ANY, VMEM],
        [((shard, 2 * hid), F32)]
        + [((shard, 2 * KDIM), F32)] * 4
        + [((shard, 256), F32), ((2 * SEQ_LEN, dim), F32), ((2 * SEQ_LEN, dim), BF16), ((8, tail), F32)],
        [ANY] * 8 + [VMEM],
        sum_scratch(width, EARLY)
        + sum_scratch(width, KDIM) * 4
        + sum_scratch(width, 128)
        + given_scratch(width, rest)
        + quad_scratch(dim) * 2
        + [vmem(row, BF16), vmem(row), vmem(row), vmem(row, BF16), vmem((8, dim))]
        + [vmem((depth, 8, width)) for depth in (8, 8, 4, 3, 3)]
        + [vmem((2, 8, tail)), vmem((8, tail))],
        280,
    )
    f_grad = jnp.concatenate([f_sum[:, :SLOTS], f_sum[:, 128 : 128 + SLOTS]], axis=1)
    return (
        block_out,
        input_grad,
        gain_sums[0],
        gain_sums[1],
        q_sum,
        k_sum,
        v_sum,
        f_grad,
        out_sum,
        gate_sum,
        up_sum,
        down_sum,
    )


def solution(mesh):
    ring = Ring(mesh.shape["dp"])
    body = body_by_kernels if ring.count == 16 else body_by_permutes
    split_one, split_two = P("dp"), P("dp", "head")
    row = P("dp", None)
    in_specs = (row, split_one, split_one, split_one, split_one) + (split_two,) * 8 + (row,)
    out_specs = (row, row, split_one, split_one) + (split_two,) * 8
    return jax.shard_map(
        functools.partial(body, ring=ring),
        mesh=mesh,
        in_specs=in_specs,
        out_specs=out_specs,
        check_vma=False,
    )
```

```python
import functools
import jax
import jax.numpy as jnp
from jax import lax
from jax.experimental import pallas as pl
from jax.experimental.pallas import tpu as pltpu
from jax.sharding import PartitionSpec as P

SLOTS = 64
KDIM = 512
SEQ_LEN = 256
HALF = 128
F32, BF16 = jnp.float32, jnp.bfloat16
WIDE = 3 * KDIM + 128
NT = (((1,), (1,)), ((), ()))
NN = (((1,), (0,)), ((), ()))
TN = (((0,), (0,)), ((), ()))
LEVELS = (8, 16, 32, 64)


def split(value):
    high = value.astype(BF16)
    return high, (value - high.astype(F32)).astype(BF16)


def dot3(left, right, dims):
    one = functools.partial(lax.dot_general, dimension_numbers=dims, preferred_element_type=F32)
    return one(left[0], right[0]) + (one(left[0], right[1]) + one(left[1], right[0]))


def silu_parts(value):
    gate = 1.0 / (1.0 + jnp.exp(-value))
    return gate, value * gate


def level_mask(size):
    row = lax.broadcasted_iota(jnp.int32, (HALF, HALF), 0) // size
    col = lax.broadcasted_iota(jnp.int32, (HALF, HALF), 1) // size
    return (row == col + 1) & (row % 2 == 1)


def band_mask(back):
    row = lax.broadcasted_iota(jnp.int32, (HALF, HALF), 0)
    col = lax.broadcasted_iota(jnp.int32, (HALF, HALF), 1)
    return (row == col + back) & (row // 8 == col // 8)


def down(value, back):
    return value if back == 0 else pltpu.roll(value, back, 0)


def up(value, back):
    return value if back == 0 else pltpu.roll(value, SEQ_LEN - back, 0)


def gates(forget):
    lane = lax.broadcasted_iota(jnp.int32, forget.shape, 1) < SLOTS
    place = lax.broadcasted_iota(jnp.int32, forget.shape, 0)
    forget = jnp.where(lane, forget, 0.0)
    tail = jnp.exp(-jnp.abs(forget))
    log_decay = (jnp.minimum(forget, 0.0) - jnp.log1p(tail)) * 0.125
    log_decay = jnp.where(lane, log_decay, 0.0)
    g = log_decay
    series = 1.0 + g * (1.0 / 7.0)
    for n in (6.0, 5.0, 4.0, 3.0, 2.0):
        series = 1.0 + g * (1.0 / n) * series
    writes = jnp.where(g > -0.3, -g * series, 1.0 - jnp.exp(g))
    writes = jnp.where(lane, writes, 0.0)
    ahead, behind = g, g
    for step in (1, 2, 4):
        ahead = ahead + jnp.where(place % 8 >= step, down(ahead, step), 0.0)
        behind = behind + jnp.where(place % 8 < 8 - step, up(behind, step), 0.0)
    behind = jnp.where(place % 8 < 7, up(behind, 1), 0.0)
    aheads, behinds = {8: ahead}, {8: behind}
    size = 8
    while size < HALF:
        first = ahead.reshape(SEQ_LEN // (2 * size), 2, size, 128)
        last = behind.reshape(SEQ_LEN // (2 * size), 2, size, 128)
        left, right = first[:, 0:1], first[:, 1:2]
        left_sum, right_sum = left[:, :, size - 1 :], right[:, :, size - 1 :]
        ahead = jnp.concatenate([left, right + left_sum], axis=1).reshape(SEQ_LEN, 128)
        behind = jnp.concatenate([last[:, 0:1] + right_sum, last[:, 1:2]], axis=1).reshape(SEQ_LEN, 128)
        size *= 2
        aheads[size], behinds[size] = ahead, behind
    return lane, place, g, writes, aheads, behinds


def near_decays(place, aheads, back):
    ahead = aheads[8]
    gap = jnp.where(place % 8 >= back, ahead - down(ahead, back), 0.0)
    return jnp.where(place % 8 >= back, jnp.exp(gap), 0.0)


def halves(value):
    return value[:HALF], value[HALF:]


def to_slots(blocks, cross, place, writes, aheads, behinds, nears):
    grow = {size: jnp.exp(aheads[size]) for size in LEVELS}
    keep = {size: split(jnp.exp(behinds[size]) * writes) for size in LEVELS}
    outs = []
    for half in range(2):
        here = slice(half * HALF, (half + 1) * HALF)
        block = blocks[half]
        parts = split(block)
        total = None
        for size in LEVELS:
            mask = level_mask(size)
            masked = tuple(jnp.where(mask, part, jnp.zeros_like(part)) for part in parts)
            term = grow[size][here] * dot3(masked, tuple(k[here] for k in keep[size]), NN)
            total = term if total is None else total + term
        for back in range(8):
            near = jnp.sum(jnp.where(band_mask(back), block, 0.0), axis=1, keepdims=True)
            total = total + near * nears[back][here]
        if half == 1:
            far = split((jnp.exp(behinds[HALF]) * writes)[:HALF])
            total = total + jnp.exp(aheads[HALF])[HALF:] * dot3(split(cross), far, NN)
        outs.append(total)
    return jnp.concatenate(outs, axis=0)


def to_tokens(slots, writes, aheads, behinds, nears):
    blocks = []
    for half in range(2):
        here = slice(half * HALF, (half + 1) * HALF)
        total = jnp.zeros((HALF, HALF), F32)
        for size in LEVELS:
            left = split((slots * jnp.exp(aheads[size]))[here])
            right = split((jnp.exp(behinds[size]) * writes)[here])
            total = jnp.where(level_mask(size), dot3(left, right, NT), total)
        for back in range(8):
            near = jnp.sum(slots[here] * nears[back][here], axis=1, keepdims=True)
            total = jnp.where(band_mask(back), near, total)
        blocks.append(total)
    left = split((slots * jnp.exp(aheads[HALF]))[HALF:])
    right = split((jnp.exp(behinds[HALF]) * writes)[:HALF])
    return blocks, dot3(left, right, NT)


def forward_kernel(q_ref, k_ref, v_ref, f_ref, o_ref, p_ref, s_ref, a_ref, b_ref):
    query = split(silu_parts(q_ref[...])[1] * KDIM ** (-0.5))
    keys = split(silu_parts(k_ref[...])[1])
    values = split(v_ref[...])
    lane, place, g, writes, aheads, behinds = gates(f_ref[...])
    nears = [near_decays(place, aheads, back) * down(writes, back) for back in range(8)]
    q0, q1 = tuple(x[:HALF] for x in query), tuple(x[HALF:] for x in query)
    k0, k1 = tuple(x[:HALF] for x in keys), tuple(x[HALF:] for x in keys)
    blocks = (dot3(q0, k0, NT), dot3(q1, k1, NT))
    cross = dot3(q1, k0, NT)
    scores = to_slots(blocks, cross, place, writes, aheads, behinds, nears)
    shown = jnp.where(lane, scores, -1e30)
    weights = jnp.exp(shown - jnp.max(shown, axis=1, keepdims=True))
    weights = jnp.where(lane, weights, 0.0)
    weights = weights / jnp.sum(weights, axis=1, keepdims=True)
    mixes, mix_cross = to_tokens(weights, writes, aheads, behinds, nears)
    v0 = tuple(x[:HALF] for x in values)
    o_ref[:HALF, :] = dot3(split(mixes[0]), v0, NN).astype(o_ref.dtype)
    row = jnp.concatenate([mix_cross, mixes[1]], axis=1)
    o_ref[HALF:, :] = dot3(split(row), values, NN).astype(o_ref.dtype)
    p_ref[...] = weights
    s_ref[...] = scores
    a_ref[:HALF, :] = jnp.concatenate([blocks[0], jnp.zeros_like(cross)], axis=1)
    a_ref[HALF:, :] = jnp.concatenate([cross, blocks[1]], axis=1)
    b_ref[:HALF, :] = jnp.concatenate([mixes[0], jnp.zeros_like(cross)], axis=1)
    b_ref[HALF:, :] = row


def backward_kernel(q_ref, k_ref, v_ref, f_ref, p_ref, s_ref, a_ref, b_ref, d_ref, out_ref):
    lane, place, g, writes, aheads, behinds = gates(f_ref[...])
    spans = [near_decays(place, aheads, back) for back in range(8)]
    nears = [spans[back] * down(writes, back) for back in range(8)]
    weights, scores = p_ref[...], s_ref[...]
    products, mixing = a_ref[...], b_ref[...]
    grad = split(d_ref[...])
    g0, g1 = tuple(x[:HALF] for x in grad), tuple(x[HALF:] for x in grad)
    values = split(v_ref[...])
    v0, v1 = tuple(x[:HALF] for x in values), tuple(x[HALF:] for x in values)
    m_parts = split(mixing)
    dv0 = dot3(tuple(x[:, :HALF] for x in m_parts), grad, TN)
    dv1 = dot3(tuple(x[HALF:, HALF:] for x in m_parts), g1, TN)
    out_ref[:HALF, 2 * KDIM : 3 * KDIM] = dv0.astype(BF16)
    out_ref[HALF:, 2 * KDIM : 3 * KDIM] = dv1.astype(BF16)
    mix_blocks = (dot3(g0, v0, NT), dot3(g1, v1, NT))
    mix_cross = dot3(g1, v0, NT)
    d_weights = to_slots(mix_blocks, mix_cross, place, writes, aheads, behinds, nears)
    inner = jnp.sum(weights * d_weights, axis=1, keepdims=True)
    d_scores = weights * (d_weights - inner)
    d_blocks, d_cross = to_tokens(d_scores, writes, aheads, behinds, nears)
    q_gate, q_act = silu_parts(q_ref[...])
    k_gate, k_act = silu_parts(k_ref[...])
    scale = KDIM ** (-0.5)
    query, keys = split(q_act * scale), split(k_act)
    k0 = tuple(x[:HALF] for x in keys)
    low = split(jnp.concatenate([d_cross, d_blocks[1]], axis=1))
    top = split(d_blocks[0])
    dq = jnp.concatenate([dot3(top, k0, NN), dot3(low, keys, NN)], axis=0)
    first = tuple(jnp.concatenate([t, l[:, :HALF]], axis=0) for t, l in zip(top, low))
    dk0 = dot3(first, query, TN)
    dk1 = dot3(tuple(x[:, HALF:] for x in low), tuple(x[HALF:] for x in query), TN)
    dk = jnp.concatenate([dk0, dk1], axis=0)
    out_ref[:, :KDIM] = (dq * scale * (q_gate + q_act * (1.0 - q_gate))).astype(BF16)
    out_ref[:, KDIM : 2 * KDIM] = (dk * (k_gate + k_act * (1.0 - k_gate))).astype(BF16)
    parts = []
    for half in range(2):
        here = slice(half * HALF, (half + 1) * HALF)
        both = jnp.concatenate([mix_blocks[half], products[here, here]], axis=0)
        both_parts = split(both)
        total = None
        for size in LEVELS:
            mask = level_mask(size)
            mask = jnp.concatenate([mask, mask], axis=0)
            grow = jnp.exp(aheads[size][here])
            right = split(jnp.concatenate([weights[here] * grow, d_scores[here] * grow], axis=0))
            left = tuple(jnp.where(mask, part, jnp.zeros_like(part)) for part in both_parts)
            term = jnp.exp(behinds[size][here]) * dot3(left, right, TN)
            total = term if total is None else total + term
        parts.append(total)
    grow = jnp.exp(aheads[HALF][HALF:])
    left = split(jnp.concatenate([mix_cross, products[HALF:, :HALF]], axis=0))
    right = split(jnp.concatenate([weights[HALF:] * grow, d_scores[HALF:] * grow], axis=0))
    parts[0] = parts[0] + jnp.exp(behinds[HALF][:HALF]) * dot3(left, right, TN)
    reach = jnp.concatenate(parts, axis=0)
    for back in range(8):
        mask = band_mask(back)
        near_mix = jnp.concatenate([jnp.sum(jnp.where(mask, mix_blocks[h], 0.0), axis=1, keepdims=True) for h in range(2)], axis=0)
        near_pro = jnp.concatenate(
            [jnp.sum(jnp.where(mask, products[h * HALF : (h + 1) * HALF, h * HALF : (h + 1) * HALF], 0.0), axis=1, keepdims=True) for h in range(2)],
            axis=0,
        )
        reach = reach + up((near_mix * weights + near_pro * d_scores) * spans[back], back)
    d_sum = weights * d_weights + d_scores * scores - writes * reach
    step = 1
    while step < SEQ_LEN:
        d_sum = d_sum + jnp.where(place < SEQ_LEN - step, up(d_sum, step), 0.0)
        step *= 2
    d_log = d_sum - reach * jnp.exp(g)
    d_forget = d_log * 0.125 / (1.0 + jnp.exp(f_ref[...]))
    out_ref[:, 3 * KDIM :] = jnp.where(lane, d_forget, 0.0).astype(BF16)


def spec(width, column):
    return pl.BlockSpec((SEQ_LEN, width), lambda i: (i, column))


IN_SPECS = [spec(KDIM, 0), spec(KDIM, 1), spec(KDIM, 2), spec(128, 3 * KDIM // 128)]


def mixer_forward(proj):
    rows = proj.shape[0]
    shape = lambda width, kind: jax.ShapeDtypeStruct((rows, width), kind)
    return pl.pallas_call(
        forward_kernel,
        grid=(rows // SEQ_LEN,),
        in_specs=IN_SPECS,
        out_specs=[spec(KDIM, 0), spec(128, 0), spec(128, 0), spec(SEQ_LEN, 0), spec(SEQ_LEN, 0)],
        out_shape=[shape(KDIM, BF16), shape(128, F32), shape(128, F32), shape(SEQ_LEN, F32), shape(SEQ_LEN, F32)],
        compiler_params=pltpu.CompilerParams(vmem_limit_bytes=48 << 20),
        cost_estimate=pl.CostEstimate(flops=rows * 3000000, bytes_accessed=rows * 10000, transcendentals=rows * 3000),
        name="mixer_forward",
    )(proj, proj, proj, proj)


def mixer_backward(proj, saved, grad):
    rows = proj.shape[0]
    weights, scores, products, mixing = saved
    return pl.pallas_call(
        backward_kernel,
        grid=(rows // SEQ_LEN,),
        in_specs=IN_SPECS + [spec(128, 0), spec(128, 0), spec(SEQ_LEN, 0), spec(SEQ_LEN, 0), spec(KDIM, 0)],
        out_specs=spec(WIDE, 0),
        out_shape=jax.ShapeDtypeStruct((rows, WIDE), BF16),
        compiler_params=pltpu.CompilerParams(vmem_limit_bytes=48 << 20),
        cost_estimate=pl.CostEstimate(flops=rows * 9000000, bytes_accessed=rows * 16000, transcendentals=rows * 5000),
        name="mixer_backward",
    )(proj, proj, proj, proj, weights, scores, products, mixing, grad)


MESH = pl.DeviceIdType.MESH
ANY = pl.BlockSpec(memory_space=pl.ANY)
VMEM = pl.BlockSpec(memory_space=pltpu.VMEM)
SMEM = pl.BlockSpec(memory_space=pltpu.SMEM)
DMA = pltpu.SemaphoreType.DMA
PIECE = 32


class Place:
    def __init__(self, all_z=False):
        dp = lax.axis_index("dp")
        self.core = lax.axis_index("head")
        self.x, self.y, self.z = dp % 2, dp // 2 % 2, dp // 4
        rest = dp % 4
        self.peers = {
            "x": (dp + 1 - 2 * self.x, self.core),
            "y": (dp + 2 - 4 * self.y, self.core),
            "up": ((self.z + 1) % 4 * 4 + rest, self.core),
            "down": ((self.z + 3) % 4 * 4 + rest, self.core),
            "core": (dp, 1 - self.core),
        }
        if all_z:
            self.peers["two"] = ((self.z + 2) % 4 * 4 + rest, self.core)

    def greet(self):
        ready = pltpu.get_barrier_semaphore()
        for peer in self.peers.values():
            pl.semaphore_signal(ready, inc=1, device_id=peer, device_id_type=MESH)
        pl.semaphore_wait(ready, len(self.peers))

    def copy(self, name, source, target, sems):
        return pltpu.make_async_remote_copy(
            src_ref=source,
            dst_ref=target,
            send_sem=sems[0],
            recv_sem=sems[1],
            device_id=self.peers[name],
            device_id_type=MESH,
        )

    def half(self, size, other=False):
        place = 1 - self.x if other else self.x
        return pl.ds(pl.multiple_of(place * size, size), size)

    def columns(self, index, size):
        natural = (self.z + index % 4) % 4 * 2 + (self.y + index // 4) % 2
        return pl.ds(pl.multiple_of(natural * size, size), size)


class Sems:
    def __init__(self, ref):
        self.ref, self.used = ref, 0

    def one(self):
        self.used += 1
        return self.ref.at[self.used - 1]

    def two(self):
        return (self.one(), self.one())

    def some(self, count):
        first = self.used
        self.used += count
        return lambda index: self.ref.at[first + index]


def pieces(rows, work):
    def step(i, carry):
        work(pl.ds(pl.multiple_of(i * PIECE, PIECE), PIECE))
        return carry

    lax.fori_loop(0, rows // PIECE, step, 0)


class Keep:
    def __init__(self, sems, source, target, stage):
        self.load = pltpu.make_async_copy(source, stage, sems.one())
        self.store = pltpu.make_async_copy(stage, target, sems.one())

    def start(self):
        self.load.start()

    def turn(self):
        self.load.wait()
        self.store.start()

    def wait(self):
        self.store.wait()


class Quad:
    def __init__(self, place, sems, source, slots):
        self.near = [] if slots[0] is None else [pltpu.make_async_copy(source, slots[0], sems.one())]
        self.swap = place.copy("x", source, slots[1], sems.two())
        self.core = place.copy("core", source, slots[2], sems.two())
        self.last = place.copy("core", slots[1], slots[3], sems.two())

    def start(self):
        self.swap.start()
        self.core.start()
        for copy in self.near:
            copy.start()

    def forward(self):
        self.swap.wait_recv()
        self.last.start()

    def finish(self):
        self.swap.wait_send()
        self.core.wait()
        self.last.wait()
        for copy in self.near:
            copy.wait()


class QuadSum:
    def __init__(self, place, sems, terms, scratch):
        self.near, self.theirs, self.far, self.swapped = scratch
        self.core = place.copy("core", terms.at[pl.ds(2, 2)], self.theirs, sems.two())
        self.load = pltpu.make_async_copy(terms.at[pl.ds(0, 2)], self.near, sems.one())
        self.swap = place.copy("x", self.far, self.swapped, sems.two())

    def start(self):
        self.core.start()
        self.load.start()

    def middle(self):
        self.core.wait()
        self.load.wait()

        def add(part):
            self.far[part] = (self.near[1, part] + self.theirs[1, part]).astype(BF16)

        pieces(SEQ_LEN, add)
        self.swap.start()

    def ready(self):
        self.swap.wait()

    def read(self, part):
        return self.near[0, part] + self.theirs[0, part] + self.swapped[part].astype(F32)


def live_rows(place, seq_count, valid_len, part):
    rows = lax.broadcasted_iota(jnp.int32, (PIECE, 128), 0) + part.start
    length = jnp.where(place.core == 0, valid_len[0], valid_len[1])
    return ((rows < length) & (place.core < seq_count[0])).astype(F32)[:, :1]


def quad_scratch(width):
    return [
        pltpu.VMEM((2, SEQ_LEN, width), F32),
        pltpu.VMEM((2, SEQ_LEN, width), F32),
        pltpu.VMEM((SEQ_LEN, width), BF16),
        pltpu.VMEM((SEQ_LEN, width), BF16),
    ]


class Leave:
    def __init__(self, place, sems, source, target):
        rows = pl.ds(pl.multiple_of(place.core * SEQ_LEN, SEQ_LEN), SEQ_LEN)
        width = source.shape[1] // 8
        self.copies, self.here = [], []
        for index in range(8):
            part = source.at[:, pl.ds(index * width, width)]
            there = target.at[rows, place.columns(index, width)]
            self.copies.append(place.copy("core", part, there, sems.two()))
            self.here.append(pltpu.make_async_copy(part, there, sems.one()))

    def start(self):
        for copy in self.copies + self.here:
            copy.start()

    def finish(self):
        for copy in self.copies + self.here:
            copy.wait()


def gather_first_kernel(
    tokens, cot, seq_count, valid_len, gain0, gain1, q_w, k_w, v_w, forget_w, out_w, gate_w, up_w, down_w, w_in, w_out, ffn, own, attn_in, d_res, d_ffn, gains,
    stage, seqs, normed, scales, turned, grads, low, small, sem
):
    place, sems = Place(), Sems(sem)
    shard = q_w.shape[0]
    rows = place.half(shard)
    hid = gate_w.shape[1] // 2
    chunks = [
        (small, 0, 128, w_in, 3 * KDIM, True),
        (q_w, 0, KDIM, w_in, 0, False),
        (k_w, 0, KDIM, w_in, KDIM, False),
        (v_w, 0, KDIM, w_in, 2 * KDIM, False),
        (out_w, 0, KDIM // 2, w_out, 0, True),
        (out_w, KDIM // 2, KDIM // 2, w_out, KDIM // 2, False),
        (gate_w, 0, hid, ffn, 0, False),
        (up_w, 0, hid, ffn, hid, False),
        (down_w, 0, hid, ffn, 2 * hid, False),
    ]
    full = len(chunks) - 3
    swaps, keeps, rises, crosses = [], [], [], []
    used = 0
    for c, (source, offset, width, target, first, y_first) in enumerate(chunks):
        cols = pl.ds(first, width)
        where = target.at[0, rows, cols] if c < full else target.at[rows, cols]
        span = source.shape[1] // 2
        here, there = (pl.ds(pl.multiple_of(at * span + offset, 128), width) for at in (place.x, 1 - place.x))
        swaps.append(place.copy("x", source.at[:, there], where, sems.two()))
        keeps.append(Keep(sems, source.at[:, here], where, stage.at[:, pl.ds(used, width)]))
        used += width
        if c >= full:
            continue

        def block(index, target=target, cols=cols):
            return target.at[index, :, cols]

        rises.append(
            [
                [place.copy("up", block((4 - step) % 4 + 4 * u), block(3 - step + 4 * u), sems.two()) for step in range(3)]
                for u in range(2 if y_first else 1)
            ]
        )
        crosses.append(
            [place.copy("y", block(i), block(4 + i), sems.two()) for i in range(1 if y_first else 4)]
        )
    width = tokens.shape[1] // 8
    mine = pl.ds(pl.multiple_of(place.core * SEQ_LEN, SEQ_LEN), SEQ_LEN)
    far, side, fetch, fetch_cot = [], [], [], []
    for index in range(8):
        part = tokens.at[mine, place.columns(index, width)]
        cols = pl.ds(index * width, width)
        far.append(place.copy("x", part, seqs.at[1, :, cols], sems.two()))
        side.append(place.copy("core", part, seqs.at[2, :, cols], sems.two()))
        fetch.append(pltpu.make_async_copy(part, seqs.at[0, :, cols], sems.one()))
        fetch_cot.append(
            pltpu.make_async_copy(cot.at[mine, place.columns(index, width)], grads.at[:, cols], sems.one())
        )
    last = place.copy("core", seqs.at[1], seqs.at[3], sems.two())
    quad = Quad(place, sems, low, [d_ffn.at[i] for i in range(4)])
    save_own = pltpu.make_async_copy(seqs.at[0], own, sems.one())
    save_res = pltpu.make_async_copy(grads, d_res, sems.one())
    save_in = [pltpu.make_async_copy(normed.at[i], attn_in.at[i], sems.one()) for i in range(4)]
    load_gains = [pltpu.make_async_copy(w_in.at[i, :, pl.ds(3 * KDIM, 128)], turned.at[i], sems.one()) for i in range(8)]
    lane = lax.broadcasted_iota(jnp.int32, (shard, 128), 1)
    column = jnp.concatenate([gain0[...].astype(F32).reshape(1, shard), gain1[...].astype(F32).reshape(1, shard)], axis=0)
    column = jnp.concatenate([column, jnp.zeros((6, shard), F32)], axis=0).T
    beside = jnp.where(lane == SLOTS, column[:, 0:1], jnp.where(lane == SLOTS + 1, column[:, 1:2], 0.0))
    heads = forget_w[...].astype(F32)
    small[:, :128] = jnp.where(lane < SLOTS, heads, beside).astype(BF16)
    small[:, 128:] = jnp.where(lane < SLOTS, pltpu.roll(heads, SLOTS, 1), beside).astype(BF16)
    place.greet()
    for swap, keep in zip(swaps[:full], keeps[:full]):
        swap.start()
        keep.start()
    for copy in far + side + fetch + fetch_cot:
        copy.start()
    for swap, keep in zip(swaps[full:], keeps[full:]):
        swap.start()
        keep.start()
    for keep in keeps:
        keep.turn()
    for c in range(full):
        keeps[c].wait()
        swaps[c].wait_recv()
        rises[c][0][0].start()
        crosses[c][0].start()
    for copy in fetch + fetch_cot:
        copy.wait()
    save_own.start()

    def mask(part):
        value = grads[part] * live_rows(place, seq_count, valid_len, part)
        grads[part] = value
        low[part] = value.astype(BF16)

    pieces(SEQ_LEN, mask)
    save_res.start()
    quad.start()
    for c in range(full):
        if chunks[c][5]:
            crosses[c][0].wait_recv()
            rises[c][1][0].start()

    def measure(slot):
        def one(part):
            scales[slot, part] = jnp.broadcast_to(rms(seqs[slot, part].astype(F32)), (PIECE, 128))

        pieces(SEQ_LEN, one)

    def norm(slot):
        def one(part):
            value = seqs[slot, part].astype(F32) * scales[slot, part, :1] * gains[0:1, :]
            normed[slot, part] = value.astype(BF16)

        pieces(SEQ_LEN, one)
        save_in[slot].start()

    for step in range(3):
        for c in range(full):
            for rise in rises[c]:
                rise[step].wait_recv()
                if step < 2:
                    rise[step + 1].start()
            if not chunks[c][5]:
                crosses[c][3 - step].start()
            if step == 0 and c == 1:
                measure(0)
            if step == 0 and c == full - 1:
                for copy in far:
                    copy.wait_recv()
                last.start()
            if step == 1:
                if c == 0:
                    for copy in side:
                        copy.wait_recv()
                    last.wait_recv()
                if 1 <= c <= 3:
                    measure(c)
            if step == 2:
                if c == 0:
                    for copy in load_gains:
                        copy.start()
                    for index, copy in enumerate(load_gains):
                        copy.wait()
                        flipped = turned[index].astype(F32).T
                        gains[0:8, index * width : (index + 1) * width] = flipped[SLOTS : SLOTS + 8]
                if 1 <= c <= 4:
                    norm(c - 1)
    quad.forward()
    for c in range(full):
        for cross in crosses[c]:
            cross.wait_send()
            if not chunks[c][5]:
                cross.wait_recv()
        for rise in rises[c]:
            for copy in rise:
                copy.wait_send()
    for swap in swaps[:full]:
        swap.wait_send()
    for swap, keep in zip(swaps[full:], keeps[full:]):
        swap.wait()
        keep.wait()
    for copy in far + side + [last]:
        copy.wait_send()
    for copy in save_in + [save_own, save_res]:
        copy.wait()
    quad.finish()


class BlockTerms:
    def __init__(self, sems, acts, grads, bufs, over, own, parts):
        self.acts, self.grads, self.bufs = acts, grads, bufs
        self.over, self.own, self.parts = over, own, parts
        self.early = over.shape[2]
        self.left, self.right = sems.some(2), sems.some(2)

    def copies(self, slot, left, right):
        early, rest = self.early, self.bufs.shape[2] - self.early
        return (
            pltpu.make_async_copy(self.bufs.at[slot, :, pl.ds(0, early)], left, self.left(slot)),
            pltpu.make_async_copy(self.bufs.at[slot, :, pl.ds(early, rest)], right, self.right(slot)),
        )

    def wait(self, slot):
        for copy in self.copies(slot, self.own.at[0], self.parts[0].at[0]):
            copy.wait()

    def run(self, start, stop):
        width = self.bufs.shape[1]

        def step(i, carry):
            slot, side, away = i % 2, i // 4, i % 4

            @pl.when(i >= 2)
            def _():
                self.wait(slot)

            cols = pl.ds(pl.multiple_of(i * width, width), width)
            self.bufs[slot] = mm(self.acts[:, cols], self.grads[...], TN, BF16)

            @pl.when(side == 0)
            def _():
                self.copies(slot, self.own.at[away], self.parts[0].at[0])[0].start()

            @pl.when(side == 1)
            def _():
                self.copies(slot, self.over.at[away], self.parts[0].at[0])[0].start()

            for place in range(4):

                @pl.when(away == place)
                def _(place=place):
                    self.copies(slot, self.own.at[0], self.parts[place].at[side])[1].start()

            return carry

        lax.fori_loop(start, stop, step, 0)

    def finish(self):
        self.wait(0)
        self.wait(1)


class WideMatmul:
    def __init__(self, sems, acts, weight, stage, sums, hidden, wide):
        self.acts, self.weight, self.stage, self.sums, self.hidden, self.wide = acts, weight, stage, sums, hidden, wide
        self.hid = hidden.shape[1]
        self.half = acts.shape[1] // 2
        self.count = self.hid // 128
        self.loads = [sems.some(2) for _ in range(2)]
        self.stores = [sems.some(2) for _ in range(2)]

    def columns(self, i, side):
        return pl.ds(pl.multiple_of(side * self.hid + i * 128, 128), 128)

    def fetch(self, i, phase):
        return [
            pltpu.make_async_copy(
                self.weight.at[pl.ds(phase * self.half, self.half), self.columns(i, side)],
                self.stage.at[i % 2, :, pl.ds(side * 128, 128)],
                self.loads[side](i % 2),
            )
            for side in range(2)
        ]

    def leave(self, i):
        return [
            pltpu.make_async_copy(
                self.sums.at[i, :, pl.ds(side * 128, 128)], self.wide.at[:, self.columns(i, side)], self.stores[side](i % 2)
            )
            for side in range(2)
        ]

    def begin(self, phase):
        for copy in self.fetch(0, phase):
            copy.start()

    def run(self, phase, start, stop):
        def step(i, carry):
            for copy in self.fetch(i, phase):
                copy.wait()

            @pl.when(i + 1 < self.count)
            def _():
                for copy in self.fetch(i + 1, phase):
                    copy.start()

            both = mm(self.acts[:, phase * self.half : (phase + 1) * self.half], self.stage[i % 2])
            if phase == 0:
                self.sums[i] = both
                return carry

            @pl.when(i >= 2)
            def _():
                for copy in self.leave(i - 2):
                    copy.wait()

            both = both + self.sums[i]
            self.sums[i] = both
            gate = both[:, :128]
            self.hidden[:, self.columns(i, 0)] = (gate / (1.0 + jnp.exp(-gate)) * both[:, 128:]).astype(BF16)
            for copy in self.leave(i):
                copy.start()
            return carry

        lax.fori_loop(start, stop, step, 0)

    def finish(self):
        for i in (self.count - 2, self.count - 1):
            for copy in self.leave(i):
                copy.wait()


def gather_ffn_kernel(
    hid, cut, b0, b3, b4, terms, tokens, gains, d_ffn,
    w_wide, w_down, resid, ffn_in, wide, hidden, down_over, down_own, down0, down1, down2, down3,
    s0, s1, s2, s3, kept, acts, inputs, stage, tiles, sums, hid_v, cots, bufs, sem
):
    place, sems = Place(), Sems(sem)
    rows = b0.shape[0]
    keeps = []

    def block(target, index, start, width):
        return target.at[pl.ds(index * rows, rows), pl.ds(start, width)]

    def chunk(first, width, target, start, y_first):
        source = pl.ds(first, width)
        at = lambda index: block(target, index, start, width)
        for i, (b, index) in enumerate(((b0, 0), (b3, 3), (b4, 4))):
            keeps.append(Keep(sems, b.at[:, source], at(index), stage.at[i, :, source]))
        low = [
            place.copy("up", b3.at[:, source], at(2), sems.two()),
            place.copy("up", at(2), at(1), sems.two()),
        ]
        if y_first:
            return (
                low,
                [
                    place.copy("up", b4.at[:, source], at(7), sems.two()),
                    place.copy("up", at(7), at(6), sems.two()),
                    place.copy("up", at(6), at(5), sems.two()),
                ],
                [],
            )
        return (
            low,
            [],
            [
                place.copy("y", b3.at[:, source], at(7), sems.two()),
                place.copy("y", at(2), at(6), sems.two()),
                place.copy("y", at(1), at(5), sems.two()),
            ],
        )

    gate = chunk(0, hid, w_wide, 0, False)
    up = chunk(hid, hid, w_wide, hid, False)
    down = chunk(2 * hid, cut, w_down, 0, False)
    rest = chunk(2 * hid + cut, hid - cut, w_down, cut, True)
    total = QuadSum(place, sems, terms, (s0, s1, s2, s3))
    slots = [acts.at[pl.ds(i * SEQ_LEN, SEQ_LEN)] for i in range(4)]
    out = Quad(place, sems, slots[0], [None] + slots[1:])
    fetch = pltpu.make_async_copy(tokens, inputs, sems.one())
    save = pltpu.make_async_copy(kept, resid, sems.one())
    save_in = pltpu.make_async_copy(acts, ffn_in, sems.one())
    save_hidden = pltpu.make_async_copy(hid_v, hidden, sems.one())
    fetch_cots = pltpu.make_async_copy(d_ffn, cots, sems.one())
    matmul = WideMatmul(sems, acts, w_wide, tiles, sums, hid_v, wide)
    grad = BlockTerms(sems, cots, hid_v, bufs, down_over, down_own, (down0, down1, down2, down3))
    place.greet()
    total.start()
    fetch.start()
    for low, _, cross in (gate, up):
        low[0].start()
        cross[0].start()
    for copy in keeps:
        copy.start()
    total.middle()
    for copy in keeps:
        copy.turn()
    fetch.wait()
    for low, _, cross in (gate, up):
        low[0].wait_recv()
        low[1].start()
        cross[1].start()
    rest[1][0].start()
    down[0][0].start()
    rest[0][0].start()
    total.ready()

    def norm(part):
        value = total.read(part) + inputs[part].astype(F32)
        kept[part] = value
        acts[part] = (value * rms(value) * gains[1:2, :]).astype(BF16)

    pieces(SEQ_LEN, norm)
    out.start()
    save.start()
    for low, _, cross in (gate, up):
        low[1].wait_recv()
        cross[2].start()
    down[2][0].start()
    fetch_cots.start()
    rest[1][0].wait_recv()
    rest[1][1].start()
    out.forward()
    for copy in keeps[:6]:
        copy.wait()
    out.finish()
    save_in.start()
    matmul.begin(0)
    matmul.run(0, 0, matmul.count // 2)
    down[0][0].wait_recv()
    down[0][1].start()
    down[2][1].start()
    matmul.run(0, matmul.count // 2, matmul.count)
    rest[0][0].wait_recv()
    rest[0][1].start()
    for copy in gate[2] + up[2]:
        copy.wait_recv()
    rest[1][1].wait_recv()
    rest[1][2].start()
    matmul.begin(1)
    matmul.run(1, 0, matmul.count // 2)
    down[0][1].wait_recv()
    down[2][2].start()
    matmul.run(1, matmul.count // 2, matmul.count)
    save_hidden.start()
    fetch_cots.wait()
    grad.run(0, 8)
    for copy in down[2]:
        copy.wait_recv()
    rest[0][1].wait_recv()
    rest[1][2].wait_recv()
    for low, high, cross in (gate, up, down, rest):
        for copy in low + high + cross:
            copy.wait_send()
    for copy in keeps[6:]:
        copy.wait()
    matmul.finish()
    grad.finish()
    save.wait()
    save_in.wait()
    save_hidden.wait()


class Sum:
    def __init__(self, place, sems, terms, given, result, first, width, scratch, span=None, start=0):
        self.own, self.other, self.from_z, self.to_z, self.final = scratch
        cols = pl.ds(first, width)
        self.loads, self.crosses = [], []
        for index in range(4):
            self.loads.append(pltpu.make_async_copy(terms.at[index, :, cols], self.own.at[index], sems.one()))
            if given is None:
                self.crosses.append(place.copy("y", terms.at[4 + index, :, cols], self.other.at[index], sems.two()))
            else:
                self.loads.append(pltpu.make_async_copy(given.at[index], self.other.at[index], sems.one()))
        self.per = len(self.loads) // 4
        self.rises = [place.copy("up", self.to_z.at[i], self.from_z.at[i], sems.two()) for i in range(3)]
        half = self.final.shape[0] // 2
        there = result.at[:, pl.ds(pl.multiple_of(place.x * (span or width) + start, 128), width)]
        self.leave = pltpu.make_async_copy(self.final.at[place.half(half)], there, sems.one())
        self.swap = place.copy("x", self.final.at[place.half(half, True)], there, sems.two())

    def start(self, step):
        index = 3 - step
        for copy in self.crosses[index : index + 1] + self.loads[index * self.per : (index + 1) * self.per]:
            copy.start()

    def step(self, step):
        index = 3 - step
        for copy in self.loads[index * self.per : (index + 1) * self.per]:
            copy.wait()
        for copy in self.crosses[index : index + 1]:
            copy.wait_recv()
        if step:
            self.rises[step - 1].wait_recv()

        def add(part):
            value = self.own[index, part].astype(F32) + self.other[index, part].astype(F32)
            if step:
                value = value + self.from_z[step - 1, part].astype(F32)
            if step < 3:
                self.to_z[step, part] = value.astype(BF16)
            else:
                self.final[part] = value

        pieces(self.final.shape[0], add)
        if step < 3:
            self.rises[step].start()
        else:
            self.swap.start()
            self.leave.start()

    def finish(self):
        for copy in self.crosses + self.rises:
            copy.wait_send()
        self.leave.wait()
        self.swap.wait()


class SumGiven:
    def __init__(self, place, sems, terms, given, result, first, width, scratch, span, start):
        self.own, self.others, self.to_y, self.from_y, self.final = scratch
        cols = pl.ds(first, width)
        self.loads = [
            pltpu.make_async_copy(terms.at[d * (terms.shape[0] // 2), :, cols], self.own.at[d], sems.one())
            for d in range(2)
        ]
        self.loads += [pltpu.make_async_copy(one, self.others.at[i], sems.one()) for i, one in enumerate(given)]
        self.cross = place.copy("y", self.to_y, self.from_y, sems.two())
        half = self.final.shape[0] // 2
        there = result.at[:, pl.ds(pl.multiple_of(place.x * span + start, 128), width)]
        self.leave = pltpu.make_async_copy(self.final.at[place.half(half)], there, sems.one())
        self.swap = place.copy("x", self.final.at[place.half(half, True)], there, sems.two())

    def start(self):
        for copy in self.loads:
            copy.start()

    def first(self):
        for copy in self.loads:
            copy.wait()

        def add(part):
            for d in (1, 0):
                value = self.own[d, part].astype(F32)
                for i in range(3):
                    value = value + self.others[i, d, part].astype(F32)
                if d:
                    self.to_y[part] = value.astype(BF16)
                else:
                    self.final[part] = value

        pieces(self.final.shape[0], add)
        self.cross.start()

    def second(self):
        self.cross.wait_recv()

        def add(part):
            self.final[part] = self.final[part] + self.from_y[part].astype(F32)

        pieces(self.final.shape[0], add)
        self.swap.start()
        self.leave.start()

    def finish(self):
        self.cross.wait_send()
        self.leave.wait()
        self.swap.wait()


def given_scratch(rows, width):
    return [
        pltpu.VMEM((2, rows, width), BF16),
        pltpu.VMEM((3, 2, rows, width), BF16),
        pltpu.VMEM((rows, width), BF16),
        pltpu.VMEM((rows, width), BF16),
        pltpu.VMEM((rows, width), F32),
    ]


def sum_scratch(rows, width):
    return [pltpu.VMEM((depth, rows, width), BF16) for depth in (4, 4, 3, 3)] + [pltpu.VMEM((rows, width), F32)]


class OutTerms:
    def __init__(self, sems, hidden, weight, stage, bufs, target):
        self.hidden, self.weight, self.stage, self.bufs, self.target = hidden, weight, stage, bufs, target
        self.loads, self.stores = sems.some(2), sems.some(2)

    def load(self, i):
        return pltpu.make_async_copy(self.weight.at[i], self.stage.at[i % 2], self.loads(i % 2))

    def store(self, i):
        width = self.bufs.shape[2]
        cols = pl.ds(pl.multiple_of(i * width, width), width)
        return pltpu.make_async_copy(self.bufs.at[i % 2], self.target.at[:, cols], self.stores(i % 2))

    def run(self, start, stop):
        def step(i, carry):
            self.load(i).wait()

            @pl.when(i < 7)
            def _():
                self.load(i + 1).start()

            @pl.when(i >= 2)
            def _():
                self.store(i).wait()

            self.bufs[i % 2] = mm(self.hidden[...], self.stage[i % 2], NT)
            self.store(i).start()
            return carry

        lax.fori_loop(start, stop, step, 0)

    def finish(self):
        self.store(6).wait()
        self.store(7).wait()


def norm_back_piece(value, gain, grad):
    scale = rms(value)
    scaled = gain * grad
    inner = jnp.mean(scaled * value, axis=-1, keepdims=True)
    gains = (grad * value * scale).reshape(PIECE // 8, 8, value.shape[1])
    return scale * scaled - value * (scale * scale * scale * inner), jnp.sum(gains, axis=0)


def thirds(columns):
    tiles = columns // 128
    wide = (tiles + 2) // 3 * 128
    return ((0, wide), (wide, wide), (2 * wide, columns - 2 * wide))


def sum_ffn_kernel(
    hid, early, gate_t, down, given, down_rest, given1, given2, given3, terms, resid, gains, d_res, ffn_in, d_wide, hidden, w_down,
    gate_sum, down_sum, d_h, d_attn, gain_sum, up_over, up_own, up0, up1, up2, up3, out_terms, *scratch
):
    *scratch, sem = scratch
    place, sems = Place(), Sems(sem)
    rest = hid - early
    down_y = Sum(place, sems, down, given, down_sum, 0, early, scratch[0:5], hid)
    down_z = SumGiven(place, sems, down_rest, (given1, given2, given3), down_sum, 0, rest, scratch[5:10], hid, early)
    gate = [
        Sum(place, sems, gate_t, None, gate_sum, first, width, scratch[10 + 5 * i : 15 + 5 * i], hid, first)
        for i, (first, width) in enumerate(thirds(hid))
    ]
    back = QuadSum(place, sems, terms, scratch[25:29])
    value, res, low, acts, ups, up_bufs, hid_v, stage, out_bufs = scratch[29:38]
    quad = Quad(place, sems, low, [d_attn.at[i] for i in range(4)])
    up = BlockTerms(sems, acts, ups, up_bufs, up_over, up_own, (up0, up1, up2, up3))
    out = OutTerms(sems, hid_v, w_down, stage, out_bufs, out_terms)
    ready = [
        pltpu.make_async_copy(ffn_in, acts, sems.one()),
        pltpu.make_async_copy(d_wide.at[:, pl.ds(hid, hid)], ups, sems.one()),
        pltpu.make_async_copy(hidden, hid_v, sems.one()),
    ]
    fetch = [pltpu.make_async_copy(resid, value, sems.one()), pltpu.make_async_copy(d_res, res, sems.one())]
    save = pltpu.make_async_copy(res, d_h, sems.one())
    place.greet()
    back.start()
    for one in (down_y, *gate):
        one.start(0)
    down_z.start()
    for copy in fetch:
        copy.start()
    for one in (down_y, *gate):
        one.start(1)
    down_y.step(0)
    down_z.first()
    for step in (2, 3):
        for one in (down_y, *gate):
            one.start(step)
    for copy in ready:
        copy.start()
    out.load(0).start()
    back.middle()
    for one in gate:
        one.step(0)
    for copy in fetch + ready:
        copy.wait()
    down_y.step(1)
    up.run(0, 4)
    back.ready()
    gain_sum[...] = jnp.zeros_like(gain_sum)

    def norm(part):
        d_norm, added = norm_back_piece(value[part], gains[1:2, :], back.read(part))
        grad = res[part] + d_norm
        res[part] = grad
        low[part] = grad.astype(BF16)
        gain_sum[...] += added

    pieces(SEQ_LEN, norm)
    quad.start()
    save.start()
    for one in gate:
        one.step(1)
    down_y.step(2)
    up.run(4, 8)
    down_z.second()
    for one in gate:
        one.step(2)
    down_y.step(3)
    out.run(0, 8)
    quad.forward()
    for one in gate:
        one.step(3)
    quad.finish()
    save.wait()
    up.finish()
    out.finish()
    for one in (down_y, down_z, *gate):
        one.finish()


def sum_last_kernel(
    hid, early, up, given, up_rest, given1, given2, given3, out_t, in_t, terms, tokens, gain_rows, d_h, ffn_gains, out_terms, resid, seq_count, valid_len,
    up_sum, out_sum, q_sum, k_sum, v_sum, f_sum, grad, block_out, gain_sum, *scratch
):
    *scratch, sem = scratch
    place, sems = Place(True), Sems(sem)
    sums = []
    for terms_in, given_in, result, first, width, span, start in (
        (up, given, up_sum, 0, early, hid, 0),
        (out_t, None, out_sum, 0, KDIM, None, 0),
        (in_t, None, q_sum, 0, KDIM, None, 0),
        (in_t, None, k_sum, KDIM, KDIM, None, 0),
        (in_t, None, v_sum, 2 * KDIM, KDIM, None, 0),
        (in_t, None, f_sum, 3 * KDIM, 128, None, 0),
    ):
        sums.append(Sum(place, sems, terms_in, given_in, result, first, width, scratch[:5], span, start))
        scratch = scratch[5:]
    up_z = SumGiven(place, sems, up_rest, (given1, given2, given3), up_sum, 0, hid - early, scratch[:5], hid, early)
    scratch = scratch[5:]
    back = QuadSum(place, sems, terms, scratch[0:4])
    ahead = QuadSum(place, sems, out_terms, scratch[4:8])
    value, res, kept, shown, gains, parts, met, crossed, risen, last, swapped = scratch[8:]
    leave = Leave(place, sems, res, grad)
    leave_out = Leave(place, sems, shown, block_out)
    fetch = [pltpu.make_async_copy(tokens, value, sems.one()), pltpu.make_async_copy(d_h, res, sems.one())]
    fetch.append(pltpu.make_async_copy(resid, kept, sems.one()))
    meet = place.copy("core", parts, met, sems.two())
    cross = place.copy("y", parts.at[pl.ds(4, 4)], crossed, sems.two())
    spread = [
        place.copy(name, parts.at[i + 1], risen.at[i], sems.two()) for i, name in enumerate(("up", "two", "down"))
    ]
    swap = place.copy("x", last.at[1 - place.x], swapped, sems.two())
    place.greet()
    back.start()
    for one in sums:
        one.start(0)
    up_z.start()
    for copy in fetch:
        copy.start()
    for one in sums:
        one.start(1)
    ahead.start()
    sums[0].step(0)
    up_z.first()
    for one in sums:
        one.start(2)
    back.middle()
    for one in sums[1:]:
        one.step(0)
    for copy in fetch:
        copy.wait()
    gains[...] = jnp.zeros_like(gains)
    back.ready()

    def norm(part):
        d_norm, added = norm_back_piece(value[part].astype(F32), gain_rows[0:1, :], back.read(part))
        res[part] = res[part] + d_norm
        gains[...] += added

    pieces(SEQ_LEN, norm)
    leave.start()
    width = res.shape[1] // 8
    parts[...] = jnp.zeros_like(parts)
    for row, source in enumerate((gains[...], ffn_gains[...])):
        summed = jnp.sum(source, axis=0, keepdims=True)
        for index in range(8):
            parts[index, row : row + 1, :] = summed[:, index * width : (index + 1) * width]
    meet.start()
    sums[0].step(1)
    meet.wait()
    parts[...] = parts[...] + met[...]
    cross.start()
    for one in sums:
        one.start(3)
    for one in sums[1:]:
        one.step(1)
    ahead.middle()
    up_z.second()
    for one in sums:
        one.step(2)
    cross.wait()
    parts[pl.ds(0, 4)] = parts[pl.ds(0, 4)] + crossed[...]
    for copy in spread:
        copy.start()
    ahead.ready()

    def show(part):
        alive = live_rows(place, seq_count, valid_len, part)
        shown[part] = (alive * (kept[part] + ahead.read(part))).astype(BF16)

    pieces(SEQ_LEN, show)
    leave_out.start()
    for one in sums:
        one.step(3)
    for copy in spread:
        copy.wait_recv()
    total = parts[0] + risen[0] + risen[1] + risen[2]
    last[0] = total[:, : width // 2]
    last[1] = total[:, width // 2 :]
    swap.start()
    swap.wait()
    gain_sum[...] = last[place.x] + swapped[...]
    for copy in spread:
        copy.wait_send()
    leave.finish()
    leave_out.finish()
    up_z.finish()
    for one in sums:
        one.finish()


def call(kernel, name, ident, inputs, specs, outputs, out_specs, scratch, sems):
    return pl.pallas_call(
        kernel,
        in_specs=specs,
        out_specs=out_specs,
        out_shape=[jax.ShapeDtypeStruct(shape, kind) for shape, kind in outputs],
        scratch_shapes=scratch + [DMA((sems,))],
        compiler_params=pltpu.CompilerParams(collective_id=ident, has_side_effects=True, vmem_limit_bytes=60 << 20),
        name=name,
    )(*inputs)


PAD = 128 - SLOTS
EARLY = 896


class Ring:
    def __init__(self, count):
        self.count = count
        self.stages = []
        left, stride = count // 2, count
        while left > 1:
            size = 4 if left % 4 == 0 else 2
            stride //= size
            left //= size
            self.stages.append((stride, size))

    def perm(self, stride, size, shift):
        moves = []
        for source in range(self.count):
            digit = source // stride % size
            moves.append((source, source + ((digit + shift) % size - digit) * stride))
        return moves

    def send(self, value, stage, shift):
        stride, size = stage
        return lax.ppermute(value, "dp", self.perm(stride, size, shift % size))

    def swap(self, value):
        return lax.ppermute(value, "dp", self.perm(1, 2, 1))

    def digit(self, stage):
        return lax.axis_index("dp") // stage[0] % stage[1]

    def gather(self, block):
        blocks = [block]
        for stage in self.stages:
            more = list(blocks)
            for shift in range(1, stage[1]):
                more += [self.send(one, stage, -shift) for one in blocks]
            blocks = more
        return blocks

    def scatter(self, make):
        def level(depth, offset, width):
            if depth == len(self.stages):
                return lambda inner: make(offset + inner)
            return None

        widths = [1]
        for stage in self.stages:
            widths.append(widths[-1] * stage[1])

        def total(depth, index):
            if depth == len(self.stages):
                return make(index)
            stage = self.stages[depth]
            parts = []
            for shift in range(1, stage[1]):
                sent = total(depth + 1, index + shift * widths[depth]).astype(BF16)
                parts.append(self.send(sent, stage, shift))
            mine = total(depth + 1, index)
            for part in parts:
                mine = mine + part.astype(F32)
            return mine

        return total(0, 0)

    def order(self, value, width, back=False):
        parts = [value[:, i * width : (i + 1) * width] for i in range(self.count // 2)]
        stages = self.stages
        if back:
            parts = self.turn_digits(parts, [s[1] for s in stages[::-1]])
        inner = len(parts)
        for stage in stages:
            size = stage[1]
            inner //= size
            digit = self.digit(stage)
            new = []
            for place in range(len(parts)):
                at = place // inner % size
                base = place - at * inner
                picks = []
                for k in range(size):
                    picks.append(parts[base + ((at - k) % size if back else (at + k) % size) * inner])
                one = picks[0]
                for k in range(1, size):
                    one = jnp.where(digit == k, picks[k], one)
                new.append(one)
            parts = new
        if not back:
            parts = self.turn_digits(parts, [s[1] for s in stages])
        return jnp.concatenate(parts, axis=1)

    def turn_digits(self, parts, sizes):
        count = len(parts)
        out = [None] * count
        for index in range(count):
            rest, digits = index, []
            for size in reversed(sizes):
                digits.append(rest % size)
                rest //= size
            new = 0
            for digit, size in zip(digits, reversed(sizes)):
                new = new * size + digit
            out[new] = parts[index]
        return out


def mm(left, right, dims=NN, kind=F32):
    return lax.dot_general(left, right, dims, preferred_element_type=F32).astype(kind)


def rms(values):
    return lax.rsqrt(jnp.mean(values * values, axis=-1, keepdims=True) + 1e-06)


def norm_back(values, gain, grad):
    scale = rms(values)
    scaled = gain * grad
    inner = jnp.mean(scaled * values, axis=-1, keepdims=True)
    return scale * scaled - values * (scale * scale * scale * inner), jnp.sum(grad * values * scale, axis=0)


def body_by_permutes(
    tokens,
    seq_count,
    valid_len,
    attn_gain,
    ffn_gain,
    q_weight,
    k_weight,
    v_weight,
    forget_weight,
    out_weight,
    gate_weight,
    up_weight,
    down_weight,
    cotangent,
    *,
    ring,
):
    shard = q_weight.shape[0]
    width = 2 * shard
    core = lax.axis_index("head")
    even = lax.axis_index("dp") % 2 == 0
    first = core == 0
    rows = tokens.shape[0]

    def other_core(value):
        return lax.ppermute(value, "head", [(0, 1), (1, 0)])

    def pair_rows(mine, theirs, axis=0):
        return jnp.where(
            even, jnp.concatenate([mine, theirs], axis=axis), jnp.concatenate([theirs, mine], axis=axis)
        )

    def gather(parts):
        left = jnp.concatenate([p[0] for p in parts], axis=1)
        right = jnp.concatenate([p[1] for p in parts], axis=1)
        mine, theirs = jnp.where(even, left, right), jnp.where(even, right, left)
        return jnp.concatenate(ring.gather(pair_rows(mine, ring.swap(theirs))), axis=0)

    def cut(weight):
        half = weight.shape[1] // 2
        return (weight[:, :half], weight[:, half:])

    def quad_gather(mine):
        chips = jnp.concatenate([mine, ring.swap(mine)], axis=0)
        return jnp.concatenate([chips, other_core(chips)], axis=0)

    def quad_scatter(make):
        theirs = other_core(make(slice(2 * SEQ_LEN, 4 * SEQ_LEN)))
        far = make(slice(SEQ_LEN, 2 * SEQ_LEN)) + theirs[SEQ_LEN:]
        near = make(slice(0, SEQ_LEN)) + theirs[:SEQ_LEN]
        return near + ring.swap(far.astype(BF16)).astype(F32)

    def whole_rows(mine):
        theirs = other_core(mine)
        return jnp.where(
            first, jnp.concatenate([mine, theirs], axis=0), jnp.concatenate([theirs, mine], axis=0)
        )

    def weight_sum(act, grads):
        def make(index):
            return mm(act[:, index * width : (index + 1) * width], grads, TN)

        done = ring.scatter(make)
        mine = jnp.where(even, done[:shard], done[shard:])
        theirs = ring.swap(jnp.where(even, done[shard:], done[:shard]))
        return (jnp.where(even, mine, theirs), jnp.where(even, theirs, mine))

    gains = jnp.concatenate(
        [attn_gain[:, None], ffn_gain[:, None], jnp.zeros((shard, PAD - 2), BF16)], axis=1
    )
    w_in = gather([cut(q_weight), cut(k_weight), cut(v_weight), cut(forget_weight), (gains, gains)])
    w_out = gather([cut(out_weight)])
    w_gate = gather([cut(gate_weight)])
    w_up = gather([cut(up_weight)])
    w_down = gather([cut(down_weight)])
    gain_attn = w_in[:, WIDE - PAD].astype(F32)[None, :]
    gain_ffn = w_in[:, WIDE - PAD + 1].astype(F32)[None, :]

    def own(value):
        return ring.order(jnp.where(first, value[:SEQ_LEN], value[SEQ_LEN:]), width)

    places = lax.broadcasted_iota(jnp.int32, (SEQ_LEN, 1), 0)
    length = jnp.where(first, valid_len[0], valid_len[1])
    live = ((core < seq_count[0]) & (places < length)).astype(F32)
    own_tokens = own(tokens)
    d_res = live * own(cotangent)
    d_ffn = quad_gather(d_res.astype(BF16))
    inputs = quad_gather(own_tokens).astype(F32)
    attn_in = (inputs * rms(inputs) * gain_attn).astype(BF16)
    proj = mm(attn_in, w_in)
    mixed, *saved = mixer_forward(proj)
    own_inputs = own_tokens.astype(F32)
    resid = own_inputs + quad_scatter(lambda r: mm(mixed[r], w_out, NT))
    ffn_in = quad_gather((resid * rms(resid) * gain_ffn).astype(BF16))
    gate, up_vals = mm(ffn_in, w_gate), mm(ffn_in, w_up)
    sig = jax.nn.sigmoid(gate)
    hidden = (gate * sig * up_vals).astype(BF16)
    d_hidden = mm(d_ffn, w_down)
    d_gate = (d_hidden * up_vals * (sig * (1.0 + gate * (1.0 - sig)))).astype(BF16)
    d_up = (d_hidden * (gate * sig)).astype(BF16)
    d_ffn_in = quad_scatter(lambda r: mm(d_gate[r], w_gate, NT) + mm(d_up[r], w_up, NT))
    down_sum = weight_sum(d_ffn, hidden)
    gate_sum = weight_sum(ffn_in, d_gate)
    up_sum = weight_sum(ffn_in, d_up)
    ffn = quad_scatter(lambda r: mm(hidden[r], w_down, NT))
    block_out = whole_rows(ring.order((live * (resid + ffn)).astype(BF16), width, back=True))
    d_norm, ffn_gain_part = norm_back(resid, gain_ffn, d_ffn_in)
    d_h = d_res + d_norm
    d_attn = quad_gather(d_h.astype(BF16))
    d_mixed = mm(d_attn, w_out)
    d_proj = mixer_backward(proj, saved, d_mixed)
    d_attn_in = quad_scatter(lambda r: mm(d_proj[r], w_in, NT))
    out_sum = weight_sum(d_attn, mixed)
    in_sum = weight_sum(attn_in, d_proj)
    d_input, attn_gain_part = norm_back(own_inputs, gain_attn, d_attn_in)
    input_grad = whole_rows(ring.order(d_h + d_input, width, back=True))

    both = jnp.stack([attn_gain_part, ffn_gain_part], axis=0)
    both = both + other_core(both)
    both = both.reshape(2, ring.count // 2, width)
    for stage in ring.stages[::-1]:
        size = stage[1]
        both = both.reshape(2, size, -1, width)
        parts = [ring.send(both[:, shift], stage, shift) for shift in range(1, size)]
        both = both[:, 0]
        for part in parts:
            both = both + part
    both = both.reshape(2, 2, shard)
    both = jnp.where(even, both[:, 0], both[:, 1]) + ring.swap(jnp.where(even, both[:, 1], both[:, 0]))

    def columns(pieces, start, stop):
        return jnp.concatenate([p[:, start:stop] for p in pieces], axis=1)

    return (
        block_out,
        input_grad,
        both[0],
        both[1],
        columns(in_sum, 0, KDIM),
        columns(in_sum, KDIM, 2 * KDIM),
        columns(in_sum, 2 * KDIM, 3 * KDIM),
        columns(in_sum, 3 * KDIM, 3 * KDIM + SLOTS),
        columns(out_sum, 0, KDIM),
        jnp.concatenate(gate_sum, axis=1),
        jnp.concatenate(up_sum, axis=1),
        jnp.concatenate(down_sum, axis=1),
    )


def body_by_kernels(
    tokens,
    seq_count,
    valid_len,
    attn_gain,
    ffn_gain,
    q_weight,
    k_weight,
    v_weight,
    forget_weight,
    out_weight,
    gate_weight,
    up_weight,
    down_weight,
    cotangent,
    *,
    ring,
):
    shard, dim = q_weight.shape[0], tokens.shape[1]
    width, hid = 2 * shard, gate_weight.shape[1] // 2
    up_z, over_y = (lambda value: ring.send(value, ring.stages[0], 1)), (lambda value: ring.send(value, ring.stages[1], 1))
    rows4 = (4, SEQ_LEN, dim)
    blocks = lambda value: value.reshape(-1, width, value.shape[-1])
    flat = lambda value: value.reshape(-1, value.shape[-1])
    half = dim // 2

    row = (SEQ_LEN, dim)
    vmem = lambda shape, kind=F32: pltpu.VMEM(shape, kind)
    w_in, w_out, part0, own, attn_in, d_res, d_ffn, gain_rows = call(
        gather_first_kernel,
        "gather_first",
        0,
        (
            tokens,
            cotangent,
            seq_count,
            valid_len,
            attn_gain,
            ffn_gain,
            q_weight,
            k_weight,
            v_weight,
            forget_weight,
            out_weight,
            gate_weight,
            up_weight,
            down_weight,
        ),
        [ANY, ANY, SMEM, SMEM, VMEM, VMEM, ANY, ANY, ANY, VMEM] + [ANY] * 4,
        [
            ((8, width, WIDE), BF16),
            ((8, width, KDIM), BF16),
            ((width, 3 * hid), BF16),
            (row, BF16),
            (rows4, BF16),
            (row, F32),
            (rows4, BF16),
            ((8, dim), F32),
        ],
        [ANY] * 7 + [VMEM],
        [
            vmem((shard, 4 * KDIM + 128 + 3 * hid), BF16),
            vmem(rows4, BF16),
            vmem(rows4, BF16),
            vmem((4, SEQ_LEN, 128)),
            vmem((8, width, 128), BF16),
            vmem(row),
            vmem(row, BF16),
            vmem((shard, 256), BF16),
        ],
        240,
    )
    part3, part4 = up_z(part0), over_y(part0)
    w_in, w_out, attn_in, d_ffn = map(flat, (w_in, w_out, attn_in, d_ffn))
    proj = mm(attn_in, w_in)
    mixed, *saved = mixer_forward(proj)
    attn_terms = mm(mixed, w_out, NT).reshape(rows4)
    cut = hid // 256 * 128 + 128
    tokens4 = 4 * SEQ_LEN
    early, rest = [((4, width, EARLY), BF16)] * 2, [((2, width, hid - EARLY), BF16)] * 4
    w_wide, w_down, resid, ffn_in, wide, hidden, down_over, down_own, *down_parts = call(
        functools.partial(gather_ffn_kernel, hid, cut),
        "gather_ffn",
        1,
        (part0, part3, part4, attn_terms, own, gain_rows, d_ffn),
        [ANY] * 5 + [VMEM, ANY],
        [
            ((dim, 2 * hid), BF16),
            ((dim, hid), BF16),
            (row, F32),
            ((tokens4, dim), BF16),
            ((tokens4, 2 * hid), F32),
            ((tokens4, hid), BF16),
        ]
        + early
        + rest,
        [ANY] * 12,
        quad_scratch(dim)
        + [vmem(row), vmem((tokens4, dim), BF16), vmem(row, BF16), vmem((3, width, 3 * hid), BF16)]
        + [vmem((2, dim // 2, 256), BF16), vmem((hid // 128, tokens4, 256)), vmem((tokens4, hid), BF16)]
        + [vmem((tokens4, dim), BF16), vmem((2, width, hid), BF16)],
        180,
    )

    def exchange(over, parts):
        return [over_y(over)] + [ring.send(parts[d], ring.stages[0], d) for d in (1, 2, 3)]

    down_given = exchange(down_over, down_parts)
    gate, up_vals = wide[:, :hid], wide[:, hid:]
    sig = jax.nn.sigmoid(gate)
    d_hidden = mm(d_ffn, w_down)
    d_gate = (d_hidden * up_vals * (sig * (1.0 + gate * (1.0 - sig)))).astype(BF16)
    d_up = (d_hidden * (gate * sig)).astype(BF16)
    d_wide = jnp.concatenate([d_gate, d_up], axis=1)
    gate_terms = mm(ffn_in, d_wide[:, :hid], TN, BF16)
    d_ffn_terms = mm(d_wide, w_wide, NT).reshape(rows4)
    gate_sum, down_sum, d_h, d_attn, ffn_gains, up_over, up_own, *up_parts, ffn_terms = call(
        functools.partial(sum_ffn_kernel, hid, EARLY),
        "sum_ffn",
        2,
        (
            blocks(gate_terms),
            down_own,
            down_given[0],
            down_parts[0],
            *down_given[1:],
            d_ffn_terms,
            resid,
            gain_rows,
            d_res,
            ffn_in,
            d_wide,
            hidden,
            blocks(w_down),
        ),
        [ANY] * 9 + [VMEM] + [ANY] * 5,
        [((shard, 2 * hid), F32), ((shard, 2 * hid), F32), (row, F32), (rows4, BF16), ((8, dim), F32)]
        + early
        + rest
        + [((4 * SEQ_LEN, dim), F32)],
        [ANY] * 4 + [VMEM] + [ANY] * 7,
        sum_scratch(width, EARLY)
        + given_scratch(width, hid - EARLY)
        + [one for _, columns in thirds(hid) for one in sum_scratch(width, columns)]
        + quad_scratch(dim)
        + [vmem(row), vmem(row), vmem(row, BF16)]
        + [vmem((4 * SEQ_LEN, dim), BF16), vmem((4 * SEQ_LEN, hid), BF16), vmem((2, width, hid), BF16)]
        + [vmem((4 * SEQ_LEN, hid), BF16), vmem((2, width, hid), BF16), vmem((2, 4 * SEQ_LEN, width))],
        220,
    )
    d_attn = flat(d_attn)
    up_given = exchange(up_over, up_parts)
    d_proj = mixer_backward(proj, saved, mm(d_attn, w_out))
    d_attn_terms = mm(d_proj, w_in, NT).reshape(rows4)
    ffn_terms = ffn_terms.reshape(rows4)
    tail = width // 2
    up_sum, out_sum, q_sum, k_sum, v_sum, f_sum, input_grad, block_out, gain_sums = call(
        functools.partial(sum_last_kernel, hid, EARLY),
        "sum_last",
        3,
        (
            up_own,
            up_given[0],
            up_parts[0],
            *up_given[1:],
            blocks(mm(d_attn, mixed, TN, BF16)),
            blocks(mm(attn_in, d_proj, TN, BF16)),
            d_attn_terms,
            own,
            gain_rows,
            d_h,
            ffn_gains,
            ffn_terms,
            resid,
            seq_count,
            valid_len,
        ),
        [ANY] * 10 + [VMEM, ANY, VMEM, ANY, ANY, SMEM, SMEM],
        [((shard, 2 * hid), F32)]
        + [((shard, 2 * KDIM), F32)] * 4
        + [((shard, 256), F32), ((2 * SEQ_LEN, dim), F32), ((2 * SEQ_LEN, dim), BF16), ((8, tail), F32)],
        [ANY] * 8 + [VMEM],
        sum_scratch(width, EARLY)
        + sum_scratch(width, KDIM) * 4
        + sum_scratch(width, 128)
        + given_scratch(width, hid - EARLY)
        + quad_scratch(dim) * 2
        + [vmem(row, BF16), vmem(row), vmem(row), vmem(row, BF16), vmem((8, dim))]
        + [vmem((depth, 8, width)) for depth in (8, 8, 4, 3)]
        + [vmem((2, 8, tail)), vmem((8, tail))],
        280,
    )
    f_grad = jnp.concatenate([f_sum[:, :SLOTS], f_sum[:, 128 : 128 + SLOTS]], axis=1)
    return (
        block_out,
        input_grad,
        gain_sums[0],
        gain_sums[1],
        q_sum,
        k_sum,
        v_sum,
        f_grad,
        out_sum,
        gate_sum,
        up_sum,
        down_sum,
    )


def solution(mesh):
    ring = Ring(mesh.shape["dp"])
    body = body_by_kernels if ring.count == 16 else body_by_permutes
    split_one, split_two = P("dp"), P("dp", "head")
    row = P("dp", None)
    in_specs = (row, split_one, split_one, split_one, split_one) + (split_two,) * 8 + (row,)
    out_specs = (row, row, split_one, split_one) + (split_two,) * 8
    return jax.shard_map(
        functools.partial(body, ring=ring),
        mesh=mesh,
        in_specs=in_specs,
        out_specs=out_specs,
        check_vma=False,
    )
```

```python
import functools
import jax
import jax.numpy as jnp
from jax import lax
from jax.experimental import pallas as pl
from jax.experimental.pallas import tpu as pltpu
from jax.sharding import PartitionSpec as P

SLOTS = 64
KDIM = 512
SEQ_LEN = 256
HALF = 128
F32, BF16 = jnp.float32, jnp.bfloat16
WIDE = 3 * KDIM + 128
NT = (((1,), (1,)), ((), ()))
NN = (((1,), (0,)), ((), ()))
TN = (((0,), (0,)), ((), ()))
LEVELS = (8, 16, 32, 64)


def split(value):
    high = value.astype(BF16)
    return high, (value - high.astype(F32)).astype(BF16)


def dot3(left, right, dims):
    one = functools.partial(lax.dot_general, dimension_numbers=dims, preferred_element_type=F32)
    return one(left[0], right[0]) + (one(left[0], right[1]) + one(left[1], right[0]))


def silu_parts(value):
    gate = 1.0 / (1.0 + jnp.exp(-value))
    return gate, value * gate


def level_mask(size):
    row = lax.broadcasted_iota(jnp.int32, (HALF, HALF), 0) // size
    col = lax.broadcasted_iota(jnp.int32, (HALF, HALF), 1) // size
    return (row == col + 1) & (row % 2 == 1)


def band_mask(back):
    row = lax.broadcasted_iota(jnp.int32, (HALF, HALF), 0)
    col = lax.broadcasted_iota(jnp.int32, (HALF, HALF), 1)
    return (row == col + back) & (row // 8 == col // 8)


def down(value, back):
    return value if back == 0 else pltpu.roll(value, back, 0)


def up(value, back):
    return value if back == 0 else pltpu.roll(value, SEQ_LEN - back, 0)


def gates(forget):
    lane = lax.broadcasted_iota(jnp.int32, forget.shape, 1) < SLOTS
    place = lax.broadcasted_iota(jnp.int32, forget.shape, 0)
    forget = jnp.where(lane, forget, 0.0)
    tail = jnp.exp(-jnp.abs(forget))
    log_decay = (jnp.minimum(forget, 0.0) - jnp.log1p(tail)) * 0.125
    log_decay = jnp.where(lane, log_decay, 0.0)
    g = log_decay
    series = 1.0 + g * (1.0 / 7.0)
    for n in (6.0, 5.0, 4.0, 3.0, 2.0):
        series = 1.0 + g * (1.0 / n) * series
    writes = jnp.where(g > -0.3, -g * series, 1.0 - jnp.exp(g))
    writes = jnp.where(lane, writes, 0.0)
    ahead, behind = g, g
    for step in (1, 2, 4):
        ahead = ahead + jnp.where(place % 8 >= step, down(ahead, step), 0.0)
        behind = behind + jnp.where(place % 8 < 8 - step, up(behind, step), 0.0)
    behind = jnp.where(place % 8 < 7, up(behind, 1), 0.0)
    aheads, behinds = {8: ahead}, {8: behind}
    size = 8
    while size < HALF:
        first = ahead.reshape(SEQ_LEN // (2 * size), 2, size, 128)
        last = behind.reshape(SEQ_LEN // (2 * size), 2, size, 128)
        left, right = first[:, 0:1], first[:, 1:2]
        left_sum, right_sum = left[:, :, size - 1 :], right[:, :, size - 1 :]
        ahead = jnp.concatenate([left, right + left_sum], axis=1).reshape(SEQ_LEN, 128)
        behind = jnp.concatenate([last[:, 0:1] + right_sum, last[:, 1:2]], axis=1).reshape(SEQ_LEN, 128)
        size *= 2
        aheads[size], behinds[size] = ahead, behind
    return lane, place, g, writes, aheads, behinds


def near_decays(place, aheads, back):
    ahead = aheads[8]
    gap = jnp.where(place % 8 >= back, ahead - down(ahead, back), 0.0)
    return jnp.where(place % 8 >= back, jnp.exp(gap), 0.0)


def halves(value):
    return value[:HALF], value[HALF:]


def to_slots(blocks, cross, place, writes, aheads, behinds, nears):
    grow = {size: jnp.exp(aheads[size]) for size in LEVELS}
    keep = {size: split(jnp.exp(behinds[size]) * writes) for size in LEVELS}
    outs = []
    for half in range(2):
        here = slice(half * HALF, (half + 1) * HALF)
        block = blocks[half]
        parts = split(block)
        total = None
        for size in LEVELS:
            mask = level_mask(size)
            masked = tuple(jnp.where(mask, part, jnp.zeros_like(part)) for part in parts)
            term = grow[size][here] * dot3(masked, tuple(k[here] for k in keep[size]), NN)
            total = term if total is None else total + term
        for back in range(8):
            near = jnp.sum(jnp.where(band_mask(back), block, 0.0), axis=1, keepdims=True)
            total = total + near * nears[back][here]
        if half == 1:
            far = split((jnp.exp(behinds[HALF]) * writes)[:HALF])
            total = total + jnp.exp(aheads[HALF])[HALF:] * dot3(split(cross), far, NN)
        outs.append(total)
    return jnp.concatenate(outs, axis=0)


def to_tokens(slots, writes, aheads, behinds, nears):
    blocks = []
    for half in range(2):
        here = slice(half * HALF, (half + 1) * HALF)
        total = jnp.zeros((HALF, HALF), F32)
        for size in LEVELS:
            left = split((slots * jnp.exp(aheads[size]))[here])
            right = split((jnp.exp(behinds[size]) * writes)[here])
            total = jnp.where(level_mask(size), dot3(left, right, NT), total)
        for back in range(8):
            near = jnp.sum(slots[here] * nears[back][here], axis=1, keepdims=True)
            total = jnp.where(band_mask(back), near, total)
        blocks.append(total)
    left = split((slots * jnp.exp(aheads[HALF]))[HALF:])
    right = split((jnp.exp(behinds[HALF]) * writes)[:HALF])
    return blocks, dot3(left, right, NT)


def forward_kernel(q_ref, k_ref, v_ref, f_ref, o_ref, p_ref, s_ref, a_ref, b_ref):
    query = split(silu_parts(q_ref[...])[1] * KDIM ** (-0.5))
    keys = split(silu_parts(k_ref[...])[1])
    values = split(v_ref[...])
    lane, place, g, writes, aheads, behinds = gates(f_ref[...])
    nears = [near_decays(place, aheads, back) * down(writes, back) for back in range(8)]
    q0, q1 = tuple(x[:HALF] for x in query), tuple(x[HALF:] for x in query)
    k0, k1 = tuple(x[:HALF] for x in keys), tuple(x[HALF:] for x in keys)
    blocks = (dot3(q0, k0, NT), dot3(q1, k1, NT))
    cross = dot3(q1, k0, NT)
    scores = to_slots(blocks, cross, place, writes, aheads, behinds, nears)
    shown = jnp.where(lane, scores, -1e30)
    weights = jnp.exp(shown - jnp.max(shown, axis=1, keepdims=True))
    weights = jnp.where(lane, weights, 0.0)
    weights = weights / jnp.sum(weights, axis=1, keepdims=True)
    mixes, mix_cross = to_tokens(weights, writes, aheads, behinds, nears)
    v0 = tuple(x[:HALF] for x in values)
    o_ref[:HALF, :] = dot3(split(mixes[0]), v0, NN).astype(o_ref.dtype)
    row = jnp.concatenate([mix_cross, mixes[1]], axis=1)
    o_ref[HALF:, :] = dot3(split(row), values, NN).astype(o_ref.dtype)
    p_ref[...] = weights
    s_ref[...] = scores
    a_ref[:HALF, :] = jnp.concatenate([blocks[0], jnp.zeros_like(cross)], axis=1)
    a_ref[HALF:, :] = jnp.concatenate([cross, blocks[1]], axis=1)
    b_ref[:HALF, :] = jnp.concatenate([mixes[0], jnp.zeros_like(cross)], axis=1)
    b_ref[HALF:, :] = row


def backward_kernel(q_ref, k_ref, v_ref, f_ref, p_ref, s_ref, a_ref, b_ref, d_ref, out_ref):
    lane, place, g, writes, aheads, behinds = gates(f_ref[...])
    spans = [near_decays(place, aheads, back) for back in range(8)]
    nears = [spans[back] * down(writes, back) for back in range(8)]
    weights, scores = p_ref[...], s_ref[...]
    products, mixing = a_ref[...], b_ref[...]
    grad = split(d_ref[...])
    g0, g1 = tuple(x[:HALF] for x in grad), tuple(x[HALF:] for x in grad)
    values = split(v_ref[...])
    v0, v1 = tuple(x[:HALF] for x in values), tuple(x[HALF:] for x in values)
    m_parts = split(mixing)
    dv0 = dot3(tuple(x[:, :HALF] for x in m_parts), grad, TN)
    dv1 = dot3(tuple(x[HALF:, HALF:] for x in m_parts), g1, TN)
    out_ref[:HALF, 2 * KDIM : 3 * KDIM] = dv0.astype(BF16)
    out_ref[HALF:, 2 * KDIM : 3 * KDIM] = dv1.astype(BF16)
    mix_blocks = (dot3(g0, v0, NT), dot3(g1, v1, NT))
    mix_cross = dot3(g1, v0, NT)
    d_weights = to_slots(mix_blocks, mix_cross, place, writes, aheads, behinds, nears)
    inner = jnp.sum(weights * d_weights, axis=1, keepdims=True)
    d_scores = weights * (d_weights - inner)
    d_blocks, d_cross = to_tokens(d_scores, writes, aheads, behinds, nears)
    q_gate, q_act = silu_parts(q_ref[...])
    k_gate, k_act = silu_parts(k_ref[...])
    scale = KDIM ** (-0.5)
    query, keys = split(q_act * scale), split(k_act)
    k0 = tuple(x[:HALF] for x in keys)
    low = split(jnp.concatenate([d_cross, d_blocks[1]], axis=1))
    top = split(d_blocks[0])
    dq = jnp.concatenate([dot3(top, k0, NN), dot3(low, keys, NN)], axis=0)
    first = tuple(jnp.concatenate([t, l[:, :HALF]], axis=0) for t, l in zip(top, low))
    dk0 = dot3(first, query, TN)
    dk1 = dot3(tuple(x[:, HALF:] for x in low), tuple(x[HALF:] for x in query), TN)
    dk = jnp.concatenate([dk0, dk1], axis=0)
    out_ref[:, :KDIM] = (dq * scale * (q_gate + q_act * (1.0 - q_gate))).astype(BF16)
    out_ref[:, KDIM : 2 * KDIM] = (dk * (k_gate + k_act * (1.0 - k_gate))).astype(BF16)
    parts = []
    for half in range(2):
        here = slice(half * HALF, (half + 1) * HALF)
        both = jnp.concatenate([mix_blocks[half], products[here, here]], axis=0)
        both_parts = split(both)
        total = None
        for size in LEVELS:
            mask = level_mask(size)
            mask = jnp.concatenate([mask, mask], axis=0)
            grow = jnp.exp(aheads[size][here])
            right = split(jnp.concatenate([weights[here] * grow, d_scores[here] * grow], axis=0))
            left = tuple(jnp.where(mask, part, jnp.zeros_like(part)) for part in both_parts)
            term = jnp.exp(behinds[size][here]) * dot3(left, right, TN)
            total = term if total is None else total + term
        parts.append(total)
    grow = jnp.exp(aheads[HALF][HALF:])
    left = split(jnp.concatenate([mix_cross, products[HALF:, :HALF]], axis=0))
    right = split(jnp.concatenate([weights[HALF:] * grow, d_scores[HALF:] * grow], axis=0))
    parts[0] = parts[0] + jnp.exp(behinds[HALF][:HALF]) * dot3(left, right, TN)
    reach = jnp.concatenate(parts, axis=0)
    for back in range(8):
        mask = band_mask(back)
        near_mix = jnp.concatenate([jnp.sum(jnp.where(mask, mix_blocks[h], 0.0), axis=1, keepdims=True) for h in range(2)], axis=0)
        near_pro = jnp.concatenate(
            [jnp.sum(jnp.where(mask, products[h * HALF : (h + 1) * HALF, h * HALF : (h + 1) * HALF], 0.0), axis=1, keepdims=True) for h in range(2)],
            axis=0,
        )
        reach = reach + up((near_mix * weights + near_pro * d_scores) * spans[back], back)
    d_sum = weights * d_weights + d_scores * scores - writes * reach
    step = 1
    while step < SEQ_LEN:
        d_sum = d_sum + jnp.where(place < SEQ_LEN - step, up(d_sum, step), 0.0)
        step *= 2
    d_log = d_sum - reach * jnp.exp(g)
    d_forget = d_log * 0.125 / (1.0 + jnp.exp(f_ref[...]))
    out_ref[:, 3 * KDIM :] = jnp.where(lane, d_forget, 0.0).astype(BF16)


def spec(width, column):
    return pl.BlockSpec((SEQ_LEN, width), lambda i: (i, column))


IN_SPECS = [spec(KDIM, 0), spec(KDIM, 1), spec(KDIM, 2), spec(128, 3 * KDIM // 128)]


def mixer_forward(proj):
    rows = proj.shape[0]
    shape = lambda width, kind: jax.ShapeDtypeStruct((rows, width), kind)
    return pl.pallas_call(
        forward_kernel,
        grid=(rows // SEQ_LEN,),
        in_specs=IN_SPECS,
        out_specs=[spec(KDIM, 0), spec(128, 0), spec(128, 0), spec(SEQ_LEN, 0), spec(SEQ_LEN, 0)],
        out_shape=[shape(KDIM, BF16), shape(128, F32), shape(128, F32), shape(SEQ_LEN, F32), shape(SEQ_LEN, F32)],
        compiler_params=pltpu.CompilerParams(vmem_limit_bytes=48 << 20),
        cost_estimate=pl.CostEstimate(flops=rows * 3000000, bytes_accessed=rows * 10000, transcendentals=rows * 3000),
        name="mixer_forward",
    )(proj, proj, proj, proj)


def mixer_backward(proj, saved, grad):
    rows = proj.shape[0]
    weights, scores, products, mixing = saved
    return pl.pallas_call(
        backward_kernel,
        grid=(rows // SEQ_LEN,),
        in_specs=IN_SPECS + [spec(128, 0), spec(128, 0), spec(SEQ_LEN, 0), spec(SEQ_LEN, 0), spec(KDIM, 0)],
        out_specs=spec(WIDE, 0),
        out_shape=jax.ShapeDtypeStruct((rows, WIDE), BF16),
        compiler_params=pltpu.CompilerParams(vmem_limit_bytes=48 << 20),
        cost_estimate=pl.CostEstimate(flops=rows * 9000000, bytes_accessed=rows * 16000, transcendentals=rows * 5000),
        name="mixer_backward",
    )(proj, proj, proj, proj, weights, scores, products, mixing, grad)


MESH = pl.DeviceIdType.MESH
ANY = pl.BlockSpec(memory_space=pl.ANY)
VMEM = pl.BlockSpec(memory_space=pltpu.VMEM)
SMEM = pl.BlockSpec(memory_space=pltpu.SMEM)
DMA = pltpu.SemaphoreType.DMA
PIECE = 32


class Place:
    def __init__(self, all_z=False):
        dp = lax.axis_index("dp")
        self.core = lax.axis_index("head")
        self.x, self.y, self.z = dp % 2, dp // 2 % 2, dp // 4
        rest = dp % 4
        self.peers = {
            "x": (dp + 1 - 2 * self.x, self.core),
            "y": (dp + 2 - 4 * self.y, self.core),
            "up": ((self.z + 1) % 4 * 4 + rest, self.core),
            "down": ((self.z + 3) % 4 * 4 + rest, self.core),
            "core": (dp, 1 - self.core),
        }
        if all_z:
            self.peers["two"] = ((self.z + 2) % 4 * 4 + rest, self.core)

    def greet(self):
        ready = pltpu.get_barrier_semaphore()
        for peer in self.peers.values():
            pl.semaphore_signal(ready, inc=1, device_id=peer, device_id_type=MESH)
        pl.semaphore_wait(ready, len(self.peers))

    def copy(self, name, source, target, sems):
        return pltpu.make_async_remote_copy(
            src_ref=source,
            dst_ref=target,
            send_sem=sems[0],
            recv_sem=sems[1],
            device_id=self.peers[name],
            device_id_type=MESH,
        )

    def half(self, size, other=False):
        place = 1 - self.x if other else self.x
        return pl.ds(pl.multiple_of(place * size, size), size)

    def columns(self, index, size):
        natural = (self.z + index % 4) % 4 * 2 + (self.y + index // 4) % 2
        return pl.ds(pl.multiple_of(natural * size, size), size)


class Sems:
    def __init__(self, ref):
        self.ref, self.used = ref, 0

    def one(self):
        self.used += 1
        return self.ref.at[self.used - 1]

    def two(self):
        return (self.one(), self.one())

    def some(self, count):
        first = self.used
        self.used += count
        return lambda index: self.ref.at[first + index]


def pieces(rows, work):
    def step(i, carry):
        work(pl.ds(pl.multiple_of(i * PIECE, PIECE), PIECE))
        return carry

    lax.fori_loop(0, rows // PIECE, step, 0)


class Keep:
    def __init__(self, sems, source, target, stage):
        self.load = pltpu.make_async_copy(source, stage, sems.one())
        self.store = pltpu.make_async_copy(stage, target, sems.one())

    def start(self):
        self.load.start()

    def turn(self):
        self.load.wait()
        self.store.start()

    def wait(self):
        self.store.wait()


class Quad:
    def __init__(self, place, sems, source, slots):
        self.near = [] if slots[0] is None else [pltpu.make_async_copy(source, slots[0], sems.one())]
        self.swap = place.copy("x", source, slots[1], sems.two())
        self.core = place.copy("core", source, slots[2], sems.two())
        self.last = place.copy("core", slots[1], slots[3], sems.two())

    def start(self):
        self.swap.start()
        self.core.start()
        for copy in self.near:
            copy.start()

    def forward(self):
        self.swap.wait_recv()
        self.last.start()

    def finish(self):
        self.swap.wait_send()
        self.core.wait()
        self.last.wait()
        for copy in self.near:
            copy.wait()


class QuadSum:
    def __init__(self, place, sems, terms, scratch):
        self.near, self.theirs, self.far, self.swapped = scratch
        self.core = place.copy("core", terms.at[pl.ds(2, 2)], self.theirs, sems.two())
        self.load = pltpu.make_async_copy(terms.at[pl.ds(0, 2)], self.near, sems.one())
        self.swap = place.copy("x", self.far, self.swapped, sems.two())

    def start(self):
        self.core.start()
        self.load.start()

    def middle(self):
        self.core.wait()
        self.load.wait()

        def add(part):
            self.far[part] = (self.near[1, part] + self.theirs[1, part]).astype(BF16)

        pieces(SEQ_LEN, add)
        self.swap.start()

    def ready(self):
        self.swap.wait()

    def read(self, part):
        return self.near[0, part] + self.theirs[0, part] + self.swapped[part].astype(F32)


def live_rows(place, seq_count, valid_len, part):
    rows = lax.broadcasted_iota(jnp.int32, (PIECE, 128), 0) + part.start
    length = jnp.where(place.core == 0, valid_len[0], valid_len[1])
    return ((rows < length) & (place.core < seq_count[0])).astype(F32)[:, :1]


def quad_scratch(width):
    return [
        pltpu.VMEM((2, SEQ_LEN, width), F32),
        pltpu.VMEM((2, SEQ_LEN, width), F32),
        pltpu.VMEM((SEQ_LEN, width), BF16),
        pltpu.VMEM((SEQ_LEN, width), BF16),
    ]


class Leave:
    def __init__(self, place, sems, source, target):
        rows = pl.ds(pl.multiple_of(place.core * SEQ_LEN, SEQ_LEN), SEQ_LEN)
        width = source.shape[1] // 8
        self.copies, self.here = [], []
        for index in range(8):
            part = source.at[:, pl.ds(index * width, width)]
            there = target.at[rows, place.columns(index, width)]
            self.copies.append(place.copy("core", part, there, sems.two()))
            self.here.append(pltpu.make_async_copy(part, there, sems.one()))

    def start(self):
        for copy in self.copies + self.here:
            copy.start()

    def finish(self):
        for copy in self.copies + self.here:
            copy.wait()


class BlockTerms:
    def __init__(self, sems, acts, grads, bufs, over, own, parts):
        self.acts, self.grads, self.bufs = acts, grads, bufs
        self.over, self.own, self.parts = over, own, parts
        self.early = over.shape[2]
        self.left, self.right = sems.some(2), sems.some(2)

    def copies(self, slot, left, right):
        early, rest = self.early, self.bufs.shape[2] - self.early
        return (
            pltpu.make_async_copy(self.bufs.at[slot, :, pl.ds(0, early)], left, self.left(slot)),
            pltpu.make_async_copy(self.bufs.at[slot, :, pl.ds(early, rest)], right, self.right(slot)),
        )

    def wait(self, slot):
        for copy in self.copies(slot, self.own.at[0], self.parts[0].at[0]):
            copy.wait()

    def run(self, start, stop):
        width = self.bufs.shape[1]

        def step(i, carry):
            slot, side, away = i % 2, i // 4, i % 4

            @pl.when(i >= 2)
            def _():
                self.wait(slot)

            cols = pl.ds(pl.multiple_of(i * width, width), width)
            self.bufs[slot] = mm(self.acts[:, cols], self.grads[...], TN, BF16)

            @pl.when(side == 0)
            def _():
                self.copies(slot, self.own.at[away], self.parts[0].at[0])[0].start()

            @pl.when(side == 1)
            def _():
                self.copies(slot, self.over.at[away], self.parts[0].at[0])[0].start()

            for place in range(4):

                @pl.when(away == place)
                def _(place=place):
                    self.copies(slot, self.own.at[0], self.parts[place].at[side])[1].start()

            return carry

        lax.fori_loop(start, stop, step, 0)

    def finish(self):
        self.wait(0)
        self.wait(1)


class WideMatmul:
    def __init__(self, sems, acts, weight, stage, sums, hidden, wide):
        self.acts, self.weight, self.stage, self.sums, self.hidden, self.wide = acts, weight, stage, sums, hidden, wide
        self.hid = hidden.shape[1]
        self.half = acts.shape[1] // 2
        self.count = self.hid // 128
        self.loads = [sems.some(2) for _ in range(2)]
        self.stores = [sems.some(2) for _ in range(2)]

    def columns(self, i, side):
        return pl.ds(pl.multiple_of(side * self.hid + i * 128, 128), 128)

    def fetch(self, i, phase):
        return [
            pltpu.make_async_copy(
                self.weight.at[pl.ds(phase * self.half, self.half), self.columns(i, side)],
                self.stage.at[i % 2, pl.ds(0, self.half), pl.ds(side * 128, 128)],
                self.loads[side](i % 2),
            )
            for side in range(2)
        ]

    def leave(self, i):
        return [
            pltpu.make_async_copy(
                self.sums.at[i, :, pl.ds(side * 128, 128)], self.wide.at[:, self.columns(i, side)], self.stores[side](i % 2)
            )
            for side in range(2)
        ]

    def begin(self, phase):
        for copy in self.fetch(0, phase):
            copy.start()

    def run(self, phase):
        def step(i, carry):
            for copy in self.fetch(i, phase):
                copy.wait()

            @pl.when(i + 1 < self.count)
            def _():
                for copy in self.fetch(i + 1, phase):
                    copy.start()

            both = mm(self.acts[:, phase * self.half : (phase + 1) * self.half], self.stage[i % 2, : self.half])
            if phase == 0:
                self.sums[i] = both
                return carry

            @pl.when(i >= 2)
            def _():
                for copy in self.leave(i - 2):
                    copy.wait()

            both = both + self.sums[i]
            self.sums[i] = both
            gate = both[:, :128]
            self.hidden[:, self.columns(i, 0)] = (gate / (1.0 + jnp.exp(-gate)) * both[:, 128:]).astype(BF16)
            for copy in self.leave(i):
                copy.start()
            return carry

        lax.fori_loop(0, self.count, step, 0)

    def finish(self):
        for i in (self.count - 2, self.count - 1):
            for copy in self.leave(i):
                copy.wait()


class Chunk:
    def __init__(self, place, sems, source, offset, width, target, first, y_first, stage):
        shard = source.shape[0]
        cols, span = pl.ds(first, width), source.shape[1] // 2
        here, there = (pl.ds(pl.multiple_of(at * span + offset, 128), width) for at in (place.x, 1 - place.x))
        where = target.at[place.half(shard), cols]
        at = lambda index: target.at[pl.ds(index * 2 * shard, 2 * shard), cols]
        self.y_first = y_first
        self.swap = place.copy("x", source.at[:, there], where, sems.two())
        self.keep = Keep(sems, source.at[:, here], where, stage)
        ring = lambda side: [
            place.copy("up", at((4 - i) % 4 + 4 * side), at(3 - i + 4 * side), sems.two()) for i in range(3)
        ]
        self.low = ring(0)
        self.high = ring(1) if y_first else []
        self.cross = [place.copy("y", at(i), at(4 + i), sems.two()) for i in ((0,) if y_first else (0, 3, 2, 1))]

    def enter(self):
        self.swap.start()
        self.keep.start()

    def launch(self):
        self.keep.wait()
        self.swap.wait_recv()

    def pass_low(self, step, cross=True):
        self.low[step].wait_recv()
        if step < 2:
            self.low[step + 1].start()
        if cross and not self.y_first:
            self.cross[step + 1].start()

    def turn(self):
        self.cross[0].wait_recv()
        self.high[0].start()

    def pass_high(self, step):
        self.high[step].wait_recv()
        if step < 2:
            self.high[step + 1].start()

    def crossed(self):
        if not self.y_first:
            for copy in self.cross:
                copy.wait_recv()

    def sent(self):
        for copy in [self.swap] + self.low + self.high + self.cross:
            copy.wait_send()


class Loaded:
    def __init__(self, value):
        self.value = value

    def __getitem__(self, index):
        return self.value


class Projections:
    def __init__(self, sems, acts, weight, stage, sums, target):
        self.acts, self.weight, self.stage, self.sums, self.target = acts, weight, stage, sums, target
        self.loads, self.stores = sems.some(2), sems.some(7)

    def fetch(self, i):
        cols = pl.ds(pl.multiple_of(i * 256, 256), 256)
        return pltpu.make_async_copy(self.weight.at[:, cols], self.stage.at[i % 2], self.loads(i % 2))

    def fetch_last(self):
        return pltpu.make_async_copy(
            self.weight.at[:, pl.ds(3 * KDIM, 128)], self.stage.at[0, :, pl.ds(0, 128)], self.loads(0)
        )

    def leave(self, i, width=256):
        cols = pl.ds(i * 256, width)
        return pltpu.make_async_copy(self.sums.at[i, :, pl.ds(0, width)], self.target.at[:, cols], self.stores(i))

    def run(self):
        self.fetch(0).start()

        def step(i, carry):
            self.fetch(i).wait()

            @pl.when(i < 5)
            def _():
                self.fetch(i + 1).start()

            self.sums[i] = mm(self.acts[...], self.stage[i % 2])
            return carry

        lax.fori_loop(0, 6, step, 0)
        last = self.fetch_last()
        last.start()
        last.wait()
        self.sums[6, :, :128] = mm(self.acts[...], self.stage[0, :, :128])
        for i in range(6):
            self.leave(i).start()
        self.leave(6, 128).start()

    def mix(self, outs):
        def step(i, carry):
            rows = pl.ds(pl.multiple_of(i * SEQ_LEN, SEQ_LEN), SEQ_LEN)
            pair = lambda j: Loaded(jnp.concatenate([self.sums[j, rows, :], self.sums[j + 1, rows, :]], axis=1))
            forget = Loaded(self.sums[6, rows, :128])
            forward_kernel(pair(0), pair(2), pair(4), forget, *(out.at[rows] for out in outs))
            return carry

        lax.fori_loop(0, 4, step, 0)

    def finish(self):
        for i in range(6):
            self.leave(i).wait()
        self.leave(6, 128).wait()


class AttnTerms:
    def __init__(self, sems, mixed, weight, bufs, target):
        self.mixed, self.weight, self.bufs, self.target = mixed, weight, bufs, target
        self.stores = sems.some(2)

    def store(self, i):
        width = self.bufs.shape[3]
        cols = pl.ds(pl.multiple_of(i * width, width), width)
        return pltpu.make_async_copy(self.bufs.at[i % 2], self.target.at[:, :, cols], self.stores(i % 2))

    def run(self):
        width = self.bufs.shape[3]

        def step(i, carry):
            @pl.when(i >= 2)
            def _():
                self.store(i).wait()

            block = self.weight[pl.ds(pl.multiple_of(i * width, width), width), :]
            self.bufs[i % 2] = mm(self.mixed[...], block, NT).reshape(4, SEQ_LEN, width)
            self.store(i).start()
            return carry

        lax.fori_loop(0, 8, step, 0)
        self.store(6).wait()
        self.store(7).wait()


def forward_all_kernel(
    hid, cut, tokens, cot, seq_count, valid_len, gain0, gain1, q_w, k_w, v_w, forget_w, out_w, gate_w, up_w, down_w,
    w_in, w_out, own, attn_in, d_res, d_ffn, gains, proj, save_p, save_s, save_a, save_b, save_mixed, terms,
    w_wide, w_down, resid, ffn_in, wide, hidden, down_over, down_own, down0, down1, down2, down3,
    stage, seqs, acts, scales, turned, grads, low, small, p_v, s_v, a_v, b_v, mixed_v, out_v, term_bufs,
    s0, s1, s2, s3, kept, inputs, tiles, sums, hid_v, bufs, sem
):
    place, sems = Place(), Sems(sem)
    shard = q_w.shape[0]
    used = 0

    def chunk(source, offset, width, target, first, y_first):
        nonlocal used
        used += width
        return Chunk(place, sems, source, offset, width, target, first, y_first, stage.at[:, pl.ds(used - width, width)])

    first_chunks = [
        chunk(small, 0, 128, w_in, 3 * KDIM, True),
        chunk(q_w, 0, KDIM, w_in, 0, False),
        chunk(k_w, 0, KDIM, w_in, KDIM, False),
        chunk(v_w, 0, KDIM, w_in, 2 * KDIM, False),
        chunk(out_w, 0, KDIM // 2, w_out, 0, True),
        chunk(out_w, KDIM // 2, KDIM // 2, w_out, KDIM // 2, False),
    ]
    gate = chunk(gate_w, 0, hid, w_wide, 0, False)
    up = chunk(up_w, 0, hid, w_wide, hid, False)
    down = chunk(down_w, 0, cut, w_down, 0, False)
    rest = chunk(down_w, cut, hid - cut, w_down, cut, True)
    ffn_chunks = [gate, up, down, rest]
    width = tokens.shape[1] // 8
    mine = pl.ds(pl.multiple_of(place.core * SEQ_LEN, SEQ_LEN), SEQ_LEN)
    slot = [pl.ds(i * SEQ_LEN, SEQ_LEN) for i in range(4)]
    far, side, fetch, fetch_cot = [], [], [], []
    for index in range(8):
        part = tokens.at[mine, place.columns(index, width)]
        cols = pl.ds(index * width, width)
        far.append(place.copy("x", part, seqs.at[slot[1], cols], sems.two()))
        side.append(place.copy("core", part, seqs.at[slot[2], cols], sems.two()))
        fetch.append(pltpu.make_async_copy(part, seqs.at[slot[0], cols], sems.one()))
        fetch_cot.append(
            pltpu.make_async_copy(cot.at[mine, place.columns(index, width)], grads.at[:, cols], sems.one())
        )
    last = place.copy("core", seqs.at[slot[1]], seqs.at[slot[3]], sems.two())
    quad = Quad(place, sems, low, [d_ffn.at[one] for one in slot])
    save_own = pltpu.make_async_copy(seqs.at[slot[0]], own, sems.one())
    keep_own = pltpu.make_async_copy(seqs.at[slot[0]], inputs, sems.one())
    save_res = pltpu.make_async_copy(grads, d_res, sems.one())
    save_attn = pltpu.make_async_copy(acts, attn_in, sems.one())
    load_gains = [
        pltpu.make_async_copy(w_in.at[pl.ds(i * width, width), pl.ds(3 * KDIM, 128)], turned.at[i], sems.one())
        for i in range(8)
    ]
    load_out = pltpu.make_async_copy(w_out, out_v, sems.one())
    projections = Projections(sems, acts, w_in, tiles, sums, proj)
    saves = [
        pltpu.make_async_copy(a, b, sems.one())
        for a, b in ((p_v, save_p), (s_v, save_s), (a_v, save_a), (b_v, save_b), (mixed_v, save_mixed))
    ]
    attn_terms = AttnTerms(sems, mixed_v, out_v, term_bufs, terms)
    total = QuadSum(place, sems, terms, (s0, s1, s2, s3))
    slots = [acts.at[one] for one in slot]
    out = Quad(place, sems, slots[0], [None] + slots[1:])
    save = pltpu.make_async_copy(kept, resid, sems.one())
    save_in = pltpu.make_async_copy(acts, ffn_in, sems.one())
    save_hidden = pltpu.make_async_copy(hid_v, hidden, sems.one())
    fetch_cots = pltpu.make_async_copy(d_ffn, seqs, sems.one())
    matmul = WideMatmul(sems, acts, w_wide, tiles, sums, hid_v, wide)
    grad = BlockTerms(sems, seqs, hid_v, bufs, down_over, down_own, (down0, down1, down2, down3))
    lane = lax.broadcasted_iota(jnp.int32, (shard, 128), 1)
    column = jnp.concatenate([gain0[...].astype(F32).reshape(1, shard), gain1[...].astype(F32).reshape(1, shard)], axis=0)
    column = jnp.concatenate([column, jnp.zeros((6, shard), F32)], axis=0).T
    beside = jnp.where(lane == SLOTS, column[:, 0:1], jnp.where(lane == SLOTS + 1, column[:, 1:2], 0.0))
    heads = forget_w[...].astype(F32)
    small[:, :128] = jnp.where(lane < SLOTS, heads, beside).astype(BF16)
    small[:, 128:] = jnp.where(lane < SLOTS, pltpu.roll(heads, SLOTS, 1), beside).astype(BF16)
    place.greet()
    for one in first_chunks:
        one.enter()
    for copy in far + side + fetch + fetch_cot:
        copy.start()
    for one in ffn_chunks:
        one.enter()
    for one in first_chunks + ffn_chunks:
        one.keep.turn()
    for one in first_chunks:
        one.launch()
        one.low[0].start()
        one.cross[0].start()
    for copy in fetch + fetch_cot:
        copy.wait()
    save_own.start()
    keep_own.start()

    def mask(part):
        value = grads[part] * live_rows(place, seq_count, valid_len, part)
        grads[part] = value
        low[part] = value.astype(BF16)

    pieces(SEQ_LEN, mask)
    save_res.start()
    quad.start()
    for one in first_chunks:
        if one.y_first:
            one.turn()

    def measure(index):
        def work(part):
            rows = pl.ds(index * SEQ_LEN + part.start, PIECE)
            scales[rows] = jnp.broadcast_to(rms(seqs[rows].astype(F32)), (PIECE, 128))

        pieces(SEQ_LEN, work)

    def norm_first(index):
        def work(part):
            rows = pl.ds(index * SEQ_LEN + part.start, PIECE)
            acts[rows] = (seqs[rows].astype(F32) * scales[rows, :1] * gains[0:1, :]).astype(BF16)

        pieces(SEQ_LEN, work)

    for step in range(3):
        for c, one in enumerate(first_chunks):
            one.pass_low(step)
            if one.y_first:
                one.pass_high(step)
            if step == 0 and c == 1:
                measure(0)
            if step == 0 and c == 5:
                for copy in far:
                    copy.wait_recv()
                last.start()
            if step == 1:
                if c == 0:
                    for copy in side:
                        copy.wait_recv()
                    last.wait_recv()
                if 1 <= c <= 3:
                    measure(c)
            if step == 2:
                if c == 0:
                    for copy in load_gains:
                        copy.start()
                    for index, copy in enumerate(load_gains):
                        copy.wait()
                        flipped = turned[index].astype(F32).T
                        gains[0:8, index * width : (index + 1) * width] = flipped[SLOTS : SLOTS + 8]
                if 1 <= c <= 4:
                    norm_first(c - 1)
        if step == 1:
            for one in ffn_chunks:
                one.launch()
                one.low[0].start()
    for one in (gate, up, rest):
        one.cross[0].start()
    save_attn.start()
    quad.forward()
    for one in first_chunks:
        one.crossed()
    load_out.start()
    projections.run()
    gate.pass_low(0)
    projections.mix((mixed_v, p_v, s_v, a_v, b_v))
    for copy in saves:
        copy.start()
    up.pass_low(0)
    load_out.wait()
    attn_terms.run()
    save_attn.wait()
    total.start()
    rest.turn()
    total.middle()
    quad.finish()
    save_own.wait()
    keep_own.wait()
    for copy in side + [last]:
        copy.wait_send()
    fetch_cots.start()
    gate.pass_low(1)
    up.pass_low(1)
    down.pass_low(0, False)
    rest.pass_low(0)
    rest.pass_high(0)
    total.ready()

    def norm(part):
        value = total.read(part) + inputs[part].astype(F32)
        kept[part] = value
        acts[part] = (value * rms(value) * gains[1:2, :]).astype(BF16)

    pieces(SEQ_LEN, norm)
    out.start()
    save.start()
    gate.pass_low(2)
    up.pass_low(2)
    down.cross[0].start()
    down.cross[1].start()
    out.forward()
    out.finish()
    save_in.start()
    projections.finish()
    matmul.begin(0)
    matmul.run(0)
    down.pass_low(1)
    rest.pass_low(1)
    rest.pass_high(1)
    gate.crossed()
    up.crossed()
    matmul.begin(1)
    matmul.run(1)
    down.pass_low(2)
    save_hidden.start()
    fetch_cots.wait()
    grad.run(0, 8)
    rest.pass_low(2)
    rest.pass_high(2)
    down.crossed()
    for one in first_chunks + ffn_chunks:
        one.sent()
    for copy in far:
        copy.wait_send()
    for copy in saves + [save_res, save, save_in, save_hidden]:
        copy.wait()
    matmul.finish()
    grad.finish()


class Sum:
    def __init__(self, place, sems, terms, given, result, first, width, scratch, span=None, start=0):
        self.own, self.other, self.from_z, self.to_z, self.final = scratch
        cols = pl.ds(first, width)
        self.loads, self.crosses = [], []
        for index in range(4):
            self.loads.append(pltpu.make_async_copy(terms.at[index, :, cols], self.own.at[index], sems.one()))
            if given is None:
                self.crosses.append(place.copy("y", terms.at[4 + index, :, cols], self.other.at[index], sems.two()))
            else:
                self.loads.append(pltpu.make_async_copy(given.at[index], self.other.at[index], sems.one()))
        self.per = len(self.loads) // 4
        self.rises = [place.copy("up", self.to_z.at[i], self.from_z.at[i], sems.two()) for i in range(3)]
        half = self.final.shape[0] // 2
        there = result.at[:, pl.ds(pl.multiple_of(place.x * (span or width) + start, 128), width)]
        self.leave = pltpu.make_async_copy(self.final.at[place.half(half)], there, sems.one())
        self.swap = place.copy("x", self.final.at[place.half(half, True)], there, sems.two())

    def start(self, step):
        index = 3 - step
        for copy in self.crosses[index : index + 1] + self.loads[index * self.per : (index + 1) * self.per]:
            copy.start()

    def step(self, step):
        index = 3 - step
        for copy in self.loads[index * self.per : (index + 1) * self.per]:
            copy.wait()
        for copy in self.crosses[index : index + 1]:
            copy.wait_recv()
        if step:
            self.rises[step - 1].wait_recv()

        def add(part):
            value = self.own[index, part].astype(F32) + self.other[index, part].astype(F32)
            if step:
                value = value + self.from_z[step - 1, part].astype(F32)
            if step < 3:
                self.to_z[step, part] = value.astype(BF16)
            else:
                self.final[part] = value

        pieces(self.final.shape[0], add)
        if step < 3:
            self.rises[step].start()
        else:
            self.swap.start()
            self.leave.start()

    def finish(self):
        for copy in self.crosses + self.rises:
            copy.wait_send()
        self.leave.wait()
        self.swap.wait()


class SumGiven:
    def __init__(self, place, sems, terms, given, result, first, width, scratch, span, start):
        self.own, self.others, self.to_y, self.from_y, self.final = scratch
        cols = pl.ds(first, width)
        self.loads = [
            pltpu.make_async_copy(terms.at[d * (terms.shape[0] // 2), :, cols], self.own.at[d], sems.one())
            for d in range(2)
        ]
        self.loads += [pltpu.make_async_copy(one, self.others.at[i], sems.one()) for i, one in enumerate(given)]
        self.cross = place.copy("y", self.to_y, self.from_y, sems.two())
        half = self.final.shape[0] // 2
        there = result.at[:, pl.ds(pl.multiple_of(place.x * span + start, 128), width)]
        self.leave = pltpu.make_async_copy(self.final.at[place.half(half)], there, sems.one())
        self.swap = place.copy("x", self.final.at[place.half(half, True)], there, sems.two())

    def start(self):
        for copy in self.loads:
            copy.start()

    def first(self):
        for copy in self.loads:
            copy.wait()

        def add(part):
            for d in (1, 0):
                value = self.own[d, part].astype(F32)
                for i in range(3):
                    value = value + self.others[i, d, part].astype(F32)
                if d:
                    self.to_y[part] = value.astype(BF16)
                else:
                    self.final[part] = value

        pieces(self.final.shape[0], add)
        self.cross.start()

    def second(self):
        self.cross.wait_recv()

        def add(part):
            self.final[part] = self.final[part] + self.from_y[part].astype(F32)

        pieces(self.final.shape[0], add)
        self.swap.start()
        self.leave.start()

    def finish(self):
        self.cross.wait_send()
        self.leave.wait()
        self.swap.wait()


def given_scratch(rows, width):
    return [
        pltpu.VMEM((2, rows, width), BF16),
        pltpu.VMEM((3, 2, rows, width), BF16),
        pltpu.VMEM((rows, width), BF16),
        pltpu.VMEM((rows, width), BF16),
        pltpu.VMEM((rows, width), F32),
    ]


def sum_scratch(rows, width):
    return [pltpu.VMEM((depth, rows, width), BF16) for depth in (4, 4, 3, 3)] + [pltpu.VMEM((rows, width), F32)]


class OutTerms:
    def __init__(self, sems, hidden, weight, stage, bufs, target):
        self.hidden, self.weight, self.stage, self.bufs, self.target = hidden, weight, stage, bufs, target
        self.loads, self.stores = sems.some(2), sems.some(2)

    def load(self, i):
        return pltpu.make_async_copy(self.weight.at[i], self.stage.at[i % 2], self.loads(i % 2))

    def store(self, i):
        width = self.bufs.shape[2]
        cols = pl.ds(pl.multiple_of(i * width, width), width)
        return pltpu.make_async_copy(self.bufs.at[i % 2], self.target.at[:, cols], self.stores(i % 2))

    def run(self, start, stop):
        def step(i, carry):
            self.load(i).wait()

            @pl.when(i < 7)
            def _():
                self.load(i + 1).start()

            @pl.when(i >= 2)
            def _():
                self.store(i).wait()

            self.bufs[i % 2] = mm(self.hidden[...], self.stage[i % 2], NT)
            self.store(i).start()
            return carry

        lax.fori_loop(start, stop, step, 0)

    def finish(self):
        self.store(6).wait()
        self.store(7).wait()


def norm_back_piece(value, gain, grad):
    scale = rms(value)
    scaled = gain * grad
    inner = jnp.mean(scaled * value, axis=-1, keepdims=True)
    gains = (grad * value * scale).reshape(PIECE // 8, 8, value.shape[1])
    return scale * scaled - value * (scale * scale * scale * inner), jnp.sum(gains, axis=0)


def thirds(columns):
    tiles = columns // 128
    wide = (tiles + 2) // 3 * 128
    return ((0, wide), (wide, wide), (2 * wide, columns - 2 * wide))


def sum_ffn_kernel(
    hid, early, gate_t, down, given, down_rest, given1, given2, given3, terms, resid, gains, d_res, ffn_in, d_wide, hidden, w_down,
    gate_sum, down_sum, d_h, d_attn, gain_sum, up_over, up_own, up0, up1, up2, up3, out_terms, *scratch
):
    *scratch, sem = scratch
    place, sems = Place(), Sems(sem)
    rest = hid - early
    down_y = Sum(place, sems, down, given, down_sum, 0, early, scratch[0:5], hid)
    down_z = SumGiven(place, sems, down_rest, (given1, given2, given3), down_sum, 0, rest, scratch[5:10], hid, early)
    gate = [
        Sum(place, sems, gate_t, None, gate_sum, first, width, scratch[10 + 5 * i : 15 + 5 * i], hid, first)
        for i, (first, width) in enumerate(thirds(hid))
    ]
    back = QuadSum(place, sems, terms, scratch[25:29])
    value, res, low, acts, ups, up_bufs, hid_v, stage, out_bufs = scratch[29:38]
    quad = Quad(place, sems, low, [d_attn.at[i] for i in range(4)])
    up = BlockTerms(sems, acts, ups, up_bufs, up_over, up_own, (up0, up1, up2, up3))
    out = OutTerms(sems, hid_v, w_down, stage, out_bufs, out_terms)
    ready = [
        pltpu.make_async_copy(ffn_in, acts, sems.one()),
        pltpu.make_async_copy(d_wide.at[:, pl.ds(hid, hid)], ups, sems.one()),
        pltpu.make_async_copy(hidden, hid_v, sems.one()),
    ]
    fetch = [pltpu.make_async_copy(resid, value, sems.one()), pltpu.make_async_copy(d_res, res, sems.one())]
    save = pltpu.make_async_copy(res, d_h, sems.one())
    place.greet()
    back.start()
    for one in (down_y, *gate):
        one.start(0)
    down_z.start()
    for copy in fetch:
        copy.start()
    for one in (down_y, *gate):
        one.start(1)
    down_y.step(0)
    down_z.first()
    for step in (2, 3):
        for one in (down_y, *gate):
            one.start(step)
    for copy in ready:
        copy.start()
    out.load(0).start()
    back.middle()
    for one in gate:
        one.step(0)
    for copy in fetch + ready:
        copy.wait()
    down_y.step(1)
    back.ready()
    gain_sum[...] = jnp.zeros_like(gain_sum)

    def norm(part):
        d_norm, added = norm_back_piece(value[part], gains[1:2, :], back.read(part))
        grad = res[part] + d_norm
        res[part] = grad
        low[part] = grad.astype(BF16)
        gain_sum[...] += added

    pieces(SEQ_LEN, norm)
    quad.start()
    save.start()
    for one in gate:
        one.step(1)
    down_y.step(2)
    up.run(0, 8)
    down_z.second()
    for one in gate:
        one.step(2)
    down_y.step(3)
    out.run(0, 8)
    quad.forward()
    for one in gate:
        one.step(3)
    quad.finish()
    save.wait()
    up.finish()
    out.finish()
    for one in (down_y, down_z, *gate):
        one.finish()


def sum_last_kernel(
    hid, early, up, given, up_rest, given1, given2, given3, out_t, in_t, terms, tokens, gain_rows, d_h, ffn_gains, out_terms, resid, seq_count, valid_len,
    up_sum, out_sum, q_sum, k_sum, v_sum, f_sum, grad, block_out, gain_sum, *scratch
):
    *scratch, sem = scratch
    place, sems = Place(True), Sems(sem)
    sums = []
    for terms_in, given_in, result, first, width, span, start in (
        (up, given, up_sum, 0, early, hid, 0),
        (out_t, None, out_sum, 0, KDIM, None, 0),
        (in_t, None, q_sum, 0, KDIM, None, 0),
        (in_t, None, k_sum, KDIM, KDIM, None, 0),
        (in_t, None, v_sum, 2 * KDIM, KDIM, None, 0),
        (in_t, None, f_sum, 3 * KDIM, 128, None, 0),
    ):
        sums.append(Sum(place, sems, terms_in, given_in, result, first, width, scratch[:5], span, start))
        scratch = scratch[5:]
    up_z = SumGiven(place, sems, up_rest, (given1, given2, given3), up_sum, 0, hid - early, scratch[:5], hid, early)
    scratch = scratch[5:]
    back = QuadSum(place, sems, terms, scratch[0:4])
    ahead = QuadSum(place, sems, out_terms, scratch[4:8])
    value, res, kept, shown, gains, parts, met, crossed, risen, last, swapped = scratch[8:]
    leave = Leave(place, sems, res, grad)
    leave_out = Leave(place, sems, shown, block_out)
    fetch = [pltpu.make_async_copy(tokens, value, sems.one()), pltpu.make_async_copy(d_h, res, sems.one())]
    fetch.append(pltpu.make_async_copy(resid, kept, sems.one()))
    meet = place.copy("core", parts, met, sems.two())
    cross = place.copy("y", parts.at[pl.ds(4, 4)], crossed, sems.two())
    spread = [
        place.copy(name, parts.at[i + 1], risen.at[i], sems.two()) for i, name in enumerate(("up", "two", "down"))
    ]
    swap = place.copy("x", last.at[1 - place.x], swapped, sems.two())
    place.greet()
    back.start()
    for one in sums:
        one.start(0)
    up_z.start()
    for copy in fetch:
        copy.start()
    for one in sums:
        one.start(1)
    ahead.start()
    sums[0].step(0)
    up_z.first()
    for one in sums:
        one.start(2)
    back.middle()
    for one in sums[1:]:
        one.step(0)
    for copy in fetch:
        copy.wait()
    gains[...] = jnp.zeros_like(gains)
    back.ready()

    def norm(part):
        d_norm, added = norm_back_piece(value[part].astype(F32), gain_rows[0:1, :], back.read(part))
        res[part] = res[part] + d_norm
        gains[...] += added

    pieces(SEQ_LEN, norm)
    leave.start()
    width = res.shape[1] // 8
    parts[...] = jnp.zeros_like(parts)
    for row, source in enumerate((gains[...], ffn_gains[...])):
        summed = jnp.sum(source, axis=0, keepdims=True)
        for index in range(8):
            parts[index, row : row + 1, :] = summed[:, index * width : (index + 1) * width]
    meet.start()
    sums[0].step(1)
    meet.wait()
    parts[...] = parts[...] + met[...]
    cross.start()
    for one in sums:
        one.start(3)
    for one in sums[1:]:
        one.step(1)
    ahead.middle()
    up_z.second()
    for one in sums:
        one.step(2)
    cross.wait()
    parts[pl.ds(0, 4)] = parts[pl.ds(0, 4)] + crossed[...]
    for copy in spread:
        copy.start()
    ahead.ready()

    def show(part):
        alive = live_rows(place, seq_count, valid_len, part)
        shown[part] = (alive * (kept[part] + ahead.read(part))).astype(BF16)

    pieces(SEQ_LEN, show)
    leave_out.start()
    for one in sums:
        one.step(3)
    for copy in spread:
        copy.wait_recv()
    total = parts[0] + risen[0] + risen[1] + risen[2]
    last[0] = total[:, : width // 2]
    last[1] = total[:, width // 2 :]
    swap.start()
    swap.wait()
    gain_sum[...] = last[place.x] + swapped[...]
    for copy in spread:
        copy.wait_send()
    leave.finish()
    leave_out.finish()
    up_z.finish()
    for one in sums:
        one.finish()


def call(kernel, name, ident, inputs, specs, outputs, out_specs, scratch, sems):
    return pl.pallas_call(
        kernel,
        in_specs=specs,
        out_specs=out_specs,
        out_shape=[jax.ShapeDtypeStruct(shape, kind) for shape, kind in outputs],
        scratch_shapes=scratch + [DMA((sems,))],
        compiler_params=pltpu.CompilerParams(collective_id=ident, has_side_effects=True, vmem_limit_bytes=60 << 20),
        name=name,
    )(*inputs)


PAD = 128 - SLOTS
EARLY = 896


class Ring:
    def __init__(self, count):
        self.count = count
        self.stages = []
        left, stride = count // 2, count
        while left > 1:
            size = 4 if left % 4 == 0 else 2
            stride //= size
            left //= size
            self.stages.append((stride, size))

    def perm(self, stride, size, shift):
        moves = []
        for source in range(self.count):
            digit = source // stride % size
            moves.append((source, source + ((digit + shift) % size - digit) * stride))
        return moves

    def send(self, value, stage, shift):
        stride, size = stage
        return lax.ppermute(value, "dp", self.perm(stride, size, shift % size))

    def swap(self, value):
        return lax.ppermute(value, "dp", self.perm(1, 2, 1))

    def digit(self, stage):
        return lax.axis_index("dp") // stage[0] % stage[1]

    def gather(self, block):
        blocks = [block]
        for stage in self.stages:
            more = list(blocks)
            for shift in range(1, stage[1]):
                more += [self.send(one, stage, -shift) for one in blocks]
            blocks = more
        return blocks

    def scatter(self, make):
        def level(depth, offset, width):
            if depth == len(self.stages):
                return lambda inner: make(offset + inner)
            return None

        widths = [1]
        for stage in self.stages:
            widths.append(widths[-1] * stage[1])

        def total(depth, index):
            if depth == len(self.stages):
                return make(index)
            stage = self.stages[depth]
            parts = []
            for shift in range(1, stage[1]):
                sent = total(depth + 1, index + shift * widths[depth]).astype(BF16)
                parts.append(self.send(sent, stage, shift))
            mine = total(depth + 1, index)
            for part in parts:
                mine = mine + part.astype(F32)
            return mine

        return total(0, 0)

    def order(self, value, width, back=False):
        parts = [value[:, i * width : (i + 1) * width] for i in range(self.count // 2)]
        stages = self.stages
        if back:
            parts = self.turn_digits(parts, [s[1] for s in stages[::-1]])
        inner = len(parts)
        for stage in stages:
            size = stage[1]
            inner //= size
            digit = self.digit(stage)
            new = []
            for place in range(len(parts)):
                at = place // inner % size
                base = place - at * inner
                picks = []
                for k in range(size):
                    picks.append(parts[base + ((at - k) % size if back else (at + k) % size) * inner])
                one = picks[0]
                for k in range(1, size):
                    one = jnp.where(digit == k, picks[k], one)
                new.append(one)
            parts = new
        if not back:
            parts = self.turn_digits(parts, [s[1] for s in stages])
        return jnp.concatenate(parts, axis=1)

    def turn_digits(self, parts, sizes):
        count = len(parts)
        out = [None] * count
        for index in range(count):
            rest, digits = index, []
            for size in reversed(sizes):
                digits.append(rest % size)
                rest //= size
            new = 0
            for digit, size in zip(digits, reversed(sizes)):
                new = new * size + digit
            out[new] = parts[index]
        return out


def mm(left, right, dims=NN, kind=F32):
    return lax.dot_general(left, right, dims, preferred_element_type=F32).astype(kind)


def rms(values):
    return lax.rsqrt(jnp.mean(values * values, axis=-1, keepdims=True) + 1e-06)


def norm_back(values, gain, grad):
    scale = rms(values)
    scaled = gain * grad
    inner = jnp.mean(scaled * values, axis=-1, keepdims=True)
    return scale * scaled - values * (scale * scale * scale * inner), jnp.sum(grad * values * scale, axis=0)


def body_by_permutes(
    tokens,
    seq_count,
    valid_len,
    attn_gain,
    ffn_gain,
    q_weight,
    k_weight,
    v_weight,
    forget_weight,
    out_weight,
    gate_weight,
    up_weight,
    down_weight,
    cotangent,
    *,
    ring,
):
    shard = q_weight.shape[0]
    width = 2 * shard
    core = lax.axis_index("head")
    even = lax.axis_index("dp") % 2 == 0
    first = core == 0
    rows = tokens.shape[0]

    def other_core(value):
        return lax.ppermute(value, "head", [(0, 1), (1, 0)])

    def pair_rows(mine, theirs, axis=0):
        return jnp.where(
            even, jnp.concatenate([mine, theirs], axis=axis), jnp.concatenate([theirs, mine], axis=axis)
        )

    def gather(parts):
        left = jnp.concatenate([p[0] for p in parts], axis=1)
        right = jnp.concatenate([p[1] for p in parts], axis=1)
        mine, theirs = jnp.where(even, left, right), jnp.where(even, right, left)
        return jnp.concatenate(ring.gather(pair_rows(mine, ring.swap(theirs))), axis=0)

    def cut(weight):
        half = weight.shape[1] // 2
        return (weight[:, :half], weight[:, half:])

    def quad_gather(mine):
        chips = jnp.concatenate([mine, ring.swap(mine)], axis=0)
        return jnp.concatenate([chips, other_core(chips)], axis=0)

    def quad_scatter(make):
        theirs = other_core(make(slice(2 * SEQ_LEN, 4 * SEQ_LEN)))
        far = make(slice(SEQ_LEN, 2 * SEQ_LEN)) + theirs[SEQ_LEN:]
        near = make(slice(0, SEQ_LEN)) + theirs[:SEQ_LEN]
        return near + ring.swap(far.astype(BF16)).astype(F32)

    def whole_rows(mine):
        theirs = other_core(mine)
        return jnp.where(
            first, jnp.concatenate([mine, theirs], axis=0), jnp.concatenate([theirs, mine], axis=0)
        )

    def weight_sum(act, grads):
        def make(index):
            return mm(act[:, index * width : (index + 1) * width], grads, TN)

        done = ring.scatter(make)
        mine = jnp.where(even, done[:shard], done[shard:])
        theirs = ring.swap(jnp.where(even, done[shard:], done[:shard]))
        return (jnp.where(even, mine, theirs), jnp.where(even, theirs, mine))

    gains = jnp.concatenate(
        [attn_gain[:, None], ffn_gain[:, None], jnp.zeros((shard, PAD - 2), BF16)], axis=1
    )
    w_in = gather([cut(q_weight), cut(k_weight), cut(v_weight), cut(forget_weight), (gains, gains)])
    w_out = gather([cut(out_weight)])
    w_gate = gather([cut(gate_weight)])
    w_up = gather([cut(up_weight)])
    w_down = gather([cut(down_weight)])
    gain_attn = w_in[:, WIDE - PAD].astype(F32)[None, :]
    gain_ffn = w_in[:, WIDE - PAD + 1].astype(F32)[None, :]

    def own(value):
        return ring.order(jnp.where(first, value[:SEQ_LEN], value[SEQ_LEN:]), width)

    places = lax.broadcasted_iota(jnp.int32, (SEQ_LEN, 1), 0)
    length = jnp.where(first, valid_len[0], valid_len[1])
    live = ((core < seq_count[0]) & (places < length)).astype(F32)
    own_tokens = own(tokens)
    d_res = live * own(cotangent)
    d_ffn = quad_gather(d_res.astype(BF16))
    inputs = quad_gather(own_tokens).astype(F32)
    attn_in = (inputs * rms(inputs) * gain_attn).astype(BF16)
    proj = mm(attn_in, w_in)
    mixed, *saved = mixer_forward(proj)
    own_inputs = own_tokens.astype(F32)
    resid = own_inputs + quad_scatter(lambda r: mm(mixed[r], w_out, NT))
    ffn_in = quad_gather((resid * rms(resid) * gain_ffn).astype(BF16))
    gate, up_vals = mm(ffn_in, w_gate), mm(ffn_in, w_up)
    sig = jax.nn.sigmoid(gate)
    hidden = (gate * sig * up_vals).astype(BF16)
    d_hidden = mm(d_ffn, w_down)
    d_gate = (d_hidden * up_vals * (sig * (1.0 + gate * (1.0 - sig)))).astype(BF16)
    d_up = (d_hidden * (gate * sig)).astype(BF16)
    d_ffn_in = quad_scatter(lambda r: mm(d_gate[r], w_gate, NT) + mm(d_up[r], w_up, NT))
    down_sum = weight_sum(d_ffn, hidden)
    gate_sum = weight_sum(ffn_in, d_gate)
    up_sum = weight_sum(ffn_in, d_up)
    ffn = quad_scatter(lambda r: mm(hidden[r], w_down, NT))
    block_out = whole_rows(ring.order((live * (resid + ffn)).astype(BF16), width, back=True))
    d_norm, ffn_gain_part = norm_back(resid, gain_ffn, d_ffn_in)
    d_h = d_res + d_norm
    d_attn = quad_gather(d_h.astype(BF16))
    d_mixed = mm(d_attn, w_out)
    d_proj = mixer_backward(proj, saved, d_mixed)
    d_attn_in = quad_scatter(lambda r: mm(d_proj[r], w_in, NT))
    out_sum = weight_sum(d_attn, mixed)
    in_sum = weight_sum(attn_in, d_proj)
    d_input, attn_gain_part = norm_back(own_inputs, gain_attn, d_attn_in)
    input_grad = whole_rows(ring.order(d_h + d_input, width, back=True))

    both = jnp.stack([attn_gain_part, ffn_gain_part], axis=0)
    both = both + other_core(both)
    both = both.reshape(2, ring.count // 2, width)
    for stage in ring.stages[::-1]:
        size = stage[1]
        both = both.reshape(2, size, -1, width)
        parts = [ring.send(both[:, shift], stage, shift) for shift in range(1, size)]
        both = both[:, 0]
        for part in parts:
            both = both + part
    both = both.reshape(2, 2, shard)
    both = jnp.where(even, both[:, 0], both[:, 1]) + ring.swap(jnp.where(even, both[:, 1], both[:, 0]))

    def columns(pieces, start, stop):
        return jnp.concatenate([p[:, start:stop] for p in pieces], axis=1)

    return (
        block_out,
        input_grad,
        both[0],
        both[1],
        columns(in_sum, 0, KDIM),
        columns(in_sum, KDIM, 2 * KDIM),
        columns(in_sum, 2 * KDIM, 3 * KDIM),
        columns(in_sum, 3 * KDIM, 3 * KDIM + SLOTS),
        columns(out_sum, 0, KDIM),
        jnp.concatenate(gate_sum, axis=1),
        jnp.concatenate(up_sum, axis=1),
        jnp.concatenate(down_sum, axis=1),
    )


def body_by_kernels(
    tokens,
    seq_count,
    valid_len,
    attn_gain,
    ffn_gain,
    q_weight,
    k_weight,
    v_weight,
    forget_weight,
    out_weight,
    gate_weight,
    up_weight,
    down_weight,
    cotangent,
    *,
    ring,
):
    shard, dim = q_weight.shape[0], tokens.shape[1]
    width, hid = 2 * shard, gate_weight.shape[1] // 2
    over_y = lambda value: ring.send(value, ring.stages[1], 1)
    rows4 = (4, SEQ_LEN, dim)
    blocks = lambda value: value.reshape(-1, width, value.shape[-1])
    flat = lambda value: value.reshape(-1, value.shape[-1])
    half = dim // 2

    row = (SEQ_LEN, dim)
    vmem = lambda shape, kind=F32: pltpu.VMEM(shape, kind)
    tokens4 = 4 * SEQ_LEN
    cut = hid // 256 * 128 + 128
    full = (tokens4, dim)
    early, rest = [((4, width, EARLY), BF16)] * 2, [((2, width, hid - EARLY), BF16)] * 4
    (
        w_in, w_out, own, attn_in, d_res, d_ffn, gain_rows, proj, *saved, mixed, _,
        w_wide, w_down, resid, ffn_in, wide, hidden, down_over, down_own, down0, down1, down2, down3,
    ) = call(
        functools.partial(forward_all_kernel, hid, cut),
        "forward_all",
        0,
        (
            tokens,
            cotangent,
            seq_count,
            valid_len,
            attn_gain,
            ffn_gain,
            q_weight,
            k_weight,
            v_weight,
            forget_weight,
            out_weight,
            gate_weight,
            up_weight,
            down_weight,
        ),
        [ANY, ANY, SMEM, SMEM, VMEM, VMEM, ANY, ANY, ANY, VMEM] + [ANY] * 4,
        [((dim, WIDE), BF16), ((dim, KDIM), BF16), (row, BF16), (full, BF16), (row, F32), (full, BF16), ((8, dim), F32)]
        + [((tokens4, WIDE), F32), ((tokens4, 128), F32), ((tokens4, 128), F32)]
        + [((tokens4, SEQ_LEN), F32), ((tokens4, SEQ_LEN), F32), ((tokens4, KDIM), BF16), (rows4, F32)]
        + [((dim, 2 * hid), BF16), ((dim, hid), BF16), (row, F32), (full, BF16)]
        + [((tokens4, 2 * hid), F32), ((tokens4, hid), BF16)]
        + early
        + rest,
        [ANY] * 6 + [VMEM] + [ANY] * 19,
        [
            vmem((shard, 4 * KDIM + 128 + 3 * hid), BF16),
            vmem(full, BF16),
            vmem(full, BF16),
            vmem((tokens4, 128)),
            vmem((8, width, 128), BF16),
            vmem(row),
            vmem(row, BF16),
            vmem((shard, 256), BF16),
            vmem((tokens4, 128)),
            vmem((tokens4, 128)),
            vmem((tokens4, SEQ_LEN)),
            vmem((tokens4, SEQ_LEN)),
            vmem((tokens4, KDIM), BF16),
            vmem((dim, KDIM), BF16),
            vmem((2, 4, SEQ_LEN, width)),
        ]
        + quad_scratch(dim)
        + [
            vmem(row),
            vmem(row, BF16),
            vmem((2, dim, 256), BF16),
            vmem((hid // 128, tokens4, 256)),
            vmem((tokens4, hid), BF16),
            vmem((2, width, hid), BF16),
        ],
        360,
    )
    down_parts = [down0, down1, down2, down3]

    def exchange(over, parts):
        return [over_y(over)] + [ring.send(parts[d], ring.stages[0], d) for d in (1, 2, 3)]

    down_given = exchange(down_over, down_parts)
    gate, up_vals = wide[:, :hid], wide[:, hid:]
    sig = jax.nn.sigmoid(gate)
    d_hidden = mm(d_ffn, w_down)
    d_gate = (d_hidden * up_vals * (sig * (1.0 + gate * (1.0 - sig)))).astype(BF16)
    d_up = (d_hidden * (gate * sig)).astype(BF16)
    d_wide = jnp.concatenate([d_gate, d_up], axis=1)
    gate_terms = mm(ffn_in, d_wide[:, :hid], TN, BF16)
    d_ffn_terms = mm(d_wide, w_wide, NT).reshape(rows4)
    gate_sum, down_sum, d_h, d_attn, ffn_gains, up_over, up_own, *up_parts, ffn_terms = call(
        functools.partial(sum_ffn_kernel, hid, EARLY),
        "sum_ffn",
        2,
        (
            blocks(gate_terms),
            down_own,
            down_given[0],
            down_parts[0],
            *down_given[1:],
            d_ffn_terms,
            resid,
            gain_rows,
            d_res,
            ffn_in,
            d_wide,
            hidden,
            blocks(w_down),
        ),
        [ANY] * 9 + [VMEM] + [ANY] * 5,
        [((shard, 2 * hid), F32), ((shard, 2 * hid), F32), (row, F32), (rows4, BF16), ((8, dim), F32)]
        + early
        + rest
        + [((4 * SEQ_LEN, dim), F32)],
        [ANY] * 4 + [VMEM] + [ANY] * 7,
        sum_scratch(width, EARLY)
        + given_scratch(width, hid - EARLY)
        + [one for _, columns in thirds(hid) for one in sum_scratch(width, columns)]
        + quad_scratch(dim)
        + [vmem(row), vmem(row), vmem(row, BF16)]
        + [vmem((4 * SEQ_LEN, dim), BF16), vmem((4 * SEQ_LEN, hid), BF16), vmem((2, width, hid), BF16)]
        + [vmem((4 * SEQ_LEN, hid), BF16), vmem((2, width, hid), BF16), vmem((2, 4 * SEQ_LEN, width))],
        220,
    )
    d_attn = flat(d_attn)
    up_given = exchange(up_over, up_parts)
    d_proj = mixer_backward(proj, saved, mm(d_attn, w_out))
    d_attn_terms = mm(d_proj, w_in, NT).reshape(rows4)
    ffn_terms = ffn_terms.reshape(rows4)
    tail = width // 2
    up_sum, out_sum, q_sum, k_sum, v_sum, f_sum, input_grad, block_out, gain_sums = call(
        functools.partial(sum_last_kernel, hid, EARLY),
        "sum_last",
        3,
        (
            up_own,
            up_given[0],
            up_parts[0],
            *up_given[1:],
            blocks(mm(d_attn, mixed, TN, BF16)),
            blocks(mm(attn_in, d_proj, TN, BF16)),
            d_attn_terms,
            own,
            gain_rows,
            d_h,
            ffn_gains,
            ffn_terms,
            resid,
            seq_count,
            valid_len,
        ),
        [ANY] * 10 + [VMEM, ANY, VMEM, ANY, ANY, SMEM, SMEM],
        [((shard, 2 * hid), F32)]
        + [((shard, 2 * KDIM), F32)] * 4
        + [((shard, 256), F32), ((2 * SEQ_LEN, dim), F32), ((2 * SEQ_LEN, dim), BF16), ((8, tail), F32)],
        [ANY] * 8 + [VMEM],
        sum_scratch(width, EARLY)
        + sum_scratch(width, KDIM) * 4
        + sum_scratch(width, 128)
        + given_scratch(width, hid - EARLY)
        + quad_scratch(dim) * 2
        + [vmem(row, BF16), vmem(row), vmem(row), vmem(row, BF16), vmem((8, dim))]
        + [vmem((depth, 8, width)) for depth in (8, 8, 4, 3)]
        + [vmem((2, 8, tail)), vmem((8, tail))],
        280,
    )
    f_grad = jnp.concatenate([f_sum[:, :SLOTS], f_sum[:, 128 : 128 + SLOTS]], axis=1)
    return (
        block_out,
        input_grad,
        gain_sums[0],
        gain_sums[1],
        q_sum,
        k_sum,
        v_sum,
        f_grad,
        out_sum,
        gate_sum,
        up_sum,
        down_sum,
    )


def solution(mesh):
    ring = Ring(mesh.shape["dp"])
    body = body_by_kernels if ring.count == 16 else body_by_permutes
    split_one, split_two = P("dp"), P("dp", "head")
    row = P("dp", None)
    in_specs = (row, split_one, split_one, split_one, split_one) + (split_two,) * 8 + (row,)
    out_specs = (row, row, split_one, split_one) + (split_two,) * 8
    return jax.shard_map(
        functools.partial(body, ring=ring),
        mesh=mesh,
        in_specs=in_specs,
        out_specs=out_specs,
        check_vma=False,
    )
```

```python
import functools
import jax
import jax.numpy as jnp
from jax import lax
from jax.experimental import pallas as pl
from jax.experimental.pallas import tpu as pltpu
from jax.sharding import PartitionSpec as P

SLOTS = 64
KDIM = 512
SEQ_LEN = 256
HALF = 128
F32, BF16 = jnp.float32, jnp.bfloat16
WIDE = 3 * KDIM + 128
NT = (((1,), (1,)), ((), ()))
NN = (((1,), (0,)), ((), ()))
TN = (((0,), (0,)), ((), ()))
LEVELS = (8, 16, 32, 64)


def split(value):
    high = value.astype(BF16)
    return high, (value - high.astype(F32)).astype(BF16)


def dot3(left, right, dims):
    one = functools.partial(lax.dot_general, dimension_numbers=dims, preferred_element_type=F32)
    return one(left[0], right[0]) + (one(left[0], right[1]) + one(left[1], right[0]))


def silu_parts(value):
    gate = 1.0 / (1.0 + jnp.exp(-value))
    return gate, value * gate


def level_mask(size):
    row = lax.broadcasted_iota(jnp.int32, (HALF, HALF), 0) // size
    col = lax.broadcasted_iota(jnp.int32, (HALF, HALF), 1) // size
    return (row == col + 1) & (row % 2 == 1)


def band_mask(back):
    row = lax.broadcasted_iota(jnp.int32, (HALF, HALF), 0)
    col = lax.broadcasted_iota(jnp.int32, (HALF, HALF), 1)
    return (row == col + back) & (row // 8 == col // 8)


def down(value, back):
    return value if back == 0 else pltpu.roll(value, back, 0)


def up(value, back):
    return value if back == 0 else pltpu.roll(value, SEQ_LEN - back, 0)


def gates(forget):
    lane = lax.broadcasted_iota(jnp.int32, forget.shape, 1) < SLOTS
    place = lax.broadcasted_iota(jnp.int32, forget.shape, 0)
    forget = jnp.where(lane, forget, 0.0)
    tail = jnp.exp(-jnp.abs(forget))
    log_decay = (jnp.minimum(forget, 0.0) - jnp.log1p(tail)) * 0.125
    log_decay = jnp.where(lane, log_decay, 0.0)
    g = log_decay
    series = 1.0 + g * (1.0 / 7.0)
    for n in (6.0, 5.0, 4.0, 3.0, 2.0):
        series = 1.0 + g * (1.0 / n) * series
    writes = jnp.where(g > -0.3, -g * series, 1.0 - jnp.exp(g))
    writes = jnp.where(lane, writes, 0.0)
    ahead, behind = g, g
    for step in (1, 2, 4):
        ahead = ahead + jnp.where(place % 8 >= step, down(ahead, step), 0.0)
        behind = behind + jnp.where(place % 8 < 8 - step, up(behind, step), 0.0)
    behind = jnp.where(place % 8 < 7, up(behind, 1), 0.0)
    aheads, behinds = {8: ahead}, {8: behind}
    size = 8
    while size < HALF:
        first = ahead.reshape(SEQ_LEN // (2 * size), 2, size, 128)
        last = behind.reshape(SEQ_LEN // (2 * size), 2, size, 128)
        left, right = first[:, 0:1], first[:, 1:2]
        left_sum, right_sum = left[:, :, size - 1 :], right[:, :, size - 1 :]
        ahead = jnp.concatenate([left, right + left_sum], axis=1).reshape(SEQ_LEN, 128)
        behind = jnp.concatenate([last[:, 0:1] + right_sum, last[:, 1:2]], axis=1).reshape(SEQ_LEN, 128)
        size *= 2
        aheads[size], behinds[size] = ahead, behind
    return lane, place, g, writes, aheads, behinds


def near_decays(place, aheads, back):
    ahead = aheads[8]
    gap = jnp.where(place % 8 >= back, ahead - down(ahead, back), 0.0)
    return jnp.where(place % 8 >= back, jnp.exp(gap), 0.0)


def halves(value):
    return value[:HALF], value[HALF:]


def to_slots(blocks, cross, place, writes, aheads, behinds, nears):
    grow = {size: jnp.exp(aheads[size]) for size in LEVELS}
    keep = {size: split(jnp.exp(behinds[size]) * writes) for size in LEVELS}
    outs = []
    for half in range(2):
        here = slice(half * HALF, (half + 1) * HALF)
        block = blocks[half]
        parts = split(block)
        total = None
        for size in LEVELS:
            mask = level_mask(size)
            masked = tuple(jnp.where(mask, part, jnp.zeros_like(part)) for part in parts)
            term = grow[size][here] * dot3(masked, tuple(k[here] for k in keep[size]), NN)
            total = term if total is None else total + term
        for back in range(8):
            near = jnp.sum(jnp.where(band_mask(back), block, 0.0), axis=1, keepdims=True)
            total = total + near * nears[back][here]
        if half == 1:
            far = split((jnp.exp(behinds[HALF]) * writes)[:HALF])
            total = total + jnp.exp(aheads[HALF])[HALF:] * dot3(split(cross), far, NN)
        outs.append(total)
    return jnp.concatenate(outs, axis=0)


def to_tokens(slots, writes, aheads, behinds, nears):
    blocks = []
    for half in range(2):
        here = slice(half * HALF, (half + 1) * HALF)
        total = jnp.zeros((HALF, HALF), F32)
        for size in LEVELS:
            left = split((slots * jnp.exp(aheads[size]))[here])
            right = split((jnp.exp(behinds[size]) * writes)[here])
            total = jnp.where(level_mask(size), dot3(left, right, NT), total)
        for back in range(8):
            near = jnp.sum(slots[here] * nears[back][here], axis=1, keepdims=True)
            total = jnp.where(band_mask(back), near, total)
        blocks.append(total)
    left = split((slots * jnp.exp(aheads[HALF]))[HALF:])
    right = split((jnp.exp(behinds[HALF]) * writes)[:HALF])
    return blocks, dot3(left, right, NT)


def forward_kernel(q_ref, k_ref, v_ref, f_ref, o_ref, p_ref, s_ref, a_ref, b_ref):
    query = split(silu_parts(q_ref[...])[1] * KDIM ** (-0.5))
    keys = split(silu_parts(k_ref[...])[1])
    values = split(v_ref[...])
    lane, place, g, writes, aheads, behinds = gates(f_ref[...])
    nears = [near_decays(place, aheads, back) * down(writes, back) for back in range(8)]
    q0, q1 = tuple(x[:HALF] for x in query), tuple(x[HALF:] for x in query)
    k0, k1 = tuple(x[:HALF] for x in keys), tuple(x[HALF:] for x in keys)
    blocks = (dot3(q0, k0, NT), dot3(q1, k1, NT))
    cross = dot3(q1, k0, NT)
    scores = to_slots(blocks, cross, place, writes, aheads, behinds, nears)
    shown = jnp.where(lane, scores, -1e30)
    weights = jnp.exp(shown - jnp.max(shown, axis=1, keepdims=True))
    weights = jnp.where(lane, weights, 0.0)
    weights = weights / jnp.sum(weights, axis=1, keepdims=True)
    mixes, mix_cross = to_tokens(weights, writes, aheads, behinds, nears)
    v0 = tuple(x[:HALF] for x in values)
    o_ref[:HALF, :] = dot3(split(mixes[0]), v0, NN).astype(o_ref.dtype)
    row = jnp.concatenate([mix_cross, mixes[1]], axis=1)
    o_ref[HALF:, :] = dot3(split(row), values, NN).astype(o_ref.dtype)
    p_ref[...] = weights
    s_ref[...] = scores
    a_ref[:HALF, :] = jnp.concatenate([blocks[0], jnp.zeros_like(cross)], axis=1)
    a_ref[HALF:, :] = jnp.concatenate([cross, blocks[1]], axis=1)
    b_ref[:HALF, :] = jnp.concatenate([mixes[0], jnp.zeros_like(cross)], axis=1)
    b_ref[HALF:, :] = row


def backward_kernel(q_ref, k_ref, v_ref, f_ref, p_ref, s_ref, a_ref, b_ref, d_ref, out_ref):
    lane, place, g, writes, aheads, behinds = gates(f_ref[...])
    spans = [near_decays(place, aheads, back) for back in range(8)]
    nears = [spans[back] * down(writes, back) for back in range(8)]
    weights, scores = p_ref[...], s_ref[...]
    products, mixing = a_ref[...], b_ref[...]
    grad = split(d_ref[...])
    g0, g1 = tuple(x[:HALF] for x in grad), tuple(x[HALF:] for x in grad)
    values = split(v_ref[...])
    v0, v1 = tuple(x[:HALF] for x in values), tuple(x[HALF:] for x in values)
    m_parts = split(mixing)
    dv0 = dot3(tuple(x[:, :HALF] for x in m_parts), grad, TN)
    dv1 = dot3(tuple(x[HALF:, HALF:] for x in m_parts), g1, TN)
    out_ref[:HALF, 2 * KDIM : 3 * KDIM] = dv0.astype(BF16)
    out_ref[HALF:, 2 * KDIM : 3 * KDIM] = dv1.astype(BF16)
    mix_blocks = (dot3(g0, v0, NT), dot3(g1, v1, NT))
    mix_cross = dot3(g1, v0, NT)
    d_weights = to_slots(mix_blocks, mix_cross, place, writes, aheads, behinds, nears)
    inner = jnp.sum(weights * d_weights, axis=1, keepdims=True)
    d_scores = weights * (d_weights - inner)
    d_blocks, d_cross = to_tokens(d_scores, writes, aheads, behinds, nears)
    q_gate, q_act = silu_parts(q_ref[...])
    k_gate, k_act = silu_parts(k_ref[...])
    scale = KDIM ** (-0.5)
    query, keys = split(q_act * scale), split(k_act)
    k0 = tuple(x[:HALF] for x in keys)
    low = split(jnp.concatenate([d_cross, d_blocks[1]], axis=1))
    top = split(d_blocks[0])
    dq = jnp.concatenate([dot3(top, k0, NN), dot3(low, keys, NN)], axis=0)
    first = tuple(jnp.concatenate([t, l[:, :HALF]], axis=0) for t, l in zip(top, low))
    dk0 = dot3(first, query, TN)
    dk1 = dot3(tuple(x[:, HALF:] for x in low), tuple(x[HALF:] for x in query), TN)
    dk = jnp.concatenate([dk0, dk1], axis=0)
    out_ref[:, :KDIM] = (dq * scale * (q_gate + q_act * (1.0 - q_gate))).astype(BF16)
    out_ref[:, KDIM : 2 * KDIM] = (dk * (k_gate + k_act * (1.0 - k_gate))).astype(BF16)
    parts = []
    for half in range(2):
        here = slice(half * HALF, (half + 1) * HALF)
        both = jnp.concatenate([mix_blocks[half], products[here, here]], axis=0)
        both_parts = split(both)
        total = None
        for size in LEVELS:
            mask = level_mask(size)
            mask = jnp.concatenate([mask, mask], axis=0)
            grow = jnp.exp(aheads[size][here])
            right = split(jnp.concatenate([weights[here] * grow, d_scores[here] * grow], axis=0))
            left = tuple(jnp.where(mask, part, jnp.zeros_like(part)) for part in both_parts)
            term = jnp.exp(behinds[size][here]) * dot3(left, right, TN)
            total = term if total is None else total + term
        parts.append(total)
    grow = jnp.exp(aheads[HALF][HALF:])
    left = split(jnp.concatenate([mix_cross, products[HALF:, :HALF]], axis=0))
    right = split(jnp.concatenate([weights[HALF:] * grow, d_scores[HALF:] * grow], axis=0))
    parts[0] = parts[0] + jnp.exp(behinds[HALF][:HALF]) * dot3(left, right, TN)
    reach = jnp.concatenate(parts, axis=0)
    for back in range(8):
        mask = band_mask(back)
        near_mix = jnp.concatenate([jnp.sum(jnp.where(mask, mix_blocks[h], 0.0), axis=1, keepdims=True) for h in range(2)], axis=0)
        near_pro = jnp.concatenate(
            [jnp.sum(jnp.where(mask, products[h * HALF : (h + 1) * HALF, h * HALF : (h + 1) * HALF], 0.0), axis=1, keepdims=True) for h in range(2)],
            axis=0,
        )
        reach = reach + up((near_mix * weights + near_pro * d_scores) * spans[back], back)
    d_sum = weights * d_weights + d_scores * scores - writes * reach
    step = 1
    while step < SEQ_LEN:
        d_sum = d_sum + jnp.where(place < SEQ_LEN - step, up(d_sum, step), 0.0)
        step *= 2
    d_log = d_sum - reach * jnp.exp(g)
    d_forget = d_log * 0.125 / (1.0 + jnp.exp(f_ref[...]))
    out_ref[:, 3 * KDIM :] = jnp.where(lane, d_forget, 0.0).astype(BF16)


def spec(width, column):
    return pl.BlockSpec((SEQ_LEN, width), lambda i: (i, column))


IN_SPECS = [spec(KDIM, 0), spec(KDIM, 1), spec(KDIM, 2), spec(128, 3 * KDIM // 128)]


def mixer_forward(proj):
    rows = proj.shape[0]
    shape = lambda width, kind: jax.ShapeDtypeStruct((rows, width), kind)
    return pl.pallas_call(
        forward_kernel,
        grid=(rows // SEQ_LEN,),
        in_specs=IN_SPECS,
        out_specs=[spec(KDIM, 0), spec(128, 0), spec(128, 0), spec(SEQ_LEN, 0), spec(SEQ_LEN, 0)],
        out_shape=[shape(KDIM, BF16), shape(128, F32), shape(128, F32), shape(SEQ_LEN, F32), shape(SEQ_LEN, F32)],
        compiler_params=pltpu.CompilerParams(vmem_limit_bytes=48 << 20),
        cost_estimate=pl.CostEstimate(flops=rows * 3000000, bytes_accessed=rows * 10000, transcendentals=rows * 3000),
        name="mixer_forward",
    )(proj, proj, proj, proj)


def mixer_backward(proj, saved, grad):
    rows = proj.shape[0]
    weights, scores, products, mixing = saved
    return pl.pallas_call(
        backward_kernel,
        grid=(rows // SEQ_LEN,),
        in_specs=IN_SPECS + [spec(128, 0), spec(128, 0), spec(SEQ_LEN, 0), spec(SEQ_LEN, 0), spec(KDIM, 0)],
        out_specs=spec(WIDE, 0),
        out_shape=jax.ShapeDtypeStruct((rows, WIDE), BF16),
        compiler_params=pltpu.CompilerParams(vmem_limit_bytes=48 << 20),
        cost_estimate=pl.CostEstimate(flops=rows * 9000000, bytes_accessed=rows * 16000, transcendentals=rows * 5000),
        name="mixer_backward",
    )(proj, proj, proj, proj, weights, scores, products, mixing, grad)


MESH = pl.DeviceIdType.MESH
ANY = pl.BlockSpec(memory_space=pl.ANY)
VMEM = pl.BlockSpec(memory_space=pltpu.VMEM)
SMEM = pl.BlockSpec(memory_space=pltpu.SMEM)
DMA = pltpu.SemaphoreType.DMA
PIECE = 32


class Place:
    def __init__(self, all_z=False):
        dp = lax.axis_index("dp")
        self.core = lax.axis_index("head")
        self.x, self.y, self.z = dp % 2, dp // 2 % 2, dp // 4
        rest = dp % 4
        self.peers = {
            "x": (dp + 1 - 2 * self.x, self.core),
            "y": (dp + 2 - 4 * self.y, self.core),
            "up": ((self.z + 1) % 4 * 4 + rest, self.core),
            "down": ((self.z + 3) % 4 * 4 + rest, self.core),
            "core": (dp, 1 - self.core),
        }
        if all_z:
            self.peers["two"] = ((self.z + 2) % 4 * 4 + rest, self.core)

    def greet(self):
        ready = pltpu.get_barrier_semaphore()
        for peer in self.peers.values():
            pl.semaphore_signal(ready, inc=1, device_id=peer, device_id_type=MESH)
        pl.semaphore_wait(ready, len(self.peers))

    def copy(self, name, source, target, sems):
        return pltpu.make_async_remote_copy(
            src_ref=source,
            dst_ref=target,
            send_sem=sems[0],
            recv_sem=sems[1],
            device_id=self.peers[name],
            device_id_type=MESH,
        )

    def half(self, size, other=False):
        place = 1 - self.x if other else self.x
        return pl.ds(pl.multiple_of(place * size, size), size)

    def columns(self, index, size):
        natural = (self.z + index % 4) % 4 * 2 + (self.y + index // 4) % 2
        return pl.ds(pl.multiple_of(natural * size, size), size)


class Sems:
    def __init__(self, ref):
        self.ref, self.used = ref, 0

    def one(self):
        self.used += 1
        return self.ref.at[self.used - 1]

    def two(self):
        return (self.one(), self.one())

    def some(self, count):
        first = self.used
        self.used += count
        return lambda index: self.ref.at[first + index]


def pieces(rows, work):
    def step(i, carry):
        work(pl.ds(pl.multiple_of(i * PIECE, PIECE), PIECE))
        return carry

    lax.fori_loop(0, rows // PIECE, step, 0)


class Keep:
    def __init__(self, sems, source, target, stage):
        self.load = pltpu.make_async_copy(source, stage, sems.one())
        self.store = pltpu.make_async_copy(stage, target, sems.one())

    def start(self):
        self.load.start()

    def turn(self):
        self.load.wait()
        self.store.start()

    def wait(self):
        self.store.wait()


class Quad:
    def __init__(self, place, sems, source, slots):
        self.near = [] if slots[0] is None else [pltpu.make_async_copy(source, slots[0], sems.one())]
        self.swap = place.copy("x", source, slots[1], sems.two())
        self.core = place.copy("core", source, slots[2], sems.two())
        self.last = place.copy("core", slots[1], slots[3], sems.two())

    def start(self):
        self.swap.start()
        self.core.start()
        for copy in self.near:
            copy.start()

    def forward(self):
        self.swap.wait_recv()
        self.last.start()

    def finish(self):
        self.swap.wait_send()
        self.core.wait()
        self.last.wait()
        for copy in self.near:
            copy.wait()


class QuadSum:
    def __init__(self, place, sems, terms, scratch):
        self.near, self.theirs, self.far, self.swapped = scratch
        self.core = place.copy("core", terms.at[pl.ds(2, 2)], self.theirs, sems.two())
        self.load = pltpu.make_async_copy(terms.at[pl.ds(0, 2)], self.near, sems.one())
        self.swap = place.copy("x", self.far, self.swapped, sems.two())

    def start(self):
        self.core.start()
        self.load.start()

    def middle(self):
        self.core.wait()
        self.load.wait()

        def add(part):
            self.far[part] = (self.near[1, part] + self.theirs[1, part]).astype(BF16)

        pieces(SEQ_LEN, add)
        self.swap.start()

    def ready(self):
        self.swap.wait()

    def read(self, part):
        return self.near[0, part] + self.theirs[0, part] + self.swapped[part].astype(F32)


def live_rows(place, seq_count, valid_len, part):
    rows = lax.broadcasted_iota(jnp.int32, (PIECE, 128), 0) + part.start
    length = jnp.where(place.core == 0, valid_len[0], valid_len[1])
    return ((rows < length) & (place.core < seq_count[0])).astype(F32)[:, :1]


def quad_scratch(width):
    return [
        pltpu.VMEM((2, SEQ_LEN, width), F32),
        pltpu.VMEM((2, SEQ_LEN, width), F32),
        pltpu.VMEM((SEQ_LEN, width), BF16),
        pltpu.VMEM((SEQ_LEN, width), BF16),
    ]


class Leave:
    def __init__(self, place, sems, source, target):
        rows = pl.ds(pl.multiple_of(place.core * SEQ_LEN, SEQ_LEN), SEQ_LEN)
        width = source.shape[1] // 8
        self.copies, self.here = [], []
        for index in range(8):
            part = source.at[:, pl.ds(index * width, width)]
            there = target.at[rows, place.columns(index, width)]
            self.copies.append(place.copy("core", part, there, sems.two()))
            self.here.append(pltpu.make_async_copy(part, there, sems.one()))

    def start(self):
        for copy in self.copies + self.here:
            copy.start()

    def finish(self):
        for copy in self.copies + self.here:
            copy.wait()


class BlockTerms:
    def __init__(self, sems, acts, grads, bufs, over, own, parts):
        self.acts, self.grads, self.bufs = acts, grads, bufs
        self.over, self.own, self.parts = over, own, parts
        self.early = over.shape[2]
        self.left, self.right = sems.some(2), sems.some(2)

    def copies(self, slot, left, right):
        early, rest = self.early, self.bufs.shape[2] - self.early
        return (
            pltpu.make_async_copy(self.bufs.at[slot, :, pl.ds(0, early)], left, self.left(slot)),
            pltpu.make_async_copy(self.bufs.at[slot, :, pl.ds(early, rest)], right, self.right(slot)),
        )

    def wait(self, slot):
        for copy in self.copies(slot, self.own.at[0], self.parts[0].at[0]):
            copy.wait()

    def run(self, start, stop):
        width = self.bufs.shape[1]

        def step(i, carry):
            slot, side, away = i % 2, i // 4, i % 4

            @pl.when(i >= 2)
            def _():
                self.wait(slot)

            cols = pl.ds(pl.multiple_of(i * width, width), width)
            self.bufs[slot] = mm(self.acts[:, cols], self.grads[...], TN, BF16)

            @pl.when(side == 0)
            def _():
                self.copies(slot, self.own.at[away], self.parts[0].at[0])[0].start()

            @pl.when(side == 1)
            def _():
                self.copies(slot, self.over.at[away], self.parts[0].at[0])[0].start()

            for place in range(4):

                @pl.when(away == place)
                def _(place=place):
                    self.copies(slot, self.own.at[0], self.parts[place].at[side])[1].start()

            return carry

        lax.fori_loop(start, stop, step, 0)

    def finish(self):
        self.wait(0)
        self.wait(1)


class WideMatmul:
    def __init__(self, sems, acts, weight, stage, sums, hidden, wide):
        self.acts, self.weight, self.stage, self.sums, self.hidden, self.wide = acts, weight, stage, sums, hidden, wide
        self.hid = hidden.shape[1]
        self.half = acts.shape[1] // 2
        self.count = self.hid // 128
        self.loads = [sems.some(2) for _ in range(2)]
        self.stores = [sems.some(2) for _ in range(2)]

    def columns(self, i, side):
        return pl.ds(pl.multiple_of(side * self.hid + i * 128, 128), 128)

    def fetch(self, i, phase):
        return [
            pltpu.make_async_copy(
                self.weight.at[pl.ds(phase * self.half, self.half), self.columns(i, side)],
                self.stage.at[i % 2, pl.ds(0, self.half), pl.ds(side * 128, 128)],
                self.loads[side](i % 2),
            )
            for side in range(2)
        ]

    def leave(self, i):
        return [
            pltpu.make_async_copy(
                self.sums.at[i, :, pl.ds(side * 128, 128)], self.wide.at[:, self.columns(i, side)], self.stores[side](i % 2)
            )
            for side in range(2)
        ]

    def begin(self, phase):
        for copy in self.fetch(0, phase):
            copy.start()

    def run(self, phase):
        def step(i, carry):
            for copy in self.fetch(i, phase):
                copy.wait()

            @pl.when(i + 1 < self.count)
            def _():
                for copy in self.fetch(i + 1, phase):
                    copy.start()

            both = mm(self.acts[:, phase * self.half : (phase + 1) * self.half], self.stage[i % 2, : self.half])
            if phase == 0:
                self.sums[i] = both
                return carry

            @pl.when(i >= 2)
            def _():
                for copy in self.leave(i - 2):
                    copy.wait()

            both = both + self.sums[i]
            self.sums[i] = both
            gate = both[:, :128]
            self.hidden[:, self.columns(i, 0)] = (gate / (1.0 + jnp.exp(-gate)) * both[:, 128:]).astype(BF16)
            for copy in self.leave(i):
                copy.start()
            return carry

        lax.fori_loop(0, self.count, step, 0)

    def finish(self):
        for i in (self.count - 2, self.count - 1):
            for copy in self.leave(i):
                copy.wait()


class Chunk:
    def __init__(self, place, sems, source, offset, width, target, first, y_first, stage):
        shard = source.shape[0]
        cols, span = pl.ds(first, width), source.shape[1] // 2
        here, there = (pl.ds(pl.multiple_of(at * span + offset, 128), width) for at in (place.x, 1 - place.x))
        where = target.at[place.half(shard), cols]
        at = lambda index: target.at[pl.ds(index * 2 * shard, 2 * shard), cols]
        self.y_first = y_first
        self.swap = place.copy("x", source.at[:, there], where, sems.two())
        self.keep = Keep(sems, source.at[:, here], where, stage)
        ring = lambda side: [
            place.copy("up", at((4 - i) % 4 + 4 * side), at(3 - i + 4 * side), sems.two()) for i in range(3)
        ]
        self.low = ring(0)
        self.high = ring(1) if y_first else []
        self.cross = [place.copy("y", at(i), at(4 + i), sems.two()) for i in ((0,) if y_first else (0, 3, 2, 1))]

    def enter(self):
        self.swap.start()
        self.keep.start()

    def launch(self):
        self.keep.wait()
        self.swap.wait_recv()

    def pass_low(self, step, cross=True):
        self.low[step].wait_recv()
        if step < 2:
            self.low[step + 1].start()
        if cross and not self.y_first:
            self.cross[step + 1].start()

    def turn(self):
        self.cross[0].wait_recv()
        self.high[0].start()

    def pass_high(self, step):
        self.high[step].wait_recv()
        if step < 2:
            self.high[step + 1].start()

    def crossed(self):
        if not self.y_first:
            for copy in self.cross:
                copy.wait_recv()

    def sent(self):
        for copy in [self.swap] + self.low + self.high + self.cross:
            copy.wait_send()


class Loaded:
    def __init__(self, value):
        self.value = value

    def __getitem__(self, index):
        return self.value


class Projections:
    def __init__(self, sems, acts, weight, stage, sums, target):
        self.acts, self.weight, self.stage, self.sums, self.target = acts, weight, stage, sums, target
        self.loads, self.stores = sems.some(2), sems.some(7)

    def fetch(self, i):
        cols = pl.ds(pl.multiple_of(i * 256, 256), 256)
        return pltpu.make_async_copy(self.weight.at[:, cols], self.stage.at[i % 2], self.loads(i % 2))

    def fetch_last(self):
        return pltpu.make_async_copy(
            self.weight.at[:, pl.ds(3 * KDIM, 128)], self.stage.at[0, :, pl.ds(0, 128)], self.loads(0)
        )

    def leave(self, i, width=256):
        cols = pl.ds(i * 256, width)
        return pltpu.make_async_copy(self.sums.at[i, :, pl.ds(0, width)], self.target.at[:, cols], self.stores(i))

    def run(self):
        self.fetch(0).start()

        def step(i, carry):
            self.fetch(i).wait()

            @pl.when(i < 5)
            def _():
                self.fetch(i + 1).start()

            self.sums[i] = mm(self.acts[...], self.stage[i % 2])
            return carry

        lax.fori_loop(0, 6, step, 0)
        last = self.fetch_last()
        last.start()
        last.wait()
        self.sums[6, :, :128] = mm(self.acts[...], self.stage[0, :, :128])
        for i in range(6):
            self.leave(i).start()
        self.leave(6, 128).start()

    def mix(self, outs):
        def step(i, carry):
            rows = pl.ds(pl.multiple_of(i * SEQ_LEN, SEQ_LEN), SEQ_LEN)
            pair = lambda j: Loaded(jnp.concatenate([self.sums[j, rows, :], self.sums[j + 1, rows, :]], axis=1))
            forget = Loaded(self.sums[6, rows, :128])
            forward_kernel(pair(0), pair(2), pair(4), forget, *(out.at[rows] for out in outs))
            return carry

        lax.fori_loop(0, 4, step, 0)

    def finish(self):
        for i in range(6):
            self.leave(i).wait()
        self.leave(6, 128).wait()


class AttnTerms:
    def __init__(self, sems, mixed, weight, bufs, target):
        self.mixed, self.weight, self.bufs, self.target = mixed, weight, bufs, target
        self.stores = sems.some(2)

    def store(self, i):
        width = self.bufs.shape[3]
        cols = pl.ds(pl.multiple_of(i * width, width), width)
        return pltpu.make_async_copy(self.bufs.at[i % 2], self.target.at[:, :, cols], self.stores(i % 2))

    def run(self):
        width = self.bufs.shape[3]

        def step(i, carry):
            @pl.when(i >= 2)
            def _():
                self.store(i).wait()

            block = self.weight[pl.ds(pl.multiple_of(i * width, width), width), :]
            self.bufs[i % 2] = mm(self.mixed[...], block, NT).reshape(4, SEQ_LEN, width)
            self.store(i).start()
            return carry

        lax.fori_loop(0, 8, step, 0)
        self.store(6).wait()
        self.store(7).wait()


def forward_all_kernel(
    hid, cut, tokens, cot, seq_count, valid_len, gain0, gain1, q_w, k_w, v_w, forget_w, out_w, gate_w, up_w, down_w,
    w_in, w_out, own, attn_in, d_res, d_ffn, gains, proj, save_p, save_s, save_a, save_b, save_mixed, terms,
    w_wide, w_down, resid, ffn_in, wide, hidden, down_over, down_own, down0, down1, down2, down3,
    stage, seqs, acts, scales, turned, grads, low, small, p_v, s_v, a_v, b_v, mixed_v, out_v, term_bufs,
    s0, s1, s2, s3, kept, inputs, tiles, sums, hid_v, bufs, sem
):
    place, sems = Place(), Sems(sem)
    shard = q_w.shape[0]
    used = 0

    def chunk(source, offset, width, target, first, y_first):
        nonlocal used
        used += width
        return Chunk(place, sems, source, offset, width, target, first, y_first, stage.at[:, pl.ds(used - width, width)])

    first_chunks = [
        chunk(small, 0, 128, w_in, 3 * KDIM, True),
        chunk(q_w, 0, KDIM, w_in, 0, False),
        chunk(k_w, 0, KDIM, w_in, KDIM, False),
        chunk(v_w, 0, KDIM, w_in, 2 * KDIM, False),
        chunk(out_w, 0, KDIM // 2, w_out, 0, True),
        chunk(out_w, KDIM // 2, KDIM // 2, w_out, KDIM // 2, False),
    ]
    gate = chunk(gate_w, 0, hid, w_wide, 0, False)
    up = chunk(up_w, 0, hid, w_wide, hid, False)
    down = chunk(down_w, 0, cut, w_down, 0, False)
    rest = chunk(down_w, cut, hid - cut, w_down, cut, True)
    ffn_chunks = [gate, up, down, rest]
    width = tokens.shape[1] // 8
    mine = pl.ds(pl.multiple_of(place.core * SEQ_LEN, SEQ_LEN), SEQ_LEN)
    slot = [pl.ds(i * SEQ_LEN, SEQ_LEN) for i in range(4)]
    far, side, fetch, fetch_cot = [], [], [], []
    for index in range(8):
        part = tokens.at[mine, place.columns(index, width)]
        cols = pl.ds(index * width, width)
        far.append(place.copy("x", part, seqs.at[slot[1], cols], sems.two()))
        side.append(place.copy("core", part, seqs.at[slot[2], cols], sems.two()))
        fetch.append(pltpu.make_async_copy(part, seqs.at[slot[0], cols], sems.one()))
        fetch_cot.append(
            pltpu.make_async_copy(cot.at[mine, place.columns(index, width)], grads.at[:, cols], sems.one())
        )
    last = place.copy("core", seqs.at[slot[1]], seqs.at[slot[3]], sems.two())
    quad = Quad(place, sems, low, [d_ffn.at[one] for one in slot])
    save_own = pltpu.make_async_copy(seqs.at[slot[0]], own, sems.one())
    keep_own = pltpu.make_async_copy(seqs.at[slot[0]], inputs, sems.one())
    save_res = pltpu.make_async_copy(grads, d_res, sems.one())
    save_attn = pltpu.make_async_copy(acts, attn_in, sems.one())
    load_gains = [
        pltpu.make_async_copy(w_in.at[pl.ds(i * width, width), pl.ds(3 * KDIM, 128)], turned.at[i], sems.one())
        for i in range(8)
    ]
    load_out = pltpu.make_async_copy(w_out, out_v, sems.one())
    projections = Projections(sems, acts, w_in, tiles, sums, proj)
    saves = [
        pltpu.make_async_copy(a, b, sems.one())
        for a, b in ((p_v, save_p), (s_v, save_s), (a_v, save_a), (b_v, save_b), (mixed_v, save_mixed))
    ]
    attn_terms = AttnTerms(sems, mixed_v, out_v, term_bufs, terms)
    total = QuadSum(place, sems, terms, (s0, s1, s2, s3))
    slots = [acts.at[one] for one in slot]
    out = Quad(place, sems, slots[0], [None] + slots[1:])
    save = pltpu.make_async_copy(kept, resid, sems.one())
    save_in = pltpu.make_async_copy(acts, ffn_in, sems.one())
    save_hidden = pltpu.make_async_copy(hid_v, hidden, sems.one())
    fetch_cots = pltpu.make_async_copy(d_ffn, seqs, sems.one())
    matmul = WideMatmul(sems, acts, w_wide, tiles, sums, hid_v, wide)
    grad = BlockTerms(sems, seqs, hid_v, bufs, down_over, down_own, (down0, down1, down2, down3))
    lane = lax.broadcasted_iota(jnp.int32, (shard, 128), 1)
    column = jnp.concatenate([gain0[...].astype(F32).reshape(1, shard), gain1[...].astype(F32).reshape(1, shard)], axis=0)
    column = jnp.concatenate([column, jnp.zeros((6, shard), F32)], axis=0).T
    beside = jnp.where(lane == SLOTS, column[:, 0:1], jnp.where(lane == SLOTS + 1, column[:, 1:2], 0.0))
    heads = forget_w[...].astype(F32)
    small[:, :128] = jnp.where(lane < SLOTS, heads, beside).astype(BF16)
    small[:, 128:] = jnp.where(lane < SLOTS, pltpu.roll(heads, SLOTS, 1), beside).astype(BF16)
    place.greet()
    for one in first_chunks:
        one.enter()
    for copy in far + side + fetch + fetch_cot:
        copy.start()
    for one in ffn_chunks:
        one.enter()
    for one in first_chunks + ffn_chunks:
        one.keep.turn()
    for one in first_chunks:
        one.launch()
        one.low[0].start()
        one.cross[0].start()
    for copy in fetch + fetch_cot:
        copy.wait()
    save_own.start()
    keep_own.start()

    def mask(part):
        value = grads[part] * live_rows(place, seq_count, valid_len, part)
        grads[part] = value
        low[part] = value.astype(BF16)

    pieces(SEQ_LEN, mask)
    save_res.start()
    quad.start()
    for one in first_chunks:
        if one.y_first:
            one.turn()

    def measure(index):
        def work(part):
            rows = pl.ds(index * SEQ_LEN + part.start, PIECE)
            scales[rows] = jnp.broadcast_to(rms(seqs[rows].astype(F32)), (PIECE, 128))

        pieces(SEQ_LEN, work)

    def norm_first(index):
        def work(part):
            rows = pl.ds(index * SEQ_LEN + part.start, PIECE)
            acts[rows] = (seqs[rows].astype(F32) * scales[rows, :1] * gains[0:1, :]).astype(BF16)

        pieces(SEQ_LEN, work)

    for step in range(3):
        for c, one in enumerate(first_chunks):
            one.pass_low(step)
            if one.y_first:
                one.pass_high(step)
            if step == 0 and c == 1:
                measure(0)
            if step == 0 and c == 5:
                for copy in far:
                    copy.wait_recv()
                last.start()
            if step == 1:
                if c == 0:
                    for copy in side:
                        copy.wait_recv()
                    last.wait_recv()
                if 1 <= c <= 3:
                    measure(c)
            if step == 2:
                if c == 0:
                    for copy in load_gains:
                        copy.start()
                    for index, copy in enumerate(load_gains):
                        copy.wait()
                        flipped = turned[index].astype(F32).T
                        gains[0:8, index * width : (index + 1) * width] = flipped[SLOTS : SLOTS + 8]
                if 1 <= c <= 4:
                    norm_first(c - 1)
        if step == 1:
            for one in ffn_chunks:
                one.launch()
                one.low[0].start()
    for one in (gate, up, rest):
        one.cross[0].start()
    save_attn.start()
    quad.forward()
    for one in first_chunks:
        one.crossed()
    load_out.start()
    projections.run()
    gate.pass_low(0)
    projections.mix((mixed_v, p_v, s_v, a_v, b_v))
    for copy in saves:
        copy.start()
    up.pass_low(0)
    load_out.wait()
    attn_terms.run()
    save_attn.wait()
    total.start()
    rest.turn()
    total.middle()
    quad.finish()
    save_own.wait()
    keep_own.wait()
    for copy in side + [last]:
        copy.wait_send()
    fetch_cots.start()
    gate.pass_low(1)
    up.pass_low(1)
    down.pass_low(0, False)
    rest.pass_low(0)
    rest.pass_high(0)
    total.ready()

    def norm(part):
        value = total.read(part) + inputs[part].astype(F32)
        kept[part] = value
        acts[part] = (value * rms(value) * gains[1:2, :]).astype(BF16)

    pieces(SEQ_LEN, norm)
    out.start()
    save.start()
    gate.pass_low(2)
    up.pass_low(2)
    down.cross[0].start()
    down.cross[1].start()
    out.forward()
    out.finish()
    save_in.start()
    projections.finish()
    matmul.begin(0)
    matmul.run(0)
    down.pass_low(1)
    rest.pass_low(1)
    rest.pass_high(1)
    gate.crossed()
    up.crossed()
    matmul.begin(1)
    matmul.run(1)
    down.pass_low(2)
    save_hidden.start()
    fetch_cots.wait()
    grad.run(0, 8)
    rest.pass_low(2)
    rest.pass_high(2)
    down.crossed()
    for one in first_chunks + ffn_chunks:
        one.sent()
    for copy in far:
        copy.wait_send()
    for copy in saves + [save_res, save, save_in, save_hidden]:
        copy.wait()
    matmul.finish()
    grad.finish()


class Sum:
    def __init__(self, place, sems, terms, given, result, first, width, scratch, span=None, start=0):
        self.own, self.other, self.from_z, self.to_z, self.final = scratch
        cols = pl.ds(first, width)
        self.loads, self.crosses = [], []
        for index in range(4):
            self.loads.append(pltpu.make_async_copy(terms.at[index, :, cols], self.own.at[index], sems.one()))
            if given is None:
                self.crosses.append(place.copy("y", terms.at[4 + index, :, cols], self.other.at[index], sems.two()))
            else:
                self.loads.append(pltpu.make_async_copy(given.at[index], self.other.at[index], sems.one()))
        self.per = len(self.loads) // 4
        self.rises = [place.copy("up", self.to_z.at[i], self.from_z.at[i], sems.two()) for i in range(3)]
        half = self.final.shape[0] // 2
        there = result.at[:, pl.ds(pl.multiple_of(place.x * (span or width) + start, 128), width)]
        self.leave = pltpu.make_async_copy(self.final.at[place.half(half)], there, sems.one())
        self.swap = place.copy("x", self.final.at[place.half(half, True)], there, sems.two())

    def start(self, step):
        index = 3 - step
        for copy in self.crosses[index : index + 1] + self.loads[index * self.per : (index + 1) * self.per]:
            copy.start()

    def step(self, step):
        index = 3 - step
        for copy in self.loads[index * self.per : (index + 1) * self.per]:
            copy.wait()
        for copy in self.crosses[index : index + 1]:
            copy.wait_recv()
        if step:
            self.rises[step - 1].wait_recv()

        def add(part):
            value = self.own[index, part].astype(F32) + self.other[index, part].astype(F32)
            if step:
                value = value + self.from_z[step - 1, part].astype(F32)
            if step < 3:
                self.to_z[step, part] = value.astype(BF16)
            else:
                self.final[part] = value

        pieces(self.final.shape[0], add)
        if step < 3:
            self.rises[step].start()
        else:
            self.swap.start()
            self.leave.start()

    def finish(self):
        for copy in self.crosses + self.rises:
            copy.wait_send()
        self.leave.wait()
        self.swap.wait()


class SumGiven:
    def __init__(self, place, sems, terms, given, result, first, width, scratch, span, start):
        self.own, self.others, self.to_y, self.from_y, self.final = scratch
        cols = pl.ds(first, width)
        self.loads = [
            pltpu.make_async_copy(terms.at[d * (terms.shape[0] // 2), :, cols], self.own.at[d], sems.one())
            for d in range(2)
        ]
        self.loads += [pltpu.make_async_copy(one, self.others.at[i], sems.one()) for i, one in enumerate(given)]
        self.cross = place.copy("y", self.to_y, self.from_y, sems.two())
        half = self.final.shape[0] // 2
        there = result.at[:, pl.ds(pl.multiple_of(place.x * span + start, 128), width)]
        self.leave = pltpu.make_async_copy(self.final.at[place.half(half)], there, sems.one())
        self.swap = place.copy("x", self.final.at[place.half(half, True)], there, sems.two())

    def start(self):
        for copy in self.loads:
            copy.start()

    def first(self):
        for copy in self.loads:
            copy.wait()

        def add(part):
            for d in (1, 0):
                value = self.own[d, part].astype(F32)
                for i in range(3):
                    value = value + self.others[i, d, part].astype(F32)
                if d:
                    self.to_y[part] = value.astype(BF16)
                else:
                    self.final[part] = value

        pieces(self.final.shape[0], add)
        self.cross.start()

    def second(self):
        self.cross.wait_recv()

        def add(part):
            self.final[part] = self.final[part] + self.from_y[part].astype(F32)

        pieces(self.final.shape[0], add)
        self.swap.start()
        self.leave.start()

    def finish(self):
        self.cross.wait_send()
        self.leave.wait()
        self.swap.wait()


def given_scratch(rows, width):
    return [
        pltpu.VMEM((2, rows, width), BF16),
        pltpu.VMEM((3, 2, rows, width), BF16),
        pltpu.VMEM((rows, width), BF16),
        pltpu.VMEM((rows, width), BF16),
        pltpu.VMEM((rows, width), F32),
    ]


def sum_scratch(rows, width):
    return [pltpu.VMEM((depth, rows, width), BF16) for depth in (4, 4, 3, 3)] + [pltpu.VMEM((rows, width), F32)]


class OutTerms:
    def __init__(self, sems, hidden, weight, stage, bufs, target):
        self.hidden, self.weight, self.stage, self.bufs, self.target = hidden, weight, stage, bufs, target
        self.loads, self.stores = sems.some(2), sems.some(2)

    def load(self, i):
        return pltpu.make_async_copy(self.weight.at[i], self.stage.at[i % 2], self.loads(i % 2))

    def store(self, i):
        width = self.bufs.shape[2]
        cols = pl.ds(pl.multiple_of(i * width, width), width)
        return pltpu.make_async_copy(self.bufs.at[i % 2], self.target.at[:, cols], self.stores(i % 2))

    def run(self, start, stop):
        def step(i, carry):
            self.load(i).wait()

            @pl.when(i < 7)
            def _():
                self.load(i + 1).start()

            @pl.when(i >= 2)
            def _():
                self.store(i).wait()

            self.bufs[i % 2] = mm(self.hidden[...], self.stage[i % 2], NT)
            self.store(i).start()
            return carry

        lax.fori_loop(start, stop, step, 0)

    def finish(self):
        self.store(6).wait()
        self.store(7).wait()


def norm_back_piece(value, gain, grad):
    scale = rms(value)
    scaled = gain * grad
    inner = jnp.mean(scaled * value, axis=-1, keepdims=True)
    gains = (grad * value * scale).reshape(PIECE // 8, 8, value.shape[1])
    return scale * scaled - value * (scale * scale * scale * inner), jnp.sum(gains, axis=0)


def thirds(columns):
    tiles = columns // 128
    wide = (tiles + 2) // 3 * 128
    return ((0, wide), (wide, wide), (2 * wide, columns - 2 * wide))


def sum_ffn_kernel(
    hid, early, gate_t, down, given, down_rest, given1, given2, given3, terms, resid, gains, d_res, ffn_in, d_wide, hidden, w_down,
    gate_sum, down_sum, d_h, d_attn, gain_sum, up_over, up_own, up0, up1, up2, up3, out_terms, *scratch
):
    *scratch, sem = scratch
    place, sems = Place(), Sems(sem)
    rest = hid - early
    down_y = Sum(place, sems, down, given, down_sum, 0, early, scratch[0:5], hid)
    down_z = SumGiven(place, sems, down_rest, (given1, given2, given3), down_sum, 0, rest, scratch[5:10], hid, early)
    gate = [
        Sum(place, sems, gate_t, None, gate_sum, first, width, scratch[10 + 5 * i : 15 + 5 * i], hid, first)
        for i, (first, width) in enumerate(thirds(hid))
    ]
    back = QuadSum(place, sems, terms, scratch[25:29])
    value, res, low, acts, ups, up_bufs, hid_v, stage, out_bufs = scratch[29:38]
    quad = Quad(place, sems, low, [d_attn.at[i] for i in range(4)])
    up = BlockTerms(sems, acts, ups, up_bufs, up_over, up_own, (up0, up1, up2, up3))
    out = OutTerms(sems, hid_v, w_down, stage, out_bufs, out_terms)
    ready = [
        pltpu.make_async_copy(ffn_in, acts, sems.one()),
        pltpu.make_async_copy(d_wide.at[:, pl.ds(hid, hid)], ups, sems.one()),
        pltpu.make_async_copy(hidden, hid_v, sems.one()),
    ]
    fetch = [pltpu.make_async_copy(resid, value, sems.one()), pltpu.make_async_copy(d_res, res, sems.one())]
    save = pltpu.make_async_copy(res, d_h, sems.one())
    place.greet()
    back.start()
    for one in (down_y, *gate):
        one.start(0)
    down_z.start()
    for copy in fetch:
        copy.start()
    for one in (down_y, *gate):
        one.start(1)
    down_y.step(0)
    down_z.first()
    for step in (2, 3):
        for one in (down_y, *gate):
            one.start(step)
    for copy in ready:
        copy.start()
    out.load(0).start()
    back.middle()
    for one in gate:
        one.step(0)
    for copy in fetch + ready:
        copy.wait()
    down_y.step(1)
    back.ready()
    gain_sum[...] = jnp.zeros_like(gain_sum)

    def norm(part):
        d_norm, added = norm_back_piece(value[part], gains[1:2, :], back.read(part))
        grad = res[part] + d_norm
        res[part] = grad
        low[part] = grad.astype(BF16)
        gain_sum[...] += added

    pieces(SEQ_LEN, norm)
    quad.start()
    save.start()
    for one in gate:
        one.step(1)
    down_y.step(2)
    up.run(0, 8)
    down_z.second()
    for one in gate:
        one.step(2)
    down_y.step(3)
    out.run(0, 8)
    quad.forward()
    for one in gate:
        one.step(3)
    quad.finish()
    save.wait()
    up.finish()
    out.finish()
    for one in (down_y, down_z, *gate):
        one.finish()


def sum_last_kernel(
    hid, early, up, given, up_rest, given1, given2, given3, out_t, in_t, terms, tokens, gain_rows, d_h, ffn_gains, out_terms, resid, seq_count, valid_len,
    up_sum, out_sum, q_sum, k_sum, v_sum, f_sum, grad, block_out, gain_sum, *scratch
):
    *scratch, sem = scratch
    place, sems = Place(True), Sems(sem)
    sums = []
    for terms_in, given_in, result, first, width, span, start in (
        (up, given, up_sum, 0, early, hid, 0),
        (out_t, None, out_sum, 0, KDIM, None, 0),
        (in_t, None, q_sum, 0, KDIM, None, 0),
        (in_t, None, k_sum, KDIM, KDIM, None, 0),
        (in_t, None, v_sum, 2 * KDIM, KDIM, None, 0),
        (in_t, None, f_sum, 3 * KDIM, 128, None, 0),
    ):
        sums.append(Sum(place, sems, terms_in, given_in, result, first, width, scratch[:5], span, start))
        scratch = scratch[5:]
    up_z = SumGiven(place, sems, up_rest, (given1, given2, given3), up_sum, 0, hid - early, scratch[:5], hid, early)
    scratch = scratch[5:]
    back = QuadSum(place, sems, terms, scratch[0:4])
    ahead = QuadSum(place, sems, out_terms, scratch[4:8])
    value, res, kept, shown, gains, parts, met, crossed, risen, last, swapped = scratch[8:]
    leave = Leave(place, sems, res, grad)
    leave_out = Leave(place, sems, shown, block_out)
    fetch = [pltpu.make_async_copy(tokens, value, sems.one()), pltpu.make_async_copy(d_h, res, sems.one())]
    fetch.append(pltpu.make_async_copy(resid, kept, sems.one()))
    meet = place.copy("core", parts, met, sems.two())
    cross = place.copy("y", parts.at[pl.ds(4, 4)], crossed, sems.two())
    spread = [
        place.copy(name, parts.at[i + 1], risen.at[i], sems.two()) for i, name in enumerate(("up", "two", "down"))
    ]
    swap = place.copy("x", last.at[1 - place.x], swapped, sems.two())
    place.greet()
    back.start()
    for one in sums:
        one.start(0)
    up_z.start()
    for copy in fetch:
        copy.start()
    for one in sums:
        one.start(1)
    ahead.start()
    sums[0].step(0)
    up_z.first()
    for one in sums:
        one.start(2)
    back.middle()
    for one in sums[1:]:
        one.step(0)
    for copy in fetch:
        copy.wait()
    gains[...] = jnp.zeros_like(gains)
    back.ready()

    def norm(part):
        d_norm, added = norm_back_piece(value[part].astype(F32), gain_rows[0:1, :], back.read(part))
        res[part] = res[part] + d_norm
        gains[...] += added

    pieces(SEQ_LEN, norm)
    leave.start()
    width = res.shape[1] // 8
    parts[...] = jnp.zeros_like(parts)
    for row, source in enumerate((gains[...], ffn_gains[...])):
        summed = jnp.sum(source, axis=0, keepdims=True)
        for index in range(8):
            parts[index, row : row + 1, :] = summed[:, index * width : (index + 1) * width]
    meet.start()
    sums[0].step(1)
    meet.wait()
    parts[...] = parts[...] + met[...]
    cross.start()
    for one in sums:
        one.start(3)
    for one in sums[1:]:
        one.step(1)
    ahead.middle()
    up_z.second()
    for one in sums:
        one.step(2)
    cross.wait()
    parts[pl.ds(0, 4)] = parts[pl.ds(0, 4)] + crossed[...]
    for copy in spread:
        copy.start()
    ahead.ready()

    def show(part):
        alive = live_rows(place, seq_count, valid_len, part)
        shown[part] = (alive * (kept[part] + ahead.read(part))).astype(BF16)

    pieces(SEQ_LEN, show)
    leave_out.start()
    for one in sums:
        one.step(3)
    for copy in spread:
        copy.wait_recv()
    total = parts[0] + risen[0] + risen[1] + risen[2]
    last[0] = total[:, : width // 2]
    last[1] = total[:, width // 2 :]
    swap.start()
    swap.wait()
    gain_sum[...] = last[place.x] + swapped[...]
    for copy in spread:
        copy.wait_send()
    leave.finish()
    leave_out.finish()
    up_z.finish()
    for one in sums:
        one.finish()


def call(kernel, name, ident, inputs, specs, outputs, out_specs, scratch, sems):
    return pl.pallas_call(
        kernel,
        in_specs=specs,
        out_specs=out_specs,
        out_shape=[jax.ShapeDtypeStruct(shape, kind) for shape, kind in outputs],
        scratch_shapes=scratch + [DMA((sems,))],
        compiler_params=pltpu.CompilerParams(collective_id=ident, has_side_effects=True, vmem_limit_bytes=60 << 20),
        name=name,
    )(*inputs)


PAD = 128 - SLOTS
EARLY = 896


class Ring:
    def __init__(self, count):
        self.count = count
        self.stages = []
        left, stride = count // 2, count
        while left > 1:
            size = 4 if left % 4 == 0 else 2
            stride //= size
            left //= size
            self.stages.append((stride, size))

    def perm(self, stride, size, shift):
        moves = []
        for source in range(self.count):
            digit = source // stride % size
            moves.append((source, source + ((digit + shift) % size - digit) * stride))
        return moves

    def send(self, value, stage, shift):
        stride, size = stage
        return lax.ppermute(value, "dp", self.perm(stride, size, shift % size))

    def swap(self, value):
        return lax.ppermute(value, "dp", self.perm(1, 2, 1))

    def digit(self, stage):
        return lax.axis_index("dp") // stage[0] % stage[1]

    def gather(self, block):
        blocks = [block]
        for stage in self.stages:
            more = list(blocks)
            for shift in range(1, stage[1]):
                more += [self.send(one, stage, -shift) for one in blocks]
            blocks = more
        return blocks

    def scatter(self, make):
        def level(depth, offset, width):
            if depth == len(self.stages):
                return lambda inner: make(offset + inner)
            return None

        widths = [1]
        for stage in self.stages:
            widths.append(widths[-1] * stage[1])

        def total(depth, index):
            if depth == len(self.stages):
                return make(index)
            stage = self.stages[depth]
            parts = []
            for shift in range(1, stage[1]):
                sent = total(depth + 1, index + shift * widths[depth]).astype(BF16)
                parts.append(self.send(sent, stage, shift))
            mine = total(depth + 1, index)
            for part in parts:
                mine = mine + part.astype(F32)
            return mine

        return total(0, 0)

    def order(self, value, width, back=False):
        parts = [value[:, i * width : (i + 1) * width] for i in range(self.count // 2)]
        stages = self.stages
        if back:
            parts = self.turn_digits(parts, [s[1] for s in stages[::-1]])
        inner = len(parts)
        for stage in stages:
            size = stage[1]
            inner //= size
            digit = self.digit(stage)
            new = []
            for place in range(len(parts)):
                at = place // inner % size
                base = place - at * inner
                picks = []
                for k in range(size):
                    picks.append(parts[base + ((at - k) % size if back else (at + k) % size) * inner])
                one = picks[0]
                for k in range(1, size):
                    one = jnp.where(digit == k, picks[k], one)
                new.append(one)
            parts = new
        if not back:
            parts = self.turn_digits(parts, [s[1] for s in stages])
        return jnp.concatenate(parts, axis=1)

    def turn_digits(self, parts, sizes):
        count = len(parts)
        out = [None] * count
        for index in range(count):
            rest, digits = index, []
            for size in reversed(sizes):
                digits.append(rest % size)
                rest //= size
            new = 0
            for digit, size in zip(digits, reversed(sizes)):
                new = new * size + digit
            out[new] = parts[index]
        return out


def mm(left, right, dims=NN, kind=F32):
    return lax.dot_general(left, right, dims, preferred_element_type=F32).astype(kind)


def rms(values):
    return lax.rsqrt(jnp.mean(values * values, axis=-1, keepdims=True) + 1e-06)


def norm_back(values, gain, grad):
    scale = rms(values)
    scaled = gain * grad
    inner = jnp.mean(scaled * values, axis=-1, keepdims=True)
    return scale * scaled - values * (scale * scale * scale * inner), jnp.sum(grad * values * scale, axis=0)


def body_by_permutes(
    tokens,
    seq_count,
    valid_len,
    attn_gain,
    ffn_gain,
    q_weight,
    k_weight,
    v_weight,
    forget_weight,
    out_weight,
    gate_weight,
    up_weight,
    down_weight,
    cotangent,
    *,
    ring,
):
    shard = q_weight.shape[0]
    width = 2 * shard
    core = lax.axis_index("head")
    even = lax.axis_index("dp") % 2 == 0
    first = core == 0
    rows = tokens.shape[0]

    def other_core(value):
        return lax.ppermute(value, "head", [(0, 1), (1, 0)])

    def pair_rows(mine, theirs, axis=0):
        return jnp.where(
            even, jnp.concatenate([mine, theirs], axis=axis), jnp.concatenate([theirs, mine], axis=axis)
        )

    def gather(parts):
        left = jnp.concatenate([p[0] for p in parts], axis=1)
        right = jnp.concatenate([p[1] for p in parts], axis=1)
        mine, theirs = jnp.where(even, left, right), jnp.where(even, right, left)
        return jnp.concatenate(ring.gather(pair_rows(mine, ring.swap(theirs))), axis=0)

    def cut(weight):
        half = weight.shape[1] // 2
        return (weight[:, :half], weight[:, half:])

    def quad_gather(mine):
        chips = jnp.concatenate([mine, ring.swap(mine)], axis=0)
        return jnp.concatenate([chips, other_core(chips)], axis=0)

    def quad_scatter(make):
        theirs = other_core(make(slice(2 * SEQ_LEN, 4 * SEQ_LEN)))
        far = make(slice(SEQ_LEN, 2 * SEQ_LEN)) + theirs[SEQ_LEN:]
        near = make(slice(0, SEQ_LEN)) + theirs[:SEQ_LEN]
        return near + ring.swap(far.astype(BF16)).astype(F32)

    def whole_rows(mine):
        theirs = other_core(mine)
        return jnp.where(
            first, jnp.concatenate([mine, theirs], axis=0), jnp.concatenate([theirs, mine], axis=0)
        )

    def weight_sum(act, grads):
        def make(index):
            return mm(act[:, index * width : (index + 1) * width], grads, TN)

        done = ring.scatter(make)
        mine = jnp.where(even, done[:shard], done[shard:])
        theirs = ring.swap(jnp.where(even, done[shard:], done[:shard]))
        return (jnp.where(even, mine, theirs), jnp.where(even, theirs, mine))

    gains = jnp.concatenate(
        [attn_gain[:, None], ffn_gain[:, None], jnp.zeros((shard, PAD - 2), BF16)], axis=1
    )
    w_in = gather([cut(q_weight), cut(k_weight), cut(v_weight), cut(forget_weight), (gains, gains)])
    w_out = gather([cut(out_weight)])
    w_gate = gather([cut(gate_weight)])
    w_up = gather([cut(up_weight)])
    w_down = gather([cut(down_weight)])
    gain_attn = w_in[:, WIDE - PAD].astype(F32)[None, :]
    gain_ffn = w_in[:, WIDE - PAD + 1].astype(F32)[None, :]

    def own(value):
        return ring.order(jnp.where(first, value[:SEQ_LEN], value[SEQ_LEN:]), width)

    places = lax.broadcasted_iota(jnp.int32, (SEQ_LEN, 1), 0)
    length = jnp.where(first, valid_len[0], valid_len[1])
    live = ((core < seq_count[0]) & (places < length)).astype(F32)
    own_tokens = own(tokens)
    d_res = live * own(cotangent)
    d_ffn = quad_gather(d_res.astype(BF16))
    inputs = quad_gather(own_tokens).astype(F32)
    attn_in = (inputs * rms(inputs) * gain_attn).astype(BF16)
    proj = mm(attn_in, w_in)
    mixed, *saved = mixer_forward(proj)
    own_inputs = own_tokens.astype(F32)
    resid = own_inputs + quad_scatter(lambda r: mm(mixed[r], w_out, NT))
    ffn_in = quad_gather((resid * rms(resid) * gain_ffn).astype(BF16))
    gate, up_vals = mm(ffn_in, w_gate), mm(ffn_in, w_up)
    sig = jax.nn.sigmoid(gate)
    hidden = (gate * sig * up_vals).astype(BF16)
    d_hidden = mm(d_ffn, w_down)
    d_gate = (d_hidden * up_vals * (sig * (1.0 + gate * (1.0 - sig)))).astype(BF16)
    d_up = (d_hidden * (gate * sig)).astype(BF16)
    d_ffn_in = quad_scatter(lambda r: mm(d_gate[r], w_gate, NT) + mm(d_up[r], w_up, NT))
    down_sum = weight_sum(d_ffn, hidden)
    gate_sum = weight_sum(ffn_in, d_gate)
    up_sum = weight_sum(ffn_in, d_up)
    ffn = quad_scatter(lambda r: mm(hidden[r], w_down, NT))
    block_out = whole_rows(ring.order((live * (resid + ffn)).astype(BF16), width, back=True))
    d_norm, ffn_gain_part = norm_back(resid, gain_ffn, d_ffn_in)
    d_h = d_res + d_norm
    d_attn = quad_gather(d_h.astype(BF16))
    d_mixed = mm(d_attn, w_out)
    d_proj = mixer_backward(proj, saved, d_mixed)
    d_attn_in = quad_scatter(lambda r: mm(d_proj[r], w_in, NT))
    out_sum = weight_sum(d_attn, mixed)
    in_sum = weight_sum(attn_in, d_proj)
    d_input, attn_gain_part = norm_back(own_inputs, gain_attn, d_attn_in)
    input_grad = whole_rows(ring.order(d_h + d_input, width, back=True))

    both = jnp.stack([attn_gain_part, ffn_gain_part], axis=0)
    both = both + other_core(both)
    both = both.reshape(2, ring.count // 2, width)
    for stage in ring.stages[::-1]:
        size = stage[1]
        both = both.reshape(2, size, -1, width)
        parts = [ring.send(both[:, shift], stage, shift) for shift in range(1, size)]
        both = both[:, 0]
        for part in parts:
            both = both + part
    both = both.reshape(2, 2, shard)
    both = jnp.where(even, both[:, 0], both[:, 1]) + ring.swap(jnp.where(even, both[:, 1], both[:, 0]))

    def columns(pieces, start, stop):
        return jnp.concatenate([p[:, start:stop] for p in pieces], axis=1)

    return (
        block_out,
        input_grad,
        both[0],
        both[1],
        columns(in_sum, 0, KDIM),
        columns(in_sum, KDIM, 2 * KDIM),
        columns(in_sum, 2 * KDIM, 3 * KDIM),
        columns(in_sum, 3 * KDIM, 3 * KDIM + SLOTS),
        columns(out_sum, 0, KDIM),
        jnp.concatenate(gate_sum, axis=1),
        jnp.concatenate(up_sum, axis=1),
        jnp.concatenate(down_sum, axis=1),
    )


def body_by_kernels(
    tokens,
    seq_count,
    valid_len,
    attn_gain,
    ffn_gain,
    q_weight,
    k_weight,
    v_weight,
    forget_weight,
    out_weight,
    gate_weight,
    up_weight,
    down_weight,
    cotangent,
    *,
    ring,
):
    shard, dim = q_weight.shape[0], tokens.shape[1]
    width, hid = 2 * shard, gate_weight.shape[1] // 2
    over_y = lambda value: ring.send(value, ring.stages[1], 1)
    rows4 = (4, SEQ_LEN, dim)
    blocks = lambda value: value.reshape(-1, width, value.shape[-1])
    flat = lambda value: value.reshape(-1, value.shape[-1])
    half = dim // 2

    row = (SEQ_LEN, dim)
    vmem = lambda shape, kind=F32: pltpu.VMEM(shape, kind)
    tokens4 = 4 * SEQ_LEN
    cut = hid // 256 * 128
    full = (tokens4, dim)
    early, rest = [((4, width, EARLY), BF16)] * 2, [((2, width, hid - EARLY), BF16)] * 4
    (
        w_in, w_out, own, attn_in, d_res, d_ffn, gain_rows, proj, *saved, mixed, _,
        w_wide, w_down, resid, ffn_in, wide, hidden, down_over, down_own, down0, down1, down2, down3,
    ) = call(
        functools.partial(forward_all_kernel, hid, cut),
        "forward_all",
        0,
        (
            tokens,
            cotangent,
            seq_count,
            valid_len,
            attn_gain,
            ffn_gain,
            q_weight,
            k_weight,
            v_weight,
            forget_weight,
            out_weight,
            gate_weight,
            up_weight,
            down_weight,
        ),
        [ANY, ANY, SMEM, SMEM, VMEM, VMEM, ANY, ANY, ANY, VMEM] + [ANY] * 4,
        [((dim, WIDE), BF16), ((dim, KDIM), BF16), (row, BF16), (full, BF16), (row, F32), (full, BF16), ((8, dim), F32)]
        + [((tokens4, WIDE), F32), ((tokens4, 128), F32), ((tokens4, 128), F32)]
        + [((tokens4, SEQ_LEN), F32), ((tokens4, SEQ_LEN), F32), ((tokens4, KDIM), BF16), (rows4, F32)]
        + [((dim, 2 * hid), BF16), ((dim, hid), BF16), (row, F32), (full, BF16)]
        + [((tokens4, 2 * hid), F32), ((tokens4, hid), BF16)]
        + early
        + rest,
        [ANY] * 6 + [VMEM] + [ANY] * 19,
        [
            vmem((shard, 4 * KDIM + 128 + 3 * hid), BF16),
            vmem(full, BF16),
            vmem(full, BF16),
            vmem((tokens4, 128)),
            vmem((8, width, 128), BF16),
            vmem(row),
            vmem(row, BF16),
            vmem((shard, 256), BF16),
            vmem((tokens4, 128)),
            vmem((tokens4, 128)),
            vmem((tokens4, SEQ_LEN)),
            vmem((tokens4, SEQ_LEN)),
            vmem((tokens4, KDIM), BF16),
            vmem((dim, KDIM), BF16),
            vmem((2, 4, SEQ_LEN, width)),
        ]
        + quad_scratch(dim)
        + [
            vmem(row),
            vmem(row, BF16),
            vmem((2, dim, 256), BF16),
            vmem((hid // 128, tokens4, 256)),
            vmem((tokens4, hid), BF16),
            vmem((2, width, hid), BF16),
        ],
        360,
    )
    down_parts = [down0, down1, down2, down3]

    def exchange(over, parts):
        return [over_y(over)] + [ring.send(parts[d], ring.stages[0], d) for d in (1, 2, 3)]

    down_given = exchange(down_over, down_parts)
    gate, up_vals = wide[:, :hid], wide[:, hid:]
    sig = jax.nn.sigmoid(gate)
    d_hidden = mm(d_ffn, w_down)
    d_gate = (d_hidden * up_vals * (sig * (1.0 + gate * (1.0 - sig)))).astype(BF16)
    d_up = (d_hidden * (gate * sig)).astype(BF16)
    d_wide = jnp.concatenate([d_gate, d_up], axis=1)
    gate_terms = mm(ffn_in, d_wide[:, :hid], TN, BF16)
    d_ffn_terms = mm(d_wide, w_wide, NT).reshape(rows4)
    gate_sum, down_sum, d_h, d_attn, ffn_gains, up_over, up_own, *up_parts, ffn_terms = call(
        functools.partial(sum_ffn_kernel, hid, EARLY),
        "sum_ffn",
        2,
        (
            blocks(gate_terms),
            down_own,
            down_given[0],
            down_parts[0],
            *down_given[1:],
            d_ffn_terms,
            resid,
            gain_rows,
            d_res,
            ffn_in,
            d_wide,
            hidden,
            blocks(w_down),
        ),
        [ANY] * 9 + [VMEM] + [ANY] * 5,
        [((shard, 2 * hid), F32), ((shard, 2 * hid), F32), (row, F32), (rows4, BF16), ((8, dim), F32)]
        + early
        + rest
        + [((4 * SEQ_LEN, dim), F32)],
        [ANY] * 4 + [VMEM] + [ANY] * 7,
        sum_scratch(width, EARLY)
        + given_scratch(width, hid - EARLY)
        + [one for _, columns in thirds(hid) for one in sum_scratch(width, columns)]
        + quad_scratch(dim)
        + [vmem(row), vmem(row), vmem(row, BF16)]
        + [vmem((4 * SEQ_LEN, dim), BF16), vmem((4 * SEQ_LEN, hid), BF16), vmem((2, width, hid), BF16)]
        + [vmem((4 * SEQ_LEN, hid), BF16), vmem((2, width, hid), BF16), vmem((2, 4 * SEQ_LEN, width))],
        220,
    )
    d_attn = flat(d_attn)
    up_given = exchange(up_over, up_parts)
    d_proj = mixer_backward(proj, saved, mm(d_attn, w_out))
    d_attn_terms = mm(d_proj, w_in, NT).reshape(rows4)
    ffn_terms = ffn_terms.reshape(rows4)
    tail = width // 2
    up_sum, out_sum, q_sum, k_sum, v_sum, f_sum, input_grad, block_out, gain_sums = call(
        functools.partial(sum_last_kernel, hid, EARLY),
        "sum_last",
        3,
        (
            up_own,
            up_given[0],
            up_parts[0],
            *up_given[1:],
            blocks(mm(d_attn, mixed, TN, BF16)),
            blocks(mm(attn_in, d_proj, TN, BF16)),
            d_attn_terms,
            own,
            gain_rows,
            d_h,
            ffn_gains,
            ffn_terms,
            resid,
            seq_count,
            valid_len,
        ),
        [ANY] * 10 + [VMEM, ANY, VMEM, ANY, ANY, SMEM, SMEM],
        [((shard, 2 * hid), F32)]
        + [((shard, 2 * KDIM), F32)] * 4
        + [((shard, 256), F32), ((2 * SEQ_LEN, dim), F32), ((2 * SEQ_LEN, dim), BF16), ((8, tail), F32)],
        [ANY] * 8 + [VMEM],
        sum_scratch(width, EARLY)
        + sum_scratch(width, KDIM) * 4
        + sum_scratch(width, 128)
        + given_scratch(width, hid - EARLY)
        + quad_scratch(dim) * 2
        + [vmem(row, BF16), vmem(row), vmem(row), vmem(row, BF16), vmem((8, dim))]
        + [vmem((depth, 8, width)) for depth in (8, 8, 4, 3)]
        + [vmem((2, 8, tail)), vmem((8, tail))],
        280,
    )
    f_grad = jnp.concatenate([f_sum[:, :SLOTS], f_sum[:, 128 : 128 + SLOTS]], axis=1)
    return (
        block_out,
        input_grad,
        gain_sums[0],
        gain_sums[1],
        q_sum,
        k_sum,
        v_sum,
        f_grad,
        out_sum,
        gate_sum,
        up_sum,
        down_sum,
    )


def solution(mesh):
    ring = Ring(mesh.shape["dp"])
    body = body_by_kernels if ring.count == 16 else body_by_permutes
    split_one, split_two = P("dp"), P("dp", "head")
    row = P("dp", None)
    in_specs = (row, split_one, split_one, split_one, split_one) + (split_two,) * 8 + (row,)
    out_specs = (row, row, split_one, split_one) + (split_two,) * 8
    return jax.shard_map(
        functools.partial(body, ring=ring),
        mesh=mesh,
        in_specs=in_specs,
        out_specs=out_specs,
        check_vma=False,
    )
```

```python
import functools
import jax
import jax.numpy as jnp
from jax import lax
from jax.experimental import pallas as pl
from jax.experimental.pallas import tpu as pltpu
from jax.sharding import PartitionSpec as P

SLOTS = 64
KDIM = 512
SEQ_LEN = 256
HALF = 128
F32, BF16 = jnp.float32, jnp.bfloat16
WIDE = 3 * KDIM + 128
NT = (((1,), (1,)), ((), ()))
NN = (((1,), (0,)), ((), ()))
TN = (((0,), (0,)), ((), ()))
LEVELS = (8, 16, 32, 64)


def split(value):
    high = value.astype(BF16)
    return high, (value - high.astype(F32)).astype(BF16)


def dot3(left, right, dims):
    one = functools.partial(lax.dot_general, dimension_numbers=dims, preferred_element_type=F32)
    return one(left[0], right[0]) + (one(left[0], right[1]) + one(left[1], right[0]))


def silu_parts(value):
    gate = 1.0 / (1.0 + jnp.exp(-value))
    return gate, value * gate


def level_mask(size):
    row = lax.broadcasted_iota(jnp.int32, (HALF, HALF), 0) // size
    col = lax.broadcasted_iota(jnp.int32, (HALF, HALF), 1) // size
    return (row == col + 1) & (row % 2 == 1)


def band_mask(back):
    row = lax.broadcasted_iota(jnp.int32, (HALF, HALF), 0)
    col = lax.broadcasted_iota(jnp.int32, (HALF, HALF), 1)
    return (row == col + back) & (row // 8 == col // 8)


def down(value, back):
    return value if back == 0 else pltpu.roll(value, back, 0)


def up(value, back):
    return value if back == 0 else pltpu.roll(value, SEQ_LEN - back, 0)


def gates(forget):
    lane = lax.broadcasted_iota(jnp.int32, forget.shape, 1) < SLOTS
    place = lax.broadcasted_iota(jnp.int32, forget.shape, 0)
    forget = jnp.where(lane, forget, 0.0)
    tail = jnp.exp(-jnp.abs(forget))
    log_decay = (jnp.minimum(forget, 0.0) - jnp.log1p(tail)) * 0.125
    log_decay = jnp.where(lane, log_decay, 0.0)
    g = log_decay
    series = 1.0 + g * (1.0 / 7.0)
    for n in (6.0, 5.0, 4.0, 3.0, 2.0):
        series = 1.0 + g * (1.0 / n) * series
    writes = jnp.where(g > -0.3, -g * series, 1.0 - jnp.exp(g))
    writes = jnp.where(lane, writes, 0.0)
    ahead, behind = g, g
    for step in (1, 2, 4):
        ahead = ahead + jnp.where(place % 8 >= step, down(ahead, step), 0.0)
        behind = behind + jnp.where(place % 8 < 8 - step, up(behind, step), 0.0)
    behind = jnp.where(place % 8 < 7, up(behind, 1), 0.0)
    aheads, behinds = {8: ahead}, {8: behind}
    size = 8
    while size < HALF:
        first = ahead.reshape(SEQ_LEN // (2 * size), 2, size, 128)
        last = behind.reshape(SEQ_LEN // (2 * size), 2, size, 128)
        left, right = first[:, 0:1], first[:, 1:2]
        left_sum, right_sum = left[:, :, size - 1 :], right[:, :, size - 1 :]
        ahead = jnp.concatenate([left, right + left_sum], axis=1).reshape(SEQ_LEN, 128)
        behind = jnp.concatenate([last[:, 0:1] + right_sum, last[:, 1:2]], axis=1).reshape(SEQ_LEN, 128)
        size *= 2
        aheads[size], behinds[size] = ahead, behind
    return lane, place, g, writes, aheads, behinds


def near_decays(place, aheads, back):
    ahead = aheads[8]
    gap = jnp.where(place % 8 >= back, ahead - down(ahead, back), 0.0)
    return jnp.where(place % 8 >= back, jnp.exp(gap), 0.0)


def halves(value):
    return value[:HALF], value[HALF:]


def to_slots(blocks, cross, place, writes, aheads, behinds, nears):
    grow = {size: jnp.exp(aheads[size]) for size in LEVELS}
    keep = {size: split(jnp.exp(behinds[size]) * writes) for size in LEVELS}
    outs = []
    for half in range(2):
        here = slice(half * HALF, (half + 1) * HALF)
        block = blocks[half]
        parts = split(block)
        total = None
        for size in LEVELS:
            mask = level_mask(size)
            masked = tuple(jnp.where(mask, part, jnp.zeros_like(part)) for part in parts)
            term = grow[size][here] * dot3(masked, tuple(k[here] for k in keep[size]), NN)
            total = term if total is None else total + term
        for back in range(8):
            near = jnp.sum(jnp.where(band_mask(back), block, 0.0), axis=1, keepdims=True)
            total = total + near * nears[back][here]
        if half == 1:
            far = split((jnp.exp(behinds[HALF]) * writes)[:HALF])
            total = total + jnp.exp(aheads[HALF])[HALF:] * dot3(split(cross), far, NN)
        outs.append(total)
    return jnp.concatenate(outs, axis=0)


def to_tokens(slots, writes, aheads, behinds, nears):
    blocks = []
    for half in range(2):
        here = slice(half * HALF, (half + 1) * HALF)
        total = jnp.zeros((HALF, HALF), F32)
        for size in LEVELS:
            left = split((slots * jnp.exp(aheads[size]))[here])
            right = split((jnp.exp(behinds[size]) * writes)[here])
            total = jnp.where(level_mask(size), dot3(left, right, NT), total)
        for back in range(8):
            near = jnp.sum(slots[here] * nears[back][here], axis=1, keepdims=True)
            total = jnp.where(band_mask(back), near, total)
        blocks.append(total)
    left = split((slots * jnp.exp(aheads[HALF]))[HALF:])
    right = split((jnp.exp(behinds[HALF]) * writes)[:HALF])
    return blocks, dot3(left, right, NT)


def forward_kernel(q_ref, k_ref, v_ref, f_ref, o_ref, p_ref, s_ref, a_ref, b_ref):
    query = split(silu_parts(q_ref[...])[1] * KDIM ** (-0.5))
    keys = split(silu_parts(k_ref[...])[1])
    values = split(v_ref[...])
    lane, place, g, writes, aheads, behinds = gates(f_ref[...])
    nears = [near_decays(place, aheads, back) * down(writes, back) for back in range(8)]
    q0, q1 = tuple(x[:HALF] for x in query), tuple(x[HALF:] for x in query)
    k0, k1 = tuple(x[:HALF] for x in keys), tuple(x[HALF:] for x in keys)
    blocks = (dot3(q0, k0, NT), dot3(q1, k1, NT))
    cross = dot3(q1, k0, NT)
    scores = to_slots(blocks, cross, place, writes, aheads, behinds, nears)
    shown = jnp.where(lane, scores, -1e30)
    weights = jnp.exp(shown - jnp.max(shown, axis=1, keepdims=True))
    weights = jnp.where(lane, weights, 0.0)
    weights = weights / jnp.sum(weights, axis=1, keepdims=True)
    mixes, mix_cross = to_tokens(weights, writes, aheads, behinds, nears)
    v0 = tuple(x[:HALF] for x in values)
    o_ref[:HALF, :] = dot3(split(mixes[0]), v0, NN).astype(o_ref.dtype)
    row = jnp.concatenate([mix_cross, mixes[1]], axis=1)
    o_ref[HALF:, :] = dot3(split(row), values, NN).astype(o_ref.dtype)
    p_ref[...] = weights
    s_ref[...] = scores
    a_ref[:HALF, :] = jnp.concatenate([blocks[0], jnp.zeros_like(cross)], axis=1)
    a_ref[HALF:, :] = jnp.concatenate([cross, blocks[1]], axis=1)
    b_ref[:HALF, :] = jnp.concatenate([mixes[0], jnp.zeros_like(cross)], axis=1)
    b_ref[HALF:, :] = row


def backward_kernel(q_ref, k_ref, v_ref, f_ref, p_ref, s_ref, a_ref, b_ref, d_ref, out_ref):
    lane, place, g, writes, aheads, behinds = gates(f_ref[...])
    spans = [near_decays(place, aheads, back) for back in range(8)]
    nears = [spans[back] * down(writes, back) for back in range(8)]
    weights, scores = p_ref[...], s_ref[...]
    products, mixing = a_ref[...], b_ref[...]
    grad = split(d_ref[...])
    g0, g1 = tuple(x[:HALF] for x in grad), tuple(x[HALF:] for x in grad)
    values = split(v_ref[...])
    v0, v1 = tuple(x[:HALF] for x in values), tuple(x[HALF:] for x in values)
    m_parts = split(mixing)
    dv0 = dot3(tuple(x[:, :HALF] for x in m_parts), grad, TN)
    dv1 = dot3(tuple(x[HALF:, HALF:] for x in m_parts), g1, TN)
    out_ref[:HALF, 2 * KDIM : 3 * KDIM] = dv0.astype(BF16)
    out_ref[HALF:, 2 * KDIM : 3 * KDIM] = dv1.astype(BF16)
    mix_blocks = (dot3(g0, v0, NT), dot3(g1, v1, NT))
    mix_cross = dot3(g1, v0, NT)
    d_weights = to_slots(mix_blocks, mix_cross, place, writes, aheads, behinds, nears)
    inner = jnp.sum(weights * d_weights, axis=1, keepdims=True)
    d_scores = weights * (d_weights - inner)
    d_blocks, d_cross = to_tokens(d_scores, writes, aheads, behinds, nears)
    q_gate, q_act = silu_parts(q_ref[...])
    k_gate, k_act = silu_parts(k_ref[...])
    scale = KDIM ** (-0.5)
    query, keys = split(q_act * scale), split(k_act)
    k0 = tuple(x[:HALF] for x in keys)
    low = split(jnp.concatenate([d_cross, d_blocks[1]], axis=1))
    top = split(d_blocks[0])
    dq = jnp.concatenate([dot3(top, k0, NN), dot3(low, keys, NN)], axis=0)
    first = tuple(jnp.concatenate([t, l[:, :HALF]], axis=0) for t, l in zip(top, low))
    dk0 = dot3(first, query, TN)
    dk1 = dot3(tuple(x[:, HALF:] for x in low), tuple(x[HALF:] for x in query), TN)
    dk = jnp.concatenate([dk0, dk1], axis=0)
    out_ref[:, :KDIM] = (dq * scale * (q_gate + q_act * (1.0 - q_gate))).astype(BF16)
    out_ref[:, KDIM : 2 * KDIM] = (dk * (k_gate + k_act * (1.0 - k_gate))).astype(BF16)
    parts = []
    for half in range(2):
        here = slice(half * HALF, (half + 1) * HALF)
        both = jnp.concatenate([mix_blocks[half], products[here, here]], axis=0)
        both_parts = split(both)
        total = None
        for size in LEVELS:
            mask = level_mask(size)
            mask = jnp.concatenate([mask, mask], axis=0)
            grow = jnp.exp(aheads[size][here])
            right = split(jnp.concatenate([weights[here] * grow, d_scores[here] * grow], axis=0))
            left = tuple(jnp.where(mask, part, jnp.zeros_like(part)) for part in both_parts)
            term = jnp.exp(behinds[size][here]) * dot3(left, right, TN)
            total = term if total is None else total + term
        parts.append(total)
    grow = jnp.exp(aheads[HALF][HALF:])
    left = split(jnp.concatenate([mix_cross, products[HALF:, :HALF]], axis=0))
    right = split(jnp.concatenate([weights[HALF:] * grow, d_scores[HALF:] * grow], axis=0))
    parts[0] = parts[0] + jnp.exp(behinds[HALF][:HALF]) * dot3(left, right, TN)
    reach = jnp.concatenate(parts, axis=0)
    for back in range(8):
        mask = band_mask(back)
        near_mix = jnp.concatenate([jnp.sum(jnp.where(mask, mix_blocks[h], 0.0), axis=1, keepdims=True) for h in range(2)], axis=0)
        near_pro = jnp.concatenate(
            [jnp.sum(jnp.where(mask, products[h * HALF : (h + 1) * HALF, h * HALF : (h + 1) * HALF], 0.0), axis=1, keepdims=True) for h in range(2)],
            axis=0,
        )
        reach = reach + up((near_mix * weights + near_pro * d_scores) * spans[back], back)
    d_sum = weights * d_weights + d_scores * scores - writes * reach
    step = 1
    while step < SEQ_LEN:
        d_sum = d_sum + jnp.where(place < SEQ_LEN - step, up(d_sum, step), 0.0)
        step *= 2
    d_log = d_sum - reach * jnp.exp(g)
    d_forget = d_log * 0.125 / (1.0 + jnp.exp(f_ref[...]))
    out_ref[:, 3 * KDIM :] = jnp.where(lane, d_forget, 0.0).astype(BF16)


def spec(width, column):
    return pl.BlockSpec((SEQ_LEN, width), lambda i: (i, column))


IN_SPECS = [spec(KDIM, 0), spec(KDIM, 1), spec(KDIM, 2), spec(128, 3 * KDIM // 128)]


def mixer_forward(proj):
    rows = proj.shape[0]
    shape = lambda width, kind: jax.ShapeDtypeStruct((rows, width), kind)
    return pl.pallas_call(
        forward_kernel,
        grid=(rows // SEQ_LEN,),
        in_specs=IN_SPECS,
        out_specs=[spec(KDIM, 0), spec(128, 0), spec(128, 0), spec(SEQ_LEN, 0), spec(SEQ_LEN, 0)],
        out_shape=[shape(KDIM, BF16), shape(128, F32), shape(128, F32), shape(SEQ_LEN, F32), shape(SEQ_LEN, F32)],
        compiler_params=pltpu.CompilerParams(vmem_limit_bytes=48 << 20),
        cost_estimate=pl.CostEstimate(flops=rows * 3000000, bytes_accessed=rows * 10000, transcendentals=rows * 3000),
        name="mixer_forward",
    )(proj, proj, proj, proj)


def mixer_backward(proj, saved, grad):
    rows = proj.shape[0]
    weights, scores, products, mixing = saved
    return pl.pallas_call(
        backward_kernel,
        grid=(rows // SEQ_LEN,),
        in_specs=IN_SPECS + [spec(128, 0), spec(128, 0), spec(SEQ_LEN, 0), spec(SEQ_LEN, 0), spec(KDIM, 0)],
        out_specs=spec(WIDE, 0),
        out_shape=jax.ShapeDtypeStruct((rows, WIDE), BF16),
        compiler_params=pltpu.CompilerParams(vmem_limit_bytes=48 << 20),
        cost_estimate=pl.CostEstimate(flops=rows * 9000000, bytes_accessed=rows * 16000, transcendentals=rows * 5000),
        name="mixer_backward",
    )(proj, proj, proj, proj, weights, scores, products, mixing, grad)


MESH = pl.DeviceIdType.MESH
ANY = pl.BlockSpec(memory_space=pl.ANY)
VMEM = pl.BlockSpec(memory_space=pltpu.VMEM)
SMEM = pl.BlockSpec(memory_space=pltpu.SMEM)
DMA = pltpu.SemaphoreType.DMA
PIECE = 32


class Place:
    def __init__(self, all_z=False):
        dp = lax.axis_index("dp")
        self.core = lax.axis_index("head")
        self.x, self.y, self.z = dp % 2, dp // 2 % 2, dp // 4
        rest = dp % 4
        self.peers = {
            "x": (dp + 1 - 2 * self.x, self.core),
            "y": (dp + 2 - 4 * self.y, self.core),
            "up": ((self.z + 1) % 4 * 4 + rest, self.core),
            "down": ((self.z + 3) % 4 * 4 + rest, self.core),
            "core": (dp, 1 - self.core),
        }
        if all_z:
            self.peers["two"] = ((self.z + 2) % 4 * 4 + rest, self.core)

    def greet(self):
        ready = pltpu.get_barrier_semaphore()
        for peer in self.peers.values():
            pl.semaphore_signal(ready, inc=1, device_id=peer, device_id_type=MESH)
        pl.semaphore_wait(ready, len(self.peers))

    def copy(self, name, source, target, sems):
        return pltpu.make_async_remote_copy(
            src_ref=source,
            dst_ref=target,
            send_sem=sems[0],
            recv_sem=sems[1],
            device_id=self.peers[name],
            device_id_type=MESH,
        )

    def half(self, size, other=False):
        place = 1 - self.x if other else self.x
        return pl.ds(pl.multiple_of(place * size, size), size)

    def columns(self, index, size):
        natural = (self.z + index % 4) % 4 * 2 + (self.y + index // 4) % 2
        return pl.ds(pl.multiple_of(natural * size, size), size)


class Sems:
    def __init__(self, ref):
        self.ref, self.used = ref, 0

    def one(self):
        self.used += 1
        return self.ref.at[self.used - 1]

    def two(self):
        return (self.one(), self.one())

    def some(self, count):
        first = self.used
        self.used += count
        return lambda index: self.ref.at[first + index]


def pieces(rows, work):
    def step(i, carry):
        work(pl.ds(pl.multiple_of(i * PIECE, PIECE), PIECE))
        return carry

    lax.fori_loop(0, rows // PIECE, step, 0)


class Keep:
    def __init__(self, sems, source, target, stage):
        self.load = pltpu.make_async_copy(source, stage, sems.one())
        self.store = pltpu.make_async_copy(stage, target, sems.one())

    def start(self):
        self.load.start()

    def turn(self):
        self.load.wait()
        self.store.start()

    def wait(self):
        self.store.wait()


class Quad:
    def __init__(self, place, sems, source, slots):
        self.near = [] if slots[0] is None else [pltpu.make_async_copy(source, slots[0], sems.one())]
        self.swap = place.copy("x", source, slots[1], sems.two())
        self.core = place.copy("core", source, slots[2], sems.two())
        self.last = place.copy("core", slots[1], slots[3], sems.two())

    def start(self):
        self.swap.start()
        self.core.start()
        for copy in self.near:
            copy.start()

    def forward(self):
        self.swap.wait_recv()
        self.last.start()

    def finish(self):
        self.swap.wait_send()
        self.core.wait()
        self.last.wait()
        for copy in self.near:
            copy.wait()


class QuadSum:
    def __init__(self, place, sems, terms, scratch):
        self.near, self.theirs, self.far, self.swapped = scratch
        self.core = place.copy("core", terms.at[pl.ds(2, 2)], self.theirs, sems.two())
        self.load = pltpu.make_async_copy(terms.at[pl.ds(0, 2)], self.near, sems.one())
        self.swap = place.copy("x", self.far, self.swapped, sems.two())

    def start(self):
        self.core.start()
        self.load.start()

    def middle(self):
        self.core.wait()
        self.load.wait()

        def add(part):
            self.far[part] = (self.near[1, part] + self.theirs[1, part]).astype(BF16)

        pieces(SEQ_LEN, add)
        self.swap.start()

    def ready(self):
        self.swap.wait()

    def read(self, part):
        return self.near[0, part] + self.theirs[0, part] + self.swapped[part].astype(F32)


def live_rows(place, seq_count, valid_len, part):
    rows = lax.broadcasted_iota(jnp.int32, (PIECE, 128), 0) + part.start
    length = jnp.where(place.core == 0, valid_len[0], valid_len[1])
    return ((rows < length) & (place.core < seq_count[0])).astype(F32)[:, :1]


def quad_scratch(width):
    return [
        pltpu.VMEM((2, SEQ_LEN, width), F32),
        pltpu.VMEM((2, SEQ_LEN, width), F32),
        pltpu.VMEM((SEQ_LEN, width), BF16),
        pltpu.VMEM((SEQ_LEN, width), BF16),
    ]


class Leave:
    def __init__(self, place, sems, source, target):
        rows = pl.ds(pl.multiple_of(place.core * SEQ_LEN, SEQ_LEN), SEQ_LEN)
        width = source.shape[1] // 8
        self.copies, self.here = [], []
        for index in range(8):
            part = source.at[:, pl.ds(index * width, width)]
            there = target.at[rows, place.columns(index, width)]
            self.copies.append(place.copy("core", part, there, sems.two()))
            self.here.append(pltpu.make_async_copy(part, there, sems.one()))

    def start(self):
        for copy in self.copies + self.here:
            copy.start()

    def finish(self):
        for copy in self.copies + self.here:
            copy.wait()


class BlockTerms:
    def __init__(self, sems, acts, grads, bufs, over, own, parts):
        self.acts, self.grads, self.bufs = acts, grads, bufs
        self.over, self.own, self.parts = over, own, parts
        self.early = over.shape[2]
        self.left, self.right = sems.some(2), sems.some(2)

    def copies(self, slot, left, right):
        early, rest = self.early, self.bufs.shape[2] - self.early
        return (
            pltpu.make_async_copy(self.bufs.at[slot, :, pl.ds(0, early)], left, self.left(slot)),
            pltpu.make_async_copy(self.bufs.at[slot, :, pl.ds(early, rest)], right, self.right(slot)),
        )

    def wait(self, slot):
        for copy in self.copies(slot, self.own.at[0], self.parts[0].at[0]):
            copy.wait()

    def run(self, start, stop):
        width = self.bufs.shape[1]

        def step(i, carry):
            slot, side, away = i % 2, i // 4, i % 4

            @pl.when(i >= 2)
            def _():
                self.wait(slot)

            cols = pl.ds(pl.multiple_of(i * width, width), width)
            self.bufs[slot] = mm(self.acts[:, cols], self.grads[...], TN, BF16)

            @pl.when(side == 0)
            def _():
                self.copies(slot, self.own.at[away], self.parts[0].at[0])[0].start()

            @pl.when(side == 1)
            def _():
                self.copies(slot, self.over.at[away], self.parts[0].at[0])[0].start()

            for place in range(4):

                @pl.when(away == place)
                def _(place=place):
                    self.copies(slot, self.own.at[0], self.parts[place].at[side])[1].start()

            return carry

        lax.fori_loop(start, stop, step, 0)

    def finish(self):
        self.wait(0)
        self.wait(1)


class WideMatmul:
    def __init__(self, sems, acts, weight, stage, sums, hidden, wide):
        self.acts, self.weight, self.stage, self.sums, self.hidden, self.wide = acts, weight, stage, sums, hidden, wide
        self.hid = hidden.shape[1]
        self.half = acts.shape[1] // 2
        self.count = self.hid // 128
        self.loads = [sems.some(2) for _ in range(2)]
        self.stores = [sems.some(2) for _ in range(2)]

    def columns(self, i, side):
        return pl.ds(pl.multiple_of(side * self.hid + i * 128, 128), 128)

    def fetch(self, i, phase):
        return [
            pltpu.make_async_copy(
                self.weight.at[pl.ds(phase * self.half, self.half), self.columns(i, side)],
                self.stage.at[i % 2, pl.ds(0, self.half), pl.ds(side * 128, 128)],
                self.loads[side](i % 2),
            )
            for side in range(2)
        ]

    def leave(self, i):
        return [
            pltpu.make_async_copy(
                self.sums.at[i, :, pl.ds(side * 128, 128)], self.wide.at[:, self.columns(i, side)], self.stores[side](i % 2)
            )
            for side in range(2)
        ]

    def begin(self, phase):
        for copy in self.fetch(0, phase):
            copy.start()

    def run(self, phase):
        def step(i, carry):
            for copy in self.fetch(i, phase):
                copy.wait()

            @pl.when(i + 1 < self.count)
            def _():
                for copy in self.fetch(i + 1, phase):
                    copy.start()

            both = mm(self.acts[:, phase * self.half : (phase + 1) * self.half], self.stage[i % 2, : self.half])
            if phase == 0:
                self.sums[i] = both
                return carry

            @pl.when(i >= 2)
            def _():
                for copy in self.leave(i - 2):
                    copy.wait()

            both = both + self.sums[i]
            self.sums[i] = both
            gate = both[:, :128]
            self.hidden[:, self.columns(i, 0)] = (gate / (1.0 + jnp.exp(-gate)) * both[:, 128:]).astype(BF16)
            for copy in self.leave(i):
                copy.start()
            return carry

        lax.fori_loop(0, self.count, step, 0)

    def finish(self):
        for i in (self.count - 2, self.count - 1):
            for copy in self.leave(i):
                copy.wait()


class Chunk:
    def __init__(self, place, sems, source, offset, width, target, first, y_first, stage):
        shard = source.shape[0]
        cols, span = pl.ds(first, width), source.shape[1] // 2
        here, there = (pl.ds(pl.multiple_of(at * span + offset, 128), width) for at in (place.x, 1 - place.x))
        where = target.at[place.half(shard), cols]
        at = lambda index: target.at[pl.ds(index * 2 * shard, 2 * shard), cols]
        self.y_first = y_first
        self.swap = place.copy("x", source.at[:, there], where, sems.two())
        self.keep = Keep(sems, source.at[:, here], where, stage)
        ring = lambda side: [
            place.copy("up", at((4 - i) % 4 + 4 * side), at(3 - i + 4 * side), sems.two()) for i in range(3)
        ]
        self.low = ring(0)
        self.high = ring(1) if y_first else []
        self.cross = [place.copy("y", at(i), at(4 + i), sems.two()) for i in ((0,) if y_first else (0, 3, 2, 1))]

    def enter(self):
        self.swap.start()
        self.keep.start()

    def launch(self):
        self.keep.wait()
        self.swap.wait_recv()

    def pass_low(self, step, cross=True):
        self.low[step].wait_recv()
        if step < 2:
            self.low[step + 1].start()
        if cross and not self.y_first:
            self.cross[step + 1].start()

    def turn(self):
        self.cross[0].wait_recv()
        self.high[0].start()

    def pass_high(self, step):
        self.high[step].wait_recv()
        if step < 2:
            self.high[step + 1].start()

    def crossed(self):
        if not self.y_first:
            for copy in self.cross:
                copy.wait_recv()

    def sent(self):
        for copy in [self.swap] + self.low + self.high + self.cross:
            copy.wait_send()


class Loaded:
    def __init__(self, value):
        self.value = value

    def __getitem__(self, index):
        return self.value


class Projections:
    def __init__(self, sems, acts, weight, stage, sums, target):
        self.acts, self.weight, self.stage, self.sums, self.target = acts, weight, stage, sums, target
        self.loads, self.stores = sems.some(2), sems.some(7)

    def fetch(self, i):
        cols = pl.ds(pl.multiple_of(i * 256, 256), 256)
        return pltpu.make_async_copy(self.weight.at[:, cols], self.stage.at[i % 2], self.loads(i % 2))

    def fetch_last(self):
        return pltpu.make_async_copy(
            self.weight.at[:, pl.ds(3 * KDIM, 128)], self.stage.at[0, :, pl.ds(0, 128)], self.loads(0)
        )

    def leave(self, i, width=256):
        cols = pl.ds(i * 256, width)
        return pltpu.make_async_copy(self.sums.at[i, :, pl.ds(0, width)], self.target.at[:, cols], self.stores(i))

    def run(self):
        self.fetch(0).start()

        def step(i, carry):
            self.fetch(i).wait()

            @pl.when(i < 5)
            def _():
                self.fetch(i + 1).start()

            self.sums[i] = mm(self.acts[...], self.stage[i % 2])
            return carry

        lax.fori_loop(0, 6, step, 0)
        last = self.fetch_last()
        last.start()
        last.wait()
        self.sums[6, :, :128] = mm(self.acts[...], self.stage[0, :, :128])
        for i in range(6):
            self.leave(i).start()
        self.leave(6, 128).start()

    def mix(self, outs):
        def step(i, carry):
            rows = pl.ds(pl.multiple_of(i * SEQ_LEN, SEQ_LEN), SEQ_LEN)
            pair = lambda j: Loaded(jnp.concatenate([self.sums[j, rows, :], self.sums[j + 1, rows, :]], axis=1))
            forget = Loaded(self.sums[6, rows, :128])
            forward_kernel(pair(0), pair(2), pair(4), forget, *(out.at[rows] for out in outs))
            return carry

        lax.fori_loop(0, 4, step, 0)

    def finish(self):
        for i in range(6):
            self.leave(i).wait()
        self.leave(6, 128).wait()


class AttnTerms:
    def __init__(self, sems, mixed, weight, bufs, target):
        self.mixed, self.weight, self.bufs, self.target = mixed, weight, bufs, target
        self.stores = sems.some(2)

    def store(self, i):
        width = self.bufs.shape[3]
        cols = pl.ds(pl.multiple_of(i * width, width), width)
        return pltpu.make_async_copy(self.bufs.at[i % 2], self.target.at[:, :, cols], self.stores(i % 2))

    def run(self):
        width = self.bufs.shape[3]

        def step(i, carry):
            @pl.when(i >= 2)
            def _():
                self.store(i).wait()

            block = self.weight[pl.ds(pl.multiple_of(i * width, width), width), :]
            self.bufs[i % 2] = mm(self.mixed[...], block, NT).reshape(4, SEQ_LEN, width)
            self.store(i).start()
            return carry

        lax.fori_loop(0, 8, step, 0)
        self.store(6).wait()
        self.store(7).wait()


def forward_all_kernel(
    hid, cut, tokens, cot, seq_count, valid_len, gain0, gain1, q_w, k_w, v_w, forget_w, out_w, gate_w, up_w, down_w,
    w_in, w_out, own, attn_in, d_res, d_ffn, gains, proj, save_p, save_s, save_a, save_b, save_mixed, terms,
    w_wide, w_down, resid, ffn_in, wide, hidden, down_over, down_own, down0, down1, down2, down3,
    stage, seqs, acts, scales, turned, grads, low, small, p_v, s_v, a_v, b_v, mixed_v, out_v, term_bufs,
    s0, s1, s2, s3, kept, inputs, tiles, sums, hid_v, bufs, sem
):
    place, sems = Place(), Sems(sem)
    shard = q_w.shape[0]
    used = 0

    def chunk(source, offset, width, target, first, y_first):
        nonlocal used
        used += width
        return Chunk(place, sems, source, offset, width, target, first, y_first, stage.at[:, pl.ds(used - width, width)])

    first_chunks = [
        chunk(small, 0, 128, w_in, 3 * KDIM, True),
        chunk(q_w, 0, KDIM, w_in, 0, False),
        chunk(k_w, 0, KDIM, w_in, KDIM, False),
        chunk(v_w, 0, KDIM, w_in, 2 * KDIM, False),
        chunk(out_w, 0, KDIM // 2, w_out, 0, True),
        chunk(out_w, KDIM // 2, KDIM // 2, w_out, KDIM // 2, False),
    ]
    gate = chunk(gate_w, 0, hid, w_wide, 0, False)
    up = chunk(up_w, 0, hid, w_wide, hid, False)
    down = chunk(down_w, 0, cut, w_down, 0, False)
    rest = chunk(down_w, cut, hid - cut, w_down, cut, True)
    ffn_chunks = [gate, up, down, rest]
    width = tokens.shape[1] // 8
    mine = pl.ds(pl.multiple_of(place.core * SEQ_LEN, SEQ_LEN), SEQ_LEN)
    slot = [pl.ds(i * SEQ_LEN, SEQ_LEN) for i in range(4)]
    far, side, fetch, fetch_cot = [], [], [], []
    for index in range(8):
        part = tokens.at[mine, place.columns(index, width)]
        cols = pl.ds(index * width, width)
        far.append(place.copy("x", part, seqs.at[slot[1], cols], sems.two()))
        side.append(place.copy("core", part, seqs.at[slot[2], cols], sems.two()))
        fetch.append(pltpu.make_async_copy(part, seqs.at[slot[0], cols], sems.one()))
        fetch_cot.append(
            pltpu.make_async_copy(cot.at[mine, place.columns(index, width)], grads.at[:, cols], sems.one())
        )
    last = place.copy("core", seqs.at[slot[1]], seqs.at[slot[3]], sems.two())
    quad = Quad(place, sems, low, [d_ffn.at[one] for one in slot])
    save_own = pltpu.make_async_copy(seqs.at[slot[0]], own, sems.one())
    keep_own = pltpu.make_async_copy(seqs.at[slot[0]], inputs, sems.one())
    save_res = pltpu.make_async_copy(grads, d_res, sems.one())
    save_attn = pltpu.make_async_copy(acts, attn_in, sems.one())
    load_gains = [
        pltpu.make_async_copy(w_in.at[pl.ds(i * width, width), pl.ds(3 * KDIM, 128)], turned.at[i], sems.one())
        for i in range(8)
    ]
    load_out = pltpu.make_async_copy(w_out, out_v, sems.one())
    projections = Projections(sems, acts, w_in, tiles, sums, proj)
    saves = [
        pltpu.make_async_copy(a, b, sems.one())
        for a, b in ((p_v, save_p), (s_v, save_s), (a_v, save_a), (b_v, save_b), (mixed_v, save_mixed))
    ]
    attn_terms = AttnTerms(sems, mixed_v, out_v, term_bufs, terms)
    total = QuadSum(place, sems, terms, (s0, s1, s2, s3))
    slots = [acts.at[one] for one in slot]
    out = Quad(place, sems, slots[0], [None] + slots[1:])
    save = pltpu.make_async_copy(kept, resid, sems.one())
    save_in = pltpu.make_async_copy(acts, ffn_in, sems.one())
    save_hidden = pltpu.make_async_copy(hid_v, hidden, sems.one())
    fetch_cots = pltpu.make_async_copy(d_ffn, seqs, sems.one())
    matmul = WideMatmul(sems, acts, w_wide, tiles, sums, hid_v, wide)
    grad = BlockTerms(sems, seqs, hid_v, bufs, down_over, down_own, (down0, down1, down2, down3))
    lane = lax.broadcasted_iota(jnp.int32, (shard, 128), 1)
    column = jnp.concatenate([gain0[...].astype(F32).reshape(1, shard), gain1[...].astype(F32).reshape(1, shard)], axis=0)
    column = jnp.concatenate([column, jnp.zeros((6, shard), F32)], axis=0).T
    beside = jnp.where(lane == SLOTS, column[:, 0:1], jnp.where(lane == SLOTS + 1, column[:, 1:2], 0.0))
    heads = forget_w[...].astype(F32)
    small[:, :128] = jnp.where(lane < SLOTS, heads, beside).astype(BF16)
    small[:, 128:] = jnp.where(lane < SLOTS, pltpu.roll(heads, SLOTS, 1), beside).astype(BF16)
    place.greet()
    for one in first_chunks:
        one.enter()
    for copy in far + side + fetch + fetch_cot:
        copy.start()
    for one in ffn_chunks:
        one.enter()
    for one in first_chunks + ffn_chunks:
        one.keep.turn()
    for one in first_chunks:
        one.launch()
        one.low[0].start()
        one.cross[0].start()
    for copy in fetch + fetch_cot:
        copy.wait()
    save_own.start()
    keep_own.start()

    def mask(part):
        value = grads[part] * live_rows(place, seq_count, valid_len, part)
        grads[part] = value
        low[part] = value.astype(BF16)

    pieces(SEQ_LEN, mask)
    save_res.start()
    quad.start()
    for one in first_chunks:
        if one.y_first:
            one.turn()

    def measure(index):
        def work(part):
            rows = pl.ds(index * SEQ_LEN + part.start, PIECE)
            scales[rows] = jnp.broadcast_to(rms(seqs[rows].astype(F32)), (PIECE, 128))

        pieces(SEQ_LEN, work)

    def norm_first(index):
        def work(part):
            rows = pl.ds(index * SEQ_LEN + part.start, PIECE)
            acts[rows] = (seqs[rows].astype(F32) * scales[rows, :1] * gains[0:1, :]).astype(BF16)

        pieces(SEQ_LEN, work)

    for step in range(3):
        for c, one in enumerate(first_chunks):
            one.pass_low(step)
            if one.y_first:
                one.pass_high(step)
            if step == 0 and c == 1:
                measure(0)
            if step == 0 and c == 5:
                for copy in far:
                    copy.wait_recv()
                last.start()
            if step == 1:
                if c == 0:
                    for copy in side:
                        copy.wait_recv()
                    last.wait_recv()
                if 1 <= c <= 3:
                    measure(c)
            if step == 2:
                if c == 0:
                    for copy in load_gains:
                        copy.start()
                    for index, copy in enumerate(load_gains):
                        copy.wait()
                        flipped = turned[index].astype(F32).T
                        gains[0:8, index * width : (index + 1) * width] = flipped[SLOTS : SLOTS + 8]
                if 1 <= c <= 4:
                    norm_first(c - 1)
        if step == 1:
            for one in ffn_chunks:
                one.launch()
                one.low[0].start()
    for one in (gate, up, rest):
        one.cross[0].start()
    save_attn.start()
    quad.forward()
    for one in first_chunks:
        one.crossed()
    load_out.start()
    projections.run()
    gate.pass_low(0)
    projections.mix((mixed_v, p_v, s_v, a_v, b_v))
    for copy in saves:
        copy.start()
    up.pass_low(0)
    load_out.wait()
    attn_terms.run()
    save_attn.wait()
    total.start()
    rest.turn()
    total.middle()
    quad.finish()
    save_own.wait()
    keep_own.wait()
    for copy in side + [last]:
        copy.wait_send()
    fetch_cots.start()
    gate.pass_low(1)
    up.pass_low(1)
    down.pass_low(0, False)
    rest.pass_low(0)
    rest.pass_high(0)
    total.ready()

    def norm(part):
        value = total.read(part) + inputs[part].astype(F32)
        kept[part] = value
        acts[part] = (value * rms(value) * gains[1:2, :]).astype(BF16)

    pieces(SEQ_LEN, norm)
    out.start()
    save.start()
    gate.pass_low(2)
    up.pass_low(2)
    down.cross[0].start()
    down.cross[1].start()
    out.forward()
    out.finish()
    save_in.start()
    projections.finish()
    matmul.begin(0)
    matmul.run(0)
    down.pass_low(1)
    rest.pass_low(1)
    rest.pass_high(1)
    gate.crossed()
    up.crossed()
    matmul.begin(1)
    matmul.run(1)
    down.pass_low(2)
    save_hidden.start()
    fetch_cots.wait()
    grad.run(0, 8)
    rest.pass_low(2)
    rest.pass_high(2)
    down.crossed()
    for one in first_chunks + ffn_chunks:
        one.sent()
    for copy in far:
        copy.wait_send()
    for copy in saves + [save_res, save, save_in, save_hidden]:
        copy.wait()
    matmul.finish()
    grad.finish()


class Sum:
    def __init__(self, place, sems, terms, given, result, first, width, scratch, span=None, start=0):
        self.own, self.other, self.from_z, self.to_z, self.final = scratch
        cols = pl.ds(first, width)
        self.loads, self.crosses = [], []
        for index in range(4):
            self.loads.append(pltpu.make_async_copy(terms.at[index, :, cols], self.own.at[index], sems.one()))
            if given is None:
                self.crosses.append(place.copy("y", terms.at[4 + index, :, cols], self.other.at[index], sems.two()))
            else:
                self.loads.append(pltpu.make_async_copy(given.at[index], self.other.at[index], sems.one()))
        self.per = len(self.loads) // 4
        self.rises = [place.copy("up", self.to_z.at[i], self.from_z.at[i], sems.two()) for i in range(3)]
        half = self.final.shape[0] // 2
        there = result.at[:, pl.ds(pl.multiple_of(place.x * (span or width) + start, 128), width)]
        self.leave = pltpu.make_async_copy(self.final.at[place.half(half)], there, sems.one())
        self.swap = place.copy("x", self.final.at[place.half(half, True)], there, sems.two())

    def start(self, step):
        index = 3 - step
        for copy in self.crosses[index : index + 1] + self.loads[index * self.per : (index + 1) * self.per]:
            copy.start()

    def step(self, step):
        index = 3 - step
        for copy in self.loads[index * self.per : (index + 1) * self.per]:
            copy.wait()
        for copy in self.crosses[index : index + 1]:
            copy.wait_recv()
        if step:
            self.rises[step - 1].wait_recv()

        def add(part):
            value = self.own[index, part].astype(F32) + self.other[index, part].astype(F32)
            if step:
                value = value + self.from_z[step - 1, part].astype(F32)
            if step < 3:
                self.to_z[step, part] = value.astype(BF16)
            else:
                self.final[part] = value

        pieces(self.final.shape[0], add)
        if step < 3:
            self.rises[step].start()
        else:
            self.swap.start()
            self.leave.start()

    def finish(self):
        for copy in self.crosses + self.rises:
            copy.wait_send()
        self.leave.wait()
        self.swap.wait()


class SumGiven:
    def __init__(self, place, sems, terms, given, result, first, width, scratch, span, start):
        self.own, self.others, self.to_y, self.from_y, self.final = scratch
        cols = pl.ds(first, width)
        self.loads = [
            pltpu.make_async_copy(terms.at[d * (terms.shape[0] // 2), :, cols], self.own.at[d], sems.one())
            for d in range(2)
        ]
        self.loads += [pltpu.make_async_copy(one, self.others.at[i], sems.one()) for i, one in enumerate(given)]
        self.cross = place.copy("y", self.to_y, self.from_y, sems.two())
        half = self.final.shape[0] // 2
        there = result.at[:, pl.ds(pl.multiple_of(place.x * span + start, 128), width)]
        self.leave = pltpu.make_async_copy(self.final.at[place.half(half)], there, sems.one())
        self.swap = place.copy("x", self.final.at[place.half(half, True)], there, sems.two())

    def start(self):
        for copy in self.loads:
            copy.start()

    def first(self):
        for copy in self.loads:
            copy.wait()

        def add(part):
            for d in (1, 0):
                value = self.own[d, part].astype(F32)
                for i in range(3):
                    value = value + self.others[i, d, part].astype(F32)
                if d:
                    self.to_y[part] = value.astype(BF16)
                else:
                    self.final[part] = value

        pieces(self.final.shape[0], add)
        self.cross.start()

    def second(self):
        self.cross.wait_recv()

        def add(part):
            self.final[part] = self.final[part] + self.from_y[part].astype(F32)

        pieces(self.final.shape[0], add)
        self.swap.start()
        self.leave.start()

    def finish(self):
        self.cross.wait_send()
        self.leave.wait()
        self.swap.wait()


def given_scratch(rows, width):
    return [
        pltpu.VMEM((2, rows, width), BF16),
        pltpu.VMEM((3, 2, rows, width), BF16),
        pltpu.VMEM((rows, width), BF16),
        pltpu.VMEM((rows, width), BF16),
        pltpu.VMEM((rows, width), F32),
    ]


def sum_scratch(rows, width):
    return [pltpu.VMEM((depth, rows, width), BF16) for depth in (4, 4, 3, 3)] + [pltpu.VMEM((rows, width), F32)]


class OutTerms:
    def __init__(self, sems, hidden, weight, stage, bufs, target):
        self.hidden, self.weight, self.stage, self.bufs, self.target = hidden, weight, stage, bufs, target
        self.loads, self.stores = sems.some(2), sems.some(2)

    def load(self, i):
        return pltpu.make_async_copy(self.weight.at[i], self.stage.at[i % 2], self.loads(i % 2))

    def store(self, i):
        width = self.bufs.shape[2]
        cols = pl.ds(pl.multiple_of(i * width, width), width)
        return pltpu.make_async_copy(self.bufs.at[i % 2], self.target.at[:, cols], self.stores(i % 2))

    def run(self, start, stop):
        def step(i, carry):
            self.load(i).wait()

            @pl.when(i < 7)
            def _():
                self.load(i + 1).start()

            @pl.when(i >= 2)
            def _():
                self.store(i).wait()

            self.bufs[i % 2] = mm(self.hidden[...], self.stage[i % 2], NT)
            self.store(i).start()
            return carry

        lax.fori_loop(start, stop, step, 0)

    def finish(self):
        self.store(6).wait()
        self.store(7).wait()


def norm_back_piece(value, gain, grad):
    scale = rms(value)
    scaled = gain * grad
    inner = jnp.mean(scaled * value, axis=-1, keepdims=True)
    gains = (grad * value * scale).reshape(PIECE // 8, 8, value.shape[1])
    return scale * scaled - value * (scale * scale * scale * inner), jnp.sum(gains, axis=0)


def thirds(columns):
    tiles = columns // 128
    wide = (tiles + 2) // 3 * 128
    return ((0, wide), (wide, wide), (2 * wide, columns - 2 * wide))


def sum_ffn_kernel(
    hid, early, gate_t, down, given, down_rest, given1, given2, given3, terms, resid, gains, d_res, ffn_in, d_wide, hidden, w_down,
    gate_sum, down_sum, d_h, d_attn, gain_sum, up_over, up_own, up0, up1, up2, up3, out_terms, *scratch
):
    *scratch, sem = scratch
    place, sems = Place(), Sems(sem)
    rest = hid - early
    down_y = Sum(place, sems, down, given, down_sum, 0, early, scratch[0:5], hid)
    down_z = SumGiven(place, sems, down_rest, (given1, given2, given3), down_sum, 0, rest, scratch[5:10], hid, early)
    gate = [
        Sum(place, sems, gate_t, None, gate_sum, first, width, scratch[10 + 5 * i : 15 + 5 * i], hid, first)
        for i, (first, width) in enumerate(thirds(hid))
    ]
    back = QuadSum(place, sems, terms, scratch[25:29])
    value, res, low, acts, ups, up_bufs, hid_v, stage, out_bufs = scratch[29:38]
    quad = Quad(place, sems, low, [d_attn.at[i] for i in range(4)])
    up = BlockTerms(sems, acts, ups, up_bufs, up_over, up_own, (up0, up1, up2, up3))
    out = OutTerms(sems, hid_v, w_down, stage, out_bufs, out_terms)
    ready = [
        pltpu.make_async_copy(ffn_in, acts, sems.one()),
        pltpu.make_async_copy(d_wide.at[:, pl.ds(hid, hid)], ups, sems.one()),
        pltpu.make_async_copy(hidden, hid_v, sems.one()),
    ]
    fetch = [pltpu.make_async_copy(resid, value, sems.one()), pltpu.make_async_copy(d_res, res, sems.one())]
    save = pltpu.make_async_copy(res, d_h, sems.one())
    place.greet()
    for one in (down_y, *gate):
        one.start(0)
    down_z.start()
    back.start()
    for copy in fetch:
        copy.start()
    for one in (down_y, *gate):
        one.start(1)
    down_y.step(0)
    down_z.first()
    for step in (2, 3):
        for one in (down_y, *gate):
            one.start(step)
    for copy in ready:
        copy.start()
    out.load(0).start()
    back.middle()
    for one in gate:
        one.step(0)
    for copy in fetch + ready:
        copy.wait()
    down_y.step(1)
    back.ready()
    gain_sum[...] = jnp.zeros_like(gain_sum)

    def norm(part):
        d_norm, added = norm_back_piece(value[part], gains[1:2, :], back.read(part))
        grad = res[part] + d_norm
        res[part] = grad
        low[part] = grad.astype(BF16)
        gain_sum[...] += added

    pieces(SEQ_LEN, norm)
    quad.start()
    save.start()
    for one in gate:
        one.step(1)
    down_y.step(2)
    up.run(0, 8)
    down_z.second()
    for one in gate:
        one.step(2)
    down_y.step(3)
    out.run(0, 8)
    quad.forward()
    for one in gate:
        one.step(3)
    quad.finish()
    save.wait()
    up.finish()
    out.finish()
    for one in (down_y, down_z, *gate):
        one.finish()


def sum_last_kernel(
    hid, early, up, given, up_rest, given1, given2, given3, out_t, in_t, terms, tokens, gain_rows, d_h, ffn_gains, out_terms, resid, seq_count, valid_len,
    up_sum, out_sum, q_sum, k_sum, v_sum, f_sum, grad, block_out, gain_sum, *scratch
):
    *scratch, sem = scratch
    place, sems = Place(True), Sems(sem)
    sums = []
    for terms_in, given_in, result, first, width, span, start in (
        (up, given, up_sum, 0, early, hid, 0),
        (out_t, None, out_sum, 0, KDIM, None, 0),
        (in_t, None, q_sum, 0, KDIM, None, 0),
        (in_t, None, k_sum, KDIM, KDIM, None, 0),
        (in_t, None, v_sum, 2 * KDIM, KDIM, None, 0),
        (in_t, None, f_sum, 3 * KDIM, 128, None, 0),
    ):
        sums.append(Sum(place, sems, terms_in, given_in, result, first, width, scratch[:5], span, start))
        scratch = scratch[5:]
    up_z = SumGiven(place, sems, up_rest, (given1, given2, given3), up_sum, 0, hid - early, scratch[:5], hid, early)
    scratch = scratch[5:]
    back = QuadSum(place, sems, terms, scratch[0:4])
    ahead = QuadSum(place, sems, out_terms, scratch[4:8])
    value, res, kept, shown, gains, parts, met, crossed, risen, last, swapped = scratch[8:]
    leave = Leave(place, sems, res, grad)
    leave_out = Leave(place, sems, shown, block_out)
    fetch = [pltpu.make_async_copy(tokens, value, sems.one()), pltpu.make_async_copy(d_h, res, sems.one())]
    fetch.append(pltpu.make_async_copy(resid, kept, sems.one()))
    meet = place.copy("core", parts, met, sems.two())
    cross = place.copy("y", parts.at[pl.ds(4, 4)], crossed, sems.two())
    spread = [
        place.copy(name, parts.at[i + 1], risen.at[i], sems.two()) for i, name in enumerate(("up", "two", "down"))
    ]
    swap = place.copy("x", last.at[1 - place.x], swapped, sems.two())
    place.greet()
    sums[0].start(0)
    for one in sums[1:]:
        one.start(0)
    up_z.start()
    back.start()
    for copy in fetch:
        copy.start()
    for one in sums:
        one.start(1)
    ahead.start()
    sums[0].step(0)
    up_z.first()
    for one in sums:
        one.start(2)
    back.middle()
    for one in sums[1:]:
        one.step(0)
    for copy in fetch:
        copy.wait()
    gains[...] = jnp.zeros_like(gains)
    back.ready()

    def norm(part):
        d_norm, added = norm_back_piece(value[part].astype(F32), gain_rows[0:1, :], back.read(part))
        res[part] = res[part] + d_norm
        gains[...] += added

    pieces(SEQ_LEN, norm)
    leave.start()
    width = res.shape[1] // 8
    parts[...] = jnp.zeros_like(parts)
    for row, source in enumerate((gains[...], ffn_gains[...])):
        summed = jnp.sum(source, axis=0, keepdims=True)
        for index in range(8):
            parts[index, row : row + 1, :] = summed[:, index * width : (index + 1) * width]
    meet.start()
    sums[0].step(1)
    meet.wait()
    parts[...] = parts[...] + met[...]
    cross.start()
    for one in sums:
        one.start(3)
    for one in sums[1:]:
        one.step(1)
    ahead.middle()
    up_z.second()
    for one in sums:
        one.step(2)
    cross.wait()
    parts[pl.ds(0, 4)] = parts[pl.ds(0, 4)] + crossed[...]
    for copy in spread:
        copy.start()
    ahead.ready()

    def show(part):
        alive = live_rows(place, seq_count, valid_len, part)
        shown[part] = (alive * (kept[part] + ahead.read(part))).astype(BF16)

    pieces(SEQ_LEN, show)
    leave_out.start()
    for one in sums:
        one.step(3)
    for copy in spread:
        copy.wait_recv()
    total = parts[0] + risen[0] + risen[1] + risen[2]
    last[0] = total[:, : width // 2]
    last[1] = total[:, width // 2 :]
    swap.start()
    swap.wait()
    gain_sum[...] = last[place.x] + swapped[...]
    for copy in spread:
        copy.wait_send()
    leave.finish()
    leave_out.finish()
    up_z.finish()
    for one in sums:
        one.finish()


def call(kernel, name, ident, inputs, specs, outputs, out_specs, scratch, sems):
    return pl.pallas_call(
        kernel,
        in_specs=specs,
        out_specs=out_specs,
        out_shape=[jax.ShapeDtypeStruct(shape, kind) for shape, kind in outputs],
        scratch_shapes=scratch + [DMA((sems,))],
        compiler_params=pltpu.CompilerParams(collective_id=ident, has_side_effects=True, vmem_limit_bytes=60 << 20),
        name=name,
    )(*inputs)


PAD = 128 - SLOTS
EARLY = 896


class Ring:
    def __init__(self, count):
        self.count = count
        self.stages = []
        left, stride = count // 2, count
        while left > 1:
            size = 4 if left % 4 == 0 else 2
            stride //= size
            left //= size
            self.stages.append((stride, size))

    def perm(self, stride, size, shift):
        moves = []
        for source in range(self.count):
            digit = source // stride % size
            moves.append((source, source + ((digit + shift) % size - digit) * stride))
        return moves

    def send(self, value, stage, shift):
        stride, size = stage
        return lax.ppermute(value, "dp", self.perm(stride, size, shift % size))

    def swap(self, value):
        return lax.ppermute(value, "dp", self.perm(1, 2, 1))

    def digit(self, stage):
        return lax.axis_index("dp") // stage[0] % stage[1]

    def gather(self, block):
        blocks = [block]
        for stage in self.stages:
            more = list(blocks)
            for shift in range(1, stage[1]):
                more += [self.send(one, stage, -shift) for one in blocks]
            blocks = more
        return blocks

    def scatter(self, make):
        def level(depth, offset, width):
            if depth == len(self.stages):
                return lambda inner: make(offset + inner)
            return None

        widths = [1]
        for stage in self.stages:
            widths.append(widths[-1] * stage[1])

        def total(depth, index):
            if depth == len(self.stages):
                return make(index)
            stage = self.stages[depth]
            parts = []
            for shift in range(1, stage[1]):
                sent = total(depth + 1, index + shift * widths[depth]).astype(BF16)
                parts.append(self.send(sent, stage, shift))
            mine = total(depth + 1, index)
            for part in parts:
                mine = mine + part.astype(F32)
            return mine

        return total(0, 0)

    def order(self, value, width, back=False):
        parts = [value[:, i * width : (i + 1) * width] for i in range(self.count // 2)]
        stages = self.stages
        if back:
            parts = self.turn_digits(parts, [s[1] for s in stages[::-1]])
        inner = len(parts)
        for stage in stages:
            size = stage[1]
            inner //= size
            digit = self.digit(stage)
            new = []
            for place in range(len(parts)):
                at = place // inner % size
                base = place - at * inner
                picks = []
                for k in range(size):
                    picks.append(parts[base + ((at - k) % size if back else (at + k) % size) * inner])
                one = picks[0]
                for k in range(1, size):
                    one = jnp.where(digit == k, picks[k], one)
                new.append(one)
            parts = new
        if not back:
            parts = self.turn_digits(parts, [s[1] for s in stages])
        return jnp.concatenate(parts, axis=1)

    def turn_digits(self, parts, sizes):
        count = len(parts)
        out = [None] * count
        for index in range(count):
            rest, digits = index, []
            for size in reversed(sizes):
                digits.append(rest % size)
                rest //= size
            new = 0
            for digit, size in zip(digits, reversed(sizes)):
                new = new * size + digit
            out[new] = parts[index]
        return out


def mm(left, right, dims=NN, kind=F32):
    return lax.dot_general(left, right, dims, preferred_element_type=F32).astype(kind)


def rms(values):
    return lax.rsqrt(jnp.mean(values * values, axis=-1, keepdims=True) + 1e-06)


def norm_back(values, gain, grad):
    scale = rms(values)
    scaled = gain * grad
    inner = jnp.mean(scaled * values, axis=-1, keepdims=True)
    return scale * scaled - values * (scale * scale * scale * inner), jnp.sum(grad * values * scale, axis=0)


def body_by_permutes(
    tokens,
    seq_count,
    valid_len,
    attn_gain,
    ffn_gain,
    q_weight,
    k_weight,
    v_weight,
    forget_weight,
    out_weight,
    gate_weight,
    up_weight,
    down_weight,
    cotangent,
    *,
    ring,
):
    shard = q_weight.shape[0]
    width = 2 * shard
    core = lax.axis_index("head")
    even = lax.axis_index("dp") % 2 == 0
    first = core == 0
    rows = tokens.shape[0]

    def other_core(value):
        return lax.ppermute(value, "head", [(0, 1), (1, 0)])

    def pair_rows(mine, theirs, axis=0):
        return jnp.where(
            even, jnp.concatenate([mine, theirs], axis=axis), jnp.concatenate([theirs, mine], axis=axis)
        )

    def gather(parts):
        left = jnp.concatenate([p[0] for p in parts], axis=1)
        right = jnp.concatenate([p[1] for p in parts], axis=1)
        mine, theirs = jnp.where(even, left, right), jnp.where(even, right, left)
        return jnp.concatenate(ring.gather(pair_rows(mine, ring.swap(theirs))), axis=0)

    def cut(weight):
        half = weight.shape[1] // 2
        return (weight[:, :half], weight[:, half:])

    def quad_gather(mine):
        chips = jnp.concatenate([mine, ring.swap(mine)], axis=0)
        return jnp.concatenate([chips, other_core(chips)], axis=0)

    def quad_scatter(make):
        theirs = other_core(make(slice(2 * SEQ_LEN, 4 * SEQ_LEN)))
        far = make(slice(SEQ_LEN, 2 * SEQ_LEN)) + theirs[SEQ_LEN:]
        near = make(slice(0, SEQ_LEN)) + theirs[:SEQ_LEN]
        return near + ring.swap(far.astype(BF16)).astype(F32)

    def whole_rows(mine):
        theirs = other_core(mine)
        return jnp.where(
            first, jnp.concatenate([mine, theirs], axis=0), jnp.concatenate([theirs, mine], axis=0)
        )

    def weight_sum(act, grads):
        def make(index):
            return mm(act[:, index * width : (index + 1) * width], grads, TN)

        done = ring.scatter(make)
        mine = jnp.where(even, done[:shard], done[shard:])
        theirs = ring.swap(jnp.where(even, done[shard:], done[:shard]))
        return (jnp.where(even, mine, theirs), jnp.where(even, theirs, mine))

    gains = jnp.concatenate(
        [attn_gain[:, None], ffn_gain[:, None], jnp.zeros((shard, PAD - 2), BF16)], axis=1
    )
    w_in = gather([cut(q_weight), cut(k_weight), cut(v_weight), cut(forget_weight), (gains, gains)])
    w_out = gather([cut(out_weight)])
    w_gate = gather([cut(gate_weight)])
    w_up = gather([cut(up_weight)])
    w_down = gather([cut(down_weight)])
    gain_attn = w_in[:, WIDE - PAD].astype(F32)[None, :]
    gain_ffn = w_in[:, WIDE - PAD + 1].astype(F32)[None, :]

    def own(value):
        return ring.order(jnp.where(first, value[:SEQ_LEN], value[SEQ_LEN:]), width)

    places = lax.broadcasted_iota(jnp.int32, (SEQ_LEN, 1), 0)
    length = jnp.where(first, valid_len[0], valid_len[1])
    live = ((core < seq_count[0]) & (places < length)).astype(F32)
    own_tokens = own(tokens)
    d_res = live * own(cotangent)
    d_ffn = quad_gather(d_res.astype(BF16))
    inputs = quad_gather(own_tokens).astype(F32)
    attn_in = (inputs * rms(inputs) * gain_attn).astype(BF16)
    proj = mm(attn_in, w_in)
    mixed, *saved = mixer_forward(proj)
    own_inputs = own_tokens.astype(F32)
    resid = own_inputs + quad_scatter(lambda r: mm(mixed[r], w_out, NT))
    ffn_in = quad_gather((resid * rms(resid) * gain_ffn).astype(BF16))
    gate, up_vals = mm(ffn_in, w_gate), mm(ffn_in, w_up)
    sig = jax.nn.sigmoid(gate)
    hidden = (gate * sig * up_vals).astype(BF16)
    d_hidden = mm(d_ffn, w_down)
    d_gate = (d_hidden * up_vals * (sig * (1.0 + gate * (1.0 - sig)))).astype(BF16)
    d_up = (d_hidden * (gate * sig)).astype(BF16)
    d_ffn_in = quad_scatter(lambda r: mm(d_gate[r], w_gate, NT) + mm(d_up[r], w_up, NT))
    down_sum = weight_sum(d_ffn, hidden)
    gate_sum = weight_sum(ffn_in, d_gate)
    up_sum = weight_sum(ffn_in, d_up)
    ffn = quad_scatter(lambda r: mm(hidden[r], w_down, NT))
    block_out = whole_rows(ring.order((live * (resid + ffn)).astype(BF16), width, back=True))
    d_norm, ffn_gain_part = norm_back(resid, gain_ffn, d_ffn_in)
    d_h = d_res + d_norm
    d_attn = quad_gather(d_h.astype(BF16))
    d_mixed = mm(d_attn, w_out)
    d_proj = mixer_backward(proj, saved, d_mixed)
    d_attn_in = quad_scatter(lambda r: mm(d_proj[r], w_in, NT))
    out_sum = weight_sum(d_attn, mixed)
    in_sum = weight_sum(attn_in, d_proj)
    d_input, attn_gain_part = norm_back(own_inputs, gain_attn, d_attn_in)
    input_grad = whole_rows(ring.order(d_h + d_input, width, back=True))

    both = jnp.stack([attn_gain_part, ffn_gain_part], axis=0)
    both = both + other_core(both)
    both = both.reshape(2, ring.count // 2, width)
    for stage in ring.stages[::-1]:
        size = stage[1]
        both = both.reshape(2, size, -1, width)
        parts = [ring.send(both[:, shift], stage, shift) for shift in range(1, size)]
        both = both[:, 0]
        for part in parts:
            both = both + part
    both = both.reshape(2, 2, shard)
    both = jnp.where(even, both[:, 0], both[:, 1]) + ring.swap(jnp.where(even, both[:, 1], both[:, 0]))

    def columns(pieces, start, stop):
        return jnp.concatenate([p[:, start:stop] for p in pieces], axis=1)

    return (
        block_out,
        input_grad,
        both[0],
        both[1],
        columns(in_sum, 0, KDIM),
        columns(in_sum, KDIM, 2 * KDIM),
        columns(in_sum, 2 * KDIM, 3 * KDIM),
        columns(in_sum, 3 * KDIM, 3 * KDIM + SLOTS),
        columns(out_sum, 0, KDIM),
        jnp.concatenate(gate_sum, axis=1),
        jnp.concatenate(up_sum, axis=1),
        jnp.concatenate(down_sum, axis=1),
    )


def body_by_kernels(
    tokens,
    seq_count,
    valid_len,
    attn_gain,
    ffn_gain,
    q_weight,
    k_weight,
    v_weight,
    forget_weight,
    out_weight,
    gate_weight,
    up_weight,
    down_weight,
    cotangent,
    *,
    ring,
):
    shard, dim = q_weight.shape[0], tokens.shape[1]
    width, hid = 2 * shard, gate_weight.shape[1] // 2
    over_y = lambda value: ring.send(value, ring.stages[1], 1)
    rows4 = (4, SEQ_LEN, dim)
    blocks = lambda value: value.reshape(-1, width, value.shape[-1])
    flat = lambda value: value.reshape(-1, value.shape[-1])
    half = dim // 2

    row = (SEQ_LEN, dim)
    vmem = lambda shape, kind=F32: pltpu.VMEM(shape, kind)
    tokens4 = 4 * SEQ_LEN
    cut = hid // 256 * 128
    full = (tokens4, dim)
    early, rest = [((4, width, EARLY), BF16)] * 2, [((2, width, hid - EARLY), BF16)] * 4
    (
        w_in, w_out, own, attn_in, d_res, d_ffn, gain_rows, proj, *saved, mixed, _,
        w_wide, w_down, resid, ffn_in, wide, hidden, down_over, down_own, down0, down1, down2, down3,
    ) = call(
        functools.partial(forward_all_kernel, hid, cut),
        "forward_all",
        0,
        (
            tokens,
            cotangent,
            seq_count,
            valid_len,
            attn_gain,
            ffn_gain,
            q_weight,
            k_weight,
            v_weight,
            forget_weight,
            out_weight,
            gate_weight,
            up_weight,
            down_weight,
        ),
        [ANY, ANY, SMEM, SMEM, VMEM, VMEM, ANY, ANY, ANY, VMEM] + [ANY] * 4,
        [((dim, WIDE), BF16), ((dim, KDIM), BF16), (row, BF16), (full, BF16), (row, F32), (full, BF16), ((8, dim), F32)]
        + [((tokens4, WIDE), F32), ((tokens4, 128), F32), ((tokens4, 128), F32)]
        + [((tokens4, SEQ_LEN), F32), ((tokens4, SEQ_LEN), F32), ((tokens4, KDIM), BF16), (rows4, F32)]
        + [((dim, 2 * hid), BF16), ((dim, hid), BF16), (row, F32), (full, BF16)]
        + [((tokens4, 2 * hid), F32), ((tokens4, hid), BF16)]
        + early
        + rest,
        [ANY] * 6 + [VMEM] + [ANY] * 19,
        [
            vmem((shard, 4 * KDIM + 128 + 3 * hid), BF16),
            vmem(full, BF16),
            vmem(full, BF16),
            vmem((tokens4, 128)),
            vmem((8, width, 128), BF16),
            vmem(row),
            vmem(row, BF16),
            vmem((shard, 256), BF16),
            vmem((tokens4, 128)),
            vmem((tokens4, 128)),
            vmem((tokens4, SEQ_LEN)),
            vmem((tokens4, SEQ_LEN)),
            vmem((tokens4, KDIM), BF16),
            vmem((dim, KDIM), BF16),
            vmem((2, 4, SEQ_LEN, width)),
        ]
        + quad_scratch(dim)
        + [
            vmem(row),
            vmem(row, BF16),
            vmem((2, dim, 256), BF16),
            vmem((hid // 128, tokens4, 256)),
            vmem((tokens4, hid), BF16),
            vmem((2, width, hid), BF16),
        ],
        360,
    )
    down_parts = [down0, down1, down2, down3]

    def exchange(over, parts):
        return [over_y(over)] + [ring.send(parts[d], ring.stages[0], d) for d in (1, 2, 3)]

    down_given = exchange(down_over, down_parts)
    gate, up_vals = wide[:, :hid], wide[:, hid:]
    sig = jax.nn.sigmoid(gate)
    d_hidden = mm(d_ffn, w_down)
    d_gate = (d_hidden * up_vals * (sig * (1.0 + gate * (1.0 - sig)))).astype(BF16)
    d_up = (d_hidden * (gate * sig)).astype(BF16)
    d_wide = jnp.concatenate([d_gate, d_up], axis=1)
    gate_terms = mm(ffn_in, d_wide[:, :hid], TN, BF16)
    d_ffn_terms = mm(d_wide, w_wide, NT).reshape(rows4)
    gate_sum, down_sum, d_h, d_attn, ffn_gains, up_over, up_own, *up_parts, ffn_terms = call(
        functools.partial(sum_ffn_kernel, hid, EARLY),
        "sum_ffn",
        2,
        (
            blocks(gate_terms),
            down_own,
            down_given[0],
            down_parts[0],
            *down_given[1:],
            d_ffn_terms,
            resid,
            gain_rows,
            d_res,
            ffn_in,
            d_wide,
            hidden,
            blocks(w_down),
        ),
        [ANY] * 9 + [VMEM] + [ANY] * 5,
        [((shard, 2 * hid), F32), ((shard, 2 * hid), F32), (row, F32), (rows4, BF16), ((8, dim), F32)]
        + early
        + rest
        + [((4 * SEQ_LEN, dim), F32)],
        [ANY] * 4 + [VMEM] + [ANY] * 7,
        sum_scratch(width, EARLY)
        + given_scratch(width, hid - EARLY)
        + [one for _, columns in thirds(hid) for one in sum_scratch(width, columns)]
        + quad_scratch(dim)
        + [vmem(row), vmem(row), vmem(row, BF16)]
        + [vmem((4 * SEQ_LEN, dim), BF16), vmem((4 * SEQ_LEN, hid), BF16), vmem((2, width, hid), BF16)]
        + [vmem((4 * SEQ_LEN, hid), BF16), vmem((2, width, hid), BF16), vmem((2, 4 * SEQ_LEN, width))],
        220,
    )
    d_attn = flat(d_attn)
    up_given = exchange(up_over, up_parts)
    d_proj = mixer_backward(proj, saved, mm(d_attn, w_out))
    d_attn_terms = mm(d_proj, w_in, NT).reshape(rows4)
    ffn_terms = ffn_terms.reshape(rows4)
    tail = width // 2
    up_sum, out_sum, q_sum, k_sum, v_sum, f_sum, input_grad, block_out, gain_sums = call(
        functools.partial(sum_last_kernel, hid, EARLY),
        "sum_last",
        3,
        (
            up_own,
            up_given[0],
            up_parts[0],
            *up_given[1:],
            blocks(mm(d_attn, mixed, TN, BF16)),
            blocks(mm(attn_in, d_proj, TN, BF16)),
            d_attn_terms,
            own,
            gain_rows,
            d_h,
            ffn_gains,
            ffn_terms,
            resid,
            seq_count,
            valid_len,
        ),
        [ANY] * 10 + [VMEM, ANY, VMEM, ANY, ANY, SMEM, SMEM],
        [((shard, 2 * hid), F32)]
        + [((shard, 2 * KDIM), F32)] * 4
        + [((shard, 256), F32), ((2 * SEQ_LEN, dim), F32), ((2 * SEQ_LEN, dim), BF16), ((8, tail), F32)],
        [ANY] * 8 + [VMEM],
        sum_scratch(width, EARLY)
        + sum_scratch(width, KDIM) * 4
        + sum_scratch(width, 128)
        + given_scratch(width, hid - EARLY)
        + quad_scratch(dim) * 2
        + [vmem(row, BF16), vmem(row), vmem(row), vmem(row, BF16), vmem((8, dim))]
        + [vmem((depth, 8, width)) for depth in (8, 8, 4, 3)]
        + [vmem((2, 8, tail)), vmem((8, tail))],
        280,
    )
    f_grad = jnp.concatenate([f_sum[:, :SLOTS], f_sum[:, 128 : 128 + SLOTS]], axis=1)
    return (
        block_out,
        input_grad,
        gain_sums[0],
        gain_sums[1],
        q_sum,
        k_sum,
        v_sum,
        f_grad,
        out_sum,
        gate_sum,
        up_sum,
        down_sum,
    )


def solution(mesh):
    ring = Ring(mesh.shape["dp"])
    body = body_by_kernels if ring.count == 16 else body_by_permutes
    split_one, split_two = P("dp"), P("dp", "head")
    row = P("dp", None)
    in_specs = (row, split_one, split_one, split_one, split_one) + (split_two,) * 8 + (row,)
    out_specs = (row, row, split_one, split_one) + (split_two,) * 8
    return jax.shard_map(
        functools.partial(body, ring=ring),
        mesh=mesh,
        in_specs=in_specs,
        out_specs=out_specs,
        check_vma=False,
    )
```
